32 devices in a mesh: dp: 2 (over x), sp: 4 (over y, core), fs: 4 (over z).
Axes of the slice: x: 2, y: 2, z: 4, core: 2. Of those that a mesh axis runs over, the one named last changes fastest.
Arguments:
- tokens: bfloat16 [8, 2048, 768], P('dp', ('sp', 'fs')), may hold values from -6 to 6
- expert_ids: int32 [8, 2048, 2], P('dp', ('sp', 'fs')), may hold values from 0 to 15, all different within a row
- fill_order: int32 [8, 2048], P('dp', ('sp', 'fs')), may hold values from 0 to 511
- attention_gain: bfloat16 [768], P(('sp', 'fs')), may hold values from 0.5 to 1.5
- query_weight: bfloat16 [768, 768], P(('sp', 'fs')), may hold values from -0.21875 to 0.21875
- key_weight: bfloat16 [768, 768], P(('sp', 'fs')), may hold values from -0.21875 to 0.21875
- value_weight: bfloat16 [768, 768], P(('sp', 'fs')), may hold values from -0.21875 to 0.21875
- output_weight: bfloat16 [768, 768], P(('sp', 'fs')), may hold values from -1.25 to 1.25
- mixer_gain: bfloat16 [768], P(('sp', 'fs')), may hold values from 0.5 to 1.5
- router_weight: bfloat16 [768, 16], P(('sp', 'fs')), may hold values from -0.15625 to 0.15625
- shared_gate: bfloat16 [768, 2048], P(('sp', 'fs')), may hold values from -0.21875 to 0.21875
- shared_up: bfloat16 [768, 2048], P(('sp', 'fs')), may hold values from -0.21875 to 0.21875
- shared_down: bfloat16 [2048, 768], P(('sp', 'fs')), may hold values from -0.125 to 0.125
- expert_gate: bfloat16 [16, 768, 2048], P('fs', 'sp'), may hold values from -0.21875 to 0.21875
- expert_up: bfloat16 [16, 768, 2048], P('fs', 'sp'), may hold values from -0.21875 to 0.21875
- expert_down: bfloat16 [16, 768, 2048], P('fs', 'sp'), may hold values from -0.125 to 0.125
- cotangent: bfloat16 [8, 2048, 768], P('dp', ('sp', 'fs')), may hold values from -6 to 6
Outputs:
- output: bfloat16 [8, 2048, 768], P('dp', ('sp', 'fs'))
- grad_tokens: float32 [8, 2048, 768], P('dp', ('sp', 'fs'))
- grad_attention_gain: float32 [768], P(('sp', 'fs'))
- grad_query_weight: float32 [768, 768], P(('sp', 'fs'))
- grad_key_weight: float32 [768, 768], P(('sp', 'fs'))
- grad_value_weight: float32 [768, 768], P(('sp', 'fs'))
- grad_output_weight: float32 [768, 768], P(('sp', 'fs'))
- grad_mixer_gain: float32 [768], P(('sp', 'fs'))
- grad_router_weight: float32 [768, 16], P(('sp', 'fs'))
- grad_shared_gate: float32 [768, 2048], P(('sp', 'fs'))
- grad_shared_up: float32 [768, 2048], P(('sp', 'fs'))
- grad_shared_down: float32 [2048, 768], P(('sp', 'fs'))
- grad_expert_gate: float32 [16, 768, 2048], P('fs', 'sp')
- grad_expert_up: float32 [16, 768, 2048], P('fs', 'sp')
- grad_expert_down: float32 [16, 768, 2048], P('fs', 'sp')
The draws below stay inside these ranges and needn't reach their ends.
Inputs may be any that keep to these rules, and one draw needn't show every extreme that they name: `expert_ids`: the 2 ids of one token differ.
All inputs are finite; a program needn't handle non-finite values.
Results may differ from the reference program's by a relative error of at most 0.024.
Values may be sent and summed in bfloat16 or wider, within the bound.
A program may use at most 320 MiB of HBM per device.

```python
import math
import jax
import jax.numpy as jnp
from jax import lax

D = 768
HEADS = 12
HEAD_DIM = 64
EFF = 2048
SFF = 2048
EXPERTS = 16
TOPK = 2
SEQ_DEV = 4
LEN_DEV = 128
SEQS = 8
LEN = 2048
CAP = 72


def draw_fill_order(key, part):
    group_count = SEQS // SEQ_DEV
    piece_count = LEN // LEN_DEV
    subkeys = jax.random.split(key, group_count * piece_count)

    def shuffle_one(subkey):
        return jax.random.permutation(subkey, SEQ_DEV * LEN_DEV).astype(jnp.int32)
    shuffled = jax.vmap(shuffle_one)(subkeys)
    arranged = shuffled.reshape(group_count, piece_count, SEQ_DEV, LEN_DEV)
    arranged = jnp.transpose(arranged, (0, 2, 1, 3))
    return arranged.reshape(SEQS, LEN).astype(jnp.int32)


def level_of(own_key, extent, cuts, least, high):
    loudness = 1.0
    for dim, parts in cuts:
        draws = jax.random.uniform(jax.random.fold_in(jax.random.fold_in(own_key, 6), dim), (parts,), jnp.float32, least / len(cuts), high / len(cuts))
        loudness = loudness * jnp.repeat(jnp.exp(draws), extent[dim] // parts).reshape((-1,) + (1,) * (len(extent) - 1 - dim))
    return loudness


def picks_of(rng, rows, count, top, lift):
    order = jax.random.permutation(jax.random.fold_in(rng, 1), count)
    boost = order
    for power in range(3):
        boost = boost * boost // count
    boost = boost * lift // count
    chance = jax.random.randint(jax.random.fold_in(rng, 2), (rows, count), 0, 4096) + boost
    holders = jax.random.permutation(jax.random.fold_in(rng, 3), rows)[jnp.arange(count) % rows]
    chance = jnp.where(jnp.arange(rows)[:, None] == holders[None, :], 1 << 14, chance)
    priority = chance * count + jnp.arange(count)
    return lax.top_k(priority.astype(jnp.int32), top)[1].astype(jnp.int32)


def scatter_about(own_key, shape, spread, limit, cuts=(), kind=jnp.bfloat16):
    loudness = level_of(own_key, shape, cuts, -0.22, 0.18) if cuts else 1.0
    drawn = jax.random.normal(own_key, shape, jnp.float32) * spread * loudness
    return jnp.minimum(jnp.maximum(drawn, -limit), limit).astype(kind)


def setup_inputs(seed: int = 0) -> dict:
    streams_of = jax.random.split(jax.random.key(seed), 18)
    tokens = scatter_about(streams_of[0], (SEQS, LEN, D), 1.0, 6.0, ((0, 2), (1, 16)))
    expert_ids = picks_of(streams_of[1], SEQS * LEN, EXPERTS, TOPK, 1024).reshape((SEQS, LEN, TOPK))
    fill_order = draw_fill_order(jax.random.fold_in(streams_of[17], 71), 0)
    attention_gain = jnp.clip(1.0 + 0.1 * jax.random.normal(streams_of[3], (D,), jnp.float32), 0.5, 1.5).astype(jnp.bfloat16)
    query_weight = scatter_about(streams_of[4], (D, D), D ** -0.5, 0.21875, ((0, 16),))
    key_weight = scatter_about(streams_of[5], (D, D), D ** -0.5, 0.21875, ((0, 16),))
    value_weight = scatter_about(streams_of[6], (D, D), D ** -0.5, 0.21875, ((0, 16),))
    output_weight = scatter_about(streams_of[7], (D, D), (D // 32) ** -0.5, 1.25, ((0, 16),))
    mixer_gain = jnp.clip(1.0 + 0.1 * jax.random.normal(streams_of[8], (D,), jnp.float32), 0.5, 1.5).astype(jnp.bfloat16)
    router_weight = scatter_about(streams_of[9], (D, EXPERTS), (2 * D) ** -0.5, 0.15625, ((0, 16),))
    shared_gate = scatter_about(streams_of[10], (D, SFF), D ** -0.5, 0.21875, ((0, 16),))
    shared_up = scatter_about(streams_of[11], (D, SFF), D ** -0.5, 0.21875, ((0, 16),))
    shared_down = scatter_about(streams_of[12], (SFF, D), SFF ** -0.5, 0.125, ((0, 16),))
    expert_gate = scatter_about(streams_of[13], (EXPERTS, D, EFF), D ** -0.5, 0.21875, ((0, 4), (1, 4)))
    expert_up = scatter_about(streams_of[14], (EXPERTS, D, EFF), D ** -0.5, 0.21875, ((0, 4), (1, 4)))
    expert_down = scatter_about(streams_of[15], (EXPERTS, D, EFF), EFF ** -0.5, 0.125, ((0, 4), (1, 4)))
    cotangent = scatter_about(streams_of[16], (SEQS, LEN, D), 1.0, 6.0, ((0, 2), (1, 16)))
    return {"tokens": tokens, "expert_ids": expert_ids, "fill_order": fill_order, "attention_gain": attention_gain, "query_weight": query_weight, "key_weight": key_weight, "value_weight": value_weight, "output_weight": output_weight, "mixer_gain": mixer_gain, "router_weight": router_weight, "shared_gate": shared_gate, "shared_up": shared_up, "shared_down": shared_down, "expert_gate": expert_gate, "expert_up": expert_up, "expert_down": expert_down, "cotangent": cotangent}


@jax.custom_vjp
def low(v):
    return lax.optimization_barrier(v.astype(jnp.bfloat16)).astype(jnp.float32)

@jax.custom_vjp
def low_back(v):
    return v

def low_keep(v):
    return (low(v), None)

def low_pass(kept, grad):
    return (grad,)

def back_keep(v):
    return (v, None)

def back_low(kept, grad):
    return (low(grad),)
low.defvjp(low_keep, low_pass)
low_back.defvjp(back_keep, back_low)
EPSILON = 1e-06
MASKED = -1e+30
HIGHEST = lax.Precision.HIGHEST

def norm_apply(values, gain_row):
    inverse_root = lax.rsqrt(lax.optimization_barrier(jnp.mean(values * values, axis=-1, keepdims=True)) + EPSILON)
    return values * inverse_root * gain_row

def swish(values):
    return values * jax.nn.sigmoid(values)

def project(values, matrix):
    return jnp.einsum('...d,df->...f', values, matrix, precision=HIGHEST)

def rotate(values, positions):
    half_dim = values.shape[-1] // 2
    frequency = 10000.0 ** (-jnp.arange(half_dim, dtype=jnp.float32) / half_dim)
    angles = positions.astype(jnp.float32)[:, None] * frequency[None, :]
    cosine_table = jnp.cos(angles)[:, None, :]
    sine_table = jnp.sin(angles)[:, None, :]
    front_part = values[..., :half_dim]
    back_part = values[..., half_dim:]
    return jnp.concatenate([front_part * cosine_table - back_part * sine_table, back_part * cosine_table + front_part * sine_table], axis=-1)

def to_blocks(array):
    trailing = array.shape[2:]
    arranged = array.reshape((SEQS // SEQ_DEV, SEQ_DEV, LEN // LEN_DEV, LEN_DEV) + trailing)
    arranged = jnp.moveaxis(arranged, 2, 1)
    return arranged.reshape((SEQS * LEN,) + trailing)

def from_blocks(array):
    trailing = array.shape[1:]
    arranged = array.reshape((SEQS // SEQ_DEV, LEN // LEN_DEV, SEQ_DEV, LEN_DEV) + trailing)
    arranged = jnp.moveaxis(arranged, 1, 2)
    return arranged.reshape((SEQS, LEN) + trailing)

def block_ranks(pair):
    choices, fill_rank = pair
    onehot_choice = (choices[:, :, None] == jnp.arange(EXPERTS, dtype=jnp.int32)[None, None, :]).astype(jnp.int32)
    per_token = lax.optimization_barrier(jnp.sum(onehot_choice, axis=1))
    earlier = (fill_rank[None, :] < fill_rank[:, None]).astype(jnp.int32)
    counts = lax.optimization_barrier(jnp.sum(earlier[:, :, None] * per_token[None, :, :], axis=1))
    return lax.optimization_barrier(jnp.sum(counts[:, None, :] * onehot_choice, axis=2))

def reference(tokens, expert_ids, fill_order, attention_gain, query_weight, key_weight, value_weight, output_weight, mixer_gain, router_weight, shared_gate, shared_up, shared_down, expert_gate, expert_up, expert_down, cotangent):
    block_count = SEQS // SEQ_DEV * (LEN // LEN_DEV)
    block_tokens = SEQ_DEV * LEN_DEV
    flat_choices = to_blocks(expert_ids)
    choices = flat_choices.reshape(block_count, block_tokens, TOPK)
    orders = to_blocks(fill_order).reshape(block_count, block_tokens)
    slot_ranks = lax.map(block_ranks, (choices, orders))
    owners = jnp.arange(block_count, dtype=jnp.int32)[:, None, None]
    dummy_slot = EXPERTS * block_count * CAP
    slots = jnp.where(slot_ranks < CAP, choices * (block_count * CAP) + owners * CAP + slot_ranks, dummy_slot).reshape(-1)
    expert_onehot = (flat_choices[:, :, None] == jnp.arange(EXPERTS, dtype=jnp.int32)[None, None, :]).astype(jnp.float32)
    score_scale = HEAD_DIM ** (-0.5)

    def attend_block(block_pair, keys_all, values_all):
        query_block, start_row = block_pair
        raw_scores = low_back(jnp.einsum('qhd,khd->hqk', query_block, keys_all, precision=HIGHEST))
        query_pos = start_row + jnp.arange(query_block.shape[0], dtype=jnp.int32)
        key_pos = jnp.arange(keys_all.shape[0], dtype=jnp.int32)
        allowed = key_pos[None, None, :] <= query_pos[None, :, None]
        scores = jnp.where(allowed, raw_scores * score_scale, MASKED)
        shifted = jnp.exp(scores - lax.optimization_barrier(jnp.max(scores, axis=-1, keepdims=True)))
        softmax_weights = shifted / lax.optimization_barrier(jnp.sum(shifted, axis=-1, keepdims=True))
        return jnp.einsum('hqk,khd->qhd', low(softmax_weights), values_all, precision=HIGHEST)

    def attend_sequence(triple):
        queries, keys_all, values_all = triple
        block_rows = math.gcd(LEN, 512)
        grouped = queries.reshape(LEN // block_rows, block_rows, HEADS, HEAD_DIM)
        starts = jnp.arange(LEN // block_rows, dtype=jnp.int32) * block_rows

        def one_block(block_pair):
            return attend_block(block_pair, keys_all, values_all)
        return lax.map(jax.checkpoint(one_block), (grouped, starts)).reshape(LEN, HEADS, HEAD_DIM)

    def forward_layer(residual, params):
        gain_one, query_matrix, key_matrix, value_matrix, output_matrix, gain_two, router_matrix, shared_gate_matrix, shared_up_matrix, shared_down_matrix, expert_gate_matrix, expert_up_matrix, expert_down_matrix = params
        normed = low(norm_apply(residual, gain_one))
        query_raw = low(low_back(project(normed, query_matrix)))
        key_raw = low(low_back(project(normed, key_matrix)))
        value_raw = low(low_back(project(normed, value_matrix)))
        head_shape = (SEQS, LEN, HEADS, HEAD_DIM)
        positions = jnp.arange(LEN, dtype=jnp.int32)
        query_rot = low(rotate(query_raw.reshape(head_shape), positions))
        key_rot = low(rotate(key_raw.reshape(head_shape), positions))
        attended = lax.map(jax.checkpoint(attend_sequence), (query_rot, key_rot, value_raw.reshape(head_shape)))
        attended = low(low_back(attended.reshape(SEQS, LEN, D)))
        middle = residual + low_back(project(attended, output_matrix))
        mixed_in = low(norm_apply(middle, gain_two))
        shared_gate_val = low_back(project(mixed_in, shared_gate_matrix))
        shared_up_val = low_back(project(mixed_in, shared_up_matrix))
        shared_hidden = low(swish(shared_gate_val) * shared_up_val)
        shared_out = low_back(project(shared_hidden, shared_down_matrix))
        token_rows = to_blocks(mixed_in)
        logits = low_back(project(token_rows, router_matrix))
        shifted = jnp.exp(logits - lax.optimization_barrier(jnp.max(logits, axis=-1, keepdims=True)))
        router_probs = shifted / lax.optimization_barrier(jnp.sum(shifted, axis=-1, keepdims=True))
        picked = lax.optimization_barrier(jnp.sum(router_probs[:, None, :] * expert_onehot, axis=2))
        gate_weights = picked / lax.optimization_barrier(jnp.sum(picked, axis=1, keepdims=True))
        buffer = jnp.zeros((dummy_slot + 1, D), jnp.float32).at[slots].add(jnp.repeat(token_rows, TOPK, axis=0))
        buffer = low_back(buffer[:dummy_slot].reshape(EXPERTS, block_count * CAP, D))
        expert_gate_val = low_back(jnp.einsum('ecd,edf->ecf', buffer, expert_gate_matrix, precision=HIGHEST))
        expert_up_val = low_back(jnp.einsum('ecd,edf->ecf', buffer, expert_up_matrix, precision=HIGHEST))
        expert_hidden = low(swish(expert_gate_val) * expert_up_val)
        expert_out = low(low_back(jnp.einsum('ecf,edf->ecd', expert_hidden, expert_down_matrix, precision=HIGHEST)))
        padded = jnp.concatenate([expert_out.reshape(dummy_slot, D), jnp.zeros((1, D), jnp.float32)], axis=0)
        returned = padded[slots].reshape(token_rows.shape[0], TOPK, D)
        combined = lax.optimization_barrier(jnp.sum(gate_weights[:, :, None] * returned, axis=1))
        return middle + shared_out + from_blocks(combined)
    start_values = tuple((argument.astype(jnp.float32) for argument in (attention_gain, query_weight, key_weight, value_weight, output_weight, mixer_gain, router_weight, shared_gate, shared_up, shared_down, expert_gate, expert_up, expert_down)))
    result, pull_back = jax.vjp(forward_layer, tokens.astype(jnp.float32), start_values)
    grad_tokens, grad_params = pull_back(cotangent.astype(jnp.float32))
    return (result.astype(jnp.bfloat16), grad_tokens, grad_params[0], grad_params[1], grad_params[2], grad_params[3], grad_params[4], grad_params[5], grad_params[6], grad_params[7], grad_params[8], grad_params[9], grad_params[10], grad_params[11], grad_params[12])
```

```python
import functools
import math

import jax
import jax.numpy as jnp
from jax import lax
from jax.experimental import pallas as pl
from jax.experimental.pallas import tpu as pltpu
from jax.sharding import PartitionSpec as P

HEADS = 12
HEAD_DIM = 64
EXPERTS = 16
TOPK = 2
CAP = 72


EPSILON = 1e-06
MASKED = -1e30


def norm_apply(values, gain_row):
    inverse_root = lax.rsqrt(jnp.mean(values * values, axis=-1, keepdims=True) + EPSILON)
    return values * inverse_root * gain_row


def swish(values):
    return values * jax.nn.sigmoid(values)


def glu_product(gate_part, up_part):
    return swish(gate_part) * up_part


def rotate(values, positions):
    half_dim = values.shape[-1] // 2
    frequency = 10000.0 ** (-jnp.arange(half_dim, dtype=jnp.float32) / half_dim)
    angles = positions.astype(jnp.float32)[:, None] * frequency[None, :]
    cosine_table = jnp.cos(angles)[:, None, :]
    sine_table = jnp.sin(angles)[:, None, :]
    front_part = values[..., :half_dim]
    back_part = values[..., half_dim:]
    return jnp.concatenate(
        [
            front_part * cosine_table - back_part * sine_table,
            back_part * cosine_table + front_part * sine_table,
        ],
        axis=-1,
    )


def place_rows(indices, quarter_rows, segment_rows, fs_count):
    source_device = indices // quarter_rows
    row_inside = indices % quarter_rows
    return (
        row_inside // segment_rows * fs_count + source_device
    ) * segment_rows + row_inside % segment_rows


def to_heads(stacked):
    return lax.all_to_all(stacked, "sp", split_axis=3, concat_axis=2, tiled=True)


def to_tokens(stacked):
    return lax.all_to_all(stacked, "sp", split_axis=2, concat_axis=3, tiled=True)


def to_experts(buffer):
    return lax.all_to_all(buffer, "fs", split_axis=1, concat_axis=0, tiled=True)


def from_experts(buffer):
    return lax.all_to_all(buffer, "fs", split_axis=0, concat_axis=1, tiled=True)


def score_grads(
    query_part,
    query_rows,
    key_part,
    value_part,
    key_rows,
    grad_part,
    lse_part,
    delta_part,
    score_scale,
):
    allowed = key_rows[None, None, None, :] <= query_rows[None, None, :, None]
    scores = (
        jnp.einsum("bqhd,bkhd->bhqk", query_part, key_part, preferred_element_type=jnp.float32)
        * score_scale
    )
    weights = jnp.where(allowed, jnp.exp(scores - lse_part[..., None]), 0.0)
    grad_value = jnp.einsum(
        "bhqk,bqhd->bkhd",
        weights.astype(jnp.bfloat16),
        grad_part,
        preferred_element_type=jnp.float32,
    )
    grad_weights = jnp.einsum(
        "bqhd,bkhd->bhqk", grad_part, value_part, preferred_element_type=jnp.float32
    )
    grad_scores = (weights * (grad_weights - delta_part[..., None]) * score_scale).astype(
        jnp.bfloat16
    )
    grad_query = jnp.einsum(
        "bhqk,bkhd->bqhd", grad_scores, key_part, preferred_element_type=jnp.float32
    )
    grad_key = jnp.einsum(
        "bhqk,bqhd->bkhd", grad_scores, query_part, preferred_element_type=jnp.float32
    )
    return (grad_query, grad_key, grad_value)


def per_device(
    tokens,
    expert_ids,
    fill_order,
    attention_gain,
    query_weight,
    key_weight,
    value_weight,
    output_weight,
    mixer_gain,
    router_weight,
    shared_gate,
    shared_up,
    shared_down,
    expert_gate,
    expert_up,
    expert_down,
    cotangent,
):
    seq_count, seg_rows, model_width = tokens.shape
    token_count = seq_count * seg_rows
    fs_count = lax.axis_size("fs")
    sp_count = lax.axis_size("sp")
    fs_place = lax.axis_index("fs")
    local_heads = HEADS // sp_count
    score_scale = HEAD_DIM ** (-0.5)
    (
        gain_full,
        query_full,
        key_full,
        value_full,
        output_full,
        mixer_full,
        router_full,
        shared_gate_full,
        shared_up_full,
        shared_down_full,
    ) = (
        lax.all_gather(attention_gain, ("sp", "fs"), axis=0, tiled=True),
        lax.all_gather(query_weight, ("sp", "fs"), axis=0, tiled=True),
        lax.all_gather(key_weight, ("sp", "fs"), axis=0, tiled=True),
        lax.all_gather(value_weight, ("sp", "fs"), axis=0, tiled=True),
        lax.all_gather(output_weight, ("sp", "fs"), axis=0, tiled=True),
        lax.all_gather(mixer_gain, ("sp", "fs"), axis=0, tiled=True),
        lax.all_gather(router_weight, ("sp", "fs"), axis=0, tiled=True),
        lax.all_gather(shared_gate, ("sp", "fs"), axis=0, tiled=True),
        lax.all_gather(shared_up, ("sp", "fs"), axis=0, tiled=True),
        lax.all_gather(shared_down, ("sp", "fs"), axis=0, tiled=True),
    )
    expert_gate_full, expert_up_full, expert_down_full = (
        lax.all_gather(expert_gate, "sp", axis=1, tiled=True),
        lax.all_gather(expert_up, "sp", axis=1, tiled=True),
        lax.all_gather(expert_down, "sp", axis=1, tiled=True),
    )
    residual = tokens.astype(jnp.float32)
    gain_one = gain_full.astype(jnp.float32)
    gain_two = mixer_full.astype(jnp.float32)
    normed = norm_apply(residual, gain_one).astype(jnp.bfloat16)
    query_raw = jnp.dot(normed, query_full, preferred_element_type=jnp.float32).astype(jnp.bfloat16)
    key_raw = jnp.dot(normed, key_full, preferred_element_type=jnp.float32).astype(jnp.bfloat16)
    value_raw = jnp.dot(normed, value_full, preferred_element_type=jnp.float32).astype(jnp.bfloat16)
    heads_view = to_heads(jnp.stack([query_raw, key_raw, value_raw]))
    quarter_rows = heads_view.shape[2]
    head_shape = (seq_count, quarter_rows, local_heads, HEAD_DIM)
    flat_width = local_heads * HEAD_DIM
    own_rows = place_rows(
        fs_place * quarter_rows + jnp.arange(quarter_rows, dtype=jnp.int32),
        quarter_rows,
        seg_rows,
        fs_count,
    )

    def rotate_own(values):
        return rotate(values, own_rows)

    query_rot = rotate_own(heads_view[0].reshape(head_shape).astype(jnp.float32)).astype(
        jnp.bfloat16
    )
    key_rot = rotate_own(heads_view[1].reshape(head_shape).astype(jnp.float32)).astype(jnp.bfloat16)
    key_flat = key_rot.reshape(seq_count, quarter_rows, flat_width)
    value_flat = heads_view[2]
    keys_all, values_all = (
        lax.all_gather(key_flat, "fs", axis=1, tiled=True),
        lax.all_gather(value_flat, "fs", axis=1, tiled=True),
    )
    total_rows = keys_all.shape[1]
    block_rows = math.gcd(quarter_rows, 512)
    part_shape = (seq_count, block_rows, local_heads, HEAD_DIM)
    offsets = jnp.arange(total_rows // block_rows, dtype=jnp.int32) * block_rows

    def key_slices(offset):
        key_part = lax.dynamic_slice_in_dim(keys_all, offset, block_rows, 1).reshape(part_shape)
        value_part = lax.dynamic_slice_in_dim(values_all, offset, block_rows, 1).reshape(part_shape)
        key_rows = place_rows(
            offset + jnp.arange(block_rows, dtype=jnp.int32), quarter_rows, seg_rows, fs_count
        )
        return (key_part, value_part, key_rows)

    def forward_block(carried, offset):
        running_max, running_sum, running_acc = carried
        key_part, value_part, key_rows = key_slices(offset)
        allowed = key_rows[None, None, None, :] <= own_rows[None, None, :, None]
        scores = (
            jnp.einsum("bqhd,bkhd->bhqk", query_rot, key_part, preferred_element_type=jnp.float32)
            * score_scale
        )
        scores = jnp.where(allowed, scores, MASKED)
        new_max = jnp.maximum(running_max, jnp.max(scores, axis=-1))
        weights = jnp.where(allowed, jnp.exp(scores - new_max[..., None]), 0.0)
        factor = jnp.exp(running_max - new_max)
        running_sum = running_sum * factor + jnp.sum(weights, axis=-1)
        running_acc = running_acc * factor[..., None] + jnp.einsum(
            "bhqk,bkhd->bhqd",
            weights.astype(jnp.bfloat16),
            value_part,
            preferred_element_type=jnp.float32,
        )
        return ((new_max, running_sum, running_acc), None)

    start_state = (
        jnp.full((seq_count, local_heads, quarter_rows), MASKED, jnp.float32),
        jnp.zeros((seq_count, local_heads, quarter_rows), jnp.float32),
        jnp.zeros((seq_count, local_heads, quarter_rows, HEAD_DIM), jnp.float32),
    )
    (final_max, final_sum, final_acc), _ = lax.scan(forward_block, start_state, offsets)
    attended_heads = (final_acc / final_sum[..., None]).astype(jnp.bfloat16)
    log_total = final_max + jnp.log(final_sum)
    attended_view = jnp.transpose(attended_heads, (0, 2, 1, 3))
    attended_flat = attended_view.reshape(seq_count, quarter_rows, flat_width)
    attended_tokens = to_tokens(attended_flat[None])[0]
    middle = residual + jnp.dot(attended_tokens, output_full, preferred_element_type=jnp.float32)
    mixed_in = norm_apply(middle, gain_two).astype(jnp.bfloat16)
    token_rows = mixed_in.reshape(token_count, model_width)
    logits = jnp.dot(token_rows, router_full, preferred_element_type=jnp.float32)
    choices = expert_ids.reshape(token_count, TOPK)
    expert_onehot = choices[:, :, None] == jnp.arange(EXPERTS, dtype=jnp.int32)[None, None, :]
    onehot_float = expert_onehot.astype(jnp.float32)

    def gate_values(raw_logits):
        shifted = jnp.exp(raw_logits - jnp.max(raw_logits, axis=-1, keepdims=True))
        router_probs = shifted / jnp.sum(shifted, axis=-1, keepdims=True)
        picked = jnp.sum(router_probs[:, None, :] * onehot_float, axis=2)
        return picked / jnp.sum(picked, axis=1, keepdims=True)

    gate_weights, gate_pull = jax.vjp(gate_values, logits)
    shared_gate_val = jnp.dot(mixed_in, shared_gate_full, preferred_element_type=jnp.float32)
    shared_up_val = jnp.dot(mixed_in, shared_up_full, preferred_element_type=jnp.float32)
    shared_hidden_full, shared_pull = jax.vjp(glu_product, shared_gate_val, shared_up_val)
    shared_hidden = shared_hidden_full.astype(jnp.bfloat16)
    shared_out = jnp.dot(shared_hidden, shared_down_full, preferred_element_type=jnp.float32)
    onehot_int = expert_onehot.astype(jnp.int32)
    per_token = jnp.sum(onehot_int, axis=1)
    fill_rank = fill_order.reshape(token_count)
    earlier = (fill_rank[None, :] < fill_rank[:, None]).astype(jnp.int32)
    counts = jnp.dot(earlier, per_token, preferred_element_type=jnp.int32)
    slot_ranks = jnp.sum(counts[:, None, :] * onehot_int, axis=2)
    slot_total = CAP * EXPERTS
    slots = jnp.where(slot_ranks < CAP, slot_ranks * EXPERTS + choices, slot_total).reshape(-1)
    outgoing = (
        jnp.zeros((slot_total, model_width), jnp.bfloat16)
        .at[slots]
        .set(jnp.repeat(token_rows, TOPK, axis=0), mode="drop")
    )
    incoming = to_experts(outgoing.reshape(CAP, EXPERTS, model_width))
    expert_gate_val = jnp.einsum(
        "red,edf->ref", incoming, expert_gate_full, preferred_element_type=jnp.float32
    )
    expert_up_val = jnp.einsum(
        "red,edf->ref", incoming, expert_up_full, preferred_element_type=jnp.float32
    )
    expert_hidden_full, expert_pull = jax.vjp(glu_product, expert_gate_val, expert_up_val)
    expert_hidden = expert_hidden_full.astype(jnp.bfloat16)
    expert_out = jnp.einsum(
        "ref,edf->red", expert_hidden, expert_down_full, preferred_element_type=jnp.float32
    ).astype(jnp.bfloat16)
    returned = from_experts(expert_out).reshape(slot_total, model_width)
    padded = jnp.concatenate([returned, jnp.zeros((1, model_width), jnp.bfloat16)], axis=0)
    picked_rows = padded[slots].reshape(token_count, TOPK, model_width).astype(jnp.float32)
    combined = jnp.sum(gate_weights[:, :, None] * picked_rows, axis=1)
    result = (
        middle.reshape(token_count, model_width)
        + shared_out.reshape(token_count, model_width)
        + combined
    )
    output = result.astype(jnp.bfloat16).reshape(seq_count, seg_rows, model_width)
    grad_result = cotangent.astype(jnp.float32).reshape(token_count, model_width)
    grad_gates = jnp.sum(grad_result[:, None, :] * picked_rows, axis=2)
    grad_slots = (
        (gate_weights[:, :, None] * grad_result[:, None, :])
        .astype(jnp.bfloat16)
        .reshape(token_count * TOPK, model_width)
    )
    grad_outgoing = (
        jnp.zeros((slot_total, model_width), jnp.bfloat16).at[slots].set(grad_slots, mode="drop")
    )
    grad_incoming = to_experts(grad_outgoing.reshape(CAP, EXPERTS, model_width))
    grad_expert_down = jnp.einsum(
        "red,ref->edf", grad_incoming, expert_hidden, preferred_element_type=jnp.float32
    )
    grad_expert_hidden = jnp.einsum(
        "red,edf->ref", grad_incoming, expert_down_full, preferred_element_type=jnp.float32
    )
    grad_gate_part, grad_up_part = expert_pull(grad_expert_hidden)
    grad_gate_part = grad_gate_part.astype(jnp.bfloat16)
    grad_up_part = grad_up_part.astype(jnp.bfloat16)
    grad_expert_gate = jnp.einsum(
        "red,ref->edf", incoming, grad_gate_part, preferred_element_type=jnp.float32
    )
    grad_expert_up = jnp.einsum(
        "red,ref->edf", incoming, grad_up_part, preferred_element_type=jnp.float32
    )
    grad_pair_rows = (
        jnp.einsum(
            "ref,edf->red", grad_gate_part, expert_gate_full, preferred_element_type=jnp.float32
        )
        + jnp.einsum(
            "ref,edf->red", grad_up_part, expert_up_full, preferred_element_type=jnp.float32
        )
    ).astype(jnp.bfloat16)
    grad_returned = from_experts(grad_pair_rows).reshape(slot_total, model_width)
    grad_padded = jnp.concatenate(
        [grad_returned, jnp.zeros((1, model_width), jnp.bfloat16)], axis=0
    )
    grad_mixed = jnp.sum(
        grad_padded[slots].reshape(token_count, TOPK, model_width).astype(jnp.float32), axis=1
    )
    (grad_logits,) = gate_pull(grad_gates)
    grad_logits = grad_logits.astype(jnp.bfloat16)
    grad_router = jnp.einsum(
        "td,te->de", token_rows, grad_logits, preferred_element_type=jnp.float32
    )
    grad_mixed = grad_mixed + jnp.einsum(
        "te,de->td", grad_logits, router_full, preferred_element_type=jnp.float32
    )
    grad_shared_out = grad_result.astype(jnp.bfloat16).reshape(seq_count, seg_rows, model_width)
    grad_shared_down = jnp.einsum(
        "blf,bld->fd", shared_hidden, grad_shared_out, preferred_element_type=jnp.float32
    )
    grad_shared_hidden = jnp.einsum(
        "bld,fd->blf", grad_shared_out, shared_down_full, preferred_element_type=jnp.float32
    )
    grad_shared_gate_part, grad_shared_up_part = shared_pull(grad_shared_hidden)
    grad_shared_gate_part = grad_shared_gate_part.astype(jnp.bfloat16)
    grad_shared_up_part = grad_shared_up_part.astype(jnp.bfloat16)
    grad_shared_gate = jnp.einsum(
        "bld,blf->df", mixed_in, grad_shared_gate_part, preferred_element_type=jnp.float32
    )
    grad_shared_up = jnp.einsum(
        "bld,blf->df", mixed_in, grad_shared_up_part, preferred_element_type=jnp.float32
    )
    grad_mixed = (
        grad_mixed.reshape(seq_count, seg_rows, model_width)
        + jnp.einsum(
            "blf,df->bld",
            grad_shared_gate_part,
            shared_gate_full,
            preferred_element_type=jnp.float32,
        )
        + jnp.einsum(
            "blf,df->bld", grad_shared_up_part, shared_up_full, preferred_element_type=jnp.float32
        )
    )
    _, norm_two_pull = jax.vjp(norm_apply, middle, gain_two)
    grad_middle_part, grad_gain_two = norm_two_pull(grad_mixed)
    grad_middle = grad_result.reshape(seq_count, seg_rows, model_width) + grad_middle_part
    grad_proj = grad_middle.astype(jnp.bfloat16)
    grad_output_matrix = jnp.einsum(
        "bld,ble->de", attended_tokens, grad_proj, preferred_element_type=jnp.float32
    )
    grad_attended = jnp.einsum(
        "ble,de->bld", grad_proj, output_full, preferred_element_type=jnp.float32
    ).astype(jnp.bfloat16)
    grad_attended_heads = to_heads(grad_attended[None])[0].reshape(head_shape)
    delta_rows = jnp.einsum(
        "bqhd,bqhd->bhq",
        grad_attended_heads,
        attended_flat.reshape(head_shape),
        preferred_element_type=jnp.float32,
    )

    def key_step(grad_query, offset):
        key_part, value_part, key_rows = key_slices(offset)
        part_query, part_key, part_value = score_grads(
            query_rot,
            own_rows,
            key_part,
            value_part,
            key_rows,
            grad_attended_heads,
            log_total,
            delta_rows,
            score_scale,
        )
        flat_shape = (seq_count, block_rows, flat_width)
        return (
            grad_query + part_query,
            (part_key.reshape(flat_shape), part_value.reshape(flat_shape)),
        )

    grad_query_rot, (key_terms, value_terms) = lax.scan(
        key_step, jnp.zeros(head_shape, jnp.float32), offsets
    )
    own_keys, own_values = (
        lax.psum_scatter(
            key_terms.astype(jnp.bfloat16), "fs", scatter_dimension=0, tiled=True
        ).astype(jnp.float32),
        lax.psum_scatter(
            value_terms.astype(jnp.bfloat16), "fs", scatter_dimension=0, tiled=True
        ).astype(jnp.float32),
    )
    grad_key_rot = jnp.moveaxis(own_keys, 0, 1).reshape(head_shape)
    grad_value = jnp.moveaxis(own_values, 0, 1).reshape(head_shape)
    _, rope_pull = jax.vjp(rotate_own, jnp.zeros(head_shape, jnp.float32))
    (grad_query_raw,) = rope_pull(grad_query_rot)
    (grad_key_raw,) = rope_pull(grad_key_rot)
    stacked_grads = (
        jnp.stack([grad_query_raw, grad_key_raw, grad_value])
        .astype(jnp.bfloat16)
        .reshape(3, seq_count, quarter_rows, flat_width)
    )
    token_grads = to_tokens(stacked_grads)
    grad_query_matrix = jnp.einsum(
        "bld,ble->de", normed, token_grads[0], preferred_element_type=jnp.float32
    )
    grad_key_matrix = jnp.einsum(
        "bld,ble->de", normed, token_grads[1], preferred_element_type=jnp.float32
    )
    grad_value_matrix = jnp.einsum(
        "bld,ble->de", normed, token_grads[2], preferred_element_type=jnp.float32
    )
    grad_normed = (
        jnp.einsum("ble,de->bld", token_grads[0], query_full, preferred_element_type=jnp.float32)
        + jnp.einsum("ble,de->bld", token_grads[1], key_full, preferred_element_type=jnp.float32)
        + jnp.einsum("ble,de->bld", token_grads[2], value_full, preferred_element_type=jnp.float32)
    )
    _, norm_one_pull = jax.vjp(norm_apply, residual, gain_one)
    grad_residual_part, grad_gain_one = norm_one_pull(grad_normed)
    grad_tokens = grad_middle + grad_residual_part
    (
        part_gain_one,
        part_query,
        part_key,
        part_value,
        part_output,
        part_gain_two,
        part_router,
        part_shared_gate,
        part_shared_up,
        part_shared_down,
    ) = (
        lax.psum_scatter(
            grad_gain_one.astype(jnp.bfloat16), ("sp", "fs"), scatter_dimension=0, tiled=True
        ).astype(jnp.float32),
        lax.psum_scatter(
            grad_query_matrix.astype(jnp.bfloat16), ("sp", "fs"), scatter_dimension=0, tiled=True
        ).astype(jnp.float32),
        lax.psum_scatter(
            grad_key_matrix.astype(jnp.bfloat16), ("sp", "fs"), scatter_dimension=0, tiled=True
        ).astype(jnp.float32),
        lax.psum_scatter(
            grad_value_matrix.astype(jnp.bfloat16), ("sp", "fs"), scatter_dimension=0, tiled=True
        ).astype(jnp.float32),
        lax.psum_scatter(
            grad_output_matrix.astype(jnp.bfloat16), ("sp", "fs"), scatter_dimension=0, tiled=True
        ).astype(jnp.float32),
        lax.psum_scatter(
            grad_gain_two.astype(jnp.bfloat16), ("sp", "fs"), scatter_dimension=0, tiled=True
        ).astype(jnp.float32),
        lax.psum_scatter(
            grad_router.astype(jnp.bfloat16), ("sp", "fs"), scatter_dimension=0, tiled=True
        ).astype(jnp.float32),
        lax.psum_scatter(
            grad_shared_gate.astype(jnp.bfloat16), ("sp", "fs"), scatter_dimension=0, tiled=True
        ).astype(jnp.float32),
        lax.psum_scatter(
            grad_shared_up.astype(jnp.bfloat16), ("sp", "fs"), scatter_dimension=0, tiled=True
        ).astype(jnp.float32),
        lax.psum_scatter(
            grad_shared_down.astype(jnp.bfloat16), ("sp", "fs"), scatter_dimension=0, tiled=True
        ).astype(jnp.float32),
    )
    own_gate, own_up, own_down = (
        lax.psum_scatter(
            grad_expert_gate.astype(jnp.bfloat16), "sp", scatter_dimension=1, tiled=True
        ).astype(jnp.float32),
        lax.psum_scatter(
            grad_expert_up.astype(jnp.bfloat16), "sp", scatter_dimension=1, tiled=True
        ).astype(jnp.float32),
        lax.psum_scatter(
            grad_expert_down.astype(jnp.bfloat16), "sp", scatter_dimension=1, tiled=True
        ).astype(jnp.float32),
    )
    (
        sum_gain_one,
        sum_query,
        sum_key,
        sum_value,
        sum_output,
        sum_gain_two,
        sum_router,
        sum_shared_gate,
        sum_shared_up,
        sum_shared_down,
        sum_gate,
        sum_up,
        sum_down,
    ) = (
        lax.psum(part_gain_one.astype(jnp.bfloat16), "dp").astype(jnp.float32),
        lax.psum(part_query.astype(jnp.bfloat16), "dp").astype(jnp.float32),
        lax.psum(part_key.astype(jnp.bfloat16), "dp").astype(jnp.float32),
        lax.psum(part_value.astype(jnp.bfloat16), "dp").astype(jnp.float32),
        lax.psum(part_output.astype(jnp.bfloat16), "dp").astype(jnp.float32),
        lax.psum(part_gain_two.astype(jnp.bfloat16), "dp").astype(jnp.float32),
        lax.psum(part_router.astype(jnp.bfloat16), "dp").astype(jnp.float32),
        lax.psum(part_shared_gate.astype(jnp.bfloat16), "dp").astype(jnp.float32),
        lax.psum(part_shared_up.astype(jnp.bfloat16), "dp").astype(jnp.float32),
        lax.psum(part_shared_down.astype(jnp.bfloat16), "dp").astype(jnp.float32),
        lax.psum(own_gate.astype(jnp.bfloat16), "dp").astype(jnp.float32),
        lax.psum(own_up.astype(jnp.bfloat16), "dp").astype(jnp.float32),
        lax.psum(own_down.astype(jnp.bfloat16), "dp").astype(jnp.float32),
    )
    return (
        output,
        grad_tokens,
        sum_gain_one,
        sum_query,
        sum_key,
        sum_value,
        sum_output,
        sum_gain_two,
        sum_router,
        sum_shared_gate,
        sum_shared_up,
        sum_shared_down,
        sum_gate,
        sum_up,
        sum_down,
    )


BF16 = jnp.bfloat16
F32 = jnp.float32


def dot32(left, right):
    return jnp.dot(left, right, preferred_element_type=F32)


def dot_nt(left, right):
    return lax.dot_general(left, right, (((1,), (1,)), ((), ())), preferred_element_type=F32)


def turn(values, cosine, sine):
    half = values.shape[0] // 2
    front, back = values[:half], values[half:]
    return jnp.concatenate([front * cosine - back * sine, back * cosine + front * sine], axis=0)


def turn_back(values, cosine, sine):
    half = values.shape[0] // 2
    front, back = values[:half], values[half:]
    return jnp.concatenate([front * cosine + back * sine, back * cosine - front * sine], axis=0)


def causal(block):
    keys = lax.broadcasted_iota(jnp.int32, (block, block), 0)
    queries = lax.broadcasted_iota(jnp.int32, (block, block), 1)
    return keys <= queries


def attend_kernel(block, scale, q_ref, k_ref, v_ref, cos_ref, sin_ref, o_ref, lse_ref, k_rot):
    place = pl.program_id(1)

    @pl.when(place == 0)
    def _():
        rotated = turn(k_ref[...].astype(F32), cos_ref[...], sin_ref[...])
        k_rot[...] = rotated.T.astype(BF16)

    start = pl.multiple_of(place * block, block)
    query = turn(
        q_ref[...].astype(F32), cos_ref[:, pl.ds(start, block)], sin_ref[:, pl.ds(start, block)]
    ).astype(BF16)

    def scores_at(offset):
        return dot32(k_rot[pl.ds(offset, block), :], query) * scale

    def weighted(offset, weights):
        return dot32(v_ref[:, pl.ds(offset, block)], weights.astype(BF16))

    scores = jnp.where(causal(block), scores_at(start), MASKED)
    first_max = jnp.max(scores, axis=0, keepdims=True)
    weights = jnp.exp(scores - first_max)
    first_sum = jnp.sum(weights, axis=0, keepdims=True)

    def step(index, carried):
        running_max, running_sum, running_acc = carried
        offset = pl.multiple_of(index * block, block)
        part = scores_at(offset)
        new_max = jnp.maximum(running_max, jnp.max(part, axis=0, keepdims=True))
        part = jnp.exp(part - new_max)
        factor = jnp.exp(running_max - new_max)
        return (
            new_max,
            running_sum * factor + jnp.sum(part, axis=0, keepdims=True),
            running_acc * factor + weighted(offset, part),
        )

    final_max, final_sum, final_acc = lax.fori_loop(
        0, place, step, (first_max, first_sum, weighted(start, weights))
    )
    o_ref[...] = (final_acc / final_sum).astype(BF16)
    lse_ref[0] = final_max + jnp.log(final_sum)


def attend_grad_kernel(
    block,
    scale,
    q_ref,
    k_ref,
    v_ref,
    cos_ref,
    sin_ref,
    o_ref,
    lse_ref,
    go_ref,
    dq_ref,
    dk_ref,
    dv_ref,
    q_feat,
    q_rows,
    k_feat,
    go_rows,
    delta,
    dq_acc,
):
    place = pl.program_id(1)
    count = pl.num_programs(1)

    @pl.when(place == 0)
    def _():
        rotated = turn(q_ref[...].astype(F32), cos_ref[...], sin_ref[...])
        q_feat[...] = rotated.astype(BF16)
        q_rows[...] = rotated.T.astype(BF16)
        k_feat[...] = turn(k_ref[...].astype(F32), cos_ref[...], sin_ref[...]).astype(BF16)
        grad = go_ref[...].astype(F32)
        go_rows[...] = grad.T.astype(BF16)
        delta[...] = jnp.sum(grad * o_ref[...].astype(F32), axis=0, keepdims=True)
        dq_acc[...] = jnp.zeros_like(dq_acc)

    start = pl.multiple_of(place * block, block)
    key_feat = k_feat[:, pl.ds(start, block)]
    key_rows = key_feat.astype(F32).T.astype(BF16)
    value_rows = v_ref[:, pl.ds(start, block)].astype(F32).T.astype(BF16)

    def terms(offset, masked):
        scores = dot32(key_rows, q_feat[:, pl.ds(offset, block)]) * scale
        weights = jnp.exp(scores - lse_ref[0, :, pl.ds(offset, block)])
        if masked:
            weights = jnp.where(causal(block), weights, 0.0)
        reach = dot32(value_rows, go_ref[:, pl.ds(offset, block)])
        slopes = (weights * (reach - delta[:, pl.ds(offset, block)]) * scale).astype(BF16)
        dq_acc[:, pl.ds(offset, block)] += dot32(key_feat, slopes)
        part_key = dot32(slopes, q_rows[pl.ds(offset, block), :])
        part_value = dot32(weights.astype(BF16), go_rows[pl.ds(offset, block), :])
        return part_key, part_value

    def step(index, carried):
        part_key, part_value = terms(pl.multiple_of(index * block, block), False)
        return carried[0] + part_key, carried[1] + part_value

    grad_key, grad_value = lax.fori_loop(place + 1, count, step, terms(start, True))
    own_cos, own_sin = cos_ref[:, pl.ds(start, block)], sin_ref[:, pl.ds(start, block)]
    dk_ref[...] = turn_back(grad_key.T, own_cos, own_sin).astype(BF16)
    dv_ref[...] = grad_value.T.astype(BF16)

    @pl.when(place == count - 1)
    def _():
        dq_ref[...] = turn_back(dq_acc[...], cos_ref[...], sin_ref[...]).astype(BF16)


def attention_block(length):
    return math.gcd(length, 512)


def attend(qkv, cosine, sine, heads, score_scale):
    length = qkv.shape[1]
    block = attention_block(length)
    half = HEAD_DIM // 2
    table = pl.BlockSpec((half, length), lambda h, i: (0, 0))
    return pl.pallas_call(
        functools.partial(attend_kernel, block, score_scale),
        grid=(heads, length // block),
        in_specs=[
            pl.BlockSpec((HEAD_DIM, block), lambda h, i: (h, i)),
            pl.BlockSpec((HEAD_DIM, length), lambda h, i: (heads + h, 0)),
            pl.BlockSpec((HEAD_DIM, length), lambda h, i: (2 * heads + h, 0)),
            table,
            table,
        ],
        out_specs=[
            pl.BlockSpec((HEAD_DIM, block), lambda h, i: (h, i)),
            pl.BlockSpec((1, 1, block), lambda h, i: (h, 0, i)),
        ],
        out_shape=[
            jax.ShapeDtypeStruct((heads * HEAD_DIM, length), BF16),
            jax.ShapeDtypeStruct((heads, 1, length), F32),
        ],
        scratch_shapes=[pltpu.VMEM((length, HEAD_DIM), BF16)],
        name="attend",
    )(qkv, qkv, qkv, cosine, sine)


def attend_grad(qkv, cosine, sine, out, lse, grad_out, heads, score_scale):
    length = qkv.shape[1]
    block = attention_block(length)
    half = HEAD_DIM // 2
    table = pl.BlockSpec((half, length), lambda h, i: (0, 0))

    def whole(base):
        return pl.BlockSpec((HEAD_DIM, length), lambda h, i: (base + h, 0))

    shape = jax.ShapeDtypeStruct((heads * HEAD_DIM, length), BF16)
    return pl.pallas_call(
        functools.partial(attend_grad_kernel, block, score_scale),
        grid=(heads, length // block),
        in_specs=[
            whole(0),
            whole(heads),
            whole(2 * heads),
            table,
            table,
            whole(0),
            pl.BlockSpec((1, 1, length), lambda h, i: (h, 0, 0)),
            whole(0),
        ],
        out_specs=[
            whole(0),
            pl.BlockSpec((HEAD_DIM, block), lambda h, i: (h, i)),
            pl.BlockSpec((HEAD_DIM, block), lambda h, i: (h, i)),
        ],
        out_shape=[shape, shape, shape],
        scratch_shapes=[
            pltpu.VMEM((HEAD_DIM, length), BF16),
            pltpu.VMEM((length, HEAD_DIM), BF16),
            pltpu.VMEM((HEAD_DIM, length), BF16),
            pltpu.VMEM((length, HEAD_DIM), BF16),
            pltpu.VMEM((1, length), F32),
            pltpu.VMEM((HEAD_DIM, length), F32),
        ],
        name="attend_grad",
    )(qkv, qkv, qkv, cosine, sine, out, lse, grad_out)


def expert_kernel(
    x_ref,
    g_ref,
    gate_ref,
    up_ref,
    down_ref,
    y_ref,
    gx_ref,
    dgate_ref,
    dup_ref,
    ddown_ref,
    x_feat,
    g_feat,
    y_acc,
    gx_acc,
):
    place = pl.program_id(0)

    @pl.when(place == 0)
    def _():
        x_feat[...] = x_ref[...].T
        g_feat[...] = g_ref[...].T
        y_acc[...] = jnp.zeros_like(y_acc)
        gx_acc[...] = jnp.zeros_like(gx_acc)

    gate_val = dot32(x_ref[...], gate_ref[...])
    up_val = dot32(x_ref[...], up_ref[...])
    sigmoid = jax.nn.sigmoid(gate_val)
    swished = gate_val * sigmoid
    hidden = (swished * up_val).astype(BF16)
    grad_hidden = dot32(g_ref[...], down_ref[...])
    slope = sigmoid * (1.0 + gate_val * (1.0 - sigmoid))
    gate_part = (grad_hidden * up_val * slope).astype(BF16)
    up_part = (grad_hidden * swished).astype(BF16)
    y_acc[...] += dot_nt(hidden, down_ref[...])
    gx_acc[...] += dot_nt(gate_part, gate_ref[...]) + dot_nt(up_part, up_ref[...])
    ddown_ref[...] = dot32(g_feat[...], hidden).astype(BF16)
    dgate_ref[...] = dot32(x_feat[...], gate_part).astype(BF16)
    dup_ref[...] = dot32(x_feat[...], up_part).astype(BF16)

    @pl.when(place == pl.num_programs(0) - 1)
    def _():
        y_ref[...] = y_acc[...].astype(BF16)
        gx_ref[...] = gx_acc[...].astype(BF16)


def expert_pass(rows, grads, gate, up, down):
    count, width = rows.shape
    hidden = gate.shape[1]
    tile = 256
    whole = pl.BlockSpec((count, width), lambda i: (0, 0), pipeline_mode=pl.Buffered(1))
    part = pl.BlockSpec((width, tile), lambda i: (0, i))
    return pl.pallas_call(
        expert_kernel,
        grid=(hidden // tile,),
        in_specs=[whole, whole, part, part, part],
        out_specs=[whole, whole, part, part, part],
        out_shape=[jax.ShapeDtypeStruct((count, width), BF16)] * 2
        + [jax.ShapeDtypeStruct((width, hidden), BF16)] * 3,
        scratch_shapes=[
            pltpu.VMEM((width, count), BF16),
            pltpu.VMEM((width, count), BF16),
            pltpu.VMEM((count, width), F32),
            pltpu.VMEM((count, width), F32),
        ],
        name="expert_pass",
    )(rows, grads, gate, up, down)


def swap_sum(value, axis):
    if lax.axis_size(axis) == 2:
        other = lax.ppermute(value, axis, [(0, 1), (1, 0)])
        return value.astype(F32) + other.astype(F32)
    return lax.psum(value, axis).astype(F32)


def exchange(chunks):
    return lax.all_to_all(chunks, ("sp", "fs"), split_axis=0, concat_axis=0, tiled=True)


def per_device_split(
    tokens,
    expert_ids,
    fill_order,
    attention_gain,
    query_weight,
    key_weight,
    value_weight,
    output_weight,
    mixer_gain,
    router_weight,
    shared_gate,
    shared_up,
    shared_down,
    expert_gate,
    expert_up,
    expert_down,
    cotangent,
):
    seq_count, seg_rows, width = tokens.shape
    token_count = seq_count * seg_rows
    fs_count = lax.axis_size("fs")
    sp_count = lax.axis_size("sp")
    place_count = fs_count * sp_count
    sp_place = lax.axis_index("sp")
    local_heads = HEADS // sp_count
    flat_width = local_heads * HEAD_DIM
    score_scale = HEAD_DIM ** (-0.5)
    length = place_count * seg_rows
    shard_rows = query_weight.shape[0]
    qkv_width = 3 * flat_width
    all_qkv = sp_count * qkv_width
    shared_width = shared_gate.shape[1]

    gathered = lax.all_to_all(tokens, "fs", split_axis=0, concat_axis=0, tiled=True)
    seq_tokens = lax.all_gather(
        gathered.reshape(fs_count * seg_rows, width), "sp", axis=0, tiled=True
    )

    grouped = jnp.stack([query_weight, key_weight, value_weight], axis=1)
    grouped = grouped.reshape(shard_rows, 3, sp_count, flat_width)
    grouped = jnp.transpose(grouped, (0, 2, 1, 3)).reshape(shard_rows, all_qkv)
    small = jnp.concatenate(
        [
            attention_gain[:, None],
            mixer_gain[:, None],
            router_weight,
            jnp.zeros((shard_rows, 128 - 2 - EXPERTS), BF16),
        ],
        axis=1,
    )
    first_pack = lax.all_gather(
        jnp.concatenate([grouped, small], axis=1), ("sp", "fs"), axis=0, tiled=True
    )
    second_pack = lax.all_gather(
        jnp.concatenate([output_weight, shared_gate, shared_up], axis=1),
        ("sp", "fs"),
        axis=0,
        tiled=True,
    )
    shared_down_full = lax.all_gather(shared_down, ("sp", "fs"), axis=0, tiled=True)
    gain_one = first_pack[:, all_qkv].astype(F32)
    gain_two = first_pack[:, all_qkv + 1].astype(F32)
    router_full = first_pack[:, all_qkv + 2 : all_qkv + 2 + EXPERTS]
    qkv_full = first_pack[:, :all_qkv]
    output_full = second_pack[:, :width]
    shared_gate_full = second_pack[:, width : width + shared_width]
    shared_up_full = second_pack[:, width + shared_width :]

    def own_expert(shard):
        moved = lax.all_to_all(shard, "sp", split_axis=0, concat_axis=0, tiled=True)
        return moved.reshape(width, shard.shape[2])

    gate_own, up_own, down_own = (
        own_expert(expert_gate),
        own_expert(expert_up),
        own_expert(expert_down),
    )

    half = HEAD_DIM // 2
    frequency = 10000.0 ** (-jnp.arange(half, dtype=F32) / half)
    angles = frequency[:, None] * jnp.arange(length, dtype=jnp.int32).astype(F32)[None, :]
    cosine, sine = jnp.cos(angles), jnp.sin(angles)

    normed_seq = norm_apply(seq_tokens.astype(F32), gain_one).astype(BF16)
    qkv_own = lax.dynamic_slice(first_pack, (0, sp_place * qkv_width), (width, qkv_width))
    qkv = jnp.einsum("de,ld->el", qkv_own, normed_seq, preferred_element_type=F32).astype(BF16)
    out_heads, lse = attend(qkv, cosine, sine, local_heads, score_scale)

    def to_places(feature_rows):
        return exchange(feature_rows.T.reshape(place_count, seg_rows, feature_rows.shape[0]))

    def to_token_rows(chunks):
        features = chunks.shape[-1]
        chunks = chunks.reshape(sp_count, token_count, features)
        return jnp.transpose(chunks, (1, 0, 2)).reshape(token_count, sp_count * features)

    attended = to_token_rows(to_places(out_heads))
    residual = tokens.astype(F32).reshape(token_count, width)
    middle = residual + dot32(attended, output_full)
    mixed_in = norm_apply(middle, gain_two).astype(BF16)

    logits = dot32(mixed_in, router_full)
    choices = expert_ids.reshape(token_count, TOPK)
    expert_onehot = choices[:, :, None] == jnp.arange(EXPERTS, dtype=jnp.int32)[None, None, :]
    onehot_float = expert_onehot.astype(F32)

    def gate_values(raw_logits):
        shifted = jnp.exp(raw_logits - jnp.max(raw_logits, axis=-1, keepdims=True))
        router_probs = shifted / jnp.sum(shifted, axis=-1, keepdims=True)
        picked = jnp.sum(router_probs[:, None, :] * onehot_float, axis=2)
        return picked / jnp.sum(picked, axis=1, keepdims=True)

    gate_weights, gate_pull = jax.vjp(gate_values, logits)

    fill_rank = fill_order.reshape(token_count)
    earlier = (fill_rank[None, :] < fill_rank[:, None]).astype(BF16)
    per_token = jnp.sum(onehot_float, axis=1).astype(BF16)
    counts = dot32(earlier, per_token)
    slot_ranks = jnp.sum(counts[:, None, :] * onehot_float, axis=2).astype(jnp.int32)
    group = EXPERTS // fs_count
    holder = (choices % group) * fs_count + choices // group
    slots = jnp.where(slot_ranks < CAP, holder * CAP + slot_ranks, -1)
    slot_total = CAP * EXPERTS
    slot_ids = jnp.arange(slot_total, dtype=jnp.int32)
    takes_a = slot_ids[:, None] == slots[None, :, 0]
    takes_b = slot_ids[:, None] == slots[None, :, 1]
    taking = (takes_a | takes_b).astype(BF16)
    gate_of_slot = jnp.sum(
        jnp.where(takes_a, gate_weights[None, :, 0], 0.0)
        + jnp.where(takes_b, gate_weights[None, :, 1], 0.0),
        axis=1,
    )
    cot_rows = cotangent.reshape(token_count, width)
    outgoing = dot32(taking, mixed_in).astype(BF16)
    grad_outgoing = (gate_of_slot[:, None] * dot32(taking, cot_rows)).astype(BF16)
    sent = jnp.concatenate(
        [
            outgoing.reshape(place_count, CAP, width),
            grad_outgoing.reshape(place_count, CAP, width),
        ],
        axis=1,
    )
    arrived = exchange(sent)
    incoming = arrived[:, :CAP].reshape(slot_total, width)
    grad_incoming = arrived[:, CAP:].reshape(slot_total, width)
    expert_out, grad_pair_rows, dgate, dup, ddown = expert_pass(
        incoming, grad_incoming, gate_own, up_own, down_own
    )

    def to_owner(grad):
        parts = grad.reshape(sp_count, width // sp_count, grad.shape[1])
        return lax.all_to_all(parts, "sp", split_axis=0, concat_axis=0, tiled=True)

    own_gate, own_up, own_down = (to_owner(dgate), to_owner(dup), to_owner(ddown))

    back = exchange(
        jnp.concatenate(
            [
                expert_out.reshape(place_count, CAP, width),
                grad_pair_rows.reshape(place_count, CAP, width),
            ],
            axis=1,
        )
    )
    returned = back[:, :CAP].reshape(slot_total, width)
    grad_returned = back[:, CAP:].reshape(slot_total, width)

    shared_gate_val = dot32(mixed_in, shared_gate_full)
    shared_up_val = dot32(mixed_in, shared_up_full)
    shared_hidden_full, shared_pull = jax.vjp(glu_product, shared_gate_val, shared_up_val)
    shared_hidden = shared_hidden_full.astype(BF16)
    shared_out = dot32(shared_hidden, shared_down_full)
    grad_shared_hidden = dot_nt(cot_rows, shared_down_full)
    grad_shared_gate_part, grad_shared_up_part = (
        part.astype(BF16) for part in shared_pull(grad_shared_hidden)
    )

    def outer(left, right):
        return lax.dot_general(left, right, (((0,), (0,)), ((), ())), preferred_element_type=F32)

    grad_shared_down = outer(shared_hidden, cot_rows)
    grad_shared_gate = outer(mixed_in, grad_shared_gate_part)
    grad_shared_up = outer(mixed_in, grad_shared_up_part)
    grad_mixed_shared = dot_nt(grad_shared_gate_part, shared_gate_full) + dot_nt(
        grad_shared_up_part, shared_up_full
    )

    grad_result = cot_rows.astype(F32)
    picked_a = dot32((slots[:, 0:1] == slot_ids[None, :]).astype(BF16), returned)
    picked_b = dot32((slots[:, 1:2] == slot_ids[None, :]).astype(BF16), returned)
    combined = gate_weights[:, 0:1] * picked_a + gate_weights[:, 1:2] * picked_b
    output = (middle + shared_out + combined).astype(BF16)
    grad_gates = jnp.stack(
        [jnp.sum(grad_result * picked_a, axis=1), jnp.sum(grad_result * picked_b, axis=1)], axis=1
    )
    (grad_logits,) = gate_pull(grad_gates)
    grad_logits = grad_logits.astype(BF16)
    grad_router = outer(mixed_in, grad_logits)
    grad_mixed = (
        outer(taking, grad_returned) + dot_nt(grad_logits, router_full) + grad_mixed_shared
    )
    _, norm_two_pull = jax.vjp(norm_apply, middle, gain_two)
    grad_middle_part, grad_gain_two = norm_two_pull(grad_mixed)
    grad_middle = grad_result + grad_middle_part
    grad_proj = grad_middle.astype(BF16)
    grad_output_matrix = outer(attended, grad_proj)
    grad_attended = dot_nt(grad_proj, output_full).astype(BF16)

    parts = grad_attended.reshape(fs_count, seg_rows, sp_count, flat_width)
    parts = jnp.transpose(parts, (2, 0, 1, 3)).reshape(place_count, seg_rows, flat_width)
    grad_heads = exchange(parts).reshape(length, flat_width).T
    dq, dk, dv = attend_grad(
        qkv, cosine, sine, out_heads, lse, grad_heads, local_heads, score_scale
    )
    dqkv = jnp.concatenate([dq, dk, dv], axis=0)
    token_grads = to_token_rows(to_places(dqkv))
    grad_qkv_matrix = jnp.einsum("ld,el->de", normed_seq, dqkv, preferred_element_type=F32)
    grad_normed = dot_nt(token_grads, qkv_full)
    _, norm_one_pull = jax.vjp(norm_apply, residual, gain_one)
    grad_residual_part, grad_gain_one = norm_one_pull(grad_normed)
    grad_tokens = grad_middle + grad_residual_part

    def column(vector, columns):
        return jnp.pad(vector[:, None], ((0, 0), (0, columns - 1)))

    dense = jnp.concatenate(
        [
            grad_output_matrix,
            grad_shared_gate,
            grad_shared_up,
            grad_router,
            column(grad_gain_two, 128 - EXPERTS),
        ],
        axis=1,
    ).astype(BF16)
    dense = lax.psum_scatter(dense, ("sp", "fs"), scatter_dimension=0, tiled=True)
    own_shared_down = lax.psum_scatter(
        grad_shared_down.astype(BF16), ("sp", "fs"), scatter_dimension=0, tiled=True
    )
    tail = jnp.concatenate([grad_qkv_matrix, column(grad_gain_one, 128)], axis=1).astype(BF16)
    tail = exchange(tail.reshape(place_count, shard_rows, tail.shape[1]))
    tail = tail.reshape(sp_count, fs_count, shard_rows, tail.shape[2]).astype(F32)
    tail = jnp.sum(tail, axis=1).astype(BF16)
    sum_gate, sum_up, sum_down = (
        swap_sum(own_gate, "dp"),
        swap_sum(own_up, "dp"),
        swap_sum(own_down, "dp"),
    )
    sum_dense = swap_sum(dense, "dp")
    sum_shared_down = swap_sum(own_shared_down, "dp")
    sum_tail = swap_sum(tail, "dp")
    sum_qkv = sum_tail[:, :, :qkv_width].reshape(sp_count, shard_rows, 3, flat_width)
    sum_qkv = jnp.transpose(sum_qkv, (2, 1, 0, 3)).reshape(3, shard_rows, width)
    sum_gain_one = jnp.sum(sum_tail[:, :, qkv_width], axis=0)
    edge = width + 2 * shared_width
    return (
        output.reshape(tokens.shape),
        grad_tokens.reshape(tokens.shape),
        sum_gain_one,
        sum_qkv[0],
        sum_qkv[1],
        sum_qkv[2],
        sum_dense[:, :width],
        sum_dense[:, edge + EXPERTS],
        sum_dense[:, edge : edge + EXPERTS],
        sum_dense[:, width : width + shared_width],
        sum_dense[:, width + shared_width : edge],
        sum_shared_down,
        sum_gate,
        sum_up,
        sum_down,
    )


def per_device_any(*shards):
    fs_count, sp_count = lax.axis_size("fs"), lax.axis_size("sp")
    if shards[0].shape[0] == fs_count and EXPERTS == sp_count * fs_count:
        return per_device_split(*shards)
    return per_device(*shards)


def solution(mesh):
    placed = (
        P("dp", ("sp", "fs"), None),
        P("dp", ("sp", "fs"), None),
        P("dp", ("sp", "fs")),
        P(("sp", "fs")),
        P(("sp", "fs"), None),
        P(("sp", "fs"), None),
        P(("sp", "fs"), None),
        P(("sp", "fs"), None),
        P(("sp", "fs")),
        P(("sp", "fs"), None),
        P(("sp", "fs"), None),
        P(("sp", "fs"), None),
        P(("sp", "fs"), None),
        P("fs", "sp", None),
        P("fs", "sp", None),
        P("fs", "sp", None),
        P("dp", ("sp", "fs"), None),
    )
    return jax.shard_map(
        per_device_any,
        mesh=mesh,
        in_specs=placed,
        out_specs=(
            P("dp", ("sp", "fs"), None),
            P("dp", ("sp", "fs"), None),
            P(("sp", "fs")),
            P(("sp", "fs"), None),
            P(("sp", "fs"), None),
            P(("sp", "fs"), None),
            P(("sp", "fs"), None),
            P(("sp", "fs")),
            P(("sp", "fs"), None),
            P(("sp", "fs"), None),
            P(("sp", "fs"), None),
            P(("sp", "fs"), None),
            P("fs", "sp", None),
            P("fs", "sp", None),
            P("fs", "sp", None),
        ),
        check_vma=False,
    )
```

```python
import functools
import math

import jax
import jax.numpy as jnp
from jax import lax
from jax.experimental import pallas as pl
from jax.experimental.pallas import tpu as pltpu
from jax.sharding import PartitionSpec as P

HEADS = 12
HEAD_DIM = 64
EXPERTS = 16
TOPK = 2
CAP = 72


EPSILON = 1e-06
MASKED = -1e30


def norm_apply(values, gain_row):
    inverse_root = lax.rsqrt(jnp.mean(values * values, axis=-1, keepdims=True) + EPSILON)
    return values * inverse_root * gain_row


def swish(values):
    return values * jax.nn.sigmoid(values)


def glu_product(gate_part, up_part):
    return swish(gate_part) * up_part


def rotate(values, positions):
    half_dim = values.shape[-1] // 2
    frequency = 10000.0 ** (-jnp.arange(half_dim, dtype=jnp.float32) / half_dim)
    angles = positions.astype(jnp.float32)[:, None] * frequency[None, :]
    cosine_table = jnp.cos(angles)[:, None, :]
    sine_table = jnp.sin(angles)[:, None, :]
    front_part = values[..., :half_dim]
    back_part = values[..., half_dim:]
    return jnp.concatenate(
        [
            front_part * cosine_table - back_part * sine_table,
            back_part * cosine_table + front_part * sine_table,
        ],
        axis=-1,
    )


def place_rows(indices, quarter_rows, segment_rows, fs_count):
    source_device = indices // quarter_rows
    row_inside = indices % quarter_rows
    return (
        row_inside // segment_rows * fs_count + source_device
    ) * segment_rows + row_inside % segment_rows


def to_heads(stacked):
    return lax.all_to_all(stacked, "sp", split_axis=3, concat_axis=2, tiled=True)


def to_tokens(stacked):
    return lax.all_to_all(stacked, "sp", split_axis=2, concat_axis=3, tiled=True)


def to_experts(buffer):
    return lax.all_to_all(buffer, "fs", split_axis=1, concat_axis=0, tiled=True)


def from_experts(buffer):
    return lax.all_to_all(buffer, "fs", split_axis=0, concat_axis=1, tiled=True)


def score_grads(
    query_part,
    query_rows,
    key_part,
    value_part,
    key_rows,
    grad_part,
    lse_part,
    delta_part,
    score_scale,
):
    allowed = key_rows[None, None, None, :] <= query_rows[None, None, :, None]
    scores = (
        jnp.einsum("bqhd,bkhd->bhqk", query_part, key_part, preferred_element_type=jnp.float32)
        * score_scale
    )
    weights = jnp.where(allowed, jnp.exp(scores - lse_part[..., None]), 0.0)
    grad_value = jnp.einsum(
        "bhqk,bqhd->bkhd",
        weights.astype(jnp.bfloat16),
        grad_part,
        preferred_element_type=jnp.float32,
    )
    grad_weights = jnp.einsum(
        "bqhd,bkhd->bhqk", grad_part, value_part, preferred_element_type=jnp.float32
    )
    grad_scores = (weights * (grad_weights - delta_part[..., None]) * score_scale).astype(
        jnp.bfloat16
    )
    grad_query = jnp.einsum(
        "bhqk,bkhd->bqhd", grad_scores, key_part, preferred_element_type=jnp.float32
    )
    grad_key = jnp.einsum(
        "bhqk,bqhd->bkhd", grad_scores, query_part, preferred_element_type=jnp.float32
    )
    return (grad_query, grad_key, grad_value)


def per_device(
    tokens,
    expert_ids,
    fill_order,
    attention_gain,
    query_weight,
    key_weight,
    value_weight,
    output_weight,
    mixer_gain,
    router_weight,
    shared_gate,
    shared_up,
    shared_down,
    expert_gate,
    expert_up,
    expert_down,
    cotangent,
):
    seq_count, seg_rows, model_width = tokens.shape
    token_count = seq_count * seg_rows
    fs_count = lax.axis_size("fs")
    sp_count = lax.axis_size("sp")
    fs_place = lax.axis_index("fs")
    local_heads = HEADS // sp_count
    score_scale = HEAD_DIM ** (-0.5)
    (
        gain_full,
        query_full,
        key_full,
        value_full,
        output_full,
        mixer_full,
        router_full,
        shared_gate_full,
        shared_up_full,
        shared_down_full,
    ) = (
        lax.all_gather(attention_gain, ("sp", "fs"), axis=0, tiled=True),
        lax.all_gather(query_weight, ("sp", "fs"), axis=0, tiled=True),
        lax.all_gather(key_weight, ("sp", "fs"), axis=0, tiled=True),
        lax.all_gather(value_weight, ("sp", "fs"), axis=0, tiled=True),
        lax.all_gather(output_weight, ("sp", "fs"), axis=0, tiled=True),
        lax.all_gather(mixer_gain, ("sp", "fs"), axis=0, tiled=True),
        lax.all_gather(router_weight, ("sp", "fs"), axis=0, tiled=True),
        lax.all_gather(shared_gate, ("sp", "fs"), axis=0, tiled=True),
        lax.all_gather(shared_up, ("sp", "fs"), axis=0, tiled=True),
        lax.all_gather(shared_down, ("sp", "fs"), axis=0, tiled=True),
    )
    expert_gate_full, expert_up_full, expert_down_full = (
        lax.all_gather(expert_gate, "sp", axis=1, tiled=True),
        lax.all_gather(expert_up, "sp", axis=1, tiled=True),
        lax.all_gather(expert_down, "sp", axis=1, tiled=True),
    )
    residual = tokens.astype(jnp.float32)
    gain_one = gain_full.astype(jnp.float32)
    gain_two = mixer_full.astype(jnp.float32)
    normed = norm_apply(residual, gain_one).astype(jnp.bfloat16)
    query_raw = jnp.dot(normed, query_full, preferred_element_type=jnp.float32).astype(jnp.bfloat16)
    key_raw = jnp.dot(normed, key_full, preferred_element_type=jnp.float32).astype(jnp.bfloat16)
    value_raw = jnp.dot(normed, value_full, preferred_element_type=jnp.float32).astype(jnp.bfloat16)
    heads_view = to_heads(jnp.stack([query_raw, key_raw, value_raw]))
    quarter_rows = heads_view.shape[2]
    head_shape = (seq_count, quarter_rows, local_heads, HEAD_DIM)
    flat_width = local_heads * HEAD_DIM
    own_rows = place_rows(
        fs_place * quarter_rows + jnp.arange(quarter_rows, dtype=jnp.int32),
        quarter_rows,
        seg_rows,
        fs_count,
    )

    def rotate_own(values):
        return rotate(values, own_rows)

    query_rot = rotate_own(heads_view[0].reshape(head_shape).astype(jnp.float32)).astype(
        jnp.bfloat16
    )
    key_rot = rotate_own(heads_view[1].reshape(head_shape).astype(jnp.float32)).astype(jnp.bfloat16)
    key_flat = key_rot.reshape(seq_count, quarter_rows, flat_width)
    value_flat = heads_view[2]
    keys_all, values_all = (
        lax.all_gather(key_flat, "fs", axis=1, tiled=True),
        lax.all_gather(value_flat, "fs", axis=1, tiled=True),
    )
    total_rows = keys_all.shape[1]
    block_rows = math.gcd(quarter_rows, 512)
    part_shape = (seq_count, block_rows, local_heads, HEAD_DIM)
    offsets = jnp.arange(total_rows // block_rows, dtype=jnp.int32) * block_rows

    def key_slices(offset):
        key_part = lax.dynamic_slice_in_dim(keys_all, offset, block_rows, 1).reshape(part_shape)
        value_part = lax.dynamic_slice_in_dim(values_all, offset, block_rows, 1).reshape(part_shape)
        key_rows = place_rows(
            offset + jnp.arange(block_rows, dtype=jnp.int32), quarter_rows, seg_rows, fs_count
        )
        return (key_part, value_part, key_rows)

    def forward_block(carried, offset):
        running_max, running_sum, running_acc = carried
        key_part, value_part, key_rows = key_slices(offset)
        allowed = key_rows[None, None, None, :] <= own_rows[None, None, :, None]
        scores = (
            jnp.einsum("bqhd,bkhd->bhqk", query_rot, key_part, preferred_element_type=jnp.float32)
            * score_scale
        )
        scores = jnp.where(allowed, scores, MASKED)
        new_max = jnp.maximum(running_max, jnp.max(scores, axis=-1))
        weights = jnp.where(allowed, jnp.exp(scores - new_max[..., None]), 0.0)
        factor = jnp.exp(running_max - new_max)
        running_sum = running_sum * factor + jnp.sum(weights, axis=-1)
        running_acc = running_acc * factor[..., None] + jnp.einsum(
            "bhqk,bkhd->bhqd",
            weights.astype(jnp.bfloat16),
            value_part,
            preferred_element_type=jnp.float32,
        )
        return ((new_max, running_sum, running_acc), None)

    start_state = (
        jnp.full((seq_count, local_heads, quarter_rows), MASKED, jnp.float32),
        jnp.zeros((seq_count, local_heads, quarter_rows), jnp.float32),
        jnp.zeros((seq_count, local_heads, quarter_rows, HEAD_DIM), jnp.float32),
    )
    (final_max, final_sum, final_acc), _ = lax.scan(forward_block, start_state, offsets)
    attended_heads = (final_acc / final_sum[..., None]).astype(jnp.bfloat16)
    log_total = final_max + jnp.log(final_sum)
    attended_view = jnp.transpose(attended_heads, (0, 2, 1, 3))
    attended_flat = attended_view.reshape(seq_count, quarter_rows, flat_width)
    attended_tokens = to_tokens(attended_flat[None])[0]
    middle = residual + jnp.dot(attended_tokens, output_full, preferred_element_type=jnp.float32)
    mixed_in = norm_apply(middle, gain_two).astype(jnp.bfloat16)
    token_rows = mixed_in.reshape(token_count, model_width)
    logits = jnp.dot(token_rows, router_full, preferred_element_type=jnp.float32)
    choices = expert_ids.reshape(token_count, TOPK)
    expert_onehot = choices[:, :, None] == jnp.arange(EXPERTS, dtype=jnp.int32)[None, None, :]
    onehot_float = expert_onehot.astype(jnp.float32)

    def gate_values(raw_logits):
        shifted = jnp.exp(raw_logits - jnp.max(raw_logits, axis=-1, keepdims=True))
        router_probs = shifted / jnp.sum(shifted, axis=-1, keepdims=True)
        picked = jnp.sum(router_probs[:, None, :] * onehot_float, axis=2)
        return picked / jnp.sum(picked, axis=1, keepdims=True)

    gate_weights, gate_pull = jax.vjp(gate_values, logits)
    shared_gate_val = jnp.dot(mixed_in, shared_gate_full, preferred_element_type=jnp.float32)
    shared_up_val = jnp.dot(mixed_in, shared_up_full, preferred_element_type=jnp.float32)
    shared_hidden_full, shared_pull = jax.vjp(glu_product, shared_gate_val, shared_up_val)
    shared_hidden = shared_hidden_full.astype(jnp.bfloat16)
    shared_out = jnp.dot(shared_hidden, shared_down_full, preferred_element_type=jnp.float32)
    onehot_int = expert_onehot.astype(jnp.int32)
    per_token = jnp.sum(onehot_int, axis=1)
    fill_rank = fill_order.reshape(token_count)
    earlier = (fill_rank[None, :] < fill_rank[:, None]).astype(jnp.int32)
    counts = jnp.dot(earlier, per_token, preferred_element_type=jnp.int32)
    slot_ranks = jnp.sum(counts[:, None, :] * onehot_int, axis=2)
    slot_total = CAP * EXPERTS
    slots = jnp.where(slot_ranks < CAP, slot_ranks * EXPERTS + choices, slot_total).reshape(-1)
    outgoing = (
        jnp.zeros((slot_total, model_width), jnp.bfloat16)
        .at[slots]
        .set(jnp.repeat(token_rows, TOPK, axis=0), mode="drop")
    )
    incoming = to_experts(outgoing.reshape(CAP, EXPERTS, model_width))
    expert_gate_val = jnp.einsum(
        "red,edf->ref", incoming, expert_gate_full, preferred_element_type=jnp.float32
    )
    expert_up_val = jnp.einsum(
        "red,edf->ref", incoming, expert_up_full, preferred_element_type=jnp.float32
    )
    expert_hidden_full, expert_pull = jax.vjp(glu_product, expert_gate_val, expert_up_val)
    expert_hidden = expert_hidden_full.astype(jnp.bfloat16)
    expert_out = jnp.einsum(
        "ref,edf->red", expert_hidden, expert_down_full, preferred_element_type=jnp.float32
    ).astype(jnp.bfloat16)
    returned = from_experts(expert_out).reshape(slot_total, model_width)
    padded = jnp.concatenate([returned, jnp.zeros((1, model_width), jnp.bfloat16)], axis=0)
    picked_rows = padded[slots].reshape(token_count, TOPK, model_width).astype(jnp.float32)
    combined = jnp.sum(gate_weights[:, :, None] * picked_rows, axis=1)
    result = (
        middle.reshape(token_count, model_width)
        + shared_out.reshape(token_count, model_width)
        + combined
    )
    output = result.astype(jnp.bfloat16).reshape(seq_count, seg_rows, model_width)
    grad_result = cotangent.astype(jnp.float32).reshape(token_count, model_width)
    grad_gates = jnp.sum(grad_result[:, None, :] * picked_rows, axis=2)
    grad_slots = (
        (gate_weights[:, :, None] * grad_result[:, None, :])
        .astype(jnp.bfloat16)
        .reshape(token_count * TOPK, model_width)
    )
    grad_outgoing = (
        jnp.zeros((slot_total, model_width), jnp.bfloat16).at[slots].set(grad_slots, mode="drop")
    )
    grad_incoming = to_experts(grad_outgoing.reshape(CAP, EXPERTS, model_width))
    grad_expert_down = jnp.einsum(
        "red,ref->edf", grad_incoming, expert_hidden, preferred_element_type=jnp.float32
    )
    grad_expert_hidden = jnp.einsum(
        "red,edf->ref", grad_incoming, expert_down_full, preferred_element_type=jnp.float32
    )
    grad_gate_part, grad_up_part = expert_pull(grad_expert_hidden)
    grad_gate_part = grad_gate_part.astype(jnp.bfloat16)
    grad_up_part = grad_up_part.astype(jnp.bfloat16)
    grad_expert_gate = jnp.einsum(
        "red,ref->edf", incoming, grad_gate_part, preferred_element_type=jnp.float32
    )
    grad_expert_up = jnp.einsum(
        "red,ref->edf", incoming, grad_up_part, preferred_element_type=jnp.float32
    )
    grad_pair_rows = (
        jnp.einsum(
            "ref,edf->red", grad_gate_part, expert_gate_full, preferred_element_type=jnp.float32
        )
        + jnp.einsum(
            "ref,edf->red", grad_up_part, expert_up_full, preferred_element_type=jnp.float32
        )
    ).astype(jnp.bfloat16)
    grad_returned = from_experts(grad_pair_rows).reshape(slot_total, model_width)
    grad_padded = jnp.concatenate(
        [grad_returned, jnp.zeros((1, model_width), jnp.bfloat16)], axis=0
    )
    grad_mixed = jnp.sum(
        grad_padded[slots].reshape(token_count, TOPK, model_width).astype(jnp.float32), axis=1
    )
    (grad_logits,) = gate_pull(grad_gates)
    grad_logits = grad_logits.astype(jnp.bfloat16)
    grad_router = jnp.einsum(
        "td,te->de", token_rows, grad_logits, preferred_element_type=jnp.float32
    )
    grad_mixed = grad_mixed + jnp.einsum(
        "te,de->td", grad_logits, router_full, preferred_element_type=jnp.float32
    )
    grad_shared_out = grad_result.astype(jnp.bfloat16).reshape(seq_count, seg_rows, model_width)
    grad_shared_down = jnp.einsum(
        "blf,bld->fd", shared_hidden, grad_shared_out, preferred_element_type=jnp.float32
    )
    grad_shared_hidden = jnp.einsum(
        "bld,fd->blf", grad_shared_out, shared_down_full, preferred_element_type=jnp.float32
    )
    grad_shared_gate_part, grad_shared_up_part = shared_pull(grad_shared_hidden)
    grad_shared_gate_part = grad_shared_gate_part.astype(jnp.bfloat16)
    grad_shared_up_part = grad_shared_up_part.astype(jnp.bfloat16)
    grad_shared_gate = jnp.einsum(
        "bld,blf->df", mixed_in, grad_shared_gate_part, preferred_element_type=jnp.float32
    )
    grad_shared_up = jnp.einsum(
        "bld,blf->df", mixed_in, grad_shared_up_part, preferred_element_type=jnp.float32
    )
    grad_mixed = (
        grad_mixed.reshape(seq_count, seg_rows, model_width)
        + jnp.einsum(
            "blf,df->bld",
            grad_shared_gate_part,
            shared_gate_full,
            preferred_element_type=jnp.float32,
        )
        + jnp.einsum(
            "blf,df->bld", grad_shared_up_part, shared_up_full, preferred_element_type=jnp.float32
        )
    )
    _, norm_two_pull = jax.vjp(norm_apply, middle, gain_two)
    grad_middle_part, grad_gain_two = norm_two_pull(grad_mixed)
    grad_middle = grad_result.reshape(seq_count, seg_rows, model_width) + grad_middle_part
    grad_proj = grad_middle.astype(jnp.bfloat16)
    grad_output_matrix = jnp.einsum(
        "bld,ble->de", attended_tokens, grad_proj, preferred_element_type=jnp.float32
    )
    grad_attended = jnp.einsum(
        "ble,de->bld", grad_proj, output_full, preferred_element_type=jnp.float32
    ).astype(jnp.bfloat16)
    grad_attended_heads = to_heads(grad_attended[None])[0].reshape(head_shape)
    delta_rows = jnp.einsum(
        "bqhd,bqhd->bhq",
        grad_attended_heads,
        attended_flat.reshape(head_shape),
        preferred_element_type=jnp.float32,
    )

    def key_step(grad_query, offset):
        key_part, value_part, key_rows = key_slices(offset)
        part_query, part_key, part_value = score_grads(
            query_rot,
            own_rows,
            key_part,
            value_part,
            key_rows,
            grad_attended_heads,
            log_total,
            delta_rows,
            score_scale,
        )
        flat_shape = (seq_count, block_rows, flat_width)
        return (
            grad_query + part_query,
            (part_key.reshape(flat_shape), part_value.reshape(flat_shape)),
        )

    grad_query_rot, (key_terms, value_terms) = lax.scan(
        key_step, jnp.zeros(head_shape, jnp.float32), offsets
    )
    own_keys, own_values = (
        lax.psum_scatter(
            key_terms.astype(jnp.bfloat16), "fs", scatter_dimension=0, tiled=True
        ).astype(jnp.float32),
        lax.psum_scatter(
            value_terms.astype(jnp.bfloat16), "fs", scatter_dimension=0, tiled=True
        ).astype(jnp.float32),
    )
    grad_key_rot = jnp.moveaxis(own_keys, 0, 1).reshape(head_shape)
    grad_value = jnp.moveaxis(own_values, 0, 1).reshape(head_shape)
    _, rope_pull = jax.vjp(rotate_own, jnp.zeros(head_shape, jnp.float32))
    (grad_query_raw,) = rope_pull(grad_query_rot)
    (grad_key_raw,) = rope_pull(grad_key_rot)
    stacked_grads = (
        jnp.stack([grad_query_raw, grad_key_raw, grad_value])
        .astype(jnp.bfloat16)
        .reshape(3, seq_count, quarter_rows, flat_width)
    )
    token_grads = to_tokens(stacked_grads)
    grad_query_matrix = jnp.einsum(
        "bld,ble->de", normed, token_grads[0], preferred_element_type=jnp.float32
    )
    grad_key_matrix = jnp.einsum(
        "bld,ble->de", normed, token_grads[1], preferred_element_type=jnp.float32
    )
    grad_value_matrix = jnp.einsum(
        "bld,ble->de", normed, token_grads[2], preferred_element_type=jnp.float32
    )
    grad_normed = (
        jnp.einsum("ble,de->bld", token_grads[0], query_full, preferred_element_type=jnp.float32)
        + jnp.einsum("ble,de->bld", token_grads[1], key_full, preferred_element_type=jnp.float32)
        + jnp.einsum("ble,de->bld", token_grads[2], value_full, preferred_element_type=jnp.float32)
    )
    _, norm_one_pull = jax.vjp(norm_apply, residual, gain_one)
    grad_residual_part, grad_gain_one = norm_one_pull(grad_normed)
    grad_tokens = grad_middle + grad_residual_part
    (
        part_gain_one,
        part_query,
        part_key,
        part_value,
        part_output,
        part_gain_two,
        part_router,
        part_shared_gate,
        part_shared_up,
        part_shared_down,
    ) = (
        lax.psum_scatter(
            grad_gain_one.astype(jnp.bfloat16), ("sp", "fs"), scatter_dimension=0, tiled=True
        ).astype(jnp.float32),
        lax.psum_scatter(
            grad_query_matrix.astype(jnp.bfloat16), ("sp", "fs"), scatter_dimension=0, tiled=True
        ).astype(jnp.float32),
        lax.psum_scatter(
            grad_key_matrix.astype(jnp.bfloat16), ("sp", "fs"), scatter_dimension=0, tiled=True
        ).astype(jnp.float32),
        lax.psum_scatter(
            grad_value_matrix.astype(jnp.bfloat16), ("sp", "fs"), scatter_dimension=0, tiled=True
        ).astype(jnp.float32),
        lax.psum_scatter(
            grad_output_matrix.astype(jnp.bfloat16), ("sp", "fs"), scatter_dimension=0, tiled=True
        ).astype(jnp.float32),
        lax.psum_scatter(
            grad_gain_two.astype(jnp.bfloat16), ("sp", "fs"), scatter_dimension=0, tiled=True
        ).astype(jnp.float32),
        lax.psum_scatter(
            grad_router.astype(jnp.bfloat16), ("sp", "fs"), scatter_dimension=0, tiled=True
        ).astype(jnp.float32),
        lax.psum_scatter(
            grad_shared_gate.astype(jnp.bfloat16), ("sp", "fs"), scatter_dimension=0, tiled=True
        ).astype(jnp.float32),
        lax.psum_scatter(
            grad_shared_up.astype(jnp.bfloat16), ("sp", "fs"), scatter_dimension=0, tiled=True
        ).astype(jnp.float32),
        lax.psum_scatter(
            grad_shared_down.astype(jnp.bfloat16), ("sp", "fs"), scatter_dimension=0, tiled=True
        ).astype(jnp.float32),
    )
    own_gate, own_up, own_down = (
        lax.psum_scatter(
            grad_expert_gate.astype(jnp.bfloat16), "sp", scatter_dimension=1, tiled=True
        ).astype(jnp.float32),
        lax.psum_scatter(
            grad_expert_up.astype(jnp.bfloat16), "sp", scatter_dimension=1, tiled=True
        ).astype(jnp.float32),
        lax.psum_scatter(
            grad_expert_down.astype(jnp.bfloat16), "sp", scatter_dimension=1, tiled=True
        ).astype(jnp.float32),
    )
    (
        sum_gain_one,
        sum_query,
        sum_key,
        sum_value,
        sum_output,
        sum_gain_two,
        sum_router,
        sum_shared_gate,
        sum_shared_up,
        sum_shared_down,
        sum_gate,
        sum_up,
        sum_down,
    ) = (
        lax.psum(part_gain_one.astype(jnp.bfloat16), "dp").astype(jnp.float32),
        lax.psum(part_query.astype(jnp.bfloat16), "dp").astype(jnp.float32),
        lax.psum(part_key.astype(jnp.bfloat16), "dp").astype(jnp.float32),
        lax.psum(part_value.astype(jnp.bfloat16), "dp").astype(jnp.float32),
        lax.psum(part_output.astype(jnp.bfloat16), "dp").astype(jnp.float32),
        lax.psum(part_gain_two.astype(jnp.bfloat16), "dp").astype(jnp.float32),
        lax.psum(part_router.astype(jnp.bfloat16), "dp").astype(jnp.float32),
        lax.psum(part_shared_gate.astype(jnp.bfloat16), "dp").astype(jnp.float32),
        lax.psum(part_shared_up.astype(jnp.bfloat16), "dp").astype(jnp.float32),
        lax.psum(part_shared_down.astype(jnp.bfloat16), "dp").astype(jnp.float32),
        lax.psum(own_gate.astype(jnp.bfloat16), "dp").astype(jnp.float32),
        lax.psum(own_up.astype(jnp.bfloat16), "dp").astype(jnp.float32),
        lax.psum(own_down.astype(jnp.bfloat16), "dp").astype(jnp.float32),
    )
    return (
        output,
        grad_tokens,
        sum_gain_one,
        sum_query,
        sum_key,
        sum_value,
        sum_output,
        sum_gain_two,
        sum_router,
        sum_shared_gate,
        sum_shared_up,
        sum_shared_down,
        sum_gate,
        sum_up,
        sum_down,
    )


BF16 = jnp.bfloat16
F32 = jnp.float32
LANES = 128
NOTE_ROWS = 8
VMEM_WHOLE = pl.BlockSpec(memory_space=pltpu.VMEM)
IN_PLACE = pl.BlockSpec(memory_space=pl.ANY)
ROOM = 60 * 1024 * 1024


def dot32(left, right):
    return jnp.dot(left, right, preferred_element_type=F32)


def dot_nt(left, right):
    return lax.dot_general(left, right, (((1,), (1,)), ((), ())), preferred_element_type=F32)


def turn(values, cosine, sine):
    half = values.shape[0] // 2
    front, back = values[:half], values[half:]
    return jnp.concatenate([front * cosine - back * sine, back * cosine + front * sine], axis=0)


def turn_back(values, cosine, sine):
    half = values.shape[0] // 2
    front, back = values[:half], values[half:]
    return jnp.concatenate([front * cosine + back * sine, back * cosine - front * sine], axis=0)


def causal(block):
    keys = lax.broadcasted_iota(jnp.int32, (block, block), 0)
    queries = lax.broadcasted_iota(jnp.int32, (block, block), 1)
    return keys <= queries


def remote_params(number):
    return pltpu.CompilerParams(
        collective_id=number, has_side_effects=True, vmem_limit_bytes=ROOM
    )


def places():
    sp_count, fs_count = lax.axis_size("sp"), lax.axis_size("fs")
    own = lax.axis_index("sp") * fs_count + lax.axis_index("fs")
    return sp_count * fs_count, own


def at_place(place):
    fs_count = lax.axis_size("fs")
    return {"sp": place // fs_count, "fs": lax.rem(place, fs_count)}


def greet_places():
    total, own = places()
    barrier = pltpu.get_barrier_semaphore()

    def greet(step, _):
        pl.semaphore_signal(
            barrier,
            inc=1,
            device_id=at_place(lax.rem(own + step, total)),
            device_id_type=pl.DeviceIdType.MESH,
        )
        return 0

    lax.fori_loop(1, total, greet, 0)


def await_places(others=0):
    pl.semaphore_wait(pltpu.get_barrier_semaphore(), places()[0] - 1 + others)


def columns(index, size):
    return pl.ds(pl.multiple_of(index * size, size), size)


class Swap:
    def __init__(self, source, target, send, recv, local):
        self.source, self.target = source, target
        self.send, self.recv, self.local = send, recv, local

    def remote(self, place, landing, mark):
        return pltpu.make_async_remote_copy(
            src_ref=self.source(place),
            dst_ref=self.target(landing),
            send_sem=self.send.at[place],
            recv_sem=self.recv.at[mark],
            device_id=at_place(place),
            device_id_type=pl.DeviceIdType.MESH,
        )

    def own(self):
        own = places()[1]
        return pltpu.make_async_copy(self.source(own), self.target(own), self.local)

    def start(self, place):
        own = places()[1]

        @pl.when(place != own)
        def _():
            self.remote(place, own, own).start()

        @pl.when(place == own)
        def _():
            self.own().start()

    def start_all(self):
        total, own = places()

        def begin(step, _):
            self.remote(lax.rem(own + step, total), own, own).start()
            return 0

        lax.fori_loop(1, total, begin, 0)
        self.own().start()

    def finish(self):
        total, own = places()

        def end(step, _):
            place = lax.rem(own + step, total)
            copy = self.remote(place, place, place)
            copy.wait_send()
            copy.wait_recv()
            return 0

        lax.fori_loop(1, total, end, 0)
        self.own().wait()


def swap_semaphores(total):
    return [
        pltpu.SemaphoreType.DMA((total,)),
        pltpu.SemaphoreType.DMA((total,)),
        pltpu.SemaphoreType.DMA,
    ]


class Spread:
    def __init__(self, shard, full, stage, near, far_send, far_recv, dp_send, dp_recv, local):
        self.shard, self.full, self.stage = shard, full, stage
        self.near, self.far_send, self.far_recv = near, far_send, far_recv
        self.dp_send, self.dp_recv, self.local = dp_send, dp_recv, local
        self.sp, self.dp = lax.axis_index("sp"), lax.axis_index("dp")
        self.core = self.sp + 1 - 2 * lax.rem(self.sp, 2)
        self.other = 2 - 2 * (self.sp // 2)
        self.half = shard.shape[1] // 2
        self.rows = pl.ds(pl.multiple_of(self.dp * self.half, self.half), self.half)
        self.dp_rows = pl.ds(pl.multiple_of((1 - self.dp) * self.half, self.half), self.half)

    def to_core(self):
        return pltpu.make_async_remote_copy(
            src_ref=self.shard.at[self.core],
            dst_ref=self.full.at[self.sp],
            send_sem=self.near.at[0],
            recv_sem=self.near.at[1],
            device_id={"sp": self.core},
            device_id_type=pl.DeviceIdType.MESH,
        )

    def to_far(self, turn):
        return pltpu.make_async_remote_copy(
            src_ref=self.shard.at[self.other + turn, self.rows],
            dst_ref=self.full.at[self.sp, self.rows],
            send_sem=self.far_send.at[turn],
            recv_sem=self.far_recv.at[lax.rem(self.sp, 2)],
            device_id={"sp": self.other + turn},
            device_id_type=pl.DeviceIdType.MESH,
        )

    def from_far(self, turn):
        return pltpu.make_async_remote_copy(
            src_ref=self.shard.at[self.other + turn, self.rows],
            dst_ref=self.full.at[self.other + turn, self.rows],
            send_sem=self.far_send.at[turn],
            recv_sem=self.far_recv.at[turn],
            device_id={"sp": self.other + turn},
            device_id_type=pl.DeviceIdType.MESH,
        )

    def to_dp(self, turn):
        block = self.full.at[self.other + turn, self.rows]
        return pltpu.make_async_remote_copy(
            src_ref=block,
            dst_ref=block,
            send_sem=self.dp_send.at[turn],
            recv_sem=self.dp_recv.at[turn],
            device_id={"dp": 1 - self.dp},
            device_id_type=pl.DeviceIdType.MESH,
        )

    def from_dp(self, turn):
        block = self.full.at[self.other + turn, self.dp_rows]
        return pltpu.make_async_remote_copy(
            src_ref=block,
            dst_ref=block,
            send_sem=self.dp_send.at[turn],
            recv_sem=self.dp_recv.at[turn],
            device_id={"dp": 1 - self.dp},
            device_id_type=pl.DeviceIdType.MESH,
        )

    def own_in(self):
        return pltpu.make_async_copy(self.shard.at[self.sp], self.stage, self.local.at[0])

    def own_out(self):
        return pltpu.make_async_copy(self.stage, self.full.at[self.sp], self.local.at[1])

    def start_cross(self):
        self.own_in().start()
        self.to_far(0).start()
        self.to_far(1).start()
        self.to_core().start()

    def finish_cross(self):
        self.own_in().wait()
        self.own_out().start()
        for turn in range(2):
            self.from_far(turn).wait_recv()
            self.to_far(turn).wait_send()
        self.to_core().wait_send()
        self.to_core().wait_recv()
        self.own_out().wait()

    def start_share(self):
        self.to_dp(0).start()
        self.to_dp(1).start()

    def finish_share(self):
        for turn in range(2):
            self.from_dp(turn).wait_recv()
            self.to_dp(turn).wait_send()


def pair_semaphores():
    return pltpu.SemaphoreType.DMA((2,))


def cross_scratch(shard):
    return [pltpu.VMEM(shard.shape[1:], shard.dtype)] + [pair_semaphores()] * 4


def share_scratch():
    return [pair_semaphores()] * 2


def crossing(shard, full, stage, near, far_send, far_recv, local):
    return Spread(shard, full, stage, near, far_send, far_recv, None, None, local)


def sharing(full, dp_send, dp_recv):
    return Spread(full, full, None, None, None, None, dp_send, dp_recv, None)


def greet_dp():
    pl.semaphore_signal(
        pltpu.get_barrier_semaphore(),
        inc=1,
        device_id={"dp": 1 - lax.axis_index("dp")},
        device_id_type=pl.DeviceIdType.MESH,
    )


def gather_kernel(
    tokens_ref,
    pack_ref,
    shard_ref,
    seq_ref,
    got_ref,
    full_ref,
    z_send,
    z_recv,
    core_send,
    core_recv,
    y_send,
    y_recv,
    late_send,
    late_recv,
    pack_send,
    pack_recv,
    up_send,
    up_recv,
    down_send,
    down_recv,
    local,
    *cross,
):
    fs_count, sp_count = lax.axis_size("fs"), lax.axis_size("sp")
    fs_place, sp_place = lax.axis_index("fs"), lax.axis_index("sp")
    core = sp_place + 1 - 2 * lax.rem(sp_place, 2)
    across = lax.rem(sp_place + 2, sp_count)
    barrier = pltpu.get_barrier_semaphore()

    def fs_peer(step):
        return lax.rem(fs_place + step, fs_count)

    def sp_peer(step):
        return lax.rem(sp_place + step, sp_count)

    def greet(where):
        pl.semaphore_signal(barrier, inc=1, device_id=where, device_id_type=pl.DeviceIdType.MESH)

    def move(source, target, send, recv, where):
        return pltpu.make_async_remote_copy(
            src_ref=source,
            dst_ref=target,
            send_sem=send,
            recv_sem=recv,
            device_id=where,
            device_id_type=pl.DeviceIdType.MESH,
        )

    def each(count, body):
        def run(index, _):
            body(index)
            return 0

        lax.fori_loop(1, count, run, 0)

    each(fs_count, lambda step: greet({"fs": fs_peer(step)}))
    each(sp_count, lambda step: greet({"sp": sp_peer(step)}))
    pl.semaphore_wait(barrier, fs_count + sp_count - 2)

    def pack_move(place, mark):
        return move(
            pack_ref.at[place],
            got_ref.at[sp_place, fs_place],
            pack_send.at[place],
            pack_recv.at[mark],
            {"sp": place},
        )

    def pack_landed(mark):
        return move(
            pack_ref.at[mark],
            got_ref.at[mark, fs_place],
            pack_send.at[mark],
            pack_recv.at[mark],
            {"sp": mark},
        )

    def z_move(place):
        return move(
            tokens_ref.at[place],
            seq_ref.at[sp_place, fs_place],
            z_send.at[place],
            z_recv.at[fs_place],
            {"fs": place},
        )

    def z_landed(mark):
        return move(
            tokens_ref.at[mark],
            seq_ref.at[sp_place, mark],
            z_send.at[mark],
            z_recv.at[mark],
            {"fs": mark},
        )

    def to_core(source, mark):
        return move(
            source, seq_ref.at[sp_place, mark], core_send.at[mark], core_recv.at[mark], {"sp": core}
        )

    def to_across(source, mark):
        return move(
            source, seq_ref.at[sp_place, mark], y_send.at[mark], y_recv.at[mark], {"sp": across}
        )

    def late(mark):
        block = seq_ref.at[across, mark]
        return move(block, block, late_send.at[mark], late_recv.at[mark], {"sp": core})

    def upward(mark):
        block = got_ref.at[:, mark]
        return move(block, block, up_send.at[mark], up_recv.at[mark], {"fs": fs_peer(1)})

    def downward(mark):
        block = got_ref.at[:, mark]
        return move(
            block, block, down_send.at[mark], down_recv.at[mark], {"fs": fs_peer(fs_count - 1)}
        )

    each(sp_count, lambda step: pack_move(sp_peer(step), sp_place).start())
    each(fs_count, lambda step: z_move(fs_peer(step)).start())
    own_tokens = tokens_ref.at[fs_place]
    to_across(own_tokens, fs_place).start()
    to_core(own_tokens, fs_place).start()
    own_seq = pltpu.make_async_copy(own_tokens, seq_ref.at[sp_place, fs_place], local.at[0])
    own_pack = pltpu.make_async_copy(
        pack_ref.at[sp_place], got_ref.at[sp_place, fs_place], local.at[1]
    )
    own_seq.start()
    own_pack.start()
    weights = crossing(shard_ref, full_ref, *cross)
    weights.start_cross()
    own_pack.wait()
    each(sp_count, lambda step: pack_landed(sp_peer(step)).wait_recv())

    has_up = fs_place < fs_count - 1
    has_down = fs_place > 0

    @pl.when(has_up)
    def _():
        upward(fs_place).start()

    @pl.when(has_down)
    def _():
        downward(fs_place).start()

    def relay(step):
        below, above = fs_place - step, fs_place + step

        @pl.when(below >= 0)
        def _():
            upward(below).wait_recv()

        @pl.when((below >= 0) & has_up)
        def _():
            upward(below).start()

        @pl.when(above < fs_count)
        def _():
            downward(above).wait_recv()

        @pl.when((above < fs_count) & has_down)
        def _():
            downward(above).start()

        mark = fs_peer(step)
        z_landed(mark).wait_recv()
        block = seq_ref.at[sp_place, mark]
        to_across(block, mark).start()
        to_core(block, mark).start()

    each(fs_count, relay)

    def pass_on(mark, _):
        to_across(own_tokens, mark).wait_recv()
        late(mark).start()
        return 0

    lax.fori_loop(0, fs_count, pass_on, 0)

    def end(mark, _):
        to_core(own_tokens, mark).wait_recv()
        late(mark).wait_recv()
        to_core(own_tokens, mark).wait_send()
        to_across(own_tokens, mark).wait_send()
        late(mark).wait_send()

        @pl.when(has_up & (mark <= fs_place))
        def _():
            upward(mark).wait_send()

        @pl.when(has_down & (mark >= fs_place))
        def _():
            downward(mark).wait_send()

        return 0

    lax.fori_loop(0, fs_count, end, 0)
    each(sp_count, lambda step: pack_move(sp_peer(step), sp_place).wait_send())
    each(fs_count, lambda step: z_move(fs_peer(step)).wait_send())
    own_seq.wait()
    weights.finish_cross()


def gather_start(tokens, pack, shard):
    sp_count, fs_count = lax.axis_size("sp"), lax.axis_size("fs")
    fs_sems = pltpu.SemaphoreType.DMA((fs_count,))
    sp_sems = pltpu.SemaphoreType.DMA((sp_count,))
    return pl.pallas_call(
        gather_kernel,
        in_specs=[IN_PLACE] * 3,
        out_specs=[IN_PLACE] * 3,
        out_shape=[
            jax.ShapeDtypeStruct((sp_count, fs_count) + tokens.shape[1:], tokens.dtype),
            jax.ShapeDtypeStruct((sp_count, fs_count) + pack.shape[1:], pack.dtype),
            jax.ShapeDtypeStruct(shard.shape, shard.dtype),
        ],
        scratch_shapes=[fs_sems] * 8
        + [sp_sems] * 2
        + [fs_sems] * 4
        + [pltpu.SemaphoreType.DMA((2,))]
        + cross_scratch(shard),
        compiler_params=remote_params(5),
        cost_estimate=pl.CostEstimate(
            flops=40_000_000_000, bytes_accessed=4_000_000, transcendentals=0
        ),
        name="gather_start",
    )(tokens, pack, shard)


def attend_kernel(
    block,
    scale,
    qkv_ref,
    cos_ref,
    sin_ref,
    crossed_ref,
    shard_ref,
    o_ref,
    lse_ref,
    got_ref,
    shared_ref,
    full_ref,
    k_rot,
    send,
    recv,
    local,
    dp_send,
    dp_recv,
    *cross,
):
    heads, length, _ = k_rot.shape
    wide = heads * HEAD_DIM
    total, own = places()
    seg = length // total
    greet_places()
    greet_dp()

    def head_rows(kind, head):
        return columns(kind * heads + head, HEAD_DIM)

    def turn_keys(head, _):
        rotated = turn(qkv_ref[head_rows(1, head), :].astype(F32), cos_ref[...], sin_ref[...])
        k_rot[head] = rotated.T.astype(BF16)
        return 0

    lax.fori_loop(0, heads, turn_keys, 0)
    await_places(1)
    share = sharing(shared_ref, dp_send, dp_recv)
    share.start_share()
    weights = crossing(shard_ref, full_ref, *cross)
    weights.start_cross()
    exchange = Swap(
        lambda place: o_ref.at[:, columns(place, seg)],
        lambda place: got_ref.at[
            columns(place // lax.axis_size("fs"), wide),
            columns(lax.rem(place, lax.axis_size("fs")), seg),
        ],
        send,
        recv,
        local,
    )

    def attend_block(place):
        own_columns = columns(place, block)

        def attend_head(head, _):
            query = turn(
                qkv_ref[head_rows(0, head), own_columns].astype(F32),
                cos_ref[:, own_columns],
                sin_ref[:, own_columns],
            ).astype(BF16)

            def scores_at(index):
                return dot32(k_rot[head, columns(index, block), :], query) * scale

            def weighted(index, weights):
                values = qkv_ref[head_rows(2, head), columns(index, block)]
                return dot32(values, weights.astype(BF16))

            scores = jnp.where(causal(block), scores_at(place), MASKED)
            first_max = jnp.max(scores, axis=0, keepdims=True)
            weights = jnp.exp(scores - first_max)
            first_sum = jnp.sum(weights, axis=0, keepdims=True)

            def step(index, carried):
                running_max, running_sum, running_acc = carried
                part = scores_at(index)
                new_max = jnp.maximum(running_max, jnp.max(part, axis=0, keepdims=True))
                part = jnp.exp(part - new_max)
                factor = jnp.exp(running_max - new_max)
                return (
                    new_max,
                    running_sum * factor + jnp.sum(part, axis=0, keepdims=True),
                    running_acc * factor + weighted(index, part),
                )

            final_max, final_sum, final_acc = lax.fori_loop(
                0, place, step, (first_max, first_sum, weighted(place, weights))
            )
            o_ref[columns(head, HEAD_DIM), own_columns] = (final_acc / final_sum).astype(BF16)
            lse_ref[head, :, own_columns] = final_max + jnp.log(final_sum)
            return 0

        lax.fori_loop(0, heads, attend_head, 0)

    def step(index, _):
        place = length // block - 1 - index
        attend_block(place)

        def begin(part, _):
            exchange.start(place * (block // seg) + part)
            return 0

        lax.fori_loop(0, block // seg, begin, 0)
        return 0

    lax.fori_loop(0, length // block, step, 0)
    exchange.finish()
    share.finish_share()
    weights.finish_cross()


def attend_grad_kernel(
    block,
    scale,
    qkv_ref,
    cos_ref,
    sin_ref,
    o_ref,
    lse_ref,
    ga_ref,
    grad_ref,
    got_ref,
    go_feat,
    q_feat,
    q_rows,
    k_feat,
    go_rows,
    delta,
    dq_acc,
    dk_acc,
    dv_acc,
    send_in,
    recv_in,
    local_in,
    send,
    recv,
    local,
):
    heads, length, _ = q_rows.shape
    wide = heads * HEAD_DIM
    total, own = places()
    seg = length // total
    fs_count = lax.axis_size("fs")
    greet_places()

    def head_rows(kind, head):
        return columns(kind * heads + head, HEAD_DIM)

    def prepare(head, _):
        rotated = turn(qkv_ref[head_rows(0, head), :].astype(F32), cos_ref[...], sin_ref[...])
        q_feat[columns(head, HEAD_DIM), :] = rotated.astype(BF16)
        q_rows[head] = rotated.T.astype(BF16)
        rotated = turn(qkv_ref[head_rows(1, head), :].astype(F32), cos_ref[...], sin_ref[...])
        k_feat[columns(head, HEAD_DIM), :] = rotated.astype(BF16)
        return 0

    arrival = Swap(
        lambda place: ga_ref.at[
            columns(place // fs_count, wide), columns(lax.rem(place, fs_count), seg)
        ],
        lambda place: go_feat.at[:, columns(place, seg)],
        send_in,
        recv_in,
        local_in,
    )
    await_places()
    arrival.start_all()
    lax.fori_loop(0, heads, prepare, 0)
    dq_acc[...] = jnp.zeros_like(dq_acc)
    arrival.finish()

    def prepare_grad(head, _):
        grad = go_feat[columns(head, HEAD_DIM), :].astype(F32)
        go_rows[head] = grad.T.astype(BF16)
        delta[head] = jnp.sum(
            grad * o_ref[columns(head, HEAD_DIM), :].astype(F32), axis=0, keepdims=True
        )
        return 0

    lax.fori_loop(0, heads, prepare_grad, 0)
    exchange = Swap(
        lambda place: grad_ref.at[:, columns(place, seg)],
        lambda place: got_ref.at[
            columns(place // fs_count, 3 * wide), columns(lax.rem(place, fs_count), seg)
        ],
        send,
        recv,
        local,
    )
    count = length // block

    def key_block(place, _):
        own_columns = columns(place, block)
        own_cos, own_sin = cos_ref[:, own_columns], sin_ref[:, own_columns]

        def key_head(head, _):
            rows = columns(head, HEAD_DIM)
            key_feat = k_feat[rows, own_columns]
            key_rows = key_feat.astype(F32).T.astype(BF16)
            value_rows = qkv_ref[head_rows(2, head), own_columns].astype(F32).T.astype(BF16)

            def terms(index, masked):
                here = columns(index, block)
                scores = dot32(key_rows, q_feat[rows, here]) * scale
                weights = jnp.exp(scores - lse_ref[head, :, here])
                if masked:
                    weights = jnp.where(causal(block), weights, 0.0)
                reach = dot32(value_rows, go_feat[rows, here])
                slopes = (weights * (reach - delta[head, :, here]) * scale).astype(BF16)
                dq_acc[rows, here] += dot32(key_feat, slopes)
                part_key = dot32(slopes, q_rows[head, here, :])
                part_value = dot32(weights.astype(BF16), go_rows[head, here, :])
                return part_key, part_value

            dk_acc[...], dv_acc[...] = terms(place, True)

            def step(index, _):
                part_key, part_value = terms(index, False)
                dk_acc[...] += part_key
                dv_acc[...] += part_value
                return 0

            lax.fori_loop(place + 1, count, step, 0)
            grad_ref[head_rows(0, head), own_columns] = turn_back(
                dq_acc[rows, own_columns], own_cos, own_sin
            ).astype(BF16)
            grad_ref[head_rows(1, head), own_columns] = turn_back(
                dk_acc[...].T, own_cos, own_sin
            ).astype(BF16)
            grad_ref[head_rows(2, head), own_columns] = dv_acc[...].T.astype(BF16)
            return 0

        lax.fori_loop(0, heads, key_head, 0)

        def begin(part, _):
            exchange.start(place * (block // seg) + part)
            return 0

        lax.fori_loop(0, block // seg, begin, 0)
        return 0

    lax.fori_loop(0, count, key_block, 0)
    exchange.finish()


def attention_block(length, seg):
    return math.gcd(length, 4 * seg)


def attend(qkv, cosine, sine, crossed, shard, heads, score_scale):
    length = qkv.shape[1]
    total = lax.axis_size("sp") * lax.axis_size("fs")
    seg = length // total
    wide = heads * HEAD_DIM
    tokens_here = lax.axis_size("fs") * seg
    return pl.pallas_call(
        functools.partial(attend_kernel, attention_block(length, seg), score_scale),
        in_specs=[VMEM_WHOLE] * 3 + [IN_PLACE] * 2,
        out_specs=[VMEM_WHOLE] * 2 + [IN_PLACE] * 3,
        out_shape=[
            jax.ShapeDtypeStruct((wide, length), BF16),
            jax.ShapeDtypeStruct((heads, 1, length), F32),
            jax.ShapeDtypeStruct((lax.axis_size("sp") * wide, tokens_here), BF16),
            jax.ShapeDtypeStruct(crossed.shape, crossed.dtype),
            jax.ShapeDtypeStruct(shard.shape, shard.dtype),
        ],
        input_output_aliases={3: 3},
        scratch_shapes=[pltpu.VMEM((heads, length, HEAD_DIM), BF16)]
        + swap_semaphores(total)
        + share_scratch()
        + cross_scratch(shard),
        compiler_params=remote_params(1),
        cost_estimate=pl.CostEstimate(
            flops=30_000_000_000, bytes_accessed=4_000_000, transcendentals=0
        ),
        name="attend",
    )(qkv, cosine, sine, crossed, shard)


def attend_grad(qkv, cosine, sine, out, lse, grad_attended, heads, score_scale):
    length = qkv.shape[1]
    total = lax.axis_size("sp") * lax.axis_size("fs")
    seg = length // total
    block = attention_block(length, seg)
    wide = heads * HEAD_DIM
    tokens_here = lax.axis_size("fs") * seg
    return pl.pallas_call(
        functools.partial(attend_grad_kernel, block, score_scale),
        in_specs=[VMEM_WHOLE] * 6,
        out_specs=[VMEM_WHOLE, IN_PLACE],
        out_shape=[
            jax.ShapeDtypeStruct((3 * wide, length), BF16),
            jax.ShapeDtypeStruct((lax.axis_size("sp") * 3 * wide, tokens_here), BF16),
        ],
        scratch_shapes=[
            pltpu.VMEM((wide, length), BF16),
            pltpu.VMEM((wide, length), BF16),
            pltpu.VMEM((heads, length, HEAD_DIM), BF16),
            pltpu.VMEM((wide, length), BF16),
            pltpu.VMEM((heads, length, HEAD_DIM), BF16),
            pltpu.VMEM((heads, 1, length), F32),
            pltpu.VMEM((wide, length), F32),
            pltpu.VMEM((block, HEAD_DIM), F32),
            pltpu.VMEM((block, HEAD_DIM), F32),
        ]
        + swap_semaphores(total)
        + swap_semaphores(total),
        compiler_params=remote_params(2),
        cost_estimate=pl.CostEstimate(
            flops=60_000_000_000, bytes_accessed=8_000_000, transcendentals=0
        ),
        name="attend_grad",
    )(qkv, cosine, sine, out, lse, grad_attended)


def slope_of(gate_val, sigmoid):
    return sigmoid * (1.0 + gate_val * (1.0 - sigmoid))


def dispatch_kernel(
    rows_ref,
    note_ref,
    crossed_ref,
    shard_ref,
    got_ref,
    got_note_ref,
    shared_ref,
    full_ref,
    send,
    recv,
    local,
    send_note,
    recv_note,
    local_note,
    dp_send,
    dp_recv,
    last_dp_send,
    last_dp_recv,
    *cross,
):
    greet_places()
    greet_dp()
    rows = Swap(
        lambda place: rows_ref.at[place], lambda place: got_ref.at[place], send, recv, local
    )
    notes = Swap(
        lambda place: note_ref.at[place],
        lambda place: got_note_ref.at[place],
        send_note,
        recv_note,
        local_note,
    )
    await_places(1)
    weights = crossing(shard_ref, full_ref, *cross)
    weights.start_cross()
    share = sharing(shared_ref, dp_send, dp_recv)
    share.start_share()
    notes.start_all()
    rows.start_all()
    weights.finish_cross()
    last = sharing(full_ref, last_dp_send, last_dp_recv)
    last.start_share()
    notes.finish()
    share.finish_share()
    rows.finish()
    last.finish_share()


def dispatch(sent, note, crossed, shard):
    total = sent.shape[0]
    return pl.pallas_call(
        dispatch_kernel,
        in_specs=[IN_PLACE] * 4,
        out_specs=[IN_PLACE] * 4,
        out_shape=[
            jax.ShapeDtypeStruct(array.shape, array.dtype)
            for array in (sent, note, crossed, shard)
        ],
        input_output_aliases={2: 2},
        scratch_shapes=swap_semaphores(total)
        + swap_semaphores(total)
        + share_scratch()
        + share_scratch()
        + cross_scratch(shard),
        compiler_params=remote_params(3),
        cost_estimate=pl.CostEstimate(
            flops=40_000_000_000, bytes_accessed=20_000_000, transcendentals=0
        ),
        name="dispatch",
    )(sent, note, crossed, shard)


def expert_kernel(
    x_ref,
    c_ref,
    note_ref,
    gate_ref,
    up_ref,
    down_ref,
    own_x_ref,
    own_g_ref,
    own_gate_ref,
    own_up_ref,
    own_down_ref,
    y_ref,
    dgate_ref,
    dup_ref,
    ddown_ref,
    own_y_ref,
    own_gx_ref,
    own_dgate_ref,
    own_dup_ref,
    own_ddown_ref,
    got_ref,
    got_note_ref,
    x_feat,
    g_feat,
    gate_of_row,
    acc,
    dots,
    hidden_all,
    gate_all,
    up_all,
    gx_send,
    dots_send,
    own_x_feat,
    send,
    recv,
    local,
    send_note,
    recv_note,
    local_note,
):
    step = pl.program_id(0)
    tiles = pl.num_programs(0) // 3
    total, cap, width = gx_send.shape
    tile = hidden_all.shape[2]
    lanes = dots.shape[1]
    rows = Swap(
        lambda place: gx_send.at[place], lambda place: got_ref.at[place], send, recv, local
    )
    notes = Swap(
        lambda place: dots_send.at[place],
        lambda place: got_note_ref.at[place],
        send_note,
        recv_note,
        local_note,
    )

    def block(place):
        return slice(place * cap, (place + 1) * cap)

    @pl.when(step == 0)
    def _():
        greet_places()
        x_feat[...] = x_ref[...].T
        for place in range(total):
            gate_of_row[block(place), :] = jnp.broadcast_to(
                note_ref[place].T[:cap, 0:1], (cap, lanes)
            )
        grads = gate_of_row[:, 0:1] * c_ref[...].astype(F32)
        g_feat[...] = grads.astype(BF16).T
        acc[...] = jnp.zeros_like(acc)
        dots[...] = jnp.zeros_like(dots)
        await_places()

    @pl.when(step < tiles)
    def _():
        gate_val = dot32(x_ref[...], gate_ref[...])
        up_val = dot32(x_ref[...], up_ref[...])
        sigmoid = jax.nn.sigmoid(gate_val)
        swished = gate_val * sigmoid
        hidden = (swished * up_val).astype(BF16)
        reach = dot32(c_ref[...], down_ref[...])
        product = hidden.astype(F32) * reach
        for part in range(tile // lanes):
            dots[...] += product[:, part * lanes : (part + 1) * lanes]
        grad_hidden = gate_of_row[:, 0:1] * reach
        gate_part = (grad_hidden * up_val * slope_of(gate_val, sigmoid)).astype(BF16)
        up_part = (grad_hidden * swished).astype(BF16)
        acc[...] += dot_nt(gate_part, gate_ref[...]) + dot_nt(up_part, up_ref[...])
        hidden_all[step] = hidden
        gate_all[step] = gate_part
        up_all[step] = up_part

    @pl.when(step == tiles - 1)
    def _():
        for place in range(total):
            gx_send[place] = acc[block(place), :].astype(BF16)
            dots_send[place, 0:1, :cap] = jnp.sum(dots[block(place), :].T, axis=0, keepdims=True)
        acc[...] = jnp.zeros_like(acc)
        rows.start_all()
        notes.start_all()

    @pl.when((step >= tiles) & (step < 2 * tiles))
    def _():
        here = step - tiles
        hidden = hidden_all[here]
        acc[...] += dot_nt(hidden, down_ref[...])
        ddown_ref[...] = dot32(g_feat[...], hidden).astype(BF16)
        dgate_ref[...] = dot32(x_feat[...], gate_all[here]).astype(BF16)
        dup_ref[...] = dot32(x_feat[...], up_all[here]).astype(BF16)

    @pl.when(step == 2 * tiles - 1)
    def _():
        for place in range(total):
            y_ref[place] = (gate_of_row[block(place), 0:1] * acc[block(place), :]).astype(BF16)
        own_x_feat[...] = own_x_ref[...].T
        own_y_ref[...] = jnp.zeros_like(own_y_ref)
        own_gx_ref[...] = jnp.zeros_like(own_gx_ref)

    @pl.when(step >= 2 * tiles)
    def _():
        gate_val = dot32(own_x_ref[...], own_gate_ref[...])
        up_val = dot32(own_x_ref[...], own_up_ref[...])
        sigmoid = jax.nn.sigmoid(gate_val)
        swished = gate_val * sigmoid
        hidden = swished * up_val
        hidden_low = hidden.astype(BF16)
        grad_hidden = dot_nt(own_g_ref[...], own_down_ref[...])
        gate_part = (grad_hidden * up_val * slope_of(gate_val, sigmoid)).astype(BF16)
        up_part = (grad_hidden * swished).astype(BF16)
        own_y_ref[...] += dot32(hidden_low, own_down_ref[...])
        own_gx_ref[...] += dot_nt(gate_part, own_gate_ref[...]) + dot_nt(up_part, own_up_ref[...])
        own_ddown_ref[...] = dot32(hidden.T.astype(BF16), own_g_ref[...]).astype(BF16)
        own_dgate_ref[...] = dot32(own_x_feat[...], gate_part).astype(BF16)
        own_dup_ref[...] = dot32(own_x_feat[...], up_part).astype(BF16)

    @pl.when(step == 3 * tiles - 1)
    def _():
        rows.finish()
        notes.finish()


def expert_pass(rows, cots, note, gate, up, down, own_x, own_g, own_gate, own_up, own_down):
    total, cap, width = rows.shape
    count = total * cap
    hidden = gate.shape[1]
    tile = 256
    tiles = hidden // tile
    own_tile = own_gate.shape[1] // tiles
    own_count = own_x.shape[0]
    lanes = note.shape[2]
    once = pl.Buffered(1)
    whole = pl.BlockSpec((count, width), lambda i: (0, 0), pipeline_mode=once)
    whole_note = pl.BlockSpec(note.shape, lambda i: (0, 0, 0), pipeline_mode=once)
    whole_own = pl.BlockSpec((own_count, width), lambda i: (0, 0), pipeline_mode=once)
    early = pl.BlockSpec((width, tile), lambda i: (0, jnp.minimum(i, tiles - 1)))
    both = pl.BlockSpec(
        (width, tile), lambda i: (0, jnp.where(i < 2 * tiles, lax.rem(i, tiles), tiles - 1))
    )
    late = pl.BlockSpec((width, tile), lambda i: (0, jnp.clip(i - tiles, 0, tiles - 1)))
    last = pl.BlockSpec((width, own_tile), lambda i: (0, jnp.maximum(i - 2 * tiles, 0)))
    last_flat = pl.BlockSpec((own_tile, width), lambda i: (jnp.maximum(i - 2 * tiles, 0), 0))
    return pl.pallas_call(
        expert_kernel,
        grid=(3 * tiles,),
        in_specs=[whole, whole, whole_note, early, early, both]
        + [whole_own, whole_own, last, last, last_flat],
        out_specs=[pl.BlockSpec(rows.shape, lambda i: (0, 0, 0), pipeline_mode=once)]
        + [late] * 3
        + [whole_own, whole_own, last, last, last_flat]
        + [IN_PLACE] * 2,
        out_shape=[jax.ShapeDtypeStruct(rows.shape, BF16)]
        + [jax.ShapeDtypeStruct((width, hidden), BF16)] * 3
        + [jax.ShapeDtypeStruct((own_count, width), F32)] * 2
        + [jax.ShapeDtypeStruct(own_gate.shape, BF16)] * 2
        + [
            jax.ShapeDtypeStruct(own_down.shape, BF16),
            jax.ShapeDtypeStruct(rows.shape, BF16),
            jax.ShapeDtypeStruct(note.shape, F32),
        ],
        scratch_shapes=[
            pltpu.VMEM((width, count), BF16),
            pltpu.VMEM((width, count), BF16),
            pltpu.VMEM((count, lanes), F32),
            pltpu.VMEM((count, width), F32),
            pltpu.VMEM((count, lanes), F32),
            pltpu.VMEM((tiles, count, tile), BF16),
            pltpu.VMEM((tiles, count, tile), BF16),
            pltpu.VMEM((tiles, count, tile), BF16),
            pltpu.VMEM(rows.shape, BF16),
            pltpu.VMEM(note.shape, F32),
            pltpu.VMEM((width, own_count), BF16),
        ]
        + swap_semaphores(total)
        + swap_semaphores(total),
        compiler_params=remote_params(4),
        cost_estimate=pl.CostEstimate(
            flops=80_000_000_000, bytes_accessed=30_000_000, transcendentals=0
        ),
        name="expert_pass",
    )(
        rows.reshape(count, width),
        cots.reshape(count, width),
        note,
        gate,
        up,
        down,
        own_x,
        own_g,
        own_gate,
        own_up,
        own_down,
    )


def swap_sum(value, axis):
    if lax.axis_size(axis) == 2:
        other = lax.ppermute(value, axis, [(0, 1), (1, 0)])
        return value.astype(F32) + other.astype(F32)
    return lax.psum(value, axis).astype(F32)


def exchange(chunks):
    return lax.all_to_all(chunks, ("sp", "fs"), split_axis=0, concat_axis=0, tiled=True)


def per_device_split(
    tokens,
    expert_ids,
    fill_order,
    attention_gain,
    query_weight,
    key_weight,
    value_weight,
    output_weight,
    mixer_gain,
    router_weight,
    shared_gate,
    shared_up,
    shared_down,
    expert_gate,
    expert_up,
    expert_down,
    cotangent,
):
    seq_count, seg_rows, width = tokens.shape
    token_count = seq_count * seg_rows
    fs_count = lax.axis_size("fs")
    sp_count = lax.axis_size("sp")
    place_count = fs_count * sp_count
    local_heads = HEADS // sp_count
    flat_width = local_heads * HEAD_DIM
    score_scale = HEAD_DIM ** (-0.5)
    length = place_count * seg_rows
    shard_rows = query_weight.shape[0]
    qkv_width = 3 * flat_width
    shared_width = shared_gate.shape[1]

    choices = expert_ids.reshape(token_count, TOPK)
    expert_onehot = choices[:, :, None] == jnp.arange(EXPERTS, dtype=jnp.int32)[None, None, :]
    onehot_float = expert_onehot.astype(F32)

    fill_rank = fill_order.reshape(token_count)
    earlier = (fill_rank[None, :] < fill_rank[:, None]).astype(BF16)
    per_token = jnp.sum(onehot_float, axis=1).astype(BF16)
    counts = dot32(earlier, per_token)
    slot_ranks = jnp.sum(counts[:, None, :] * onehot_float, axis=2).astype(jnp.int32)
    group = EXPERTS // fs_count
    holder = (choices % group) * fs_count + choices // group
    slots = jnp.where(slot_ranks < CAP, holder * CAP + slot_ranks, -1)
    slot_total = CAP * EXPERTS
    slot_ids = jnp.arange(slot_total, dtype=jnp.int32)
    takes_a = slot_ids[:, None] == slots[None, :, 0]
    takes_b = slot_ids[:, None] == slots[None, :, 1]
    taking = (takes_a | takes_b).astype(BF16)
    cot_rows = cotangent.reshape(token_count, width)
    cot_outgoing = dot32(taking, cot_rows).astype(BF16).reshape(place_count, CAP, width)
    grouped = jnp.stack([query_weight, key_weight, value_weight], axis=1)
    grouped = grouped.reshape(shard_rows, 3, sp_count, flat_width)
    small = jnp.concatenate([attention_gain[:, None], mixer_gain[:, None], router_weight], axis=1)
    grouped = jnp.transpose(grouped, (2, 0, 1, 3)).reshape(sp_count, shard_rows, qkv_width)
    pack_width = -(-(qkv_width + small.shape[1]) // LANES) * LANES
    pack = jnp.concatenate(
        [
            grouped,
            jnp.broadcast_to(small[None], (sp_count,) + small.shape),
            jnp.zeros((sp_count, shard_rows, pack_width - qkv_width - small.shape[1]), BF16),
        ],
        axis=2,
    )
    seq_tokens, own_pack, gate_crossed = gather_start(tokens, pack, expert_gate)
    seq_tokens = seq_tokens.reshape(length, width)
    own_pack = own_pack.reshape(width, pack_width)
    qkv_own = own_pack[:, :qkv_width]
    gain_one = own_pack[:, qkv_width].astype(F32)
    gain_two = own_pack[:, qkv_width + 1].astype(F32)
    router_full = own_pack[:, qkv_width + 2 : qkv_width + 2 + EXPERTS]

    def gather_all(shard):
        return lax.all_gather(shard, ("sp", "fs"), axis=0, tiled=True)

    output_full = gather_all(output_weight)
    shared_pack, shared_down_sent, cot_sent, seq_tokens = lax.optimization_barrier(
        (
            jnp.concatenate([shared_gate, shared_up], axis=1),
            shared_down,
            cot_outgoing,
            seq_tokens,
        )
    )
    arrived_cots = exchange(cot_sent)
    shared_pack = gather_all(shared_pack)
    shared_down_full = gather_all(shared_down_sent)
    shared_gate_full = shared_pack[:, :shared_width]
    shared_up_full = shared_pack[:, shared_width:]

    half = HEAD_DIM // 2
    frequency = 10000.0 ** (-jnp.arange(half, dtype=F32) / half)
    angles = frequency[:, None] * jnp.arange(length, dtype=jnp.int32).astype(F32)[None, :]
    cosine, sine = jnp.cos(angles), jnp.sin(angles)

    normed_seq = norm_apply(seq_tokens.astype(F32), gain_one).astype(BF16)
    qkv = jnp.einsum("de,ld->el", qkv_own, normed_seq, preferred_element_type=F32).astype(BF16)
    out_heads, lse, attended, gate_own, up_crossed = attend(
        qkv, cosine, sine, gate_crossed, expert_up, local_heads, score_scale
    )
    residual = tokens.astype(F32).reshape(token_count, width)

    def outer(left, right):
        return lax.dot_general(left, right, (((0,), (0,)), ((), ())), preferred_element_type=F32)

    middle = residual + outer(attended, output_full)
    mixed_in = norm_apply(middle, gain_two).astype(BF16)

    logits = dot32(mixed_in, router_full)
    def gate_values(raw_logits):
        shifted = jnp.exp(raw_logits - jnp.max(raw_logits, axis=-1, keepdims=True))
        router_probs = shifted / jnp.sum(shifted, axis=-1, keepdims=True)
        picked = jnp.sum(router_probs[:, None, :] * onehot_float, axis=2)
        return picked / jnp.sum(picked, axis=1, keepdims=True)

    gate_weights, gate_pull = jax.vjp(gate_values, logits)

    gate_of_slot = jnp.sum(
        jnp.where(takes_a, gate_weights[None, :, 0], 0.0)
        + jnp.where(takes_b, gate_weights[None, :, 1], 0.0),
        axis=1,
    )
    outgoing = dot32(taking, mixed_in).astype(BF16)
    note = jnp.pad(
        gate_of_slot.reshape(place_count, 1, CAP), ((0, 0), (0, NOTE_ROWS - 1), (0, LANES - CAP))
    )
    rows, notes, up_own, down_own = dispatch(
        outgoing.reshape(place_count, CAP, width), note, up_crossed, expert_down
    )
    qkv_pack, rows = lax.optimization_barrier(
        (jnp.transpose(grouped, (1, 0, 2)).reshape(shard_rows, sp_count * qkv_width), rows)
    )
    qkv_full = gather_all(qkv_pack)
    (
        expert_out,
        dgate,
        dup,
        ddown,
        shared_out,
        grad_mixed_shared,
        grad_shared_gate,
        grad_shared_up,
        grad_shared_down,
        grad_returned,
        dots,
    ) = expert_pass(
        rows,
        arrived_cots,
        notes,
        gate_own.reshape(width, -1),
        up_own.reshape(width, -1),
        down_own.reshape(width, -1),
        mixed_in,
        cot_rows,
        shared_gate_full,
        shared_up_full,
        shared_down_full,
    )
    returned = exchange(expert_out).reshape(slot_total, width)
    grad_returned = grad_returned.reshape(slot_total, width)
    dots = dots[:, 0, :CAP].reshape(slot_total)

    sp_place = lax.axis_index("sp")
    part_rows = width // sp_count

    def partner(step):
        return lax.bitwise_xor(sp_place, step)

    def rows_of(grad, step):
        return lax.dynamic_slice_in_dim(grad, partner(step) * part_rows, part_rows, 0)

    def to_sp(value, step):
        return lax.ppermute(value, "sp", [(i, i ^ step) for i in range(sp_count)])

    def to_dp(value):
        return lax.ppermute(value, "dp", [(0, 1), (1, 0)])

    def placed(parts):
        whole = jnp.zeros((sp_count,) + parts[0].shape, F32)
        for step, part in enumerate(parts):
            whole = lax.dynamic_update_slice(whole, part[None], (partner(step), 0, 0))
        return whole

    def sum_then_spread(grad):
        other = to_dp(grad)
        sums = [
            rows_of(grad, step).astype(F32) + rows_of(other, step).astype(F32)
            for step in range(sp_count)
        ]
        moved = [to_sp(sums[step].astype(BF16), step).astype(F32) for step in range(1, sp_count)]
        return placed([sums[0]] + moved)

    def spread_then_sum(grad):
        parts = [rows_of(grad, 0)] + [
            to_sp(rows_of(grad, step), step) for step in range(1, sp_count)
        ]
        return placed([part.astype(F32) + to_dp(part).astype(F32) for part in parts])

    sum_gate, sum_up, sum_down = (
        spread_then_sum(dgate),
        spread_then_sum(dup),
        sum_then_spread(ddown),
    )

    grad_result = cot_rows.astype(F32)
    output = (middle + shared_out + outer(taking, returned)).astype(BF16)
    grad_gates = jnp.stack(
        [
            jnp.sum(jnp.where(slots[:, j : j + 1] == slot_ids[None, :], dots[None, :], 0.0), axis=1)
            for j in range(TOPK)
        ],
        axis=1,
    )
    (grad_logits,) = gate_pull(grad_gates)
    grad_logits = grad_logits.astype(BF16)
    grad_router = outer(mixed_in, grad_logits)
    grad_mixed = (
        outer(taking, grad_returned) + dot_nt(grad_logits, router_full) + grad_mixed_shared
    )
    _, norm_two_pull = jax.vjp(norm_apply, middle, gain_two)
    grad_middle_part, grad_gain_two = norm_two_pull(grad_mixed)
    grad_middle = grad_result + grad_middle_part
    grad_proj = grad_middle.astype(BF16)
    grad_output_matrix = dot32(attended, grad_proj)
    grad_attended = dot_nt(output_full, grad_proj).astype(BF16)
    dqkv, token_grads = attend_grad(
        qkv, cosine, sine, out_heads, lse, grad_attended, local_heads, score_scale
    )
    grad_qkv_matrix = jnp.einsum("ld,el->de", normed_seq, dqkv, preferred_element_type=F32)
    grad_normed = jnp.einsum("et,de->td", token_grads, qkv_full, preferred_element_type=F32)
    _, norm_one_pull = jax.vjp(norm_apply, residual, gain_one)
    grad_residual_part, grad_gain_one = norm_one_pull(grad_normed)
    grad_tokens = grad_middle + grad_residual_part

    def column(vector, columns):
        return jnp.pad(vector[:, None], ((0, 0), (0, columns - 1)))

    dense = jnp.concatenate(
        [
            grad_output_matrix.astype(BF16),
            grad_shared_gate,
            grad_shared_up,
            grad_router.astype(BF16),
            column(grad_gain_two, 128 - EXPERTS).astype(BF16),
        ],
        axis=1,
    )
    dense = lax.psum_scatter(dense, ("sp", "fs"), scatter_dimension=0, tiled=True)
    own_shared_down = lax.psum_scatter(
        grad_shared_down, ("sp", "fs"), scatter_dimension=0, tiled=True
    )
    tail = jnp.concatenate([grad_qkv_matrix, column(grad_gain_one, 128)], axis=1).astype(BF16)
    tail = exchange(tail.reshape(place_count, shard_rows, tail.shape[1]))
    tail = tail.reshape(sp_count, fs_count, shard_rows, tail.shape[2]).astype(F32)
    tail = jnp.sum(tail, axis=1).astype(BF16)
    sum_dense = swap_sum(dense, "dp")
    sum_shared_down = swap_sum(own_shared_down, "dp")
    sum_tail = swap_sum(tail, "dp")
    sum_qkv = sum_tail[:, :, :qkv_width].reshape(sp_count, shard_rows, 3, flat_width)
    sum_qkv = jnp.transpose(sum_qkv, (2, 1, 0, 3)).reshape(3, shard_rows, width)
    sum_gain_one = jnp.sum(sum_tail[:, :, qkv_width], axis=0)
    edge = width + 2 * shared_width
    return (
        output.reshape(tokens.shape),
        grad_tokens.reshape(tokens.shape),
        sum_gain_one,
        sum_qkv[0],
        sum_qkv[1],
        sum_qkv[2],
        sum_dense[:, :width],
        sum_dense[:, edge + EXPERTS],
        sum_dense[:, edge : edge + EXPERTS],
        sum_dense[:, width : width + shared_width],
        sum_dense[:, width + shared_width : edge],
        sum_shared_down,
        sum_gate,
        sum_up,
        sum_down,
    )


def per_device_any(*shards):
    fs_count, sp_count = lax.axis_size("fs"), lax.axis_size("sp")
    same = shards[0].shape[0] == fs_count and EXPERTS == 4 * fs_count
    if same and sp_count == 4 and lax.axis_size("dp") == 2:
        return per_device_split(*shards)
    return per_device(*shards)


def solution(mesh):
    placed = (
        P("dp", ("sp", "fs"), None),
        P("dp", ("sp", "fs"), None),
        P("dp", ("sp", "fs")),
        P(("sp", "fs")),
        P(("sp", "fs"), None),
        P(("sp", "fs"), None),
        P(("sp", "fs"), None),
        P(("sp", "fs"), None),
        P(("sp", "fs")),
        P(("sp", "fs"), None),
        P(("sp", "fs"), None),
        P(("sp", "fs"), None),
        P(("sp", "fs"), None),
        P("fs", "sp", None),
        P("fs", "sp", None),
        P("fs", "sp", None),
        P("dp", ("sp", "fs"), None),
    )
    return jax.shard_map(
        per_device_any,
        mesh=mesh,
        in_specs=placed,
        out_specs=(
            P("dp", ("sp", "fs"), None),
            P("dp", ("sp", "fs"), None),
            P(("sp", "fs")),
            P(("sp", "fs"), None),
            P(("sp", "fs"), None),
            P(("sp", "fs"), None),
            P(("sp", "fs"), None),
            P(("sp", "fs")),
            P(("sp", "fs"), None),
            P(("sp", "fs"), None),
            P(("sp", "fs"), None),
            P(("sp", "fs"), None),
            P("fs", "sp", None),
            P("fs", "sp", None),
            P("fs", "sp", None),
        ),
        check_vma=False,
    )
```

```python
import functools
import math

import jax
import jax.numpy as jnp
from jax import lax
from jax.experimental import pallas as pl
from jax.experimental.pallas import tpu as pltpu
from jax.sharding import PartitionSpec as P

HEADS = 12
HEAD_DIM = 64
EXPERTS = 16
TOPK = 2
CAP = 72


EPSILON = 1e-06
MASKED = -1e30


def norm_apply(values, gain_row):
    inverse_root = lax.rsqrt(jnp.mean(values * values, axis=-1, keepdims=True) + EPSILON)
    return values * inverse_root * gain_row


def swish(values):
    return values * jax.nn.sigmoid(values)


def glu_product(gate_part, up_part):
    return swish(gate_part) * up_part


def rotate(values, positions):
    half_dim = values.shape[-1] // 2
    frequency = 10000.0 ** (-jnp.arange(half_dim, dtype=jnp.float32) / half_dim)
    angles = positions.astype(jnp.float32)[:, None] * frequency[None, :]
    cosine_table = jnp.cos(angles)[:, None, :]
    sine_table = jnp.sin(angles)[:, None, :]
    front_part = values[..., :half_dim]
    back_part = values[..., half_dim:]
    return jnp.concatenate(
        [
            front_part * cosine_table - back_part * sine_table,
            back_part * cosine_table + front_part * sine_table,
        ],
        axis=-1,
    )


def place_rows(indices, quarter_rows, segment_rows, fs_count):
    source_device = indices // quarter_rows
    row_inside = indices % quarter_rows
    return (
        row_inside // segment_rows * fs_count + source_device
    ) * segment_rows + row_inside % segment_rows


def to_heads(stacked):
    return lax.all_to_all(stacked, "sp", split_axis=3, concat_axis=2, tiled=True)


def to_tokens(stacked):
    return lax.all_to_all(stacked, "sp", split_axis=2, concat_axis=3, tiled=True)


def to_experts(buffer):
    return lax.all_to_all(buffer, "fs", split_axis=1, concat_axis=0, tiled=True)


def from_experts(buffer):
    return lax.all_to_all(buffer, "fs", split_axis=0, concat_axis=1, tiled=True)


def score_grads(
    query_part,
    query_rows,
    key_part,
    value_part,
    key_rows,
    grad_part,
    lse_part,
    delta_part,
    score_scale,
):
    allowed = key_rows[None, None, None, :] <= query_rows[None, None, :, None]
    scores = (
        jnp.einsum("bqhd,bkhd->bhqk", query_part, key_part, preferred_element_type=jnp.float32)
        * score_scale
    )
    weights = jnp.where(allowed, jnp.exp(scores - lse_part[..., None]), 0.0)
    grad_value = jnp.einsum(
        "bhqk,bqhd->bkhd",
        weights.astype(jnp.bfloat16),
        grad_part,
        preferred_element_type=jnp.float32,
    )
    grad_weights = jnp.einsum(
        "bqhd,bkhd->bhqk", grad_part, value_part, preferred_element_type=jnp.float32
    )
    grad_scores = (weights * (grad_weights - delta_part[..., None]) * score_scale).astype(
        jnp.bfloat16
    )
    grad_query = jnp.einsum(
        "bhqk,bkhd->bqhd", grad_scores, key_part, preferred_element_type=jnp.float32
    )
    grad_key = jnp.einsum(
        "bhqk,bqhd->bkhd", grad_scores, query_part, preferred_element_type=jnp.float32
    )
    return (grad_query, grad_key, grad_value)


def per_device(
    tokens,
    expert_ids,
    fill_order,
    attention_gain,
    query_weight,
    key_weight,
    value_weight,
    output_weight,
    mixer_gain,
    router_weight,
    shared_gate,
    shared_up,
    shared_down,
    expert_gate,
    expert_up,
    expert_down,
    cotangent,
):
    seq_count, seg_rows, model_width = tokens.shape
    token_count = seq_count * seg_rows
    fs_count = lax.axis_size("fs")
    sp_count = lax.axis_size("sp")
    fs_place = lax.axis_index("fs")
    local_heads = HEADS // sp_count
    score_scale = HEAD_DIM ** (-0.5)
    (
        gain_full,
        query_full,
        key_full,
        value_full,
        output_full,
        mixer_full,
        router_full,
        shared_gate_full,
        shared_up_full,
        shared_down_full,
    ) = (
        lax.all_gather(attention_gain, ("sp", "fs"), axis=0, tiled=True),
        lax.all_gather(query_weight, ("sp", "fs"), axis=0, tiled=True),
        lax.all_gather(key_weight, ("sp", "fs"), axis=0, tiled=True),
        lax.all_gather(value_weight, ("sp", "fs"), axis=0, tiled=True),
        lax.all_gather(output_weight, ("sp", "fs"), axis=0, tiled=True),
        lax.all_gather(mixer_gain, ("sp", "fs"), axis=0, tiled=True),
        lax.all_gather(router_weight, ("sp", "fs"), axis=0, tiled=True),
        lax.all_gather(shared_gate, ("sp", "fs"), axis=0, tiled=True),
        lax.all_gather(shared_up, ("sp", "fs"), axis=0, tiled=True),
        lax.all_gather(shared_down, ("sp", "fs"), axis=0, tiled=True),
    )
    expert_gate_full, expert_up_full, expert_down_full = (
        lax.all_gather(expert_gate, "sp", axis=1, tiled=True),
        lax.all_gather(expert_up, "sp", axis=1, tiled=True),
        lax.all_gather(expert_down, "sp", axis=1, tiled=True),
    )
    residual = tokens.astype(jnp.float32)
    gain_one = gain_full.astype(jnp.float32)
    gain_two = mixer_full.astype(jnp.float32)
    normed = norm_apply(residual, gain_one).astype(jnp.bfloat16)
    query_raw = jnp.dot(normed, query_full, preferred_element_type=jnp.float32).astype(jnp.bfloat16)
    key_raw = jnp.dot(normed, key_full, preferred_element_type=jnp.float32).astype(jnp.bfloat16)
    value_raw = jnp.dot(normed, value_full, preferred_element_type=jnp.float32).astype(jnp.bfloat16)
    heads_view = to_heads(jnp.stack([query_raw, key_raw, value_raw]))
    quarter_rows = heads_view.shape[2]
    head_shape = (seq_count, quarter_rows, local_heads, HEAD_DIM)
    flat_width = local_heads * HEAD_DIM
    own_rows = place_rows(
        fs_place * quarter_rows + jnp.arange(quarter_rows, dtype=jnp.int32),
        quarter_rows,
        seg_rows,
        fs_count,
    )

    def rotate_own(values):
        return rotate(values, own_rows)

    query_rot = rotate_own(heads_view[0].reshape(head_shape).astype(jnp.float32)).astype(
        jnp.bfloat16
    )
    key_rot = rotate_own(heads_view[1].reshape(head_shape).astype(jnp.float32)).astype(jnp.bfloat16)
    key_flat = key_rot.reshape(seq_count, quarter_rows, flat_width)
    value_flat = heads_view[2]
    keys_all, values_all = (
        lax.all_gather(key_flat, "fs", axis=1, tiled=True),
        lax.all_gather(value_flat, "fs", axis=1, tiled=True),
    )
    total_rows = keys_all.shape[1]
    block_rows = math.gcd(quarter_rows, 512)
    part_shape = (seq_count, block_rows, local_heads, HEAD_DIM)
    offsets = jnp.arange(total_rows // block_rows, dtype=jnp.int32) * block_rows

    def key_slices(offset):
        key_part = lax.dynamic_slice_in_dim(keys_all, offset, block_rows, 1).reshape(part_shape)
        value_part = lax.dynamic_slice_in_dim(values_all, offset, block_rows, 1).reshape(part_shape)
        key_rows = place_rows(
            offset + jnp.arange(block_rows, dtype=jnp.int32), quarter_rows, seg_rows, fs_count
        )
        return (key_part, value_part, key_rows)

    def forward_block(carried, offset):
        running_max, running_sum, running_acc = carried
        key_part, value_part, key_rows = key_slices(offset)
        allowed = key_rows[None, None, None, :] <= own_rows[None, None, :, None]
        scores = (
            jnp.einsum("bqhd,bkhd->bhqk", query_rot, key_part, preferred_element_type=jnp.float32)
            * score_scale
        )
        scores = jnp.where(allowed, scores, MASKED)
        new_max = jnp.maximum(running_max, jnp.max(scores, axis=-1))
        weights = jnp.where(allowed, jnp.exp(scores - new_max[..., None]), 0.0)
        factor = jnp.exp(running_max - new_max)
        running_sum = running_sum * factor + jnp.sum(weights, axis=-1)
        running_acc = running_acc * factor[..., None] + jnp.einsum(
            "bhqk,bkhd->bhqd",
            weights.astype(jnp.bfloat16),
            value_part,
            preferred_element_type=jnp.float32,
        )
        return ((new_max, running_sum, running_acc), None)

    start_state = (
        jnp.full((seq_count, local_heads, quarter_rows), MASKED, jnp.float32),
        jnp.zeros((seq_count, local_heads, quarter_rows), jnp.float32),
        jnp.zeros((seq_count, local_heads, quarter_rows, HEAD_DIM), jnp.float32),
    )
    (final_max, final_sum, final_acc), _ = lax.scan(forward_block, start_state, offsets)
    attended_heads = (final_acc / final_sum[..., None]).astype(jnp.bfloat16)
    log_total = final_max + jnp.log(final_sum)
    attended_view = jnp.transpose(attended_heads, (0, 2, 1, 3))
    attended_flat = attended_view.reshape(seq_count, quarter_rows, flat_width)
    attended_tokens = to_tokens(attended_flat[None])[0]
    middle = residual + jnp.dot(attended_tokens, output_full, preferred_element_type=jnp.float32)
    mixed_in = norm_apply(middle, gain_two).astype(jnp.bfloat16)
    token_rows = mixed_in.reshape(token_count, model_width)
    logits = jnp.dot(token_rows, router_full, preferred_element_type=jnp.float32)
    choices = expert_ids.reshape(token_count, TOPK)
    expert_onehot = choices[:, :, None] == jnp.arange(EXPERTS, dtype=jnp.int32)[None, None, :]
    onehot_float = expert_onehot.astype(jnp.float32)

    def gate_values(raw_logits):
        shifted = jnp.exp(raw_logits - jnp.max(raw_logits, axis=-1, keepdims=True))
        router_probs = shifted / jnp.sum(shifted, axis=-1, keepdims=True)
        picked = jnp.sum(router_probs[:, None, :] * onehot_float, axis=2)
        return picked / jnp.sum(picked, axis=1, keepdims=True)

    gate_weights, gate_pull = jax.vjp(gate_values, logits)
    shared_gate_val = jnp.dot(mixed_in, shared_gate_full, preferred_element_type=jnp.float32)
    shared_up_val = jnp.dot(mixed_in, shared_up_full, preferred_element_type=jnp.float32)
    shared_hidden_full, shared_pull = jax.vjp(glu_product, shared_gate_val, shared_up_val)
    shared_hidden = shared_hidden_full.astype(jnp.bfloat16)
    shared_out = jnp.dot(shared_hidden, shared_down_full, preferred_element_type=jnp.float32)
    onehot_int = expert_onehot.astype(jnp.int32)
    per_token = jnp.sum(onehot_int, axis=1)
    fill_rank = fill_order.reshape(token_count)
    earlier = (fill_rank[None, :] < fill_rank[:, None]).astype(jnp.int32)
    counts = jnp.dot(earlier, per_token, preferred_element_type=jnp.int32)
    slot_ranks = jnp.sum(counts[:, None, :] * onehot_int, axis=2)
    slot_total = CAP * EXPERTS
    slots = jnp.where(slot_ranks < CAP, slot_ranks * EXPERTS + choices, slot_total).reshape(-1)
    outgoing = (
        jnp.zeros((slot_total, model_width), jnp.bfloat16)
        .at[slots]
        .set(jnp.repeat(token_rows, TOPK, axis=0), mode="drop")
    )
    incoming = to_experts(outgoing.reshape(CAP, EXPERTS, model_width))
    expert_gate_val = jnp.einsum(
        "red,edf->ref", incoming, expert_gate_full, preferred_element_type=jnp.float32
    )
    expert_up_val = jnp.einsum(
        "red,edf->ref", incoming, expert_up_full, preferred_element_type=jnp.float32
    )
    expert_hidden_full, expert_pull = jax.vjp(glu_product, expert_gate_val, expert_up_val)
    expert_hidden = expert_hidden_full.astype(jnp.bfloat16)
    expert_out = jnp.einsum(
        "ref,edf->red", expert_hidden, expert_down_full, preferred_element_type=jnp.float32
    ).astype(jnp.bfloat16)
    returned = from_experts(expert_out).reshape(slot_total, model_width)
    padded = jnp.concatenate([returned, jnp.zeros((1, model_width), jnp.bfloat16)], axis=0)
    picked_rows = padded[slots].reshape(token_count, TOPK, model_width).astype(jnp.float32)
    combined = jnp.sum(gate_weights[:, :, None] * picked_rows, axis=1)
    result = (
        middle.reshape(token_count, model_width)
        + shared_out.reshape(token_count, model_width)
        + combined
    )
    output = result.astype(jnp.bfloat16).reshape(seq_count, seg_rows, model_width)
    grad_result = cotangent.astype(jnp.float32).reshape(token_count, model_width)
    grad_gates = jnp.sum(grad_result[:, None, :] * picked_rows, axis=2)
    grad_slots = (
        (gate_weights[:, :, None] * grad_result[:, None, :])
        .astype(jnp.bfloat16)
        .reshape(token_count * TOPK, model_width)
    )
    grad_outgoing = (
        jnp.zeros((slot_total, model_width), jnp.bfloat16).at[slots].set(grad_slots, mode="drop")
    )
    grad_incoming = to_experts(grad_outgoing.reshape(CAP, EXPERTS, model_width))
    grad_expert_down = jnp.einsum(
        "red,ref->edf", grad_incoming, expert_hidden, preferred_element_type=jnp.float32
    )
    grad_expert_hidden = jnp.einsum(
        "red,edf->ref", grad_incoming, expert_down_full, preferred_element_type=jnp.float32
    )
    grad_gate_part, grad_up_part = expert_pull(grad_expert_hidden)
    grad_gate_part = grad_gate_part.astype(jnp.bfloat16)
    grad_up_part = grad_up_part.astype(jnp.bfloat16)
    grad_expert_gate = jnp.einsum(
        "red,ref->edf", incoming, grad_gate_part, preferred_element_type=jnp.float32
    )
    grad_expert_up = jnp.einsum(
        "red,ref->edf", incoming, grad_up_part, preferred_element_type=jnp.float32
    )
    grad_pair_rows = (
        jnp.einsum(
            "ref,edf->red", grad_gate_part, expert_gate_full, preferred_element_type=jnp.float32
        )
        + jnp.einsum(
            "ref,edf->red", grad_up_part, expert_up_full, preferred_element_type=jnp.float32
        )
    ).astype(jnp.bfloat16)
    grad_returned = from_experts(grad_pair_rows).reshape(slot_total, model_width)
    grad_padded = jnp.concatenate(
        [grad_returned, jnp.zeros((1, model_width), jnp.bfloat16)], axis=0
    )
    grad_mixed = jnp.sum(
        grad_padded[slots].reshape(token_count, TOPK, model_width).astype(jnp.float32), axis=1
    )
    (grad_logits,) = gate_pull(grad_gates)
    grad_logits = grad_logits.astype(jnp.bfloat16)
    grad_router = jnp.einsum(
        "td,te->de", token_rows, grad_logits, preferred_element_type=jnp.float32
    )
    grad_mixed = grad_mixed + jnp.einsum(
        "te,de->td", grad_logits, router_full, preferred_element_type=jnp.float32
    )
    grad_shared_out = grad_result.astype(jnp.bfloat16).reshape(seq_count, seg_rows, model_width)
    grad_shared_down = jnp.einsum(
        "blf,bld->fd", shared_hidden, grad_shared_out, preferred_element_type=jnp.float32
    )
    grad_shared_hidden = jnp.einsum(
        "bld,fd->blf", grad_shared_out, shared_down_full, preferred_element_type=jnp.float32
    )
    grad_shared_gate_part, grad_shared_up_part = shared_pull(grad_shared_hidden)
    grad_shared_gate_part = grad_shared_gate_part.astype(jnp.bfloat16)
    grad_shared_up_part = grad_shared_up_part.astype(jnp.bfloat16)
    grad_shared_gate = jnp.einsum(
        "bld,blf->df", mixed_in, grad_shared_gate_part, preferred_element_type=jnp.float32
    )
    grad_shared_up = jnp.einsum(
        "bld,blf->df", mixed_in, grad_shared_up_part, preferred_element_type=jnp.float32
    )
    grad_mixed = (
        grad_mixed.reshape(seq_count, seg_rows, model_width)
        + jnp.einsum(
            "blf,df->bld",
            grad_shared_gate_part,
            shared_gate_full,
            preferred_element_type=jnp.float32,
        )
        + jnp.einsum(
            "blf,df->bld", grad_shared_up_part, shared_up_full, preferred_element_type=jnp.float32
        )
    )
    _, norm_two_pull = jax.vjp(norm_apply, middle, gain_two)
    grad_middle_part, grad_gain_two = norm_two_pull(grad_mixed)
    grad_middle = grad_result.reshape(seq_count, seg_rows, model_width) + grad_middle_part
    grad_proj = grad_middle.astype(jnp.bfloat16)
    grad_output_matrix = jnp.einsum(
        "bld,ble->de", attended_tokens, grad_proj, preferred_element_type=jnp.float32
    )
    grad_attended = jnp.einsum(
        "ble,de->bld", grad_proj, output_full, preferred_element_type=jnp.float32
    ).astype(jnp.bfloat16)
    grad_attended_heads = to_heads(grad_attended[None])[0].reshape(head_shape)
    delta_rows = jnp.einsum(
        "bqhd,bqhd->bhq",
        grad_attended_heads,
        attended_flat.reshape(head_shape),
        preferred_element_type=jnp.float32,
    )

    def key_step(grad_query, offset):
        key_part, value_part, key_rows = key_slices(offset)
        part_query, part_key, part_value = score_grads(
            query_rot,
            own_rows,
            key_part,
            value_part,
            key_rows,
            grad_attended_heads,
            log_total,
            delta_rows,
            score_scale,
        )
        flat_shape = (seq_count, block_rows, flat_width)
        return (
            grad_query + part_query,
            (part_key.reshape(flat_shape), part_value.reshape(flat_shape)),
        )

    grad_query_rot, (key_terms, value_terms) = lax.scan(
        key_step, jnp.zeros(head_shape, jnp.float32), offsets
    )
    own_keys, own_values = (
        lax.psum_scatter(
            key_terms.astype(jnp.bfloat16), "fs", scatter_dimension=0, tiled=True
        ).astype(jnp.float32),
        lax.psum_scatter(
            value_terms.astype(jnp.bfloat16), "fs", scatter_dimension=0, tiled=True
        ).astype(jnp.float32),
    )
    grad_key_rot = jnp.moveaxis(own_keys, 0, 1).reshape(head_shape)
    grad_value = jnp.moveaxis(own_values, 0, 1).reshape(head_shape)
    _, rope_pull = jax.vjp(rotate_own, jnp.zeros(head_shape, jnp.float32))
    (grad_query_raw,) = rope_pull(grad_query_rot)
    (grad_key_raw,) = rope_pull(grad_key_rot)
    stacked_grads = (
        jnp.stack([grad_query_raw, grad_key_raw, grad_value])
        .astype(jnp.bfloat16)
        .reshape(3, seq_count, quarter_rows, flat_width)
    )
    token_grads = to_tokens(stacked_grads)
    grad_query_matrix = jnp.einsum(
        "bld,ble->de", normed, token_grads[0], preferred_element_type=jnp.float32
    )
    grad_key_matrix = jnp.einsum(
        "bld,ble->de", normed, token_grads[1], preferred_element_type=jnp.float32
    )
    grad_value_matrix = jnp.einsum(
        "bld,ble->de", normed, token_grads[2], preferred_element_type=jnp.float32
    )
    grad_normed = (
        jnp.einsum("ble,de->bld", token_grads[0], query_full, preferred_element_type=jnp.float32)
        + jnp.einsum("ble,de->bld", token_grads[1], key_full, preferred_element_type=jnp.float32)
        + jnp.einsum("ble,de->bld", token_grads[2], value_full, preferred_element_type=jnp.float32)
    )
    _, norm_one_pull = jax.vjp(norm_apply, residual, gain_one)
    grad_residual_part, grad_gain_one = norm_one_pull(grad_normed)
    grad_tokens = grad_middle + grad_residual_part
    (
        part_gain_one,
        part_query,
        part_key,
        part_value,
        part_output,
        part_gain_two,
        part_router,
        part_shared_gate,
        part_shared_up,
        part_shared_down,
    ) = (
        lax.psum_scatter(
            grad_gain_one.astype(jnp.bfloat16), ("sp", "fs"), scatter_dimension=0, tiled=True
        ).astype(jnp.float32),
        lax.psum_scatter(
            grad_query_matrix.astype(jnp.bfloat16), ("sp", "fs"), scatter_dimension=0, tiled=True
        ).astype(jnp.float32),
        lax.psum_scatter(
            grad_key_matrix.astype(jnp.bfloat16), ("sp", "fs"), scatter_dimension=0, tiled=True
        ).astype(jnp.float32),
        lax.psum_scatter(
            grad_value_matrix.astype(jnp.bfloat16), ("sp", "fs"), scatter_dimension=0, tiled=True
        ).astype(jnp.float32),
        lax.psum_scatter(
            grad_output_matrix.astype(jnp.bfloat16), ("sp", "fs"), scatter_dimension=0, tiled=True
        ).astype(jnp.float32),
        lax.psum_scatter(
            grad_gain_two.astype(jnp.bfloat16), ("sp", "fs"), scatter_dimension=0, tiled=True
        ).astype(jnp.float32),
        lax.psum_scatter(
            grad_router.astype(jnp.bfloat16), ("sp", "fs"), scatter_dimension=0, tiled=True
        ).astype(jnp.float32),
        lax.psum_scatter(
            grad_shared_gate.astype(jnp.bfloat16), ("sp", "fs"), scatter_dimension=0, tiled=True
        ).astype(jnp.float32),
        lax.psum_scatter(
            grad_shared_up.astype(jnp.bfloat16), ("sp", "fs"), scatter_dimension=0, tiled=True
        ).astype(jnp.float32),
        lax.psum_scatter(
            grad_shared_down.astype(jnp.bfloat16), ("sp", "fs"), scatter_dimension=0, tiled=True
        ).astype(jnp.float32),
    )
    own_gate, own_up, own_down = (
        lax.psum_scatter(
            grad_expert_gate.astype(jnp.bfloat16), "sp", scatter_dimension=1, tiled=True
        ).astype(jnp.float32),
        lax.psum_scatter(
            grad_expert_up.astype(jnp.bfloat16), "sp", scatter_dimension=1, tiled=True
        ).astype(jnp.float32),
        lax.psum_scatter(
            grad_expert_down.astype(jnp.bfloat16), "sp", scatter_dimension=1, tiled=True
        ).astype(jnp.float32),
    )
    (
        sum_gain_one,
        sum_query,
        sum_key,
        sum_value,
        sum_output,
        sum_gain_two,
        sum_router,
        sum_shared_gate,
        sum_shared_up,
        sum_shared_down,
        sum_gate,
        sum_up,
        sum_down,
    ) = (
        lax.psum(part_gain_one.astype(jnp.bfloat16), "dp").astype(jnp.float32),
        lax.psum(part_query.astype(jnp.bfloat16), "dp").astype(jnp.float32),
        lax.psum(part_key.astype(jnp.bfloat16), "dp").astype(jnp.float32),
        lax.psum(part_value.astype(jnp.bfloat16), "dp").astype(jnp.float32),
        lax.psum(part_output.astype(jnp.bfloat16), "dp").astype(jnp.float32),
        lax.psum(part_gain_two.astype(jnp.bfloat16), "dp").astype(jnp.float32),
        lax.psum(part_router.astype(jnp.bfloat16), "dp").astype(jnp.float32),
        lax.psum(part_shared_gate.astype(jnp.bfloat16), "dp").astype(jnp.float32),
        lax.psum(part_shared_up.astype(jnp.bfloat16), "dp").astype(jnp.float32),
        lax.psum(part_shared_down.astype(jnp.bfloat16), "dp").astype(jnp.float32),
        lax.psum(own_gate.astype(jnp.bfloat16), "dp").astype(jnp.float32),
        lax.psum(own_up.astype(jnp.bfloat16), "dp").astype(jnp.float32),
        lax.psum(own_down.astype(jnp.bfloat16), "dp").astype(jnp.float32),
    )
    return (
        output,
        grad_tokens,
        sum_gain_one,
        sum_query,
        sum_key,
        sum_value,
        sum_output,
        sum_gain_two,
        sum_router,
        sum_shared_gate,
        sum_shared_up,
        sum_shared_down,
        sum_gate,
        sum_up,
        sum_down,
    )


BF16 = jnp.bfloat16
F32 = jnp.float32
LANES = 128
NOTE_ROWS = 8
VMEM_WHOLE = pl.BlockSpec(memory_space=pltpu.VMEM)
IN_PLACE = pl.BlockSpec(memory_space=pl.ANY)
ROOM = 60 * 1024 * 1024


def dot32(left, right):
    return jnp.dot(left, right, preferred_element_type=F32)


def dot_nt(left, right):
    return lax.dot_general(left, right, (((1,), (1,)), ((), ())), preferred_element_type=F32)


def turn(values, cosine, sine):
    half = values.shape[0] // 2
    front, back = values[:half], values[half:]
    return jnp.concatenate([front * cosine - back * sine, back * cosine + front * sine], axis=0)


def turn_back(values, cosine, sine):
    half = values.shape[0] // 2
    front, back = values[:half], values[half:]
    return jnp.concatenate([front * cosine + back * sine, back * cosine - front * sine], axis=0)


def causal(block):
    keys = lax.broadcasted_iota(jnp.int32, (block, block), 0)
    queries = lax.broadcasted_iota(jnp.int32, (block, block), 1)
    return keys <= queries


def remote_params(number):
    return pltpu.CompilerParams(
        collective_id=number, has_side_effects=True, vmem_limit_bytes=ROOM
    )


def places():
    sp_count, fs_count = lax.axis_size("sp"), lax.axis_size("fs")
    own = lax.axis_index("sp") * fs_count + lax.axis_index("fs")
    return sp_count * fs_count, own


def at_place(place):
    fs_count = lax.axis_size("fs")
    return {"sp": place // fs_count, "fs": lax.rem(place, fs_count)}


def greet_places():
    total, own = places()
    barrier = pltpu.get_barrier_semaphore()

    def greet(step, _):
        pl.semaphore_signal(
            barrier,
            inc=1,
            device_id=at_place(lax.rem(own + step, total)),
            device_id_type=pl.DeviceIdType.MESH,
        )
        return 0

    lax.fori_loop(1, total, greet, 0)


def await_places(others=0):
    pl.semaphore_wait(pltpu.get_barrier_semaphore(), places()[0] - 1 + others)


def columns(index, size):
    return pl.ds(pl.multiple_of(index * size, size), size)


class Swap:
    def __init__(self, source, target, send, recv, local):
        self.source, self.target = source, target
        self.send, self.recv, self.local = send, recv, local

    def remote(self, place, landing, mark):
        return pltpu.make_async_remote_copy(
            src_ref=self.source(place),
            dst_ref=self.target(landing),
            send_sem=self.send.at[place],
            recv_sem=self.recv.at[mark],
            device_id=at_place(place),
            device_id_type=pl.DeviceIdType.MESH,
        )

    def own(self):
        own = places()[1]
        return pltpu.make_async_copy(self.source(own), self.target(own), self.local)

    def start(self, place):
        own = places()[1]

        @pl.when(place != own)
        def _():
            self.remote(place, own, own).start()

        @pl.when(place == own)
        def _():
            self.own().start()

    def start_all(self):
        total, own = places()

        def begin(step, _):
            self.remote(lax.rem(own + step, total), own, own).start()
            return 0

        lax.fori_loop(1, total, begin, 0)
        self.own().start()

    def finish(self):
        total, own = places()

        def end(step, _):
            place = lax.rem(own + step, total)
            copy = self.remote(place, place, place)
            copy.wait_send()
            copy.wait_recv()
            return 0

        lax.fori_loop(1, total, end, 0)
        self.own().wait()


def swap_semaphores(total):
    return [
        pltpu.SemaphoreType.DMA((total,)),
        pltpu.SemaphoreType.DMA((total,)),
        pltpu.SemaphoreType.DMA,
    ]


class Spread:
    def __init__(self, shard, full, stage, near, far_send, far_recv, dp_send, dp_recv, local):
        self.shard, self.full, self.stage = shard, full, stage
        self.near, self.far_send, self.far_recv = near, far_send, far_recv
        self.dp_send, self.dp_recv, self.local = dp_send, dp_recv, local
        self.sp, self.dp = lax.axis_index("sp"), lax.axis_index("dp")
        self.core = self.sp + 1 - 2 * lax.rem(self.sp, 2)
        self.other = 2 - 2 * (self.sp // 2)
        self.half = shard.shape[1] // 2
        self.rows = pl.ds(pl.multiple_of(self.dp * self.half, self.half), self.half)
        self.dp_rows = pl.ds(pl.multiple_of((1 - self.dp) * self.half, self.half), self.half)

    def to_core(self):
        return pltpu.make_async_remote_copy(
            src_ref=self.shard.at[self.core],
            dst_ref=self.full.at[self.sp],
            send_sem=self.near.at[0],
            recv_sem=self.near.at[1],
            device_id={"sp": self.core},
            device_id_type=pl.DeviceIdType.MESH,
        )

    def to_far(self, turn):
        return pltpu.make_async_remote_copy(
            src_ref=self.shard.at[self.other + turn, self.rows],
            dst_ref=self.full.at[self.sp, self.rows],
            send_sem=self.far_send.at[turn],
            recv_sem=self.far_recv.at[lax.rem(self.sp, 2)],
            device_id={"sp": self.other + turn},
            device_id_type=pl.DeviceIdType.MESH,
        )

    def from_far(self, turn):
        return pltpu.make_async_remote_copy(
            src_ref=self.shard.at[self.other + turn, self.rows],
            dst_ref=self.full.at[self.other + turn, self.rows],
            send_sem=self.far_send.at[turn],
            recv_sem=self.far_recv.at[turn],
            device_id={"sp": self.other + turn},
            device_id_type=pl.DeviceIdType.MESH,
        )

    def to_dp(self, turn):
        block = self.full.at[self.other + turn, self.rows]
        return pltpu.make_async_remote_copy(
            src_ref=block,
            dst_ref=block,
            send_sem=self.dp_send.at[turn],
            recv_sem=self.dp_recv.at[turn],
            device_id={"dp": 1 - self.dp},
            device_id_type=pl.DeviceIdType.MESH,
        )

    def from_dp(self, turn):
        block = self.full.at[self.other + turn, self.dp_rows]
        return pltpu.make_async_remote_copy(
            src_ref=block,
            dst_ref=block,
            send_sem=self.dp_send.at[turn],
            recv_sem=self.dp_recv.at[turn],
            device_id={"dp": 1 - self.dp},
            device_id_type=pl.DeviceIdType.MESH,
        )

    def own_in(self):
        return pltpu.make_async_copy(self.shard.at[self.sp], self.stage, self.local.at[0])

    def own_out(self):
        return pltpu.make_async_copy(self.stage, self.full.at[self.sp], self.local.at[1])

    def start_cross(self):
        self.own_in().start()
        self.to_far(0).start()
        self.to_far(1).start()
        self.to_core().start()

    def finish_cross(self):
        self.own_in().wait()
        self.own_out().start()
        for turn in range(2):
            self.from_far(turn).wait_recv()
            self.to_far(turn).wait_send()
        self.to_core().wait_send()
        self.to_core().wait_recv()
        self.own_out().wait()

    def start_share(self):
        self.to_dp(0).start()
        self.to_dp(1).start()

    def finish_share(self):
        for turn in range(2):
            self.from_dp(turn).wait_recv()
            self.to_dp(turn).wait_send()


def pair_semaphores():
    return pltpu.SemaphoreType.DMA((2,))


def cross_scratch(shard):
    return [pltpu.VMEM(shard.shape[1:], shard.dtype)] + [pair_semaphores()] * 4


def share_scratch():
    return [pair_semaphores()] * 2


def crossing(shard, full, stage, near, far_send, far_recv, local):
    return Spread(shard, full, stage, near, far_send, far_recv, None, None, local)


def sharing(full, dp_send, dp_recv):
    return Spread(full, full, None, None, None, None, dp_send, dp_recv, None)


def greet_dp():
    pl.semaphore_signal(
        pltpu.get_barrier_semaphore(),
        inc=1,
        device_id={"dp": 1 - lax.axis_index("dp")},
        device_id_type=pl.DeviceIdType.MESH,
    )


def route(ids_ref, fill_ref, slots_ref, taking_ref):
    count = fill_ref.shape[1]
    group = EXPERTS // lax.axis_size("fs")
    fill_row = fill_ref[...].astype(F32)
    fill_column = jnp.broadcast_to(fill_row, (8, count)).T[:, 0:1]
    earlier = (fill_column < fill_row).astype(BF16)
    experts = lax.broadcasted_iota(jnp.int32, (EXPERTS, count), 0)
    named = [(experts == ids_ref[j : j + 1, :]).astype(F32) for j in range(TOPK)]
    counts = dot32((named[0] + named[1]).astype(BF16), earlier)
    slots = []
    for j in range(TOPK):
        rank = jnp.sum(counts * named[j], axis=0, keepdims=True).astype(jnp.int32)
        choice = ids_ref[j : j + 1, :]
        holder = lax.rem(choice, group) * lax.axis_size("fs") + choice // group
        slots.append(jnp.where(rank < CAP, holder * CAP + rank, -1))
        slots_ref[j : j + 1, :] = slots[j]
    total = taking_ref.shape[0]
    half = total // 2
    for start in (0, half):
        slot_ids = start + lax.broadcasted_iota(jnp.int32, (half, count), 0)
        taken = (slot_ids == slots[0]) | (slot_ids == slots[1])
        taking_ref[start : start + half, :] = taken.astype(F32).astype(BF16)


def spread_rows(taking_ref, rows_ref, out_ref):
    total, cap, _ = out_ref.shape
    half = total // 2
    for first in (0, half):
        rows = dot32(taking_ref[first * cap : (first + half) * cap, :], rows_ref[...])
        for place in range(half):
            out_ref[first + place] = rows[place * cap : (place + 1) * cap].astype(BF16)


def cot_swap(source, target, rows, send, recv, local):
    return Swap(
        lambda place: source.at[place, rows], lambda place: target.at[place, rows], send, recv, local
    )


def gather_kernel(
    first_rows,
    tokens_ref,
    query_ref,
    key_ref,
    value_ref,
    small_ref,
    ids_ref,
    fill_ref,
    cot_ref,
    shard_ref,
    seq_ref,
    got_ref,
    full_ref,
    slots_ref,
    taking_ref,
    cot_out_ref,
    cots_ref,
    pack_ref,
    z_send,
    z_recv,
    core_send,
    core_recv,
    y_send,
    y_recv,
    late_send,
    late_recv,
    pack_send,
    pack_recv,
    up_send,
    up_recv,
    down_send,
    down_recv,
    local,
    cot_send,
    cot_recv,
    cot_local,
    *cross,
):
    fs_count, sp_count = lax.axis_size("fs"), lax.axis_size("sp")
    fs_place, sp_place = lax.axis_index("fs"), lax.axis_index("sp")
    core = sp_place + 1 - 2 * lax.rem(sp_place, 2)
    across = lax.rem(sp_place + 2, sp_count)

    def fs_peer(step):
        return lax.rem(fs_place + step, fs_count)

    def sp_peer(step):
        return lax.rem(sp_place + step, sp_count)

    def move(source, target, send, recv, where):
        return pltpu.make_async_remote_copy(
            src_ref=source,
            dst_ref=target,
            send_sem=send,
            recv_sem=recv,
            device_id=where,
            device_id_type=pl.DeviceIdType.MESH,
        )

    def each(count, body):
        def run(index, _):
            body(index)
            return 0

        lax.fori_loop(1, count, run, 0)

    greet_places()
    part = query_ref.shape[1] // sp_count
    for place in range(sp_count):
        for kind, source in enumerate((query_ref, key_ref, value_ref)):
            pack_ref[place, :, kind * part : (kind + 1) * part] = source[
                :, place * part : (place + 1) * part
            ]
        pack_ref[place, :, 3 * part :] = small_ref[:, : pack_ref.shape[2] - 3 * part]
    await_places()

    def pack_move(place, mark):
        return move(
            pack_ref.at[place],
            got_ref.at[sp_place, fs_place],
            pack_send.at[place],
            pack_recv.at[mark],
            {"sp": place},
        )

    def pack_landed(mark):
        return move(
            pack_ref.at[mark],
            got_ref.at[mark, fs_place],
            pack_send.at[mark],
            pack_recv.at[mark],
            {"sp": mark},
        )

    def z_move(place):
        return move(
            tokens_ref.at[place],
            seq_ref.at[sp_place, fs_place],
            z_send.at[place],
            z_recv.at[fs_place],
            {"fs": place},
        )

    def z_landed(mark):
        return move(
            tokens_ref.at[mark],
            seq_ref.at[sp_place, mark],
            z_send.at[mark],
            z_recv.at[mark],
            {"fs": mark},
        )

    def to_core(source, mark):
        return move(
            source, seq_ref.at[sp_place, mark], core_send.at[mark], core_recv.at[mark], {"sp": core}
        )

    def to_across(source, mark):
        return move(
            source, seq_ref.at[sp_place, mark], y_send.at[mark], y_recv.at[mark], {"sp": across}
        )

    def late(mark):
        block = seq_ref.at[across, mark]
        return move(block, block, late_send.at[mark], late_recv.at[mark], {"sp": core})

    def upward(mark):
        block = got_ref.at[:, mark]
        return move(block, block, up_send.at[mark], up_recv.at[mark], {"fs": fs_peer(1)})

    def downward(mark):
        block = got_ref.at[:, mark]
        return move(
            block, block, down_send.at[mark], down_recv.at[mark], {"fs": fs_peer(fs_count - 1)}
        )

    each(sp_count, lambda step: pack_move(sp_peer(step), sp_place).start())
    each(fs_count, lambda step: z_move(fs_peer(step)).start())
    own_tokens = tokens_ref.at[fs_place]
    to_across(own_tokens, fs_place).start()
    to_core(own_tokens, fs_place).start()
    own_seq = pltpu.make_async_copy(own_tokens, seq_ref.at[sp_place, fs_place], local.at[0])
    own_pack = pltpu.make_async_copy(
        pack_ref.at[sp_place], got_ref.at[sp_place, fs_place], local.at[1]
    )
    own_seq.start()
    own_pack.start()
    own_pack.wait()
    each(sp_count, lambda step: pack_landed(sp_peer(step)).wait_recv())

    has_up = fs_place < fs_count - 1
    has_down = fs_place > 0

    @pl.when(has_up)
    def _():
        upward(fs_place).start()

    @pl.when(has_down)
    def _():
        downward(fs_place).start()

    route(ids_ref, fill_ref, slots_ref, taking_ref)
    spread_rows(taking_ref, cot_ref, cot_out_ref)

    def relay(step):
        below, above = fs_place - step, fs_place + step

        @pl.when(below >= 0)
        def _():
            upward(below).wait_recv()

        @pl.when((below >= 0) & has_up)
        def _():
            upward(below).start()

        @pl.when(above < fs_count)
        def _():
            downward(above).wait_recv()

        @pl.when((above < fs_count) & has_down)
        def _():
            downward(above).start()

        mark = fs_peer(step)
        z_landed(mark).wait_recv()
        block = seq_ref.at[sp_place, mark]
        to_across(block, mark).start()
        to_core(block, mark).start()

    each(fs_count, relay)

    def pass_on(mark, _):
        to_across(own_tokens, mark).wait_recv()
        late(mark).start()
        return 0

    cots = cot_swap(cot_out_ref, cots_ref, pl.ds(0, first_rows), cot_send, cot_recv, cot_local)
    cots.start_all()
    weights = crossing(shard_ref, full_ref, *cross)
    weights.start_cross()
    lax.fori_loop(0, fs_count, pass_on, 0)

    def end(mark, _):
        to_core(own_tokens, mark).wait_recv()
        late(mark).wait_recv()
        to_core(own_tokens, mark).wait_send()
        to_across(own_tokens, mark).wait_send()
        late(mark).wait_send()

        @pl.when(has_up & (mark <= fs_place))
        def _():
            upward(mark).wait_send()

        @pl.when(has_down & (mark >= fs_place))
        def _():
            downward(mark).wait_send()

        return 0

    lax.fori_loop(0, fs_count, end, 0)
    each(sp_count, lambda step: pack_move(sp_peer(step), sp_place).wait_send())
    each(fs_count, lambda step: z_move(fs_peer(step)).wait_send())
    own_seq.wait()
    cots.finish()
    weights.finish_cross()


FIRST_ROWS = 32


def gather_start(tokens, query, key, value, small, ids, fill, cots, shard):
    sp_count, fs_count = lax.axis_size("sp"), lax.axis_size("fs")
    total = sp_count * fs_count
    fs_sems = pltpu.SemaphoreType.DMA((fs_count,))
    sp_sems = pltpu.SemaphoreType.DMA((sp_count,))
    rows, width = query.shape
    pack = (rows, -(-(3 * width // sp_count + 2 + EXPERTS) // LANES) * LANES)
    count = ids.shape[1]
    slot_rows = (total, CAP, width)
    return pl.pallas_call(
        functools.partial(gather_kernel, FIRST_ROWS),
        in_specs=[IN_PLACE] + [VMEM_WHOLE] * 7 + [IN_PLACE],
        out_specs=[IN_PLACE] * 3 + [VMEM_WHOLE] * 3 + [IN_PLACE],
        out_shape=[
            jax.ShapeDtypeStruct((sp_count, fs_count) + tokens.shape[1:], tokens.dtype),
            jax.ShapeDtypeStruct((sp_count, fs_count) + pack, query.dtype),
            jax.ShapeDtypeStruct(shard.shape, shard.dtype),
            jax.ShapeDtypeStruct((TOPK, count), jnp.int32),
            jax.ShapeDtypeStruct((total * CAP, count), BF16),
            jax.ShapeDtypeStruct(slot_rows, BF16),
            jax.ShapeDtypeStruct(slot_rows, BF16),
        ],
        scratch_shapes=[pltpu.VMEM((sp_count,) + pack, query.dtype)]
        + [fs_sems] * 8
        + [sp_sems] * 2
        + [fs_sems] * 4
        + [pltpu.SemaphoreType.DMA((2,))]
        + swap_semaphores(total)
        + cross_scratch(shard),
        compiler_params=remote_params(5),
        cost_estimate=pl.CostEstimate(
            flops=40_000_000_000, bytes_accessed=4_000_000, transcendentals=0
        ),
        name="gather_start",
    )(tokens, query, key, value, small, ids, fill, cots, shard)


def attend_kernel(
    block,
    scale,
    qkv_ref,
    cos_ref,
    sin_ref,
    crossed_ref,
    shard_ref,
    other_shard_ref,
    cot_out_ref,
    cots_in_ref,
    o_ref,
    lse_ref,
    got_ref,
    shared_ref,
    full_ref,
    other_full_ref,
    cots_ref,
    k_rot,
    send,
    recv,
    local,
    dp_send,
    dp_recv,
    cot_send,
    cot_recv,
    cot_local,
    *cross,
):
    heads, length, _ = k_rot.shape
    wide = heads * HEAD_DIM
    total, own = places()
    seg = length // total
    greet_places()
    greet_dp()

    def head_rows(kind, head):
        return columns(kind * heads + head, HEAD_DIM)

    def turn_keys(head, _):
        rotated = turn(qkv_ref[head_rows(1, head), :].astype(F32), cos_ref[...], sin_ref[...])
        k_rot[head] = rotated.T.astype(BF16)
        return 0

    lax.fori_loop(0, heads, turn_keys, 0)
    await_places(1)
    share = sharing(shared_ref, dp_send, dp_recv)
    share.start_share()
    cap = cots_ref.shape[1]
    cots = cot_swap(
        cot_out_ref,
        cots_ref,
        pl.ds(FIRST_ROWS, cap - FIRST_ROWS),
        cot_send,
        cot_recv,
        cot_local,
    )
    cots.start_all()
    half = len(cross) // 2
    weights = crossing(shard_ref, full_ref, *cross[:half])
    weights.start_cross()
    other_weights = crossing(other_shard_ref, other_full_ref, *cross[half:])
    other_weights.start_cross()
    exchange = Swap(
        lambda place: o_ref.at[:, columns(place, seg)],
        lambda place: got_ref.at[
            columns(place // lax.axis_size("fs"), wide),
            columns(lax.rem(place, lax.axis_size("fs")), seg),
        ],
        send,
        recv,
        local,
    )

    def attend_block(place):
        own_columns = columns(place, block)

        def attend_head(head, _):
            query = turn(
                qkv_ref[head_rows(0, head), own_columns].astype(F32),
                cos_ref[:, own_columns],
                sin_ref[:, own_columns],
            ).astype(BF16)

            def scores_at(index):
                return dot32(k_rot[head, columns(index, block), :], query) * scale

            def weighted(index, weights):
                values = qkv_ref[head_rows(2, head), columns(index, block)]
                return dot32(values, weights.astype(BF16))

            scores = jnp.where(causal(block), scores_at(place), MASKED)
            first_max = jnp.max(scores, axis=0, keepdims=True)
            weights = jnp.exp(scores - first_max)
            first_sum = jnp.sum(weights, axis=0, keepdims=True)

            def step(index, carried):
                running_max, running_sum, running_acc = carried
                part = scores_at(index)
                new_max = jnp.maximum(running_max, jnp.max(part, axis=0, keepdims=True))
                part = jnp.exp(part - new_max)
                factor = jnp.exp(running_max - new_max)
                return (
                    new_max,
                    running_sum * factor + jnp.sum(part, axis=0, keepdims=True),
                    running_acc * factor + weighted(index, part),
                )

            final_max, final_sum, final_acc = lax.fori_loop(
                0, place, step, (first_max, first_sum, weighted(place, weights))
            )
            o_ref[columns(head, HEAD_DIM), own_columns] = (final_acc / final_sum).astype(BF16)
            lse_ref[head, :, own_columns] = final_max + jnp.log(final_sum)
            return 0

        lax.fori_loop(0, heads, attend_head, 0)

    def step(index, _):
        place = length // block - 1 - index
        attend_block(place)

        def begin(part, _):
            exchange.start(place * (block // seg) + part)
            return 0

        lax.fori_loop(0, block // seg, begin, 0)
        return 0

    lax.fori_loop(0, length // block, step, 0)
    exchange.finish()
    share.finish_share()
    weights.finish_cross()
    other_weights.finish_cross()
    cots.finish()


def attend_grad_kernel(
    block,
    scale,
    qkv_ref,
    cos_ref,
    sin_ref,
    o_ref,
    lse_ref,
    ga_ref,
    normed_ref,
    weight_ref,
    back_out_ref,
    sums_ref,
    got_ref,
    tail_ref,
    back_ref,
    spread_ref,
    grad_ref,
    part_send,
    part_got,
    own_part,
    reduced,
    go_feat,
    q_feat,
    q_rows,
    k_feat,
    go_rows,
    delta,
    dq_acc,
    dk_acc,
    dv_acc,
    weight_acc,
    tail_send,
    stage,
    send_in,
    recv_in,
    local_in,
    send_part,
    recv_part,
    send_z,
    recv_z,
    local_z,
    send_tail,
    recv_tail,
    local_tail,
    send_back,
    recv_back,
    local_back,
    send_sums,
    recv_sums,
    local_sums,
):
    heads, length, _ = q_rows.shape
    wide = heads * HEAD_DIM
    total, own = places()
    seg = length // total
    fs_count, sp_count = lax.axis_size("fs"), lax.axis_size("sp")
    fs_place, sp_place = lax.axis_index("fs"), lax.axis_index("sp")
    greet_places()

    def head_rows(kind, head):
        return columns(kind * heads + head, HEAD_DIM)

    def prepare(head, _):
        rotated = turn(qkv_ref[head_rows(0, head), :].astype(F32), cos_ref[...], sin_ref[...])
        q_feat[columns(head, HEAD_DIM), :] = rotated.astype(BF16)
        q_rows[head] = rotated.T.astype(BF16)
        rotated = turn(qkv_ref[head_rows(1, head), :].astype(F32), cos_ref[...], sin_ref[...])
        k_feat[columns(head, HEAD_DIM), :] = rotated.astype(BF16)
        return 0

    arrival = Swap(
        lambda place: ga_ref.at[
            columns(place // fs_count, wide), columns(lax.rem(place, fs_count), seg)
        ],
        lambda place: go_feat.at[:, columns(place, seg)],
        send_in,
        recv_in,
        local_in,
    )
    await_places()
    arrival.start_all()
    back = Swap(
        lambda place: back_out_ref.at[place],
        lambda place: back_ref.at[place],
        send_back,
        recv_back,
        local_back,
    )
    back.start_all()
    lax.fori_loop(0, heads, prepare, 0)
    dq_acc[...] = jnp.zeros_like(dq_acc)
    weight_acc[...] = jnp.zeros_like(weight_acc)
    arrival.finish()

    def prepare_grad(head, _):
        grad = go_feat[columns(head, HEAD_DIM), :].astype(F32)
        go_rows[head] = grad.T.astype(BF16)
        delta[head] = jnp.sum(
            grad * o_ref[columns(head, HEAD_DIM), :].astype(F32), axis=0, keepdims=True
        )
        return 0

    lax.fori_loop(0, heads, prepare_grad, 0)

    def to_sp(place, mark):
        return pltpu.make_async_remote_copy(
            src_ref=part_send.at[place],
            dst_ref=part_got.at[mark],
            send_sem=send_part.at[place],
            recv_sem=recv_part.at[mark],
            device_id={"sp": place},
            device_id_type=pl.DeviceIdType.MESH,
        )

    def to_fs(place, mark):
        return pltpu.make_async_remote_copy(
            src_ref=reduced.at[:, columns(place, seg)],
            dst_ref=got_ref.at[:, columns(mark, seg)],
            send_sem=send_z.at[place],
            recv_sem=recv_z.at[mark],
            device_id={"fs": place},
            device_id_type=pl.DeviceIdType.MESH,
        )

    count = length // block

    def key_block(place, _):
        own_columns = columns(place, block)
        own_cos, own_sin = cos_ref[:, own_columns], sin_ref[:, own_columns]

        def key_head(head, _):
            rows = columns(head, HEAD_DIM)
            key_feat = k_feat[rows, own_columns]
            key_rows = key_feat.astype(F32).T.astype(BF16)
            value_rows = qkv_ref[head_rows(2, head), own_columns].astype(F32).T.astype(BF16)

            def terms(index, masked):
                here = columns(index, block)
                scores = dot32(key_rows, q_feat[rows, here]) * scale
                weights = jnp.exp(scores - lse_ref[head, :, here])
                if masked:
                    weights = jnp.where(causal(block), weights, 0.0)
                reach = dot32(value_rows, go_feat[rows, here])
                slopes = (weights * (reach - delta[head, :, here]) * scale).astype(BF16)
                dq_acc[rows, here] += dot32(key_feat, slopes)
                part_key = dot32(slopes, q_rows[head, here, :])
                part_value = dot32(weights.astype(BF16), go_rows[head, here, :])
                return part_key, part_value

            dk_acc[...], dv_acc[...] = terms(place, True)

            def step(index, _):
                part_key, part_value = terms(index, False)
                dk_acc[...] += part_key
                dv_acc[...] += part_value
                return 0

            lax.fori_loop(place + 1, count, step, 0)
            grad_ref[head_rows(0, head), own_columns] = turn_back(
                dq_acc[rows, own_columns], own_cos, own_sin
            ).astype(BF16)
            grad_ref[head_rows(1, head), own_columns] = turn_back(
                dk_acc[...].T, own_cos, own_sin
            ).astype(BF16)
            grad_ref[head_rows(2, head), own_columns] = dv_acc[...].T.astype(BF16)
            return 0

        lax.fori_loop(0, heads, key_head, 0)

        part = dot32(weight_ref[...], grad_ref[:, own_columns])

        @pl.when(place == sp_place)
        def _():
            own_part[...] = part

        @pl.when(place != sp_place)
        def _():
            part_send[place] = part.astype(BF16)
            to_sp(place, sp_place).start()

        weight_acc[...] += dot32(grad_ref[:, own_columns], normed_ref[own_columns, :])
        return 0

    lax.fori_loop(0, count, key_block, 0)

    def to_owner(place, mark):
        return pltpu.make_async_remote_copy(
            src_ref=sums_ref.at[place],
            dst_ref=spread_ref.at[mark],
            send_sem=send_sums.at[place],
            recv_sem=recv_sums.at[mark],
            device_id={"sp": place},
            device_id_type=pl.DeviceIdType.MESH,
        )

    def begin_sums(step, _):
        to_owner(lax.rem(sp_place + step, sp_count), sp_place).start()
        return 0

    lax.fori_loop(1, sp_count, begin_sums, 0)
    own_in = pltpu.make_async_copy(sums_ref.at[sp_place], stage, local_sums.at[0])
    own_out = pltpu.make_async_copy(stage, spread_ref.at[sp_place], local_sums.at[1])
    own_in.start()
    shard, wide_all = tail_send.shape[1], 3 * wide
    flipped = weight_acc[...].T
    for place in range(tail_send.shape[0]):
        tail_send[place, :, :wide_all] = flipped[place * shard : (place + 1) * shard].astype(BF16)
    tail = Swap(
        lambda place: tail_send.at[place],
        lambda place: tail_ref.at[place],
        send_tail,
        recv_tail,
        local_tail,
    )

    def add_part(step, _):
        mark = lax.rem(sp_place + step, sp_count)
        to_sp(mark, mark).wait_recv()
        own_part[...] += part_got[mark].astype(F32)
        return 0

    lax.fori_loop(1, sp_count, add_part, 0)
    reduced[...] = own_part[...].astype(BF16)

    def begin_z(step, _):
        to_fs(lax.rem(fs_place + step, fs_count), fs_place).start()
        return 0

    lax.fori_loop(1, fs_count, begin_z, 0)
    own_z = pltpu.make_async_copy(
        reduced.at[:, columns(fs_place, seg)], got_ref.at[:, columns(fs_place, seg)], local_z
    )
    own_z.start()
    tail.start_all()

    def end_part(step, _):
        place = lax.rem(sp_place + step, sp_count)
        to_sp(place, place).wait_send()
        return 0

    lax.fori_loop(1, sp_count, end_part, 0)

    def end_z(step, _):
        place = lax.rem(fs_place + step, fs_count)
        to_fs(place, place).wait_recv()
        to_fs(place, place).wait_send()
        return 0

    lax.fori_loop(1, fs_count, end_z, 0)
    own_z.wait()
    own_in.wait()
    own_out.start()

    def end_sums(step, _):
        place = lax.rem(sp_place + step, sp_count)
        to_owner(place, place).wait_recv()
        to_owner(place, place).wait_send()
        return 0

    lax.fori_loop(1, sp_count, end_sums, 0)
    own_out.wait()
    back.finish()
    tail.finish()


def attention_block(length, seg):
    return lax.axis_size("fs") * seg


def attend(
    qkv, cosine, sine, crossed, shard, other_shard, cot_out, cots, heads, score_scale
):
    length = qkv.shape[1]
    total = lax.axis_size("sp") * lax.axis_size("fs")
    seg = length // total
    wide = heads * HEAD_DIM
    tokens_here = lax.axis_size("fs") * seg
    return pl.pallas_call(
        functools.partial(attend_kernel, attention_block(length, seg), score_scale),
        in_specs=[VMEM_WHOLE] * 3 + [IN_PLACE] * 5,
        out_specs=[VMEM_WHOLE] * 2 + [IN_PLACE] * 5,
        out_shape=[
            jax.ShapeDtypeStruct((wide, length), BF16),
            jax.ShapeDtypeStruct((heads, 1, length), F32),
            jax.ShapeDtypeStruct((lax.axis_size("sp") * wide, tokens_here), BF16),
            jax.ShapeDtypeStruct(crossed.shape, crossed.dtype),
            jax.ShapeDtypeStruct(shard.shape, shard.dtype),
            jax.ShapeDtypeStruct(other_shard.shape, other_shard.dtype),
            jax.ShapeDtypeStruct(cots.shape, cots.dtype),
        ],
        input_output_aliases={3: 3, 7: 6},
        scratch_shapes=[pltpu.VMEM((heads, length, HEAD_DIM), BF16)]
        + swap_semaphores(total)
        + share_scratch()
        + swap_semaphores(total)
        + cross_scratch(shard)
        + cross_scratch(other_shard),
        compiler_params=remote_params(1),
        cost_estimate=pl.CostEstimate(
            flops=30_000_000_000, bytes_accessed=4_000_000, transcendentals=0
        ),
        name="attend",
    )(qkv, cosine, sine, crossed, shard, other_shard, cot_out, cots)


def attend_grad(
    qkv, cosine, sine, out, lse, grad_attended, normed, weight, back, sums, heads, score_scale
):
    length = qkv.shape[1]
    sp_count, fs_count = lax.axis_size("sp"), lax.axis_size("fs")
    total = sp_count * fs_count
    seg = length // total
    block = attention_block(length, seg)
    wide = heads * HEAD_DIM
    width = normed.shape[1]
    tail = (total, width // total, -(-3 * wide // LANES) * LANES)
    sp_sems = pltpu.SemaphoreType.DMA((sp_count,))
    fs_sems = pltpu.SemaphoreType.DMA((fs_count,))
    return pl.pallas_call(
        functools.partial(attend_grad_kernel, block, score_scale),
        in_specs=[VMEM_WHOLE] * 8 + [IN_PLACE] * 2,
        out_specs=[IN_PLACE] * 4,
        out_shape=[
            jax.ShapeDtypeStruct((width, block), BF16),
            jax.ShapeDtypeStruct(tail, BF16),
            jax.ShapeDtypeStruct(back.shape, BF16),
            jax.ShapeDtypeStruct(sums.shape, BF16),
        ],
        scratch_shapes=[
            pltpu.VMEM((3 * wide, length), BF16),
            pltpu.VMEM((sp_count, width, block), BF16),
            pltpu.VMEM((sp_count, width, block), BF16),
            pltpu.VMEM((width, block), F32),
            pltpu.VMEM((width, block), BF16),
            pltpu.VMEM((wide, length), BF16),
            pltpu.VMEM((wide, length), BF16),
            pltpu.VMEM((heads, length, HEAD_DIM), BF16),
            pltpu.VMEM((wide, length), BF16),
            pltpu.VMEM((heads, length, HEAD_DIM), BF16),
            pltpu.VMEM((heads, 1, length), F32),
            pltpu.VMEM((wide, length), F32),
            pltpu.VMEM((block, HEAD_DIM), F32),
            pltpu.VMEM((block, HEAD_DIM), F32),
            pltpu.VMEM((3 * wide, width), F32),
            pltpu.VMEM(tail, BF16),
            pltpu.VMEM(sums.shape[1:], BF16),
        ]
        + swap_semaphores(total)
        + [sp_sems, sp_sems, fs_sems, fs_sems, pltpu.SemaphoreType.DMA]
        + swap_semaphores(total)
        + swap_semaphores(total)
        + [sp_sems, sp_sems, pair_semaphores()],
        compiler_params=remote_params(2),
        cost_estimate=pl.CostEstimate(
            flops=60_000_000_000, bytes_accessed=8_000_000, transcendentals=0
        ),
        name="attend_grad",
    )(qkv, cosine, sine, out, lse, grad_attended, normed, weight, back, sums)


def slope_of(gate_val, sigmoid):
    return sigmoid * (1.0 + gate_val * (1.0 - sigmoid))


def dispatch_kernel(
    rows_ref,
    note_ref,
    up_in_ref,
    down_in_ref,
    got_ref,
    got_note_ref,
    up_ref,
    down_ref,
    send,
    recv,
    local,
    send_note,
    recv_note,
    local_note,
    up_send,
    up_recv,
    down_send,
    down_recv,
):
    greet_places()
    greet_dp()
    rows = Swap(
        lambda place: rows_ref.at[place], lambda place: got_ref.at[place], send, recv, local
    )
    notes = Swap(
        lambda place: note_ref.at[place],
        lambda place: got_note_ref.at[place],
        send_note,
        recv_note,
        local_note,
    )
    await_places(1)
    notes.start_all()
    rows.start_all()
    up_share = sharing(up_ref, up_send, up_recv)
    down_share = sharing(down_ref, down_send, down_recv)
    up_share.start_share()
    down_share.start_share()
    notes.finish()
    rows.finish()
    up_share.finish_share()
    down_share.finish_share()


def dispatch(sent, note, up_crossed, down_crossed):
    total = sent.shape[0]
    return pl.pallas_call(
        dispatch_kernel,
        in_specs=[IN_PLACE] * 4,
        out_specs=[IN_PLACE] * 4,
        out_shape=[
            jax.ShapeDtypeStruct(array.shape, array.dtype)
            for array in (sent, note, up_crossed, down_crossed)
        ],
        input_output_aliases={2: 2, 3: 3},
        scratch_shapes=swap_semaphores(total)
        + swap_semaphores(total)
        + share_scratch()
        + share_scratch(),
        compiler_params=remote_params(3),
        cost_estimate=pl.CostEstimate(
            flops=40_000_000_000, bytes_accessed=20_000_000, transcendentals=0
        ),
        name="dispatch",
    )(sent, note, up_crossed, down_crossed)


def expert_kernel(
    x_ref,
    c_ref,
    note_ref,
    gate_ref,
    up_ref,
    down_ref,
    own_x_ref,
    own_g_ref,
    own_gate_ref,
    own_up_ref,
    own_down_ref,
    y_ref,
    dgate_ref,
    dup_ref,
    ddown_ref,
    own_y_ref,
    own_gx_ref,
    own_grads_ref,
    other_ddown_ref,
    got_ref,
    got_note_ref,
    x_feat,
    g_feat,
    gate_of_row,
    acc,
    dots,
    hidden_all,
    gate_all,
    up_all,
    gx_send,
    dots_send,
    own_x_feat,
    ddown_all,
    gate_stage,
    up_stage,
    down_stage,
    send,
    recv,
    local,
    send_note,
    recv_note,
    local_note,
    ddown_send,
    ddown_recv,
    stage_sem,
):
    step = pl.program_id(0)
    tiles = pl.num_programs(0) // 3
    total, cap, width = gx_send.shape
    tile = hidden_all.shape[2]
    own_tile = own_gate_ref.shape[1]
    lanes = dots.shape[1]
    rows = Swap(
        lambda place: gx_send.at[place], lambda place: got_ref.at[place], send, recv, local
    )
    notes = Swap(
        lambda place: dots_send.at[place],
        lambda place: got_note_ref.at[place],
        send_note,
        recv_note,
        local_note,
    )

    def to_dp(index):
        return pltpu.make_async_remote_copy(
            src_ref=ddown_all.at[index],
            dst_ref=other_ddown_ref.at[:, columns(index, tile)],
            send_sem=ddown_send.at[index],
            recv_sem=ddown_recv.at[index],
            device_id={"dp": 1 - lax.axis_index("dp")},
            device_id_type=pl.DeviceIdType.MESH,
        )

    def to_grads(index):
        turn = lax.rem(index, 2)
        high = gate_stage.shape[2]
        weight_rows = own_grads_ref.shape[1] // 3
        owners, lane_rows = down_stage.shape[1], down_stage.shape[2]
        return [
            pltpu.make_async_copy(
                gate_stage.at[turn], own_grads_ref.at[:, columns(index, high)], stage_sem.at[0, turn]
            ),
            pltpu.make_async_copy(
                up_stage.at[turn],
                own_grads_ref.at[
                    :, pl.ds(pl.multiple_of(weight_rows + index * high, high), high)
                ],
                stage_sem.at[1, turn],
            ),
            pltpu.make_async_copy(
                down_stage.at[turn],
                own_grads_ref.at[
                    pl.ds(index * owners, owners), pl.ds(2 * weight_rows, lane_rows)
                ],
                stage_sem.at[2, turn],
            ),
        ]

    def block(place):
        return slice(place * cap, (place + 1) * cap)

    @pl.when(step == 0)
    def _():
        greet_places()
        greet_dp()
        x_feat[...] = x_ref[...].T
        for place in range(total):
            gate_of_row[block(place), :] = jnp.broadcast_to(
                note_ref[place].T[:cap, 0:1], (cap, lanes)
            )
        grads = gate_of_row[:, 0:1] * c_ref[...].astype(F32)
        g_feat[...] = grads.astype(BF16).T
        acc[...] = jnp.zeros_like(acc)
        dots[...] = jnp.zeros_like(dots)
        await_places(1)

    @pl.when(step < tiles)
    def _():
        gate_val = dot32(x_ref[...], gate_ref[...])
        up_val = dot32(x_ref[...], up_ref[...])
        sigmoid = jax.nn.sigmoid(gate_val)
        swished = gate_val * sigmoid
        hidden = (swished * up_val).astype(BF16)
        reach = dot32(c_ref[...], down_ref[...])
        product = hidden.astype(F32) * reach
        for part in range(tile // lanes):
            dots[...] += product[:, part * lanes : (part + 1) * lanes]
        grad_hidden = gate_of_row[:, 0:1] * reach
        gate_part = (grad_hidden * up_val * slope_of(gate_val, sigmoid)).astype(BF16)
        up_part = (grad_hidden * swished).astype(BF16)
        acc[...] += dot_nt(gate_part, gate_ref[...]) + dot_nt(up_part, up_ref[...])
        hidden_all[step] = hidden
        gate_all[step] = gate_part
        up_all[step] = up_part
        ddown = dot32(g_feat[...], hidden).astype(BF16)
        ddown_ref[...] = ddown
        ddown_all[step] = ddown
        to_dp(step).start()

    @pl.when(step == tiles - 1)
    def _():
        for place in range(total):
            gx_send[place] = acc[block(place), :].astype(BF16)
            dots_send[place, 0:1, :cap] = jnp.sum(dots[block(place), :].T, axis=0, keepdims=True)
        acc[...] = jnp.zeros_like(acc)
        rows.start_all()
        notes.start_all()

    @pl.when((step >= tiles) & (step < 2 * tiles))
    def _():
        here = step - tiles
        hidden = hidden_all[here]
        acc[...] += dot_nt(hidden, down_ref[...])
        dgate_ref[...] = dot32(x_feat[...], gate_all[here]).astype(BF16)
        dup_ref[...] = dot32(x_feat[...], up_all[here]).astype(BF16)

    @pl.when(step == 2 * tiles - 1)
    def _():
        for place in range(total):
            y_ref[place] = (gate_of_row[block(place), 0:1] * acc[block(place), :]).astype(BF16)
        own_x_feat[...] = own_x_ref[...].T
        own_y_ref[...] = jnp.zeros_like(own_y_ref)
        own_gx_ref[...] = jnp.zeros_like(own_gx_ref)

    @pl.when(step >= 2 * tiles)
    def _():
        gate_val = dot32(own_x_ref[...], own_gate_ref[...])
        up_val = dot32(own_x_ref[...], own_up_ref[...])
        sigmoid = jax.nn.sigmoid(gate_val)
        swished = gate_val * sigmoid
        hidden = swished * up_val
        hidden_low = hidden.astype(BF16)
        grad_hidden = dot_nt(own_g_ref[...], own_down_ref[...])
        gate_part = (grad_hidden * up_val * slope_of(gate_val, sigmoid)).astype(BF16)
        up_part = (grad_hidden * swished).astype(BF16)
        own_y_ref[...] += dot32(hidden_low, own_down_ref[...])
        own_gx_ref[...] += dot_nt(gate_part, own_gate_ref[...]) + dot_nt(up_part, own_up_ref[...])
        ddown = dot32(hidden.T.astype(BF16), own_g_ref[...]).astype(BF16)
        dgate = dot32(own_x_feat[...], gate_part).astype(BF16)
        dup = dot32(own_x_feat[...], up_part).astype(BF16)
        here = step - 2 * tiles
        turn = lax.rem(here, 2)

        @pl.when(here >= 2)
        def _():
            for copy in to_grads(here - 2):
                copy.wait()

        shard = width // total
        for part in range(own_tile // LANES):
            lanes_here = slice(part * LANES, (part + 1) * LANES)
            rows_here = slice(part * shard, (part + 1) * shard)
            gate_stage[turn, :, rows_here, :] = dgate[:, lanes_here].reshape(total, shard, LANES)
            up_stage[turn, :, rows_here, :] = dup[:, lanes_here].reshape(total, shard, LANES)
        owners, owned = down_stage.shape[1], own_tile // down_stage.shape[1]
        for part in range(width // LANES):
            down_stage[turn, :, part * owned : (part + 1) * owned, :] = ddown[
                :, part * LANES : (part + 1) * LANES
            ].reshape(owners, owned, LANES)
        for copy in to_grads(here):
            copy.start()

    @pl.when(step == 3 * tiles - 1)
    def _():
        for index in (tiles - 2, tiles - 1):
            for copy in to_grads(index):
                copy.wait()
        rows.finish()
        notes.finish()

        def end(index, _):
            to_dp(index).wait()
            return 0

        lax.fori_loop(0, tiles, end, 0)


def expert_pass(rows, cots, note, gate, up, down, own_x, own_g, own_pack, own_down):
    total, cap, width = rows.shape
    count = total * cap
    hidden = gate.shape[1]
    tile = 256
    tiles = hidden // tile
    own_tile = own_down.shape[0] // tiles
    own_count = own_x.shape[0]
    lanes = note.shape[2]
    once = pl.Buffered(1)
    whole = pl.BlockSpec((count, width), lambda i: (0, 0), pipeline_mode=once)
    whole_note = pl.BlockSpec(note.shape, lambda i: (0, 0, 0), pipeline_mode=once)
    whole_own = pl.BlockSpec((own_count, width), lambda i: (0, 0), pipeline_mode=once)
    early = pl.BlockSpec((width, tile), lambda i: (0, jnp.minimum(i, tiles - 1)))
    both = pl.BlockSpec(
        (width, tile), lambda i: (0, jnp.where(i < 2 * tiles, lax.rem(i, tiles), tiles - 1))
    )
    late = pl.BlockSpec((width, tile), lambda i: (0, jnp.clip(i - tiles, 0, tiles - 1)))
    last = pl.BlockSpec((width, own_tile), lambda i: (0, jnp.maximum(i - 2 * tiles, 0)))
    last_up = pl.BlockSpec((width, own_tile), lambda i: (0, jnp.maximum(i - tiles, tiles)))
    owners = own_tile * total // own_down.shape[0]
    high = own_tile // LANES * (width // total)
    last_flat = pl.BlockSpec((own_tile, width), lambda i: (jnp.maximum(i - 2 * tiles, 0), 0))
    return pl.pallas_call(
        expert_kernel,
        grid=(3 * tiles,),
        in_specs=[whole, whole, whole_note, early, early, both]
        + [whole_own, whole_own, last, last_up, last_flat],
        out_specs=[pl.BlockSpec(rows.shape, lambda i: (0, 0, 0), pipeline_mode=once)]
        + [late, late, early]
        + [whole_own, whole_own]
        + [IN_PLACE] * 4,
        out_shape=[jax.ShapeDtypeStruct(rows.shape, BF16)]
        + [jax.ShapeDtypeStruct((width, hidden), BF16)] * 3
        + [jax.ShapeDtypeStruct((own_count, width), F32)] * 2
        + [
            jax.ShapeDtypeStruct((total, 3 * own_down.size // total // LANES, LANES), BF16),
            jax.ShapeDtypeStruct((width, hidden), BF16),
            jax.ShapeDtypeStruct(rows.shape, BF16),
            jax.ShapeDtypeStruct(note.shape, F32),
        ],
        scratch_shapes=[
            pltpu.VMEM((width, count), BF16),
            pltpu.VMEM((width, count), BF16),
            pltpu.VMEM((count, lanes), F32),
            pltpu.VMEM((count, width), F32),
            pltpu.VMEM((count, lanes), F32),
            pltpu.VMEM((tiles, count, tile), BF16),
            pltpu.VMEM((tiles, count, tile), BF16),
            pltpu.VMEM((tiles, count, tile), BF16),
            pltpu.VMEM(rows.shape, BF16),
            pltpu.VMEM(note.shape, F32),
            pltpu.VMEM((width, own_count), BF16),
            pltpu.VMEM((tiles, width, tile), BF16),
            pltpu.VMEM((2, total, high, LANES), BF16),
            pltpu.VMEM((2, total, high, LANES), BF16),
            pltpu.VMEM((2, owners, own_tile // owners * (width // LANES), LANES), BF16),
        ]
        + swap_semaphores(total)
        + swap_semaphores(total)
        + [
            pltpu.SemaphoreType.DMA((tiles,)),
            pltpu.SemaphoreType.DMA((tiles,)),
            pltpu.SemaphoreType.DMA((3, 2)),
        ],
        compiler_params=remote_params(4),
        cost_estimate=pl.CostEstimate(
            flops=80_000_000_000, bytes_accessed=30_000_000, transcendentals=0
        ),
        name="expert_pass",
    )(
        rows.reshape(count, width),
        cots.reshape(count, width),
        note,
        gate,
        up,
        down,
        own_x,
        own_g,
        own_pack,
        own_pack,
        own_down,
    )


def swap_sum(value, axis):
    if lax.axis_size(axis) == 2:
        other = lax.ppermute(value, axis, [(0, 1), (1, 0)])
        return value.astype(F32) + other.astype(F32)
    return lax.psum(value, axis).astype(F32)


def exchange(chunks):
    return lax.all_to_all(chunks, ("sp", "fs"), split_axis=0, concat_axis=0, tiled=True)


def per_device_split(
    tokens,
    expert_ids,
    fill_order,
    attention_gain,
    query_weight,
    key_weight,
    value_weight,
    output_weight,
    mixer_gain,
    router_weight,
    shared_gate,
    shared_up,
    shared_down,
    expert_gate,
    expert_up,
    expert_down,
    cotangent,
):
    seq_count, seg_rows, width = tokens.shape
    token_count = seq_count * seg_rows
    fs_count = lax.axis_size("fs")
    sp_count = lax.axis_size("sp")
    place_count = fs_count * sp_count
    local_heads = HEADS // sp_count
    flat_width = local_heads * HEAD_DIM
    score_scale = HEAD_DIM ** (-0.5)
    length = place_count * seg_rows
    shard_rows = query_weight.shape[0]
    qkv_width = 3 * flat_width

    cot_rows = cotangent.reshape(token_count, width)
    small = jnp.concatenate(
        [
            attention_gain[:, None],
            mixer_gain[:, None],
            router_weight,
            jnp.zeros((shard_rows, LANES - 2 - EXPERTS), BF16),
        ],
        axis=1,
    )
    seq_tokens, own_pack, gate_crossed, slots, taking, cot_outgoing, cots = gather_start(
        tokens,
        query_weight,
        key_weight,
        value_weight,
        small,
        expert_ids.reshape(token_count, TOPK).T,
        fill_order.reshape(1, token_count),
        cot_rows,
        expert_gate,
    )
    seq_tokens = seq_tokens.reshape(length, width)
    own_pack = own_pack.reshape(width, own_pack.shape[-1])
    qkv_own = own_pack[:, :qkv_width]
    gain_one = own_pack[:, qkv_width].astype(F32)
    gain_two = own_pack[:, qkv_width + 1].astype(F32)
    router_full = own_pack[:, qkv_width + 2 : qkv_width + 2 + EXPERTS]

    def gather_all(shard):
        return lax.all_gather(shard, ("sp", "fs"), axis=0, tiled=True)

    output_sent, shared_pack, shared_down_sent, seq_tokens = lax.optimization_barrier(
        (
            output_weight,
            jnp.concatenate([shared_gate, shared_up], axis=1),
            shared_down,
            seq_tokens,
        )
    )
    output_full = gather_all(output_sent)
    shared_pack = gather_all(shared_pack)
    shared_down_full = gather_all(shared_down_sent)
    slot_total = CAP * EXPERTS

    half = HEAD_DIM // 2
    frequency = 10000.0 ** (-jnp.arange(half, dtype=F32) / half)
    angles = frequency[:, None] * jnp.arange(length, dtype=jnp.int32).astype(F32)[None, :]
    cosine, sine = jnp.cos(angles), jnp.sin(angles)

    normed_seq = norm_apply(seq_tokens.astype(F32), gain_one).astype(BF16)
    qkv = jnp.einsum("de,ld->el", qkv_own, normed_seq, preferred_element_type=F32).astype(BF16)
    out_heads, lse, attended, gate_own, up_crossed, down_crossed, arrived_cots = attend(
        qkv,
        cosine,
        sine,
        gate_crossed,
        expert_up,
        expert_down,
        cot_outgoing,
        cots,
        local_heads,
        score_scale,
    )
    residual = tokens.astype(F32).reshape(token_count, width)

    def outer(left, right):
        return lax.dot_general(left, right, (((0,), (0,)), ((), ())), preferred_element_type=F32)

    middle = residual + outer(attended, output_full)
    mixed_in = norm_apply(middle, gain_two).astype(BF16)

    logits = dot32(mixed_in, router_full)
    def gate_values(raw_logits):
        shifted = jnp.exp(raw_logits - jnp.max(raw_logits, axis=-1, keepdims=True))
        router_probs = shifted / jnp.sum(shifted, axis=-1, keepdims=True)
        picked = jnp.sum(router_probs[:, None, :] * onehot_float, axis=2)
        return picked / jnp.sum(picked, axis=1, keepdims=True)

    choices = expert_ids.reshape(token_count, TOPK)
    expert_onehot = choices[:, :, None] == jnp.arange(EXPERTS, dtype=jnp.int32)[None, None, :]
    onehot_float = expert_onehot.astype(F32)
    gate_weights, gate_pull = jax.vjp(gate_values, logits)
    slot_ids = jnp.arange(slot_total, dtype=jnp.int32)
    takes_a = slot_ids[:, None] == slots[0][None, :]
    takes_b = slot_ids[:, None] == slots[1][None, :]

    gate_of_slot = jnp.sum(
        jnp.where(takes_a, gate_weights[None, :, 0], 0.0)
        + jnp.where(takes_b, gate_weights[None, :, 1], 0.0),
        axis=1,
    )
    outgoing = dot32(taking, mixed_in).astype(BF16)
    note = jnp.pad(
        gate_of_slot.reshape(place_count, 1, CAP), ((0, 0), (0, NOTE_ROWS - 1), (0, LANES - CAP))
    )
    rows, notes, up_own, down_own = dispatch(
        outgoing.reshape(place_count, CAP, width), note, up_crossed, down_crossed
    )
    (
        expert_out,
        dgate,
        dup,
        ddown,
        shared_out,
        grad_mixed_shared,
        grad_shared,
        ddown_other,
        grad_returned,
        dots,
    ) = expert_pass(
        rows,
        arrived_cots,
        notes,
        gate_own.reshape(width, -1),
        up_own.reshape(width, -1),
        down_own.reshape(width, -1),
        mixed_in,
        cot_rows,
        shared_pack,
        shared_down_full,
    )
    grad_shared = lax.psum_scatter(grad_shared, ("sp", "fs"), scatter_dimension=0)
    grad_returned = grad_returned.reshape(slot_total, width)
    dots = dots[:, 0, :CAP].reshape(slot_total)

    def to_dp(value):
        return lax.ppermute(value, "dp", [(0, 1), (1, 0)])

    def sum_of(grad, other):
        total = (grad.astype(F32) + other.astype(F32)).astype(BF16)
        return total.reshape(sp_count, width // sp_count, grad.shape[1])

    def spread(parts):
        return lax.all_to_all(parts, "sp", split_axis=0, concat_axis=0, tiled=True).astype(F32)

    other_gate, other_up = to_dp(dgate), to_dp(dup)

    grad_result = cot_rows.astype(F32)
    grad_gates = jnp.stack(
        [
            jnp.sum(jnp.where(slots[j][:, None] == slot_ids[None, :], dots[None, :], 0.0), axis=1)
            for j in range(TOPK)
        ],
        axis=1,
    )
    (grad_logits,) = gate_pull(grad_gates)
    grad_logits = grad_logits.astype(BF16)
    grad_router = outer(mixed_in, grad_logits)
    grad_mixed = (
        outer(taking, grad_returned) + dot_nt(grad_logits, router_full) + grad_mixed_shared
    )
    _, norm_two_pull = jax.vjp(norm_apply, middle, gain_two)
    grad_middle_part, grad_gain_two = norm_two_pull(grad_mixed)
    grad_middle = grad_result + grad_middle_part
    grad_proj = grad_middle.astype(BF16)
    grad_output_matrix = dot32(attended, grad_proj)
    grad_attended = dot_nt(output_full, grad_proj).astype(BF16)
    grad_normed, tail, returned, sum_down = attend_grad(
        qkv,
        cosine,
        sine,
        out_heads,
        lse,
        grad_attended,
        normed_seq,
        qkv_own,
        expert_out,
        sum_of(ddown, ddown_other),
        local_heads,
        score_scale,
    )
    sum_down = sum_down.astype(F32)
    other_gate, other_up, grad_normed = lax.optimization_barrier(
        (other_gate, other_up, grad_normed)
    )
    sum_up = spread(sum_of(dup, other_up))
    sum_gate = spread(sum_of(dgate, other_gate))
    output = (middle + shared_out + outer(taking, returned.reshape(slot_total, width))).astype(BF16)
    grad_normed = grad_normed.T.astype(F32)
    _, norm_one_pull = jax.vjp(lambda values: norm_apply(values, gain_one), residual)
    (grad_residual_part,) = norm_one_pull(grad_normed)
    grad_tokens = grad_middle + grad_residual_part

    dense = jnp.concatenate(
        [
            grad_output_matrix.astype(BF16),
            grad_router.astype(BF16),
            jnp.pad(grad_gain_two[:, None], ((0, 0), (0, LANES - EXPERTS - 1))).astype(BF16),
        ],
        axis=1,
    )
    dense = lax.psum_scatter(dense, ("sp", "fs"), scatter_dimension=0, tiled=True)
    tail = tail.reshape(sp_count, fs_count, shard_rows, tail.shape[2])[:, :, :, :qkv_width]
    tail = jnp.sum(tail.astype(F32), axis=1).astype(BF16)
    sum_dense = swap_sum(dense, "dp")
    sum_shared = swap_sum(grad_shared, "dp")
    sum_tail = swap_sum(tail, "dp")
    sum_qkv = sum_tail.reshape(sp_count, shard_rows, 3, flat_width)
    sum_qkv = jnp.transpose(sum_qkv, (2, 1, 0, 3)).reshape(3, shard_rows, width)
    sum_gain_one = sum(
        jnp.sum(weight.astype(F32) * grad, axis=1)
        for weight, grad in zip((query_weight, key_weight, value_weight), sum_qkv)
    ) / attention_gain.astype(F32)
    weight_rows = grad_shared.shape[0] // 3

    def lane_blocks(flat, high):
        blocks = flat.reshape(-1, high, LANES)
        return jnp.transpose(blocks, (1, 0, 2)).reshape(high, -1)

    sum_shared_gate = lane_blocks(sum_shared[:weight_rows], shard_rows)
    sum_shared_up = lane_blocks(sum_shared[weight_rows : 2 * weight_rows], shard_rows)
    sum_shared_down = lane_blocks(sum_shared[2 * weight_rows :], shared_down.shape[0])
    return (
        output.reshape(tokens.shape),
        grad_tokens.reshape(tokens.shape),
        sum_gain_one,
        sum_qkv[0],
        sum_qkv[1],
        sum_qkv[2],
        sum_dense[:, :width],
        sum_dense[:, width + EXPERTS],
        sum_dense[:, width : width + EXPERTS],
        sum_shared_gate,
        sum_shared_up,
        sum_shared_down,
        sum_gate,
        sum_up,
        sum_down,
    )


def per_device_any(*shards):
    fs_count, sp_count = lax.axis_size("fs"), lax.axis_size("sp")
    same = shards[0].shape[0] == fs_count and EXPERTS == 4 * fs_count
    if same and sp_count == 4 and lax.axis_size("dp") == 2:
        return per_device_split(*shards)
    return per_device(*shards)


def solution(mesh):
    placed = (
        P("dp", ("sp", "fs"), None),
        P("dp", ("sp", "fs"), None),
        P("dp", ("sp", "fs")),
        P(("sp", "fs")),
        P(("sp", "fs"), None),
        P(("sp", "fs"), None),
        P(("sp", "fs"), None),
        P(("sp", "fs"), None),
        P(("sp", "fs")),
        P(("sp", "fs"), None),
        P(("sp", "fs"), None),
        P(("sp", "fs"), None),
        P(("sp", "fs"), None),
        P("fs", "sp", None),
        P("fs", "sp", None),
        P("fs", "sp", None),
        P("dp", ("sp", "fs"), None),
    )
    return jax.shard_map(
        per_device_any,
        mesh=mesh,
        in_specs=placed,
        out_specs=(
            P("dp", ("sp", "fs"), None),
            P("dp", ("sp", "fs"), None),
            P(("sp", "fs")),
            P(("sp", "fs"), None),
            P(("sp", "fs"), None),
            P(("sp", "fs"), None),
            P(("sp", "fs"), None),
            P(("sp", "fs")),
            P(("sp", "fs"), None),
            P(("sp", "fs"), None),
            P(("sp", "fs"), None),
            P(("sp", "fs"), None),
            P("fs", "sp", None),
            P("fs", "sp", None),
            P("fs", "sp", None),
        ),
        check_vma=False,
    )
```

```python
import functools
import math

import jax
import jax.numpy as jnp
from jax import lax
from jax.experimental import pallas as pl
from jax.experimental.pallas import tpu as pltpu
from jax.sharding import PartitionSpec as P

HEADS = 12
HEAD_DIM = 64
EXPERTS = 16
TOPK = 2
CAP = 72


EPSILON = 1e-06
MASKED = -1e30


def norm_apply(values, gain_row):
    inverse_root = lax.rsqrt(jnp.mean(values * values, axis=-1, keepdims=True) + EPSILON)
    return values * inverse_root * gain_row


def swish(values):
    return values * jax.nn.sigmoid(values)


def glu_product(gate_part, up_part):
    return swish(gate_part) * up_part


def rotate(values, positions):
    half_dim = values.shape[-1] // 2
    frequency = 10000.0 ** (-jnp.arange(half_dim, dtype=jnp.float32) / half_dim)
    angles = positions.astype(jnp.float32)[:, None] * frequency[None, :]
    cosine_table = jnp.cos(angles)[:, None, :]
    sine_table = jnp.sin(angles)[:, None, :]
    front_part = values[..., :half_dim]
    back_part = values[..., half_dim:]
    return jnp.concatenate(
        [
            front_part * cosine_table - back_part * sine_table,
            back_part * cosine_table + front_part * sine_table,
        ],
        axis=-1,
    )


def place_rows(indices, quarter_rows, segment_rows, fs_count):
    source_device = indices // quarter_rows
    row_inside = indices % quarter_rows
    return (
        row_inside // segment_rows * fs_count + source_device
    ) * segment_rows + row_inside % segment_rows


def to_heads(stacked):
    return lax.all_to_all(stacked, "sp", split_axis=3, concat_axis=2, tiled=True)


def to_tokens(stacked):
    return lax.all_to_all(stacked, "sp", split_axis=2, concat_axis=3, tiled=True)


def to_experts(buffer):
    return lax.all_to_all(buffer, "fs", split_axis=1, concat_axis=0, tiled=True)


def from_experts(buffer):
    return lax.all_to_all(buffer, "fs", split_axis=0, concat_axis=1, tiled=True)


def score_grads(
    query_part,
    query_rows,
    key_part,
    value_part,
    key_rows,
    grad_part,
    lse_part,
    delta_part,
    score_scale,
):
    allowed = key_rows[None, None, None, :] <= query_rows[None, None, :, None]
    scores = (
        jnp.einsum("bqhd,bkhd->bhqk", query_part, key_part, preferred_element_type=jnp.float32)
        * score_scale
    )
    weights = jnp.where(allowed, jnp.exp(scores - lse_part[..., None]), 0.0)
    grad_value = jnp.einsum(
        "bhqk,bqhd->bkhd",
        weights.astype(jnp.bfloat16),
        grad_part,
        preferred_element_type=jnp.float32,
    )
    grad_weights = jnp.einsum(
        "bqhd,bkhd->bhqk", grad_part, value_part, preferred_element_type=jnp.float32
    )
    grad_scores = (weights * (grad_weights - delta_part[..., None]) * score_scale).astype(
        jnp.bfloat16
    )
    grad_query = jnp.einsum(
        "bhqk,bkhd->bqhd", grad_scores, key_part, preferred_element_type=jnp.float32
    )
    grad_key = jnp.einsum(
        "bhqk,bqhd->bkhd", grad_scores, query_part, preferred_element_type=jnp.float32
    )
    return (grad_query, grad_key, grad_value)


def per_device(
    tokens,
    expert_ids,
    fill_order,
    attention_gain,
    query_weight,
    key_weight,
    value_weight,
    output_weight,
    mixer_gain,
    router_weight,
    shared_gate,
    shared_up,
    shared_down,
    expert_gate,
    expert_up,
    expert_down,
    cotangent,
):
    seq_count, seg_rows, model_width = tokens.shape
    token_count = seq_count * seg_rows
    fs_count = lax.axis_size("fs")
    sp_count = lax.axis_size("sp")
    fs_place = lax.axis_index("fs")
    local_heads = HEADS // sp_count
    score_scale = HEAD_DIM ** (-0.5)
    (
        gain_full,
        query_full,
        key_full,
        value_full,
        output_full,
        mixer_full,
        router_full,
        shared_gate_full,
        shared_up_full,
        shared_down_full,
    ) = (
        lax.all_gather(attention_gain, ("sp", "fs"), axis=0, tiled=True),
        lax.all_gather(query_weight, ("sp", "fs"), axis=0, tiled=True),
        lax.all_gather(key_weight, ("sp", "fs"), axis=0, tiled=True),
        lax.all_gather(value_weight, ("sp", "fs"), axis=0, tiled=True),
        lax.all_gather(output_weight, ("sp", "fs"), axis=0, tiled=True),
        lax.all_gather(mixer_gain, ("sp", "fs"), axis=0, tiled=True),
        lax.all_gather(router_weight, ("sp", "fs"), axis=0, tiled=True),
        lax.all_gather(shared_gate, ("sp", "fs"), axis=0, tiled=True),
        lax.all_gather(shared_up, ("sp", "fs"), axis=0, tiled=True),
        lax.all_gather(shared_down, ("sp", "fs"), axis=0, tiled=True),
    )
    expert_gate_full, expert_up_full, expert_down_full = (
        lax.all_gather(expert_gate, "sp", axis=1, tiled=True),
        lax.all_gather(expert_up, "sp", axis=1, tiled=True),
        lax.all_gather(expert_down, "sp", axis=1, tiled=True),
    )
    residual = tokens.astype(jnp.float32)
    gain_one = gain_full.astype(jnp.float32)
    gain_two = mixer_full.astype(jnp.float32)
    normed = norm_apply(residual, gain_one).astype(jnp.bfloat16)
    query_raw = jnp.dot(normed, query_full, preferred_element_type=jnp.float32).astype(jnp.bfloat16)
    key_raw = jnp.dot(normed, key_full, preferred_element_type=jnp.float32).astype(jnp.bfloat16)
    value_raw = jnp.dot(normed, value_full, preferred_element_type=jnp.float32).astype(jnp.bfloat16)
    heads_view = to_heads(jnp.stack([query_raw, key_raw, value_raw]))
    quarter_rows = heads_view.shape[2]
    head_shape = (seq_count, quarter_rows, local_heads, HEAD_DIM)
    flat_width = local_heads * HEAD_DIM
    own_rows = place_rows(
        fs_place * quarter_rows + jnp.arange(quarter_rows, dtype=jnp.int32),
        quarter_rows,
        seg_rows,
        fs_count,
    )

    def rotate_own(values):
        return rotate(values, own_rows)

    query_rot = rotate_own(heads_view[0].reshape(head_shape).astype(jnp.float32)).astype(
        jnp.bfloat16
    )
    key_rot = rotate_own(heads_view[1].reshape(head_shape).astype(jnp.float32)).astype(jnp.bfloat16)
    key_flat = key_rot.reshape(seq_count, quarter_rows, flat_width)
    value_flat = heads_view[2]
    keys_all, values_all = (
        lax.all_gather(key_flat, "fs", axis=1, tiled=True),
        lax.all_gather(value_flat, "fs", axis=1, tiled=True),
    )
    total_rows = keys_all.shape[1]
    block_rows = math.gcd(quarter_rows, 512)
    part_shape = (seq_count, block_rows, local_heads, HEAD_DIM)
    offsets = jnp.arange(total_rows // block_rows, dtype=jnp.int32) * block_rows

    def key_slices(offset):
        key_part = lax.dynamic_slice_in_dim(keys_all, offset, block_rows, 1).reshape(part_shape)
        value_part = lax.dynamic_slice_in_dim(values_all, offset, block_rows, 1).reshape(part_shape)
        key_rows = place_rows(
            offset + jnp.arange(block_rows, dtype=jnp.int32), quarter_rows, seg_rows, fs_count
        )
        return (key_part, value_part, key_rows)

    def forward_block(carried, offset):
        running_max, running_sum, running_acc = carried
        key_part, value_part, key_rows = key_slices(offset)
        allowed = key_rows[None, None, None, :] <= own_rows[None, None, :, None]
        scores = (
            jnp.einsum("bqhd,bkhd->bhqk", query_rot, key_part, preferred_element_type=jnp.float32)
            * score_scale
        )
        scores = jnp.where(allowed, scores, MASKED)
        new_max = jnp.maximum(running_max, jnp.max(scores, axis=-1))
        weights = jnp.where(allowed, jnp.exp(scores - new_max[..., None]), 0.0)
        factor = jnp.exp(running_max - new_max)
        running_sum = running_sum * factor + jnp.sum(weights, axis=-1)
        running_acc = running_acc * factor[..., None] + jnp.einsum(
            "bhqk,bkhd->bhqd",
            weights.astype(jnp.bfloat16),
            value_part,
            preferred_element_type=jnp.float32,
        )
        return ((new_max, running_sum, running_acc), None)

    start_state = (
        jnp.full((seq_count, local_heads, quarter_rows), MASKED, jnp.float32),
        jnp.zeros((seq_count, local_heads, quarter_rows), jnp.float32),
        jnp.zeros((seq_count, local_heads, quarter_rows, HEAD_DIM), jnp.float32),
    )
    (final_max, final_sum, final_acc), _ = lax.scan(forward_block, start_state, offsets)
    attended_heads = (final_acc / final_sum[..., None]).astype(jnp.bfloat16)
    log_total = final_max + jnp.log(final_sum)
    attended_view = jnp.transpose(attended_heads, (0, 2, 1, 3))
    attended_flat = attended_view.reshape(seq_count, quarter_rows, flat_width)
    attended_tokens = to_tokens(attended_flat[None])[0]
    middle = residual + jnp.dot(attended_tokens, output_full, preferred_element_type=jnp.float32)
    mixed_in = norm_apply(middle, gain_two).astype(jnp.bfloat16)
    token_rows = mixed_in.reshape(token_count, model_width)
    logits = jnp.dot(token_rows, router_full, preferred_element_type=jnp.float32)
    choices = expert_ids.reshape(token_count, TOPK)
    expert_onehot = choices[:, :, None] == jnp.arange(EXPERTS, dtype=jnp.int32)[None, None, :]
    onehot_float = expert_onehot.astype(jnp.float32)

    def gate_values(raw_logits):
        shifted = jnp.exp(raw_logits - jnp.max(raw_logits, axis=-1, keepdims=True))
        router_probs = shifted / jnp.sum(shifted, axis=-1, keepdims=True)
        picked = jnp.sum(router_probs[:, None, :] * onehot_float, axis=2)
        return picked / jnp.sum(picked, axis=1, keepdims=True)

    gate_weights, gate_pull = jax.vjp(gate_values, logits)
    shared_gate_val = jnp.dot(mixed_in, shared_gate_full, preferred_element_type=jnp.float32)
    shared_up_val = jnp.dot(mixed_in, shared_up_full, preferred_element_type=jnp.float32)
    shared_hidden_full, shared_pull = jax.vjp(glu_product, shared_gate_val, shared_up_val)
    shared_hidden = shared_hidden_full.astype(jnp.bfloat16)
    shared_out = jnp.dot(shared_hidden, shared_down_full, preferred_element_type=jnp.float32)
    onehot_int = expert_onehot.astype(jnp.int32)
    per_token = jnp.sum(onehot_int, axis=1)
    fill_rank = fill_order.reshape(token_count)
    earlier = (fill_rank[None, :] < fill_rank[:, None]).astype(jnp.int32)
    counts = jnp.dot(earlier, per_token, preferred_element_type=jnp.int32)
    slot_ranks = jnp.sum(counts[:, None, :] * onehot_int, axis=2)
    slot_total = CAP * EXPERTS
    slots = jnp.where(slot_ranks < CAP, slot_ranks * EXPERTS + choices, slot_total).reshape(-1)
    outgoing = (
        jnp.zeros((slot_total, model_width), jnp.bfloat16)
        .at[slots]
        .set(jnp.repeat(token_rows, TOPK, axis=0), mode="drop")
    )
    incoming = to_experts(outgoing.reshape(CAP, EXPERTS, model_width))
    expert_gate_val = jnp.einsum(
        "red,edf->ref", incoming, expert_gate_full, preferred_element_type=jnp.float32
    )
    expert_up_val = jnp.einsum(
        "red,edf->ref", incoming, expert_up_full, preferred_element_type=jnp.float32
    )
    expert_hidden_full, expert_pull = jax.vjp(glu_product, expert_gate_val, expert_up_val)
    expert_hidden = expert_hidden_full.astype(jnp.bfloat16)
    expert_out = jnp.einsum(
        "ref,edf->red", expert_hidden, expert_down_full, preferred_element_type=jnp.float32
    ).astype(jnp.bfloat16)
    returned = from_experts(expert_out).reshape(slot_total, model_width)
    padded = jnp.concatenate([returned, jnp.zeros((1, model_width), jnp.bfloat16)], axis=0)
    picked_rows = padded[slots].reshape(token_count, TOPK, model_width).astype(jnp.float32)
    combined = jnp.sum(gate_weights[:, :, None] * picked_rows, axis=1)
    result = (
        middle.reshape(token_count, model_width)
        + shared_out.reshape(token_count, model_width)
        + combined
    )
    output = result.astype(jnp.bfloat16).reshape(seq_count, seg_rows, model_width)
    grad_result = cotangent.astype(jnp.float32).reshape(token_count, model_width)
    grad_gates = jnp.sum(grad_result[:, None, :] * picked_rows, axis=2)
    grad_slots = (
        (gate_weights[:, :, None] * grad_result[:, None, :])
        .astype(jnp.bfloat16)
        .reshape(token_count * TOPK, model_width)
    )
    grad_outgoing = (
        jnp.zeros((slot_total, model_width), jnp.bfloat16).at[slots].set(grad_slots, mode="drop")
    )
    grad_incoming = to_experts(grad_outgoing.reshape(CAP, EXPERTS, model_width))
    grad_expert_down = jnp.einsum(
        "red,ref->edf", grad_incoming, expert_hidden, preferred_element_type=jnp.float32
    )
    grad_expert_hidden = jnp.einsum(
        "red,edf->ref", grad_incoming, expert_down_full, preferred_element_type=jnp.float32
    )
    grad_gate_part, grad_up_part = expert_pull(grad_expert_hidden)
    grad_gate_part = grad_gate_part.astype(jnp.bfloat16)
    grad_up_part = grad_up_part.astype(jnp.bfloat16)
    grad_expert_gate = jnp.einsum(
        "red,ref->edf", incoming, grad_gate_part, preferred_element_type=jnp.float32
    )
    grad_expert_up = jnp.einsum(
        "red,ref->edf", incoming, grad_up_part, preferred_element_type=jnp.float32
    )
    grad_pair_rows = (
        jnp.einsum(
            "ref,edf->red", grad_gate_part, expert_gate_full, preferred_element_type=jnp.float32
        )
        + jnp.einsum(
            "ref,edf->red", grad_up_part, expert_up_full, preferred_element_type=jnp.float32
        )
    ).astype(jnp.bfloat16)
    grad_returned = from_experts(grad_pair_rows).reshape(slot_total, model_width)
    grad_padded = jnp.concatenate(
        [grad_returned, jnp.zeros((1, model_width), jnp.bfloat16)], axis=0
    )
    grad_mixed = jnp.sum(
        grad_padded[slots].reshape(token_count, TOPK, model_width).astype(jnp.float32), axis=1
    )
    (grad_logits,) = gate_pull(grad_gates)
    grad_logits = grad_logits.astype(jnp.bfloat16)
    grad_router = jnp.einsum(
        "td,te->de", token_rows, grad_logits, preferred_element_type=jnp.float32
    )
    grad_mixed = grad_mixed + jnp.einsum(
        "te,de->td", grad_logits, router_full, preferred_element_type=jnp.float32
    )
    grad_shared_out = grad_result.astype(jnp.bfloat16).reshape(seq_count, seg_rows, model_width)
    grad_shared_down = jnp.einsum(
        "blf,bld->fd", shared_hidden, grad_shared_out, preferred_element_type=jnp.float32
    )
    grad_shared_hidden = jnp.einsum(
        "bld,fd->blf", grad_shared_out, shared_down_full, preferred_element_type=jnp.float32
    )
    grad_shared_gate_part, grad_shared_up_part = shared_pull(grad_shared_hidden)
    grad_shared_gate_part = grad_shared_gate_part.astype(jnp.bfloat16)
    grad_shared_up_part = grad_shared_up_part.astype(jnp.bfloat16)
    grad_shared_gate = jnp.einsum(
        "bld,blf->df", mixed_in, grad_shared_gate_part, preferred_element_type=jnp.float32
    )
    grad_shared_up = jnp.einsum(
        "bld,blf->df", mixed_in, grad_shared_up_part, preferred_element_type=jnp.float32
    )
    grad_mixed = (
        grad_mixed.reshape(seq_count, seg_rows, model_width)
        + jnp.einsum(
            "blf,df->bld",
            grad_shared_gate_part,
            shared_gate_full,
            preferred_element_type=jnp.float32,
        )
        + jnp.einsum(
            "blf,df->bld", grad_shared_up_part, shared_up_full, preferred_element_type=jnp.float32
        )
    )
    _, norm_two_pull = jax.vjp(norm_apply, middle, gain_two)
    grad_middle_part, grad_gain_two = norm_two_pull(grad_mixed)
    grad_middle = grad_result.reshape(seq_count, seg_rows, model_width) + grad_middle_part
    grad_proj = grad_middle.astype(jnp.bfloat16)
    grad_output_matrix = jnp.einsum(
        "bld,ble->de", attended_tokens, grad_proj, preferred_element_type=jnp.float32
    )
    grad_attended = jnp.einsum(
        "ble,de->bld", grad_proj, output_full, preferred_element_type=jnp.float32
    ).astype(jnp.bfloat16)
    grad_attended_heads = to_heads(grad_attended[None])[0].reshape(head_shape)
    delta_rows = jnp.einsum(
        "bqhd,bqhd->bhq",
        grad_attended_heads,
        attended_flat.reshape(head_shape),
        preferred_element_type=jnp.float32,
    )

    def key_step(grad_query, offset):
        key_part, value_part, key_rows = key_slices(offset)
        part_query, part_key, part_value = score_grads(
            query_rot,
            own_rows,
            key_part,
            value_part,
            key_rows,
            grad_attended_heads,
            log_total,
            delta_rows,
            score_scale,
        )
        flat_shape = (seq_count, block_rows, flat_width)
        return (
            grad_query + part_query,
            (part_key.reshape(flat_shape), part_value.reshape(flat_shape)),
        )

    grad_query_rot, (key_terms, value_terms) = lax.scan(
        key_step, jnp.zeros(head_shape, jnp.float32), offsets
    )
    own_keys, own_values = (
        lax.psum_scatter(
            key_terms.astype(jnp.bfloat16), "fs", scatter_dimension=0, tiled=True
        ).astype(jnp.float32),
        lax.psum_scatter(
            value_terms.astype(jnp.bfloat16), "fs", scatter_dimension=0, tiled=True
        ).astype(jnp.float32),
    )
    grad_key_rot = jnp.moveaxis(own_keys, 0, 1).reshape(head_shape)
    grad_value = jnp.moveaxis(own_values, 0, 1).reshape(head_shape)
    _, rope_pull = jax.vjp(rotate_own, jnp.zeros(head_shape, jnp.float32))
    (grad_query_raw,) = rope_pull(grad_query_rot)
    (grad_key_raw,) = rope_pull(grad_key_rot)
    stacked_grads = (
        jnp.stack([grad_query_raw, grad_key_raw, grad_value])
        .astype(jnp.bfloat16)
        .reshape(3, seq_count, quarter_rows, flat_width)
    )
    token_grads = to_tokens(stacked_grads)
    grad_query_matrix = jnp.einsum(
        "bld,ble->de", normed, token_grads[0], preferred_element_type=jnp.float32
    )
    grad_key_matrix = jnp.einsum(
        "bld,ble->de", normed, token_grads[1], preferred_element_type=jnp.float32
    )
    grad_value_matrix = jnp.einsum(
        "bld,ble->de", normed, token_grads[2], preferred_element_type=jnp.float32
    )
    grad_normed = (
        jnp.einsum("ble,de->bld", token_grads[0], query_full, preferred_element_type=jnp.float32)
        + jnp.einsum("ble,de->bld", token_grads[1], key_full, preferred_element_type=jnp.float32)
        + jnp.einsum("ble,de->bld", token_grads[2], value_full, preferred_element_type=jnp.float32)
    )
    _, norm_one_pull = jax.vjp(norm_apply, residual, gain_one)
    grad_residual_part, grad_gain_one = norm_one_pull(grad_normed)
    grad_tokens = grad_middle + grad_residual_part
    (
        part_gain_one,
        part_query,
        part_key,
        part_value,
        part_output,
        part_gain_two,
        part_router,
        part_shared_gate,
        part_shared_up,
        part_shared_down,
    ) = (
        lax.psum_scatter(
            grad_gain_one.astype(jnp.bfloat16), ("sp", "fs"), scatter_dimension=0, tiled=True
        ).astype(jnp.float32),
        lax.psum_scatter(
            grad_query_matrix.astype(jnp.bfloat16), ("sp", "fs"), scatter_dimension=0, tiled=True
        ).astype(jnp.float32),
        lax.psum_scatter(
            grad_key_matrix.astype(jnp.bfloat16), ("sp", "fs"), scatter_dimension=0, tiled=True
        ).astype(jnp.float32),
        lax.psum_scatter(
            grad_value_matrix.astype(jnp.bfloat16), ("sp", "fs"), scatter_dimension=0, tiled=True
        ).astype(jnp.float32),
        lax.psum_scatter(
            grad_output_matrix.astype(jnp.bfloat16), ("sp", "fs"), scatter_dimension=0, tiled=True
        ).astype(jnp.float32),
        lax.psum_scatter(
            grad_gain_two.astype(jnp.bfloat16), ("sp", "fs"), scatter_dimension=0, tiled=True
        ).astype(jnp.float32),
        lax.psum_scatter(
            grad_router.astype(jnp.bfloat16), ("sp", "fs"), scatter_dimension=0, tiled=True
        ).astype(jnp.float32),
        lax.psum_scatter(
            grad_shared_gate.astype(jnp.bfloat16), ("sp", "fs"), scatter_dimension=0, tiled=True
        ).astype(jnp.float32),
        lax.psum_scatter(
            grad_shared_up.astype(jnp.bfloat16), ("sp", "fs"), scatter_dimension=0, tiled=True
        ).astype(jnp.float32),
        lax.psum_scatter(
            grad_shared_down.astype(jnp.bfloat16), ("sp", "fs"), scatter_dimension=0, tiled=True
        ).astype(jnp.float32),
    )
    own_gate, own_up, own_down = (
        lax.psum_scatter(
            grad_expert_gate.astype(jnp.bfloat16), "sp", scatter_dimension=1, tiled=True
        ).astype(jnp.float32),
        lax.psum_scatter(
            grad_expert_up.astype(jnp.bfloat16), "sp", scatter_dimension=1, tiled=True
        ).astype(jnp.float32),
        lax.psum_scatter(
            grad_expert_down.astype(jnp.bfloat16), "sp", scatter_dimension=1, tiled=True
        ).astype(jnp.float32),
    )
    (
        sum_gain_one,
        sum_query,
        sum_key,
        sum_value,
        sum_output,
        sum_gain_two,
        sum_router,
        sum_shared_gate,
        sum_shared_up,
        sum_shared_down,
        sum_gate,
        sum_up,
        sum_down,
    ) = (
        lax.psum(part_gain_one.astype(jnp.bfloat16), "dp").astype(jnp.float32),
        lax.psum(part_query.astype(jnp.bfloat16), "dp").astype(jnp.float32),
        lax.psum(part_key.astype(jnp.bfloat16), "dp").astype(jnp.float32),
        lax.psum(part_value.astype(jnp.bfloat16), "dp").astype(jnp.float32),
        lax.psum(part_output.astype(jnp.bfloat16), "dp").astype(jnp.float32),
        lax.psum(part_gain_two.astype(jnp.bfloat16), "dp").astype(jnp.float32),
        lax.psum(part_router.astype(jnp.bfloat16), "dp").astype(jnp.float32),
        lax.psum(part_shared_gate.astype(jnp.bfloat16), "dp").astype(jnp.float32),
        lax.psum(part_shared_up.astype(jnp.bfloat16), "dp").astype(jnp.float32),
        lax.psum(part_shared_down.astype(jnp.bfloat16), "dp").astype(jnp.float32),
        lax.psum(own_gate.astype(jnp.bfloat16), "dp").astype(jnp.float32),
        lax.psum(own_up.astype(jnp.bfloat16), "dp").astype(jnp.float32),
        lax.psum(own_down.astype(jnp.bfloat16), "dp").astype(jnp.float32),
    )
    return (
        output,
        grad_tokens,
        sum_gain_one,
        sum_query,
        sum_key,
        sum_value,
        sum_output,
        sum_gain_two,
        sum_router,
        sum_shared_gate,
        sum_shared_up,
        sum_shared_down,
        sum_gate,
        sum_up,
        sum_down,
    )


BF16 = jnp.bfloat16
F32 = jnp.float32
LANES = 128
NOTE_ROWS = 8
VMEM_WHOLE = pl.BlockSpec(memory_space=pltpu.VMEM)
IN_PLACE = pl.BlockSpec(memory_space=pl.ANY)
ROOM = 60 * 1024 * 1024


def dot32(left, right):
    return jnp.dot(left, right, preferred_element_type=F32)


def dot_nt(left, right):
    return lax.dot_general(left, right, (((1,), (1,)), ((), ())), preferred_element_type=F32)


def turn(values, cosine, sine):
    half = values.shape[0] // 2
    front, back = values[:half], values[half:]
    return jnp.concatenate([front * cosine - back * sine, back * cosine + front * sine], axis=0)


def turn_back(values, cosine, sine):
    half = values.shape[0] // 2
    front, back = values[:half], values[half:]
    return jnp.concatenate([front * cosine + back * sine, back * cosine - front * sine], axis=0)


def causal(block):
    keys = lax.broadcasted_iota(jnp.int32, (block, block), 0)
    queries = lax.broadcasted_iota(jnp.int32, (block, block), 1)
    return keys <= queries


def remote_params(number):
    return pltpu.CompilerParams(
        collective_id=number, has_side_effects=True, vmem_limit_bytes=ROOM
    )


def places():
    sp_count, fs_count = lax.axis_size("sp"), lax.axis_size("fs")
    own = lax.axis_index("sp") * fs_count + lax.axis_index("fs")
    return sp_count * fs_count, own


def at_place(place):
    fs_count = lax.axis_size("fs")
    return {"sp": place // fs_count, "fs": lax.rem(place, fs_count)}


def greet_places():
    total, own = places()
    barrier = pltpu.get_barrier_semaphore()

    def greet(step, _):
        pl.semaphore_signal(
            barrier,
            inc=1,
            device_id=at_place(lax.rem(own + step, total)),
            device_id_type=pl.DeviceIdType.MESH,
        )
        return 0

    lax.fori_loop(1, total, greet, 0)


def await_places(others=0):
    pl.semaphore_wait(pltpu.get_barrier_semaphore(), places()[0] - 1 + others)


def columns(index, size):
    return pl.ds(pl.multiple_of(index * size, size), size)


class Swap:
    def __init__(self, source, target, send, recv, local):
        self.source, self.target = source, target
        self.send, self.recv, self.local = send, recv, local

    def remote(self, place, landing, mark):
        return pltpu.make_async_remote_copy(
            src_ref=self.source(place),
            dst_ref=self.target(landing),
            send_sem=self.send.at[place],
            recv_sem=self.recv.at[mark],
            device_id=at_place(place),
            device_id_type=pl.DeviceIdType.MESH,
        )

    def own(self):
        own = places()[1]
        return pltpu.make_async_copy(self.source(own), self.target(own), self.local)

    def start(self, place):
        own = places()[1]

        @pl.when(place != own)
        def _():
            self.remote(place, own, own).start()

        @pl.when(place == own)
        def _():
            self.own().start()

    def start_all(self):
        total, own = places()

        def begin(step, _):
            self.remote(lax.rem(own + step, total), own, own).start()
            return 0

        lax.fori_loop(1, total, begin, 0)
        self.own().start()

    def finish(self):
        total, own = places()

        def end(step, _):
            place = lax.rem(own + step, total)
            copy = self.remote(place, place, place)
            copy.wait_send()
            copy.wait_recv()
            return 0

        lax.fori_loop(1, total, end, 0)
        self.own().wait()


def swap_semaphores(total):
    return [
        pltpu.SemaphoreType.DMA((total,)),
        pltpu.SemaphoreType.DMA((total,)),
        pltpu.SemaphoreType.DMA,
    ]


class Spread:
    def __init__(self, shard, full, stage, near, far_send, far_recv, dp_send, dp_recv, local):
        self.shard, self.full, self.stage = shard, full, stage
        self.near, self.far_send, self.far_recv = near, far_send, far_recv
        self.dp_send, self.dp_recv, self.local = dp_send, dp_recv, local
        self.sp, self.dp = lax.axis_index("sp"), lax.axis_index("dp")
        self.core = self.sp + 1 - 2 * lax.rem(self.sp, 2)
        self.other = 2 - 2 * (self.sp // 2)
        self.half = shard.shape[1] // 2
        self.rows = pl.ds(pl.multiple_of(self.dp * self.half, self.half), self.half)
        self.dp_rows = pl.ds(pl.multiple_of((1 - self.dp) * self.half, self.half), self.half)

    def to_core(self):
        return pltpu.make_async_remote_copy(
            src_ref=self.shard.at[self.core],
            dst_ref=self.full.at[self.sp],
            send_sem=self.near.at[0],
            recv_sem=self.near.at[1],
            device_id={"sp": self.core},
            device_id_type=pl.DeviceIdType.MESH,
        )

    def to_far(self, turn):
        return pltpu.make_async_remote_copy(
            src_ref=self.shard.at[self.other + turn, self.rows],
            dst_ref=self.full.at[self.sp, self.rows],
            send_sem=self.far_send.at[turn],
            recv_sem=self.far_recv.at[lax.rem(self.sp, 2)],
            device_id={"sp": self.other + turn},
            device_id_type=pl.DeviceIdType.MESH,
        )

    def from_far(self, turn):
        return pltpu.make_async_remote_copy(
            src_ref=self.shard.at[self.other + turn, self.rows],
            dst_ref=self.full.at[self.other + turn, self.rows],
            send_sem=self.far_send.at[turn],
            recv_sem=self.far_recv.at[turn],
            device_id={"sp": self.other + turn},
            device_id_type=pl.DeviceIdType.MESH,
        )

    def to_dp(self, turn):
        block = self.full.at[self.other + turn, self.rows]
        return pltpu.make_async_remote_copy(
            src_ref=block,
            dst_ref=block,
            send_sem=self.dp_send.at[turn],
            recv_sem=self.dp_recv.at[turn],
            device_id={"dp": 1 - self.dp},
            device_id_type=pl.DeviceIdType.MESH,
        )

    def from_dp(self, turn):
        block = self.full.at[self.other + turn, self.dp_rows]
        return pltpu.make_async_remote_copy(
            src_ref=block,
            dst_ref=block,
            send_sem=self.dp_send.at[turn],
            recv_sem=self.dp_recv.at[turn],
            device_id={"dp": 1 - self.dp},
            device_id_type=pl.DeviceIdType.MESH,
        )

    def own_in(self):
        return pltpu.make_async_copy(self.shard.at[self.sp], self.stage, self.local.at[0])

    def own_out(self):
        return pltpu.make_async_copy(self.stage, self.full.at[self.sp], self.local.at[1])

    def start_cross(self):
        self.own_in().start()
        self.to_far(0).start()
        self.to_far(1).start()
        self.to_core().start()

    def finish_cross(self):
        self.own_in().wait()
        self.own_out().start()
        for turn in range(2):
            self.from_far(turn).wait_recv()
            self.to_far(turn).wait_send()
        self.to_core().wait_send()
        self.to_core().wait_recv()
        self.own_out().wait()

    def start_share(self):
        self.to_dp(0).start()
        self.to_dp(1).start()

    def finish_share(self):
        for turn in range(2):
            self.from_dp(turn).wait_recv()
            self.to_dp(turn).wait_send()


def pair_semaphores():
    return pltpu.SemaphoreType.DMA((2,))


def cross_scratch(shard):
    return [pltpu.VMEM(shard.shape[1:], shard.dtype)] + [pair_semaphores()] * 4


def share_scratch():
    return [pair_semaphores()] * 2


def crossing(shard, full, stage, near, far_send, far_recv, local):
    return Spread(shard, full, stage, near, far_send, far_recv, None, None, local)


def sharing(full, dp_send, dp_recv):
    return Spread(full, full, None, None, None, None, dp_send, dp_recv, None)


def greet_dp():
    pl.semaphore_signal(
        pltpu.get_barrier_semaphore(),
        inc=1,
        device_id={"dp": 1 - lax.axis_index("dp")},
        device_id_type=pl.DeviceIdType.MESH,
    )


def route(ids_ref, fill_ref, slots_ref, taking_ref):
    count = fill_ref.shape[1]
    group = EXPERTS // lax.axis_size("fs")
    fill_row = fill_ref[...].astype(F32)
    fill_column = jnp.broadcast_to(fill_row, (8, count)).T[:, 0:1]
    earlier = (fill_column < fill_row).astype(BF16)
    experts = lax.broadcasted_iota(jnp.int32, (EXPERTS, count), 0)
    named = [(experts == ids_ref[j : j + 1, :]).astype(F32) for j in range(TOPK)]
    counts = dot32((named[0] + named[1]).astype(BF16), earlier)
    slots = []
    for j in range(TOPK):
        rank = jnp.sum(counts * named[j], axis=0, keepdims=True).astype(jnp.int32)
        choice = ids_ref[j : j + 1, :]
        holder = lax.rem(choice, group) * lax.axis_size("fs") + choice // group
        slots.append(jnp.where(rank < CAP, holder * CAP + rank, -1))
        slots_ref[j : j + 1, :] = slots[j]
    total = taking_ref.shape[0]
    half = total // 2
    for start in (0, half):
        slot_ids = start + lax.broadcasted_iota(jnp.int32, (half, count), 0)
        taken = (slot_ids == slots[0]) | (slot_ids == slots[1])
        taking_ref[start : start + half, :] = taken.astype(F32).astype(BF16)


def spread_rows(taking_ref, rows_ref, out_ref):
    total, cap, _ = out_ref.shape
    half = total // 2
    for first in (0, half):
        rows = dot32(taking_ref[first * cap : (first + half) * cap, :], rows_ref[...])
        for place in range(half):
            out_ref[first + place] = rows[place * cap : (place + 1) * cap].astype(BF16)


def front_kernel(
    scale,
    tokens_ref,
    query_ref,
    key_ref,
    value_ref,
    small_ref,
    ids_ref,
    fill_ref,
    cot_ref,
    cos_ref,
    sin_ref,
    gate_shard,
    up_shard,
    down_shard,
    slots_ref,
    taking_ref,
    normed_ref,
    weight_ref,
    qkv_ref,
    o_ref,
    lse_ref,
    got_ref,
    cots_ref,
    gate_full,
    up_full,
    down_full,
    seq,
    pack,
    pack_got,
    weight_feat,
    cot_out,
    k_rot,
    z_send,
    z_recv,
    core_send,
    core_recv,
    y_send,
    y_recv,
    late_send,
    late_recv,
    up_send,
    up_recv,
    down_send,
    down_recv,
    pack_send,
    pack_recv,
    local,
    cot_send,
    cot_recv,
    cot_local,
    send,
    recv,
    out_local,
    gate_dp_send,
    gate_dp_recv,
    up_dp_send,
    up_dp_recv,
    *cross,
):
    fs_count, sp_count = lax.axis_size("fs"), lax.axis_size("sp")
    fs_place, sp_place = lax.axis_index("fs"), lax.axis_index("sp")
    heads, length, _ = k_rot.shape
    wide = heads * HEAD_DIM
    seg = tokens_ref.shape[1]
    block = fs_count * seg
    core = sp_place + 1 - 2 * lax.rem(sp_place, 2)
    across = lax.rem(sp_place + 2, sp_count)
    beyond = lax.rem(core + 2, sp_count)

    def fs_peer(step):
        return lax.rem(fs_place + step, fs_count)

    def sp_peer(step):
        return lax.rem(sp_place + step, sp_count)

    def move(source, target, send_sem, recv_sem, where):
        return pltpu.make_async_remote_copy(
            src_ref=source,
            dst_ref=target,
            send_sem=send_sem,
            recv_sem=recv_sem,
            device_id=where,
            device_id_type=pl.DeviceIdType.MESH,
        )

    def each(count, body):
        def run(index, _):
            body(index)
            return 0

        lax.fori_loop(1, count, run, 0)

    greet_places()
    greet_dp()
    part = query_ref.shape[1] // sp_count
    for place in range(sp_count):
        for kind, source in enumerate((query_ref, key_ref, value_ref)):
            pack[place, :, kind * part : (kind + 1) * part] = source[
                :, place * part : (place + 1) * part
            ]
        pack[place, :, 3 * part :] = small_ref[:, : pack.shape[2] - 3 * part]
    await_places(1)

    def pack_move(place, owner, mark):
        return move(
            pack.at[place],
            pack_got.at[owner, fs_place],
            pack_send.at[place],
            pack_recv.at[mark],
            {"sp": place},
        )

    def z_move(place, owner):
        return move(
            tokens_ref.at[place],
            seq.at[sp_place, owner],
            z_send.at[place],
            z_recv.at[owner],
            {"fs": place},
        )

    def to_core(source, mark):
        return move(
            source, seq.at[sp_place, mark], core_send.at[mark], core_recv.at[mark], {"sp": core}
        )

    def to_across(source, mark):
        return move(
            source, seq.at[sp_place, mark], y_send.at[mark], y_recv.at[mark], {"sp": across}
        )

    def late(mark):
        rows = seq.at[across, mark]
        return move(rows, rows, late_send.at[mark], late_recv.at[mark], {"sp": core})

    def upward(mark):
        rows = pack_got.at[:, mark]
        return move(rows, rows, up_send.at[mark], up_recv.at[mark], {"fs": fs_peer(1)})

    def downward(mark):
        rows = pack_got.at[:, mark]
        return move(
            rows, rows, down_send.at[mark], down_recv.at[mark], {"fs": fs_peer(fs_count - 1)}
        )

    each(sp_count, lambda step: pack_move(sp_peer(step), sp_place, sp_place).start())
    each(fs_count, lambda step: z_move(fs_peer(step), fs_place).start())
    own_tokens = tokens_ref.at[fs_place]
    to_across(own_tokens, fs_place).start()
    to_core(own_tokens, fs_place).start()
    own_seq = pltpu.make_async_copy(own_tokens, seq.at[sp_place, fs_place], local.at[0])
    own_pack = pltpu.make_async_copy(
        pack.at[sp_place], pack_got.at[sp_place, fs_place], local.at[1]
    )
    own_seq.start()
    own_pack.start()
    own_pack.wait()

    def pack_here(step):
        mark = sp_peer(step)
        pack_move(mark, mark, mark).wait_recv()

    each(sp_count, pack_here)
    has_up = fs_place < fs_count - 1
    has_down = fs_place > 0

    @pl.when(has_up)
    def _():
        upward(fs_place).start()

    @pl.when(has_down)
    def _():
        downward(fs_place).start()

    route(ids_ref, fill_ref, slots_ref, taking_ref)
    spread_rows(taking_ref, cot_ref, cot_out)

    def relay(step):
        below, above = fs_place - step, fs_place + step

        @pl.when(below >= 0)
        def _():
            upward(below).wait_recv()

        @pl.when((below >= 0) & has_up)
        def _():
            upward(below).start()

        @pl.when(above < fs_count)
        def _():
            downward(above).wait_recv()

        @pl.when((above < fs_count) & has_down)
        def _():
            downward(above).start()

        mark = fs_peer(step)
        z_move(mark, mark).wait_recv()
        rows = seq.at[sp_place, mark]
        to_across(rows, mark).start()
        to_core(rows, mark).start()

    each(fs_count, relay)
    cots = Swap(
        lambda place: cot_out.at[place],
        lambda place: cots_ref.at[place],
        cot_send,
        cot_recv,
        cot_local,
    )
    cots.start_all()
    size = len(cross) // 3
    gate = crossing(gate_shard, gate_full, *cross[:size])
    up = crossing(up_shard, up_full, *cross[size : 2 * size])
    down = crossing(down_shard, down_full, *cross[2 * size :])
    gate.start_cross()
    up.start_cross()
    down.start_cross()

    def pass_on(mark, _):
        to_across(own_tokens, mark).wait_recv()
        late(mark).start()
        return 0

    lax.fori_loop(0, fs_count, pass_on, 0)
    own_seq.wait()
    packed = pack_got[...].reshape(weight_ref.shape)
    weight_ref[...] = packed
    weight_feat[...] = packed.T
    gain_row = weight_feat[3 * wide : 3 * wide + 1, :].astype(F32)

    def head_rows(kind, head):
        return columns(kind * heads + head, HEAD_DIM)

    def project(place):
        own_columns = columns(place, block)
        rows = seq[place].reshape(block, seq.shape[3]).astype(F32)
        scaled = lax.rsqrt(jnp.mean(rows * rows, axis=-1, keepdims=True) + EPSILON)
        normed = (rows * scaled * gain_row).astype(BF16)
        normed_ref[own_columns, :] = normed
        qkv_ref[:, own_columns] = dot_nt(weight_feat[: 3 * wide, :], normed).astype(BF16)

        def turn_keys(head, _):
            rotated = turn(
                qkv_ref[head_rows(1, head), own_columns].astype(F32),
                cos_ref[:, own_columns],
                sin_ref[:, own_columns],
            )
            k_rot[head, own_columns, :] = rotated.T.astype(BF16)
            return 0

        lax.fori_loop(0, heads, turn_keys, 0)

    def from_core(mark, _):
        to_core(own_tokens, mark).wait_recv()
        return 0

    def from_late(mark, _):
        late(mark).wait_recv()
        return 0

    lax.fori_loop(0, fs_count, from_core, 0)
    lax.fori_loop(0, fs_count, from_late, 0)

    def project_step(step, _):
        project(sp_peer(step))
        return 0

    lax.fori_loop(0, sp_count, project_step, 0)

    exchange = Swap(
        lambda place: o_ref.at[:, columns(place, seg)],
        lambda place: got_ref.at[
            columns(place // fs_count, wide), columns(lax.rem(place, fs_count), seg)
        ],
        send,
        recv,
        out_local,
    )

    def attend_block(place):
        own_columns = columns(place, block)

        def attend_head(head, _):
            query = turn(
                qkv_ref[head_rows(0, head), own_columns].astype(F32),
                cos_ref[:, own_columns],
                sin_ref[:, own_columns],
            ).astype(BF16)

            def scores_at(index):
                return dot32(k_rot[head, columns(index, block), :], query) * scale

            def weighted(index, weights):
                values = qkv_ref[head_rows(2, head), columns(index, block)]
                return dot32(values, weights.astype(BF16))

            scores = jnp.where(causal(block), scores_at(place), MASKED)
            first_max = jnp.max(scores, axis=0, keepdims=True)
            weights = jnp.exp(scores - first_max)
            first_sum = jnp.sum(weights, axis=0, keepdims=True)

            def step(index, carried):
                running_max, running_sum, running_acc = carried
                part = scores_at(index)
                new_max = jnp.maximum(running_max, jnp.max(part, axis=0, keepdims=True))
                part = jnp.exp(part - new_max)
                factor = jnp.exp(running_max - new_max)
                return (
                    new_max,
                    running_sum * factor + jnp.sum(part, axis=0, keepdims=True),
                    running_acc * factor + weighted(index, part),
                )

            final_max, final_sum, final_acc = lax.fori_loop(
                0, place, step, (first_max, first_sum, weighted(place, weights))
            )
            o_ref[columns(head, HEAD_DIM), own_columns] = (final_acc / final_sum).astype(BF16)
            lse_ref[head, :, own_columns] = final_max + jnp.log(final_sum)
            return 0

        lax.fori_loop(0, heads, attend_head, 0)

    gate_share = sharing(gate_full, gate_dp_send, gate_dp_recv)
    up_share = sharing(up_full, up_dp_send, up_dp_recv)

    def step(index, _):
        place = length // block - 1 - index
        attend_block(place)

        def begin(part, _):
            exchange.start(place * fs_count + part)
            return 0

        lax.fori_loop(0, fs_count, begin, 0)

        @pl.when(index == 0)
        def _():
            gate.finish_cross()
            gate_share.start_share()

        @pl.when(index == 1)
        def _():
            up.finish_cross()
            up_share.start_share()

        return 0

    lax.fori_loop(0, length // block, step, 0)
    exchange.finish()
    cots.finish()
    down.finish_cross()
    gate_share.finish_share()
    up_share.finish_share()

    def end(mark, _):
        to_core(own_tokens, mark).wait_send()
        to_across(own_tokens, mark).wait_send()
        late(mark).wait_send()

        @pl.when(has_up & (mark <= fs_place))
        def _():
            upward(mark).wait_send()

        @pl.when(has_down & (mark >= fs_place))
        def _():
            downward(mark).wait_send()

        return 0

    lax.fori_loop(0, fs_count, end, 0)
    each(sp_count, lambda step: pack_move(sp_peer(step), sp_place, sp_place).wait_send())
    each(fs_count, lambda step: z_move(fs_peer(step), fs_place).wait_send())


def front(
    tokens, query, key, value, small, ids, fill, cots, cosine, sine, gate, up, down, score_scale
):
    sp_count, fs_count = lax.axis_size("sp"), lax.axis_size("fs")
    total = sp_count * fs_count
    fs_sems = pltpu.SemaphoreType.DMA((fs_count,))
    sp_sems = pltpu.SemaphoreType.DMA((sp_count,))
    rows, width = query.shape
    wide = width // sp_count
    heads = wide // HEAD_DIM
    seg = tokens.shape[1]
    length = total * seg
    pack = (rows, -(-(3 * wide + 2 + EXPERTS) // LANES) * LANES)
    count = ids.shape[1]
    slot_rows = (total, CAP, width)
    return pl.pallas_call(
        functools.partial(front_kernel, score_scale),
        in_specs=[IN_PLACE] + [VMEM_WHOLE] * 9 + [IN_PLACE] * 3,
        out_specs=[VMEM_WHOLE] * 7 + [IN_PLACE] * 5,
        out_shape=[
            jax.ShapeDtypeStruct((TOPK, count), jnp.int32),
            jax.ShapeDtypeStruct((total * CAP, count), BF16),
            jax.ShapeDtypeStruct((length, width), BF16),
            jax.ShapeDtypeStruct((width, pack[1]), BF16),
            jax.ShapeDtypeStruct((3 * wide, length), BF16),
            jax.ShapeDtypeStruct((wide, length), BF16),
            jax.ShapeDtypeStruct((heads, 1, length), F32),
            jax.ShapeDtypeStruct((width, fs_count * seg), BF16),
            jax.ShapeDtypeStruct(slot_rows, BF16),
        ]
        + [jax.ShapeDtypeStruct(shard.shape, shard.dtype) for shard in (gate, up, down)],
        scratch_shapes=[
            pltpu.VMEM((sp_count, fs_count) + tokens.shape[1:], BF16),
            pltpu.VMEM((sp_count,) + pack, BF16),
            pltpu.VMEM((sp_count, fs_count) + pack, BF16),
            pltpu.VMEM((pack[1], width), BF16),
            pltpu.VMEM(slot_rows, BF16),
            pltpu.VMEM((heads, length, HEAD_DIM), BF16),
        ]
        + [fs_sems] * 12
        + [sp_sems] * 2
        + [pair_semaphores()]
        + swap_semaphores(total)
        + swap_semaphores(total)
        + share_scratch()
        + share_scratch()
        + cross_scratch(gate)
        + cross_scratch(up)
        + cross_scratch(down),
        compiler_params=remote_params(1),
        cost_estimate=pl.CostEstimate(
            flops=100_000_000_000, bytes_accessed=4_000_000, transcendentals=0
        ),
        name="front",
    )(tokens, query, key, value, small, ids, fill, cots, cosine, sine, gate, up, down)


def attend_grad_kernel(
    block,
    scale,
    qkv_ref,
    cos_ref,
    sin_ref,
    o_ref,
    lse_ref,
    ga_ref,
    normed_ref,
    weight_ref,
    sums_ref,
    back_out_ref,
    got_ref,
    spread_ref,
    back_ref,
    tail_ref,
    grad_ref,
    near_out,
    near_got,
    pair_out,
    pair_got,
    far_out,
    far_got,
    own_part,
    reduced,
    go_feat,
    q_feat,
    q_rows,
    k_feat,
    k_rows,
    v_rows,
    go_rows,
    delta,
    dq_acc,
    dk_acc,
    dv_acc,
    probs,
    weight_acc,
    tail_send,
    stage,
    send_in,
    recv_in,
    local_in,
    part_sems,
    send_z,
    recv_z,
    local_z,
    send_sums,
    recv_sums,
    local_sums,
    send_back,
    recv_back,
    local_back,
    send_tail,
    recv_tail,
    local_tail,
):
    heads, length, _ = q_rows.shape
    wide = heads * HEAD_DIM
    total, own = places()
    seg = length // total
    fs_count, sp_count = lax.axis_size("fs"), lax.axis_size("sp")
    fs_place, sp_place = lax.axis_index("fs"), lax.axis_index("sp")
    greet_places()

    def head_rows(kind, head):
        return columns(kind * heads + head, HEAD_DIM)

    def prepare(head, _):
        rotated = turn(qkv_ref[head_rows(0, head), :].astype(F32), cos_ref[...], sin_ref[...])
        q_feat[columns(head, HEAD_DIM), :] = rotated.astype(BF16)
        q_rows[head] = rotated.T.astype(BF16)
        rotated = turn(qkv_ref[head_rows(1, head), :].astype(F32), cos_ref[...], sin_ref[...])
        k_feat[columns(head, HEAD_DIM), :] = rotated.astype(BF16)
        k_rows[head] = rotated.T.astype(BF16)
        v_rows[head] = qkv_ref[head_rows(2, head), :].astype(F32).T.astype(BF16)
        return 0

    arrival = Swap(
        lambda place: ga_ref.at[
            columns(place // fs_count, wide), columns(lax.rem(place, fs_count), seg)
        ],
        lambda place: go_feat.at[:, columns(place, seg)],
        send_in,
        recv_in,
        local_in,
    )
    await_places()
    arrival.start_all()
    back = Swap(
        lambda place: back_out_ref.at[place],
        lambda place: back_ref.at[place],
        send_back,
        recv_back,
        local_back,
    )
    back.start_all()
    lax.fori_loop(0, heads, prepare, 0)
    dq_acc[...] = jnp.zeros_like(dq_acc)
    weight_acc[...] = jnp.zeros_like(weight_acc)
    dk_acc[...] = jnp.zeros_like(dk_acc)
    dv_acc[...] = jnp.zeros_like(dv_acc)
    count = length // block
    down = 1 - sp_place // (sp_count // 2)

    def pair_columns(turn_index, step):
        place = turn_index + down * (count - 1 - 2 * turn_index)
        other = place + step - 2 * step * down
        queries = columns(other + down * (place - other), block)
        return queries, columns(place + down * (other - place), block)

    def pair_slot(turn_index, step):
        return turn_index * (2 * count - turn_index + 1) // 2 + step

    def form(head, _):
        rows = columns(head, HEAD_DIM)

        def pair(turn_index, step, masked):
            queries, keys = pair_columns(turn_index, step)
            scores = dot32(k_rows[head, keys, :], q_feat[rows, queries]) * scale
            weights = jnp.exp(scores - lse_ref[head, :, queries])
            if masked:
                weights = jnp.where(causal(block), weights, 0.0)
            probs[head, pair_slot(turn_index, step)] = weights.astype(BF16)

        def turns(turn_index, _):
            pair(turn_index, 0, True)

            def steps(step, _):
                pair(turn_index, step, False)
                return 0

            lax.fori_loop(1, count - turn_index, steps, 0)
            return 0

        lax.fori_loop(0, count, turns, 0)
        return 0

    lax.fori_loop(0, heads, form, 0)
    arrival.finish()

    def prepare_grad(head, _):
        grad = go_feat[columns(head, HEAD_DIM), :].astype(F32)
        go_rows[head] = grad.T.astype(BF16)
        delta[head] = jnp.sum(
            grad * o_ref[columns(head, HEAD_DIM), :].astype(F32), axis=0, keepdims=True
        )
        return 0

    lax.fori_loop(0, heads, prepare_grad, 0)

    core = sp_place + 1 - 2 * lax.rem(sp_place, 2)
    across = lax.rem(sp_place + 2, sp_count)

    def part_move(index, source, target, place):
        return pltpu.make_async_remote_copy(
            src_ref=source,
            dst_ref=target,
            send_sem=part_sems.at[0, index],
            recv_sem=part_sems.at[1, index],
            device_id={"sp": place},
            device_id_type=pl.DeviceIdType.MESH,
        )

    to_near = part_move(0, near_out, near_got, core)
    to_pair = part_move(1, pair_out, pair_got, core)
    to_far = part_move(2, far_out, far_got, across)

    def to_fs(place, mark):
        return pltpu.make_async_remote_copy(
            src_ref=reduced.at[columns(place, seg), :],
            dst_ref=got_ref.at[columns(mark, seg), :],
            send_sem=send_z.at[place],
            recv_sem=recv_z.at[mark],
            device_id={"fs": place},
            device_id_type=pl.DeviceIdType.MESH,
        )


    def segment(turn_index, _):
        place = turn_index + down * (count - 1 - 2 * turn_index)
        own_columns = columns(place, block)
        own_cos, own_sin = cos_ref[:, own_columns], sin_ref[:, own_columns]

        def segment_head(head, _):
            rows = columns(head, HEAD_DIM)

            def pair(step):
                queries, keys = pair_columns(turn_index, step)
                low = probs[head, pair_slot(turn_index, step)]
                weights = low.astype(F32)
                reach = dot32(v_rows[head, keys, :], go_feat[rows, queries])
                slopes = (weights * (reach - delta[head, :, queries]) * scale).astype(BF16)
                dq_acc[rows, queries] += dot32(k_feat[rows, keys], slopes)
                dk_acc[head, keys, :] += dot32(slopes, q_rows[head, queries, :])
                dv_acc[head, keys, :] += dot32(low, go_rows[head, queries, :])

            pair(0)

            def step(index, _):
                pair(index)
                return 0

            lax.fori_loop(1, count - turn_index, step, 0)
            grad_ref[head_rows(0, head), own_columns] = turn_back(
                dq_acc[rows, own_columns], own_cos, own_sin
            ).astype(BF16)
            grad_ref[head_rows(1, head), own_columns] = turn_back(
                dk_acc[head, own_columns, :].T, own_cos, own_sin
            ).astype(BF16)
            grad_ref[head_rows(2, head), own_columns] = dv_acc[head, own_columns, :].T.astype(BF16)
            return 0

        lax.fori_loop(0, heads, segment_head, 0)
        part = dot32(weight_ref[...], grad_ref[:, own_columns])

        @pl.when(place == sp_place)
        def _():
            own_part[...] = part

        @pl.when(place == core)
        def _():
            near_out[...] = part.astype(BF16)
            to_near.start()

        @pl.when(place == lax.rem(core + 2, sp_count))
        def _():
            pair_out[...] = part.astype(BF16)
            to_pair.start()

        @pl.when(place == across)
        def _():
            to_pair.wait_recv()
            far_out[...] = (part + pair_got[...].astype(F32)).astype(BF16)
            to_far.start()

        weight_acc[...] += dot32(grad_ref[:, own_columns], normed_ref[own_columns, :])
        return 0

    lax.fori_loop(0, count, segment, 0)

    def to_owner(place, mark):
        return pltpu.make_async_remote_copy(
            src_ref=sums_ref.at[place],
            dst_ref=spread_ref.at[mark],
            send_sem=send_sums.at[place],
            recv_sem=recv_sums.at[mark],
            device_id={"sp": place},
            device_id_type=pl.DeviceIdType.MESH,
        )

    def begin_sums(step, _):
        to_owner(lax.rem(sp_place + step, sp_count), sp_place).start()
        return 0

    lax.fori_loop(1, sp_count, begin_sums, 0)
    own_in = pltpu.make_async_copy(sums_ref.at[sp_place], stage, local_sums.at[0])
    own_out = pltpu.make_async_copy(stage, spread_ref.at[sp_place], local_sums.at[1])
    own_in.start()
    shard, wide_all = tail_send.shape[1], 3 * wide
    flipped = weight_acc[...].T
    for place in range(tail_send.shape[0]):
        tail_send[place, :, :wide_all] = flipped[place * shard : (place + 1) * shard].astype(BF16)
    tail = Swap(
        lambda place: tail_send.at[place],
        lambda place: tail_ref.at[place],
        send_tail,
        recv_tail,
        local_tail,
    )

    to_near.wait_recv()
    own_part[...] += near_got[...].astype(F32)
    to_far.wait_recv()
    own_part[...] += far_got[...].astype(F32)
    reduced[...] = own_part[...].T.astype(BF16)

    def begin_z(step, _):
        to_fs(lax.rem(fs_place + step, fs_count), fs_place).start()
        return 0

    lax.fori_loop(1, fs_count, begin_z, 0)
    own_z = pltpu.make_async_copy(
        reduced.at[columns(fs_place, seg), :], got_ref.at[columns(fs_place, seg), :], local_z
    )
    own_z.start()
    tail.start_all()

    to_near.wait_send()
    to_pair.wait_send()
    to_far.wait_send()

    def end_z(step, _):
        place = lax.rem(fs_place + step, fs_count)
        to_fs(place, place).wait_recv()
        to_fs(place, place).wait_send()
        return 0

    lax.fori_loop(1, fs_count, end_z, 0)
    own_z.wait()
    own_in.wait()
    own_out.start()

    def end_sums(step, _):
        place = lax.rem(sp_place + step, sp_count)
        to_owner(place, place).wait_recv()
        to_owner(place, place).wait_send()
        return 0

    lax.fori_loop(1, sp_count, end_sums, 0)
    own_out.wait()
    back.finish()
    tail.finish()


def attention_block(length, seg):
    return lax.axis_size("fs") * seg


def attend_grad(
    qkv, cosine, sine, out, lse, grad_attended, normed, weight, sums, back, score_scale
):
    length = qkv.shape[1]
    heads = qkv.shape[0] // (3 * HEAD_DIM)
    sp_count, fs_count = lax.axis_size("sp"), lax.axis_size("fs")
    total = sp_count * fs_count
    seg = length // total
    block = attention_block(length, seg)
    wide = heads * HEAD_DIM
    width = normed.shape[1]
    tail = (total, width // total, -(-3 * wide // LANES) * LANES)
    sp_sems = pltpu.SemaphoreType.DMA((sp_count,))
    fs_sems = pltpu.SemaphoreType.DMA((fs_count,))
    return pl.pallas_call(
        functools.partial(attend_grad_kernel, block, score_scale),
        in_specs=[VMEM_WHOLE] * 8 + [IN_PLACE] * 2,
        out_specs=[IN_PLACE] * 4,
        out_shape=[
            jax.ShapeDtypeStruct((block, width), BF16),
            jax.ShapeDtypeStruct(sums.shape, BF16),
            jax.ShapeDtypeStruct(back.shape, BF16),
            jax.ShapeDtypeStruct(tail, BF16),
        ],
        scratch_shapes=[
            pltpu.VMEM((3 * wide, length), BF16),
            pltpu.VMEM((width, block), BF16),
            pltpu.VMEM((width, block), BF16),
            pltpu.VMEM((width, block), BF16),
            pltpu.VMEM((width, block), BF16),
            pltpu.VMEM((width, block), BF16),
            pltpu.VMEM((width, block), BF16),
            pltpu.VMEM((width, block), F32),
            pltpu.VMEM((block, width), BF16),
            pltpu.VMEM((wide, length), BF16),
            pltpu.VMEM((wide, length), BF16),
            pltpu.VMEM((heads, length, HEAD_DIM), BF16),
            pltpu.VMEM((wide, length), BF16),
            pltpu.VMEM((heads, length, HEAD_DIM), BF16),
            pltpu.VMEM((heads, length, HEAD_DIM), BF16),
            pltpu.VMEM((heads, length, HEAD_DIM), BF16),
            pltpu.VMEM((heads, 1, length), F32),
            pltpu.VMEM((wide, length), F32),
            pltpu.VMEM((heads, length, HEAD_DIM), F32),
            pltpu.VMEM((heads, length, HEAD_DIM), F32),
            pltpu.VMEM((heads, sp_count * (sp_count + 1) // 2, block, block), BF16),
            pltpu.VMEM((3 * wide, width), F32),
            pltpu.VMEM(tail, BF16),
            pltpu.VMEM(sums.shape[1:], BF16),
        ]
        + swap_semaphores(total)
        + [pltpu.SemaphoreType.DMA((2, 3)), fs_sems, fs_sems, pltpu.SemaphoreType.DMA]
        + [sp_sems, sp_sems, pair_semaphores()]
        + swap_semaphores(total)
        + swap_semaphores(total),
        compiler_params=remote_params(2),
        cost_estimate=pl.CostEstimate(
            flops=60_000_000_000, bytes_accessed=8_000_000, transcendentals=0
        ),
        name="attend_grad",
    )(qkv, cosine, sine, out, lse, grad_attended, normed, weight, sums, back)


def slope_of(gate_val, sigmoid):
    return sigmoid * (1.0 + gate_val * (1.0 - sigmoid))


def dispatch_kernel(
    x_ref,
    g_ref,
    gate_ref,
    up_ref,
    down_ref,
    rows_ref,
    note_ref,
    crossed_ref,
    y_ref,
    gx_ref,
    grads_ref,
    got_ref,
    got_note_ref,
    full_ref,
    x_feat,
    gate_stage,
    up_stage,
    down_stage,
    send,
    recv,
    local,
    send_note,
    recv_note,
    local_note,
    dp_send,
    dp_recv,
    stage_sem,
):
    step = pl.program_id(0)
    tiles = pl.num_programs(0)
    total = rows_ref.shape[0]
    width = x_ref.shape[1]
    own_tile = gate_ref.shape[1] // (width // total) * LANES
    rows = Swap(
        lambda place: rows_ref.at[place], lambda place: got_ref.at[place], send, recv, local
    )
    notes = Swap(
        lambda place: note_ref.at[place],
        lambda place: got_note_ref.at[place],
        send_note,
        recv_note,
        local_note,
    )
    share = sharing(full_ref, dp_send, dp_recv)

    def to_grads(index):
        turn = lax.rem(index, 2)
        high = gate_stage.shape[2]
        weight_rows = grads_ref.shape[1] // 3
        owners, lane_rows = down_stage.shape[1], down_stage.shape[2]
        return [
            pltpu.make_async_copy(
                gate_stage.at[turn], grads_ref.at[:, columns(index, high)], stage_sem.at[0, turn]
            ),
            pltpu.make_async_copy(
                up_stage.at[turn],
                grads_ref.at[
                    :, pl.ds(pl.multiple_of(weight_rows + index * high, high), high)
                ],
                stage_sem.at[1, turn],
            ),
            pltpu.make_async_copy(
                down_stage.at[turn],
                grads_ref.at[
                    pl.ds(index * owners, owners), pl.ds(2 * weight_rows, lane_rows)
                ],
                stage_sem.at[2, turn],
            ),
        ]

    @pl.when(step == 0)
    def _():
        greet_places()
        greet_dp()
        x_feat[...] = x_ref[...].T
        y_ref[...] = jnp.zeros_like(y_ref)
        gx_ref[...] = jnp.zeros_like(gx_ref)
        await_places(1)
        notes.start_all()
        rows.start_all()
        share.start_share()

    own_gate = from_lane_blocks(gate_ref, width // total)
    own_up = from_lane_blocks(up_ref, width // total)
    own_down = from_lane_blocks(down_ref, LANES * down_ref.shape[1] // width)
    gate_val = dot32(x_ref[...], own_gate)
    up_val = dot32(x_ref[...], own_up)
    sigmoid = jax.nn.sigmoid(gate_val)
    swished = gate_val * sigmoid
    hidden = swished * up_val
    hidden_low = hidden.astype(BF16)
    grad_hidden = dot_nt(g_ref[...], own_down)
    gate_part = (grad_hidden * up_val * slope_of(gate_val, sigmoid)).astype(BF16)
    up_part = (grad_hidden * swished).astype(BF16)
    y_ref[...] += dot32(hidden_low, own_down)
    gx_ref[...] += dot_nt(gate_part, own_gate) + dot_nt(up_part, own_up)
    ddown = dot32(hidden.T.astype(BF16), g_ref[...]).astype(BF16)
    dgate = dot32(x_feat[...], gate_part).astype(BF16)
    dup = dot32(x_feat[...], up_part).astype(BF16)
    turn = lax.rem(step, 2)

    @pl.when(step >= 2)
    def _():
        for copy in to_grads(step - 2):
            copy.wait()

    shard = width // total
    for part in range(own_tile // LANES):
        lanes_here = slice(part * LANES, (part + 1) * LANES)
        rows_here = slice(part * shard, (part + 1) * shard)
        gate_stage[turn, :, rows_here, :] = dgate[:, lanes_here].reshape(total, shard, LANES)
        up_stage[turn, :, rows_here, :] = dup[:, lanes_here].reshape(total, shard, LANES)
    owners, owned = down_stage.shape[1], own_tile // down_stage.shape[1]
    for part in range(width // LANES):
        down_stage[turn, :, part * owned : (part + 1) * owned, :] = ddown[
            :, part * LANES : (part + 1) * LANES
        ].reshape(owners, owned, LANES)
    for copy in to_grads(step):
        copy.start()

    @pl.when(step == tiles - 1)
    def _():
        for index in (tiles - 2, tiles - 1):
            for copy in to_grads(index):
                copy.wait()
        notes.finish()
        rows.finish()
        share.finish_share()


def dispatch(own_x, own_g, own_pack, sent, note, crossed):
    total, cap, width = sent.shape
    own_rows = own_pack.shape[1] // 3
    tiles = own_rows * total * LANES // width // 256
    own_count = own_x.shape[0]
    high = own_rows // tiles
    owners = total // tiles
    whole = pl.BlockSpec((own_count, width), lambda i: (0, 0), pipeline_mode=pl.Buffered(1))
    return pl.pallas_call(
        dispatch_kernel,
        grid=(tiles,),
        in_specs=[
            whole,
            whole,
            pl.BlockSpec((total, high, LANES), lambda i: (0, i, 0)),
            pl.BlockSpec((total, high, LANES), lambda i: (0, tiles + i, 0)),
            pl.BlockSpec((owners, own_rows, LANES), lambda i: (i, 2, 0)),
        ]
        + [IN_PLACE] * 3,
        out_specs=[whole, whole] + [IN_PLACE] * 4,
        out_shape=[jax.ShapeDtypeStruct((own_count, width), F32)] * 2
        + [
            jax.ShapeDtypeStruct(array.shape, array.dtype)
            for array in (own_pack, sent, note, crossed)
        ],
        input_output_aliases={7: 5},
        scratch_shapes=[
            pltpu.VMEM((width, own_count), BF16),
            pltpu.VMEM((2, total, high, LANES), BF16),
            pltpu.VMEM((2, total, high, LANES), BF16),
            pltpu.VMEM((2, owners, own_rows, LANES), BF16),
        ]
        + swap_semaphores(total)
        + swap_semaphores(total)
        + share_scratch()
        + [pltpu.SemaphoreType.DMA((3, 2))],
        compiler_params=remote_params(3),
        cost_estimate=pl.CostEstimate(
            flops=40_000_000_000, bytes_accessed=20_000_000, transcendentals=0
        ),
        name="dispatch",
    )(own_x, own_g, own_pack, own_pack, own_pack, sent, note, crossed)


def from_lane_blocks(ref, rows):
    owners, high, lanes = ref.shape
    return jnp.concatenate(
        [
            ref[:, part * rows : (part + 1) * rows, :].reshape(owners * rows, lanes)
            for part in range(high // rows)
        ],
        axis=1,
    )


def to_lane_blocks(matrix):
    rows, wide = matrix.shape
    blocks = jnp.transpose(matrix.reshape(rows, wide // LANES, LANES), (1, 0, 2))
    return blocks.reshape(rows * wide // LANES, LANES)


def expert_kernel(
    x_ref,
    c_ref,
    note_ref,
    gate_ref,
    up_ref,
    down_ref,
    y_ref,
    dgate_ref,
    dup_ref,
    sum_ref,
    got_ref,
    got_note_ref,
    x_feat,
    g_feat,
    gate_of_row,
    acc,
    dots,
    hidden_all,
    gate_all,
    up_all,
    gx_send,
    dots_send,
    ddown_all,
    other_all,
    send,
    recv,
    local,
    send_note,
    recv_note,
    local_note,
    ddown_send,
    ddown_recv,
    sum_sem,
):
    step = pl.program_id(0)
    tiles = pl.num_programs(0) // 2
    total, cap, width = gx_send.shape
    tile = hidden_all.shape[2]
    lanes = dots.shape[1]
    rows = Swap(
        lambda place: gx_send.at[place], lambda place: got_ref.at[place], send, recv, local
    )
    notes = Swap(
        lambda place: dots_send.at[place],
        lambda place: got_note_ref.at[place],
        send_note,
        recv_note,
        local_note,
    )

    def to_dp(index):
        return pltpu.make_async_remote_copy(
            src_ref=ddown_all.at[index],
            dst_ref=other_all.at[index],
            send_sem=ddown_send.at[index],
            recv_sem=ddown_recv.at[index],
            device_id={"dp": 1 - lax.axis_index("dp")},
            device_id_type=pl.DeviceIdType.MESH,
        )

    def block(place):
        return slice(place * cap, (place + 1) * cap)

    @pl.when(step == 0)
    def _():
        greet_places()
        greet_dp()
        x_feat[...] = x_ref[...].T
        for place in range(total):
            gate_of_row[block(place), :] = jnp.broadcast_to(
                note_ref[place].T[:cap, 0:1], (cap, lanes)
            )
        grads = gate_of_row[:, 0:1] * c_ref[...].astype(F32)
        g_feat[...] = grads.astype(BF16).T
        acc[...] = jnp.zeros_like(acc)
        dots[...] = jnp.zeros_like(dots)
        await_places(1)

    @pl.when(step < tiles)
    def _():
        gate_val = dot32(x_ref[...], gate_ref[...])
        up_val = dot32(x_ref[...], up_ref[...])
        sigmoid = jax.nn.sigmoid(gate_val)
        swished = gate_val * sigmoid
        hidden = (swished * up_val).astype(BF16)
        reach = dot32(c_ref[...], down_ref[...])
        product = hidden.astype(F32) * reach
        for part in range(tile // lanes):
            dots[...] += product[:, part * lanes : (part + 1) * lanes]
        grad_hidden = gate_of_row[:, 0:1] * reach
        gate_part = (grad_hidden * up_val * slope_of(gate_val, sigmoid)).astype(BF16)
        up_part = (grad_hidden * swished).astype(BF16)
        acc[...] += dot_nt(gate_part, gate_ref[...]) + dot_nt(up_part, up_ref[...])
        hidden_all[step] = hidden
        gate_all[step] = gate_part
        up_all[step] = up_part
        ddown = dot32(g_feat[...], hidden).astype(BF16)
        ddown_all[step] = ddown
        to_dp(step).start()

    @pl.when(step == tiles - 1)
    def _():
        for place in range(total):
            gx_send[place] = acc[block(place), :].astype(BF16)
            dots_send[place, 0:1, :cap] = jnp.sum(dots[block(place), :].T, axis=0, keepdims=True)
        acc[...] = jnp.zeros_like(acc)
        rows.start_all()
        notes.start_all()

    @pl.when(step >= tiles)
    def _():
        here = step - tiles
        hidden = hidden_all[here]
        acc[...] += dot_nt(hidden, down_ref[...])
        dgate_ref[...] = dot32(x_feat[...], gate_all[here]).astype(BF16)
        dup_ref[...] = dot32(x_feat[...], up_all[here]).astype(BF16)

    @pl.when(step == 2 * tiles - 1)
    def _():
        for place in range(total):
            y_ref[place] = (gate_of_row[block(place), 0:1] * acc[block(place), :]).astype(BF16)

        def out(index):
            return pltpu.make_async_copy(
                other_all.at[index], sum_ref.at[:, columns(index, tile)], sum_sem.at[index]
            )

        def add(index, _):
            to_dp(index).wait()
            total = ddown_all[index].astype(F32) + other_all[index].astype(F32)
            other_all[index] = total.astype(BF16)
            out(index).start()
            return 0

        lax.fori_loop(0, tiles, add, 0)
        rows.finish()
        notes.finish()

        def end(index, _):
            out(index).wait()
            return 0

        lax.fori_loop(0, tiles, end, 0)


def expert_pass(rows, cots, note, gate, up, down):
    total, cap, width = rows.shape
    count = total * cap
    hidden = gate.shape[1]
    tile = 256
    tiles = hidden // tile
    lanes = note.shape[2]
    once = pl.Buffered(1)
    whole = pl.BlockSpec((count, width), lambda i: (0, 0), pipeline_mode=once)
    whole_note = pl.BlockSpec(note.shape, lambda i: (0, 0, 0), pipeline_mode=once)
    early = pl.BlockSpec((width, tile), lambda i: (0, jnp.minimum(i, tiles - 1)))
    both = pl.BlockSpec((width, tile), lambda i: (0, lax.rem(i, tiles)))
    late = pl.BlockSpec((width, tile), lambda i: (0, jnp.clip(i - tiles, 0, tiles - 1)))
    return pl.pallas_call(
        expert_kernel,
        grid=(2 * tiles,),
        in_specs=[whole, whole, whole_note, early, early, both],
        out_specs=[pl.BlockSpec(rows.shape, lambda i: (0, 0, 0), pipeline_mode=once)]
        + [late, late]
        + [IN_PLACE] * 3,
        out_shape=[jax.ShapeDtypeStruct(rows.shape, BF16)]
        + [jax.ShapeDtypeStruct((width, hidden), BF16)] * 2
        + [
            jax.ShapeDtypeStruct((width, hidden), BF16),
            jax.ShapeDtypeStruct(rows.shape, BF16),
            jax.ShapeDtypeStruct(note.shape, F32),
        ],
        scratch_shapes=[
            pltpu.VMEM((width, count), BF16),
            pltpu.VMEM((width, count), BF16),
            pltpu.VMEM((count, lanes), F32),
            pltpu.VMEM((count, width), F32),
            pltpu.VMEM((count, lanes), F32),
            pltpu.VMEM((tiles, count, tile), BF16),
            pltpu.VMEM((tiles, count, tile), BF16),
            pltpu.VMEM((tiles, count, tile), BF16),
            pltpu.VMEM(rows.shape, BF16),
            pltpu.VMEM(note.shape, F32),
            pltpu.VMEM((tiles, width, tile), BF16),
            pltpu.VMEM((tiles, width, tile), BF16),
        ]
        + swap_semaphores(total)
        + swap_semaphores(total)
        + [
            pltpu.SemaphoreType.DMA((tiles,)),
            pltpu.SemaphoreType.DMA((tiles,)),
            pltpu.SemaphoreType.DMA((tiles,)),
        ],
        compiler_params=remote_params(4),
        cost_estimate=pl.CostEstimate(
            flops=80_000_000_000, bytes_accessed=30_000_000, transcendentals=0
        ),
        name="expert_pass",
    )(
        rows.reshape(count, width),
        cots.reshape(count, width),
        note,
        gate,
        up,
        down,
    )


def swap_sum(value, axis):
    if lax.axis_size(axis) == 2:
        other = lax.ppermute(value, axis, [(0, 1), (1, 0)])
        return value.astype(F32) + other.astype(F32)
    return lax.psum(value, axis).astype(F32)


def exchange(chunks):
    return lax.all_to_all(chunks, ("sp", "fs"), split_axis=0, concat_axis=0, tiled=True)


def per_device_split(
    tokens,
    expert_ids,
    fill_order,
    attention_gain,
    query_weight,
    key_weight,
    value_weight,
    output_weight,
    mixer_gain,
    router_weight,
    shared_gate,
    shared_up,
    shared_down,
    expert_gate,
    expert_up,
    expert_down,
    cotangent,
):
    seq_count, seg_rows, width = tokens.shape
    token_count = seq_count * seg_rows
    fs_count = lax.axis_size("fs")
    sp_count = lax.axis_size("sp")
    place_count = fs_count * sp_count
    local_heads = HEADS // sp_count
    flat_width = local_heads * HEAD_DIM
    score_scale = HEAD_DIM ** (-0.5)
    length = place_count * seg_rows
    shard_rows = query_weight.shape[0]
    qkv_width = 3 * flat_width

    cot_rows = cotangent.reshape(token_count, width)
    small = jnp.concatenate(
        [
            attention_gain[:, None],
            mixer_gain[:, None],
            router_weight,
            jnp.zeros((shard_rows, LANES - 2 - EXPERTS), BF16),
        ],
        axis=1,
    )
    def gather_all(shard):
        return lax.all_gather(shard, ("sp", "fs"), axis=0, tiled=True)

    half = HEAD_DIM // 2
    frequency = 10000.0 ** (-jnp.arange(half, dtype=F32) / half)
    angles = frequency[:, None] * jnp.arange(length, dtype=jnp.int32).astype(F32)[None, :]
    cosine, sine = jnp.cos(angles), jnp.sin(angles)
    output_full = gather_all(output_weight)
    shared_pack = gather_all(
        jnp.concatenate(
            [to_lane_blocks(shared_gate), to_lane_blocks(shared_up), to_lane_blocks(shared_down)]
        )[None]
    )
    slot_total = CAP * EXPERTS
    (
        slots,
        taking,
        normed_seq,
        own_pack,
        qkv,
        out_heads,
        lse,
        attended,
        arrived_cots,
        gate_own,
        up_own,
        down_crossed,
    ) = front(
        tokens,
        query_weight,
        key_weight,
        value_weight,
        small,
        expert_ids.reshape(token_count, TOPK).T,
        fill_order.reshape(1, token_count),
        cot_rows,
        cosine,
        sine,
        expert_gate,
        expert_up,
        expert_down,
        score_scale,
    )
    qkv_own = own_pack[:, :qkv_width]
    gain_one = own_pack[:, qkv_width].astype(F32)
    gain_two = own_pack[:, qkv_width + 1].astype(F32)
    router_full = own_pack[:, qkv_width + 2 : qkv_width + 2 + EXPERTS]
    residual = tokens.astype(F32).reshape(token_count, width)

    def outer(left, right):
        return lax.dot_general(left, right, (((0,), (0,)), ((), ())), preferred_element_type=F32)

    middle = residual + outer(attended, output_full)
    mixed_in = norm_apply(middle, gain_two).astype(BF16)

    logits = dot32(mixed_in, router_full)
    def gate_values(raw_logits):
        shifted = jnp.exp(raw_logits - jnp.max(raw_logits, axis=-1, keepdims=True))
        router_probs = shifted / jnp.sum(shifted, axis=-1, keepdims=True)
        picked = jnp.sum(router_probs[:, None, :] * onehot_float, axis=2)
        return picked / jnp.sum(picked, axis=1, keepdims=True)

    choices = expert_ids.reshape(token_count, TOPK)
    expert_onehot = choices[:, :, None] == jnp.arange(EXPERTS, dtype=jnp.int32)[None, None, :]
    onehot_float = expert_onehot.astype(F32)
    gate_weights, gate_pull = jax.vjp(gate_values, logits)
    slot_ids = jnp.arange(slot_total, dtype=jnp.int32)
    takes_a = slot_ids[:, None] == slots[0][None, :]
    takes_b = slot_ids[:, None] == slots[1][None, :]

    gate_of_slot = jnp.sum(
        jnp.where(takes_a, gate_weights[None, :, 0], 0.0)
        + jnp.where(takes_b, gate_weights[None, :, 1], 0.0),
        axis=1,
    )
    outgoing = dot32(taking, mixed_in).astype(BF16)
    note = jnp.pad(
        gate_of_slot.reshape(place_count, 1, CAP), ((0, 0), (0, NOTE_ROWS - 1), (0, LANES - CAP))
    )
    shared_out, grad_mixed_shared, grad_shared, rows, notes, down_own = dispatch(
        mixed_in,
        cot_rows,
        shared_pack,
        outgoing.reshape(place_count, CAP, width),
        note,
        down_crossed,
    )
    grad_shared = lax.psum_scatter(grad_shared, ("sp", "fs"), scatter_dimension=0)
    expert_out, dgate, dup, sum_down, grad_returned, dots = expert_pass(
        rows,
        arrived_cots,
        notes,
        gate_own.reshape(width, -1),
        up_own.reshape(width, -1),
        down_own.reshape(width, -1),
    )
    grad_returned = grad_returned.reshape(slot_total, width)
    dots = dots[:, 0, :CAP].reshape(slot_total)

    def to_dp(value):
        return lax.ppermute(value, "dp", [(0, 1), (1, 0)])

    def sum_of(grad, other):
        total = (grad.astype(F32) + other.astype(F32)).astype(BF16)
        return total.reshape(sp_count, width // sp_count, grad.shape[1])

    def spread(parts):
        return lax.all_to_all(parts, "sp", split_axis=0, concat_axis=0, tiled=True).astype(F32)

    other_gate, other_up = to_dp(dgate), to_dp(dup)

    grad_result = cot_rows.astype(F32)
    grad_gates = jnp.stack(
        [
            jnp.sum(jnp.where(slots[j][:, None] == slot_ids[None, :], dots[None, :], 0.0), axis=1)
            for j in range(TOPK)
        ],
        axis=1,
    )
    (grad_logits,) = gate_pull(grad_gates)
    grad_logits = grad_logits.astype(BF16)
    grad_router = outer(mixed_in, grad_logits)
    grad_mixed = (
        outer(taking, grad_returned) + dot_nt(grad_logits, router_full) + grad_mixed_shared
    )
    _, norm_two_pull = jax.vjp(norm_apply, middle, gain_two)
    grad_middle_part, grad_gain_two = norm_two_pull(grad_mixed)
    grad_middle = grad_result + grad_middle_part
    grad_proj = grad_middle.astype(BF16)
    grad_output_matrix = dot32(attended, grad_proj)
    grad_attended = dot_nt(output_full, grad_proj).astype(BF16)
    dense = jnp.concatenate(
        [
            grad_output_matrix.astype(BF16),
            grad_router.astype(BF16),
            jnp.pad(grad_gain_two[:, None], ((0, 0), (0, LANES - EXPERTS - 1))).astype(BF16),
        ],
        axis=1,
    )
    grad_normed, sum_down, returned, tail = attend_grad(
        qkv,
        cosine,
        sine,
        out_heads,
        lse,
        grad_attended,
        normed_seq,
        qkv_own,
        sum_down.reshape(sp_count, width // sp_count, -1),
        expert_out,
        score_scale,
    )
    other_gate, other_up, grad_shared, dense, grad_normed = lax.optimization_barrier(
        (other_gate, other_up, grad_shared, dense, grad_normed)
    )
    dense = lax.psum_scatter(dense, ("sp", "fs"), scatter_dimension=0, tiled=True)
    sum_up = spread(sum_of(dup, other_up))
    sum_gate = spread(sum_of(dgate, other_gate))
    sum_down = sum_down.astype(F32)
    output = (middle + shared_out + outer(taking, returned.reshape(slot_total, width))).astype(BF16)
    grad_normed = grad_normed.astype(F32)
    _, norm_one_pull = jax.vjp(lambda values: norm_apply(values, gain_one), residual)
    (grad_residual_part,) = norm_one_pull(grad_normed)
    grad_tokens = grad_middle + grad_residual_part

    tail = tail.reshape(sp_count, fs_count, shard_rows, tail.shape[2])[:, :, :, :qkv_width]
    tail = jnp.sum(tail.astype(F32), axis=1).astype(BF16)
    sum_dense = swap_sum(dense, "dp")
    sum_shared = swap_sum(grad_shared, "dp")
    sum_tail = swap_sum(tail, "dp")
    sum_qkv = sum_tail.reshape(sp_count, shard_rows, 3, flat_width)
    sum_qkv = jnp.transpose(sum_qkv, (2, 1, 0, 3)).reshape(3, shard_rows, width)
    sum_gain_one = sum(
        jnp.sum(weight.astype(F32) * grad, axis=1)
        for weight, grad in zip((query_weight, key_weight, value_weight), sum_qkv)
    ) / attention_gain.astype(F32)
    weight_rows = grad_shared.shape[0] // 3

    def lane_blocks(flat, high):
        blocks = flat.reshape(-1, high, LANES)
        return jnp.transpose(blocks, (1, 0, 2)).reshape(high, -1)

    sum_shared_gate = lane_blocks(sum_shared[:weight_rows], shard_rows)
    sum_shared_up = lane_blocks(sum_shared[weight_rows : 2 * weight_rows], shard_rows)
    sum_shared_down = lane_blocks(sum_shared[2 * weight_rows :], shared_down.shape[0])
    return (
        output.reshape(tokens.shape),
        grad_tokens.reshape(tokens.shape),
        sum_gain_one,
        sum_qkv[0],
        sum_qkv[1],
        sum_qkv[2],
        sum_dense[:, :width],
        sum_dense[:, width + EXPERTS],
        sum_dense[:, width : width + EXPERTS],
        sum_shared_gate,
        sum_shared_up,
        sum_shared_down,
        sum_gate,
        sum_up,
        sum_down,
    )


def per_device_any(*shards):
    fs_count, sp_count = lax.axis_size("fs"), lax.axis_size("sp")
    same = shards[0].shape[0] == fs_count and EXPERTS == 4 * fs_count
    if same and sp_count == 4 and lax.axis_size("dp") == 2:
        return per_device_split(*shards)
    return per_device(*shards)


def solution(mesh):
    placed = (
        P("dp", ("sp", "fs"), None),
        P("dp", ("sp", "fs"), None),
        P("dp", ("sp", "fs")),
        P(("sp", "fs")),
        P(("sp", "fs"), None),
        P(("sp", "fs"), None),
        P(("sp", "fs"), None),
        P(("sp", "fs"), None),
        P(("sp", "fs")),
        P(("sp", "fs"), None),
        P(("sp", "fs"), None),
        P(("sp", "fs"), None),
        P(("sp", "fs"), None),
        P("fs", "sp", None),
        P("fs", "sp", None),
        P("fs", "sp", None),
        P("dp", ("sp", "fs"), None),
    )
    return jax.shard_map(
        per_device_any,
        mesh=mesh,
        in_specs=placed,
        out_specs=(
            P("dp", ("sp", "fs"), None),
            P("dp", ("sp", "fs"), None),
            P(("sp", "fs")),
            P(("sp", "fs"), None),
            P(("sp", "fs"), None),
            P(("sp", "fs"), None),
            P(("sp", "fs"), None),
            P(("sp", "fs")),
            P(("sp", "fs"), None),
            P(("sp", "fs"), None),
            P(("sp", "fs"), None),
            P(("sp", "fs"), None),
            P("fs", "sp", None),
            P("fs", "sp", None),
            P("fs", "sp", None),
        ),
        check_vma=False,
    )
```

```python
import functools
import math

import jax
import jax.numpy as jnp
from jax import lax
from jax.experimental import pallas as pl
from jax.experimental.pallas import tpu as pltpu
from jax.sharding import PartitionSpec as P

HEADS = 12
HEAD_DIM = 64
EXPERTS = 16
TOPK = 2
CAP = 72


EPSILON = 1e-06
MASKED = -1e30


def norm_apply(values, gain_row):
    inverse_root = lax.rsqrt(jnp.mean(values * values, axis=-1, keepdims=True) + EPSILON)
    return values * inverse_root * gain_row


def swish(values):
    return values * jax.nn.sigmoid(values)


def glu_product(gate_part, up_part):
    return swish(gate_part) * up_part


def rotate(values, positions):
    half_dim = values.shape[-1] // 2
    frequency = 10000.0 ** (-jnp.arange(half_dim, dtype=jnp.float32) / half_dim)
    angles = positions.astype(jnp.float32)[:, None] * frequency[None, :]
    cosine_table = jnp.cos(angles)[:, None, :]
    sine_table = jnp.sin(angles)[:, None, :]
    front_part = values[..., :half_dim]
    back_part = values[..., half_dim:]
    return jnp.concatenate(
        [
            front_part * cosine_table - back_part * sine_table,
            back_part * cosine_table + front_part * sine_table,
        ],
        axis=-1,
    )


def place_rows(indices, quarter_rows, segment_rows, fs_count):
    source_device = indices // quarter_rows
    row_inside = indices % quarter_rows
    return (
        row_inside // segment_rows * fs_count + source_device
    ) * segment_rows + row_inside % segment_rows


def to_heads(stacked):
    return lax.all_to_all(stacked, "sp", split_axis=3, concat_axis=2, tiled=True)


def to_tokens(stacked):
    return lax.all_to_all(stacked, "sp", split_axis=2, concat_axis=3, tiled=True)


def to_experts(buffer):
    return lax.all_to_all(buffer, "fs", split_axis=1, concat_axis=0, tiled=True)


def from_experts(buffer):
    return lax.all_to_all(buffer, "fs", split_axis=0, concat_axis=1, tiled=True)


def score_grads(
    query_part,
    query_rows,
    key_part,
    value_part,
    key_rows,
    grad_part,
    lse_part,
    delta_part,
    score_scale,
):
    allowed = key_rows[None, None, None, :] <= query_rows[None, None, :, None]
    scores = (
        jnp.einsum("bqhd,bkhd->bhqk", query_part, key_part, preferred_element_type=jnp.float32)
        * score_scale
    )
    weights = jnp.where(allowed, jnp.exp(scores - lse_part[..., None]), 0.0)
    grad_value = jnp.einsum(
        "bhqk,bqhd->bkhd",
        weights.astype(jnp.bfloat16),
        grad_part,
        preferred_element_type=jnp.float32,
    )
    grad_weights = jnp.einsum(
        "bqhd,bkhd->bhqk", grad_part, value_part, preferred_element_type=jnp.float32
    )
    grad_scores = (weights * (grad_weights - delta_part[..., None]) * score_scale).astype(
        jnp.bfloat16
    )
    grad_query = jnp.einsum(
        "bhqk,bkhd->bqhd", grad_scores, key_part, preferred_element_type=jnp.float32
    )
    grad_key = jnp.einsum(
        "bhqk,bqhd->bkhd", grad_scores, query_part, preferred_element_type=jnp.float32
    )
    return (grad_query, grad_key, grad_value)


def per_device(
    tokens,
    expert_ids,
    fill_order,
    attention_gain,
    query_weight,
    key_weight,
    value_weight,
    output_weight,
    mixer_gain,
    router_weight,
    shared_gate,
    shared_up,
    shared_down,
    expert_gate,
    expert_up,
    expert_down,
    cotangent,
):
    seq_count, seg_rows, model_width = tokens.shape
    token_count = seq_count * seg_rows
    fs_count = lax.axis_size("fs")
    sp_count = lax.axis_size("sp")
    fs_place = lax.axis_index("fs")
    local_heads = HEADS // sp_count
    score_scale = HEAD_DIM ** (-0.5)
    (
        gain_full,
        query_full,
        key_full,
        value_full,
        output_full,
        mixer_full,
        router_full,
        shared_gate_full,
        shared_up_full,
        shared_down_full,
    ) = (
        lax.all_gather(attention_gain, ("sp", "fs"), axis=0, tiled=True),
        lax.all_gather(query_weight, ("sp", "fs"), axis=0, tiled=True),
        lax.all_gather(key_weight, ("sp", "fs"), axis=0, tiled=True),
        lax.all_gather(value_weight, ("sp", "fs"), axis=0, tiled=True),
        lax.all_gather(output_weight, ("sp", "fs"), axis=0, tiled=True),
        lax.all_gather(mixer_gain, ("sp", "fs"), axis=0, tiled=True),
        lax.all_gather(router_weight, ("sp", "fs"), axis=0, tiled=True),
        lax.all_gather(shared_gate, ("sp", "fs"), axis=0, tiled=True),
        lax.all_gather(shared_up, ("sp", "fs"), axis=0, tiled=True),
        lax.all_gather(shared_down, ("sp", "fs"), axis=0, tiled=True),
    )
    expert_gate_full, expert_up_full, expert_down_full = (
        lax.all_gather(expert_gate, "sp", axis=1, tiled=True),
        lax.all_gather(expert_up, "sp", axis=1, tiled=True),
        lax.all_gather(expert_down, "sp", axis=1, tiled=True),
    )
    residual = tokens.astype(jnp.float32)
    gain_one = gain_full.astype(jnp.float32)
    gain_two = mixer_full.astype(jnp.float32)
    normed = norm_apply(residual, gain_one).astype(jnp.bfloat16)
    query_raw = jnp.dot(normed, query_full, preferred_element_type=jnp.float32).astype(jnp.bfloat16)
    key_raw = jnp.dot(normed, key_full, preferred_element_type=jnp.float32).astype(jnp.bfloat16)
    value_raw = jnp.dot(normed, value_full, preferred_element_type=jnp.float32).astype(jnp.bfloat16)
    heads_view = to_heads(jnp.stack([query_raw, key_raw, value_raw]))
    quarter_rows = heads_view.shape[2]
    head_shape = (seq_count, quarter_rows, local_heads, HEAD_DIM)
    flat_width = local_heads * HEAD_DIM
    own_rows = place_rows(
        fs_place * quarter_rows + jnp.arange(quarter_rows, dtype=jnp.int32),
        quarter_rows,
        seg_rows,
        fs_count,
    )

    def rotate_own(values):
        return rotate(values, own_rows)

    query_rot = rotate_own(heads_view[0].reshape(head_shape).astype(jnp.float32)).astype(
        jnp.bfloat16
    )
    key_rot = rotate_own(heads_view[1].reshape(head_shape).astype(jnp.float32)).astype(jnp.bfloat16)
    key_flat = key_rot.reshape(seq_count, quarter_rows, flat_width)
    value_flat = heads_view[2]
    keys_all, values_all = (
        lax.all_gather(key_flat, "fs", axis=1, tiled=True),
        lax.all_gather(value_flat, "fs", axis=1, tiled=True),
    )
    total_rows = keys_all.shape[1]
    block_rows = math.gcd(quarter_rows, 512)
    part_shape = (seq_count, block_rows, local_heads, HEAD_DIM)
    offsets = jnp.arange(total_rows // block_rows, dtype=jnp.int32) * block_rows

    def key_slices(offset):
        key_part = lax.dynamic_slice_in_dim(keys_all, offset, block_rows, 1).reshape(part_shape)
        value_part = lax.dynamic_slice_in_dim(values_all, offset, block_rows, 1).reshape(part_shape)
        key_rows = place_rows(
            offset + jnp.arange(block_rows, dtype=jnp.int32), quarter_rows, seg_rows, fs_count
        )
        return (key_part, value_part, key_rows)

    def forward_block(carried, offset):
        running_max, running_sum, running_acc = carried
        key_part, value_part, key_rows = key_slices(offset)
        allowed = key_rows[None, None, None, :] <= own_rows[None, None, :, None]
        scores = (
            jnp.einsum("bqhd,bkhd->bhqk", query_rot, key_part, preferred_element_type=jnp.float32)
            * score_scale
        )
        scores = jnp.where(allowed, scores, MASKED)
        new_max = jnp.maximum(running_max, jnp.max(scores, axis=-1))
        weights = jnp.where(allowed, jnp.exp(scores - new_max[..., None]), 0.0)
        factor = jnp.exp(running_max - new_max)
        running_sum = running_sum * factor + jnp.sum(weights, axis=-1)
        running_acc = running_acc * factor[..., None] + jnp.einsum(
            "bhqk,bkhd->bhqd",
            weights.astype(jnp.bfloat16),
            value_part,
            preferred_element_type=jnp.float32,
        )
        return ((new_max, running_sum, running_acc), None)

    start_state = (
        jnp.full((seq_count, local_heads, quarter_rows), MASKED, jnp.float32),
        jnp.zeros((seq_count, local_heads, quarter_rows), jnp.float32),
        jnp.zeros((seq_count, local_heads, quarter_rows, HEAD_DIM), jnp.float32),
    )
    (final_max, final_sum, final_acc), _ = lax.scan(forward_block, start_state, offsets)
    attended_heads = (final_acc / final_sum[..., None]).astype(jnp.bfloat16)
    log_total = final_max + jnp.log(final_sum)
    attended_view = jnp.transpose(attended_heads, (0, 2, 1, 3))
    attended_flat = attended_view.reshape(seq_count, quarter_rows, flat_width)
    attended_tokens = to_tokens(attended_flat[None])[0]
    middle = residual + jnp.dot(attended_tokens, output_full, preferred_element_type=jnp.float32)
    mixed_in = norm_apply(middle, gain_two).astype(jnp.bfloat16)
    token_rows = mixed_in.reshape(token_count, model_width)
    logits = jnp.dot(token_rows, router_full, preferred_element_type=jnp.float32)
    choices = expert_ids.reshape(token_count, TOPK)
    expert_onehot = choices[:, :, None] == jnp.arange(EXPERTS, dtype=jnp.int32)[None, None, :]
    onehot_float = expert_onehot.astype(jnp.float32)

    def gate_values(raw_logits):
        shifted = jnp.exp(raw_logits - jnp.max(raw_logits, axis=-1, keepdims=True))
        router_probs = shifted / jnp.sum(shifted, axis=-1, keepdims=True)
        picked = jnp.sum(router_probs[:, None, :] * onehot_float, axis=2)
        return picked / jnp.sum(picked, axis=1, keepdims=True)

    gate_weights, gate_pull = jax.vjp(gate_values, logits)
    shared_gate_val = jnp.dot(mixed_in, shared_gate_full, preferred_element_type=jnp.float32)
    shared_up_val = jnp.dot(mixed_in, shared_up_full, preferred_element_type=jnp.float32)
    shared_hidden_full, shared_pull = jax.vjp(glu_product, shared_gate_val, shared_up_val)
    shared_hidden = shared_hidden_full.astype(jnp.bfloat16)
    shared_out = jnp.dot(shared_hidden, shared_down_full, preferred_element_type=jnp.float32)
    onehot_int = expert_onehot.astype(jnp.int32)
    per_token = jnp.sum(onehot_int, axis=1)
    fill_rank = fill_order.reshape(token_count)
    earlier = (fill_rank[None, :] < fill_rank[:, None]).astype(jnp.int32)
    counts = jnp.dot(earlier, per_token, preferred_element_type=jnp.int32)
    slot_ranks = jnp.sum(counts[:, None, :] * onehot_int, axis=2)
    slot_total = CAP * EXPERTS
    slots = jnp.where(slot_ranks < CAP, slot_ranks * EXPERTS + choices, slot_total).reshape(-1)
    outgoing = (
        jnp.zeros((slot_total, model_width), jnp.bfloat16)
        .at[slots]
        .set(jnp.repeat(token_rows, TOPK, axis=0), mode="drop")
    )
    incoming = to_experts(outgoing.reshape(CAP, EXPERTS, model_width))
    expert_gate_val = jnp.einsum(
        "red,edf->ref", incoming, expert_gate_full, preferred_element_type=jnp.float32
    )
    expert_up_val = jnp.einsum(
        "red,edf->ref", incoming, expert_up_full, preferred_element_type=jnp.float32
    )
    expert_hidden_full, expert_pull = jax.vjp(glu_product, expert_gate_val, expert_up_val)
    expert_hidden = expert_hidden_full.astype(jnp.bfloat16)
    expert_out = jnp.einsum(
        "ref,edf->red", expert_hidden, expert_down_full, preferred_element_type=jnp.float32
    ).astype(jnp.bfloat16)
    returned = from_experts(expert_out).reshape(slot_total, model_width)
    padded = jnp.concatenate([returned, jnp.zeros((1, model_width), jnp.bfloat16)], axis=0)
    picked_rows = padded[slots].reshape(token_count, TOPK, model_width).astype(jnp.float32)
    combined = jnp.sum(gate_weights[:, :, None] * picked_rows, axis=1)
    result = (
        middle.reshape(token_count, model_width)
        + shared_out.reshape(token_count, model_width)
        + combined
    )
    output = result.astype(jnp.bfloat16).reshape(seq_count, seg_rows, model_width)
    grad_result = cotangent.astype(jnp.float32).reshape(token_count, model_width)
    grad_gates = jnp.sum(grad_result[:, None, :] * picked_rows, axis=2)
    grad_slots = (
        (gate_weights[:, :, None] * grad_result[:, None, :])
        .astype(jnp.bfloat16)
        .reshape(token_count * TOPK, model_width)
    )
    grad_outgoing = (
        jnp.zeros((slot_total, model_width), jnp.bfloat16).at[slots].set(grad_slots, mode="drop")
    )
    grad_incoming = to_experts(grad_outgoing.reshape(CAP, EXPERTS, model_width))
    grad_expert_down = jnp.einsum(
        "red,ref->edf", grad_incoming, expert_hidden, preferred_element_type=jnp.float32
    )
    grad_expert_hidden = jnp.einsum(
        "red,edf->ref", grad_incoming, expert_down_full, preferred_element_type=jnp.float32
    )
    grad_gate_part, grad_up_part = expert_pull(grad_expert_hidden)
    grad_gate_part = grad_gate_part.astype(jnp.bfloat16)
    grad_up_part = grad_up_part.astype(jnp.bfloat16)
    grad_expert_gate = jnp.einsum(
        "red,ref->edf", incoming, grad_gate_part, preferred_element_type=jnp.float32
    )
    grad_expert_up = jnp.einsum(
        "red,ref->edf", incoming, grad_up_part, preferred_element_type=jnp.float32
    )
    grad_pair_rows = (
        jnp.einsum(
            "ref,edf->red", grad_gate_part, expert_gate_full, preferred_element_type=jnp.float32
        )
        + jnp.einsum(
            "ref,edf->red", grad_up_part, expert_up_full, preferred_element_type=jnp.float32
        )
    ).astype(jnp.bfloat16)
    grad_returned = from_experts(grad_pair_rows).reshape(slot_total, model_width)
    grad_padded = jnp.concatenate(
        [grad_returned, jnp.zeros((1, model_width), jnp.bfloat16)], axis=0
    )
    grad_mixed = jnp.sum(
        grad_padded[slots].reshape(token_count, TOPK, model_width).astype(jnp.float32), axis=1
    )
    (grad_logits,) = gate_pull(grad_gates)
    grad_logits = grad_logits.astype(jnp.bfloat16)
    grad_router = jnp.einsum(
        "td,te->de", token_rows, grad_logits, preferred_element_type=jnp.float32
    )
    grad_mixed = grad_mixed + jnp.einsum(
        "te,de->td", grad_logits, router_full, preferred_element_type=jnp.float32
    )
    grad_shared_out = grad_result.astype(jnp.bfloat16).reshape(seq_count, seg_rows, model_width)
    grad_shared_down = jnp.einsum(
        "blf,bld->fd", shared_hidden, grad_shared_out, preferred_element_type=jnp.float32
    )
    grad_shared_hidden = jnp.einsum(
        "bld,fd->blf", grad_shared_out, shared_down_full, preferred_element_type=jnp.float32
    )
    grad_shared_gate_part, grad_shared_up_part = shared_pull(grad_shared_hidden)
    grad_shared_gate_part = grad_shared_gate_part.astype(jnp.bfloat16)
    grad_shared_up_part = grad_shared_up_part.astype(jnp.bfloat16)
    grad_shared_gate = jnp.einsum(
        "bld,blf->df", mixed_in, grad_shared_gate_part, preferred_element_type=jnp.float32
    )
    grad_shared_up = jnp.einsum(
        "bld,blf->df", mixed_in, grad_shared_up_part, preferred_element_type=jnp.float32
    )
    grad_mixed = (
        grad_mixed.reshape(seq_count, seg_rows, model_width)
        + jnp.einsum(
            "blf,df->bld",
            grad_shared_gate_part,
            shared_gate_full,
            preferred_element_type=jnp.float32,
        )
        + jnp.einsum(
            "blf,df->bld", grad_shared_up_part, shared_up_full, preferred_element_type=jnp.float32
        )
    )
    _, norm_two_pull = jax.vjp(norm_apply, middle, gain_two)
    grad_middle_part, grad_gain_two = norm_two_pull(grad_mixed)
    grad_middle = grad_result.reshape(seq_count, seg_rows, model_width) + grad_middle_part
    grad_proj = grad_middle.astype(jnp.bfloat16)
    grad_output_matrix = jnp.einsum(
        "bld,ble->de", attended_tokens, grad_proj, preferred_element_type=jnp.float32
    )
    grad_attended = jnp.einsum(
        "ble,de->bld", grad_proj, output_full, preferred_element_type=jnp.float32
    ).astype(jnp.bfloat16)
    grad_attended_heads = to_heads(grad_attended[None])[0].reshape(head_shape)
    delta_rows = jnp.einsum(
        "bqhd,bqhd->bhq",
        grad_attended_heads,
        attended_flat.reshape(head_shape),
        preferred_element_type=jnp.float32,
    )

    def key_step(grad_query, offset):
        key_part, value_part, key_rows = key_slices(offset)
        part_query, part_key, part_value = score_grads(
            query_rot,
            own_rows,
            key_part,
            value_part,
            key_rows,
            grad_attended_heads,
            log_total,
            delta_rows,
            score_scale,
        )
        flat_shape = (seq_count, block_rows, flat_width)
        return (
            grad_query + part_query,
            (part_key.reshape(flat_shape), part_value.reshape(flat_shape)),
        )

    grad_query_rot, (key_terms, value_terms) = lax.scan(
        key_step, jnp.zeros(head_shape, jnp.float32), offsets
    )
    own_keys, own_values = (
        lax.psum_scatter(
            key_terms.astype(jnp.bfloat16), "fs", scatter_dimension=0, tiled=True
        ).astype(jnp.float32),
        lax.psum_scatter(
            value_terms.astype(jnp.bfloat16), "fs", scatter_dimension=0, tiled=True
        ).astype(jnp.float32),
    )
    grad_key_rot = jnp.moveaxis(own_keys, 0, 1).reshape(head_shape)
    grad_value = jnp.moveaxis(own_values, 0, 1).reshape(head_shape)
    _, rope_pull = jax.vjp(rotate_own, jnp.zeros(head_shape, jnp.float32))
    (grad_query_raw,) = rope_pull(grad_query_rot)
    (grad_key_raw,) = rope_pull(grad_key_rot)
    stacked_grads = (
        jnp.stack([grad_query_raw, grad_key_raw, grad_value])
        .astype(jnp.bfloat16)
        .reshape(3, seq_count, quarter_rows, flat_width)
    )
    token_grads = to_tokens(stacked_grads)
    grad_query_matrix = jnp.einsum(
        "bld,ble->de", normed, token_grads[0], preferred_element_type=jnp.float32
    )
    grad_key_matrix = jnp.einsum(
        "bld,ble->de", normed, token_grads[1], preferred_element_type=jnp.float32
    )
    grad_value_matrix = jnp.einsum(
        "bld,ble->de", normed, token_grads[2], preferred_element_type=jnp.float32
    )
    grad_normed = (
        jnp.einsum("ble,de->bld", token_grads[0], query_full, preferred_element_type=jnp.float32)
        + jnp.einsum("ble,de->bld", token_grads[1], key_full, preferred_element_type=jnp.float32)
        + jnp.einsum("ble,de->bld", token_grads[2], value_full, preferred_element_type=jnp.float32)
    )
    _, norm_one_pull = jax.vjp(norm_apply, residual, gain_one)
    grad_residual_part, grad_gain_one = norm_one_pull(grad_normed)
    grad_tokens = grad_middle + grad_residual_part
    (
        part_gain_one,
        part_query,
        part_key,
        part_value,
        part_output,
        part_gain_two,
        part_router,
        part_shared_gate,
        part_shared_up,
        part_shared_down,
    ) = (
        lax.psum_scatter(
            grad_gain_one.astype(jnp.bfloat16), ("sp", "fs"), scatter_dimension=0, tiled=True
        ).astype(jnp.float32),
        lax.psum_scatter(
            grad_query_matrix.astype(jnp.bfloat16), ("sp", "fs"), scatter_dimension=0, tiled=True
        ).astype(jnp.float32),
        lax.psum_scatter(
            grad_key_matrix.astype(jnp.bfloat16), ("sp", "fs"), scatter_dimension=0, tiled=True
        ).astype(jnp.float32),
        lax.psum_scatter(
            grad_value_matrix.astype(jnp.bfloat16), ("sp", "fs"), scatter_dimension=0, tiled=True
        ).astype(jnp.float32),
        lax.psum_scatter(
            grad_output_matrix.astype(jnp.bfloat16), ("sp", "fs"), scatter_dimension=0, tiled=True
        ).astype(jnp.float32),
        lax.psum_scatter(
            grad_gain_two.astype(jnp.bfloat16), ("sp", "fs"), scatter_dimension=0, tiled=True
        ).astype(jnp.float32),
        lax.psum_scatter(
            grad_router.astype(jnp.bfloat16), ("sp", "fs"), scatter_dimension=0, tiled=True
        ).astype(jnp.float32),
        lax.psum_scatter(
            grad_shared_gate.astype(jnp.bfloat16), ("sp", "fs"), scatter_dimension=0, tiled=True
        ).astype(jnp.float32),
        lax.psum_scatter(
            grad_shared_up.astype(jnp.bfloat16), ("sp", "fs"), scatter_dimension=0, tiled=True
        ).astype(jnp.float32),
        lax.psum_scatter(
            grad_shared_down.astype(jnp.bfloat16), ("sp", "fs"), scatter_dimension=0, tiled=True
        ).astype(jnp.float32),
    )
    own_gate, own_up, own_down = (
        lax.psum_scatter(
            grad_expert_gate.astype(jnp.bfloat16), "sp", scatter_dimension=1, tiled=True
        ).astype(jnp.float32),
        lax.psum_scatter(
            grad_expert_up.astype(jnp.bfloat16), "sp", scatter_dimension=1, tiled=True
        ).astype(jnp.float32),
        lax.psum_scatter(
            grad_expert_down.astype(jnp.bfloat16), "sp", scatter_dimension=1, tiled=True
        ).astype(jnp.float32),
    )
    (
        sum_gain_one,
        sum_query,
        sum_key,
        sum_value,
        sum_output,
        sum_gain_two,
        sum_router,
        sum_shared_gate,
        sum_shared_up,
        sum_shared_down,
        sum_gate,
        sum_up,
        sum_down,
    ) = (
        lax.psum(part_gain_one.astype(jnp.bfloat16), "dp").astype(jnp.float32),
        lax.psum(part_query.astype(jnp.bfloat16), "dp").astype(jnp.float32),
        lax.psum(part_key.astype(jnp.bfloat16), "dp").astype(jnp.float32),
        lax.psum(part_value.astype(jnp.bfloat16), "dp").astype(jnp.float32),
        lax.psum(part_output.astype(jnp.bfloat16), "dp").astype(jnp.float32),
        lax.psum(part_gain_two.astype(jnp.bfloat16), "dp").astype(jnp.float32),
        lax.psum(part_router.astype(jnp.bfloat16), "dp").astype(jnp.float32),
        lax.psum(part_shared_gate.astype(jnp.bfloat16), "dp").astype(jnp.float32),
        lax.psum(part_shared_up.astype(jnp.bfloat16), "dp").astype(jnp.float32),
        lax.psum(part_shared_down.astype(jnp.bfloat16), "dp").astype(jnp.float32),
        lax.psum(own_gate.astype(jnp.bfloat16), "dp").astype(jnp.float32),
        lax.psum(own_up.astype(jnp.bfloat16), "dp").astype(jnp.float32),
        lax.psum(own_down.astype(jnp.bfloat16), "dp").astype(jnp.float32),
    )
    return (
        output,
        grad_tokens,
        sum_gain_one,
        sum_query,
        sum_key,
        sum_value,
        sum_output,
        sum_gain_two,
        sum_router,
        sum_shared_gate,
        sum_shared_up,
        sum_shared_down,
        sum_gate,
        sum_up,
        sum_down,
    )


BF16 = jnp.bfloat16
F32 = jnp.float32
LANES = 128
NOTE_ROWS = 8
VMEM_WHOLE = pl.BlockSpec(memory_space=pltpu.VMEM)
IN_PLACE = pl.BlockSpec(memory_space=pl.ANY)
ROOM = 60 * 1024 * 1024


def dot32(left, right):
    return jnp.dot(left, right, preferred_element_type=F32)


def dot_nt(left, right):
    return lax.dot_general(left, right, (((1,), (1,)), ((), ())), preferred_element_type=F32)


def turn(values, cosine, sine):
    half = values.shape[0] // 2
    front, back = values[:half], values[half:]
    return jnp.concatenate([front * cosine - back * sine, back * cosine + front * sine], axis=0)


def turn_back(values, cosine, sine):
    half = values.shape[0] // 2
    front, back = values[:half], values[half:]
    return jnp.concatenate([front * cosine + back * sine, back * cosine - front * sine], axis=0)


def causal(block):
    keys = lax.broadcasted_iota(jnp.int32, (block, block), 0)
    queries = lax.broadcasted_iota(jnp.int32, (block, block), 1)
    return keys <= queries


def remote_params(number):
    return pltpu.CompilerParams(
        collective_id=number, has_side_effects=True, vmem_limit_bytes=ROOM
    )


def places():
    sp_count, fs_count = lax.axis_size("sp"), lax.axis_size("fs")
    own = lax.axis_index("sp") * fs_count + lax.axis_index("fs")
    return sp_count * fs_count, own


def at_place(place):
    fs_count = lax.axis_size("fs")
    return {"sp": place // fs_count, "fs": lax.rem(place, fs_count)}


def greet_places():
    total, own = places()
    barrier = pltpu.get_barrier_semaphore()

    def greet(step, _):
        pl.semaphore_signal(
            barrier,
            inc=1,
            device_id=at_place(lax.rem(own + step, total)),
            device_id_type=pl.DeviceIdType.MESH,
        )
        return 0

    lax.fori_loop(1, total, greet, 0)


def await_places(others=0):
    pl.semaphore_wait(pltpu.get_barrier_semaphore(), places()[0] - 1 + others)


def columns(index, size):
    return pl.ds(pl.multiple_of(index * size, size), size)


class Swap:
    def __init__(self, source, target, send, recv, local):
        self.source, self.target = source, target
        self.send, self.recv, self.local = send, recv, local

    def remote(self, place, landing, mark):
        return pltpu.make_async_remote_copy(
            src_ref=self.source(place),
            dst_ref=self.target(landing),
            send_sem=self.send.at[place],
            recv_sem=self.recv.at[mark],
            device_id=at_place(place),
            device_id_type=pl.DeviceIdType.MESH,
        )

    def own(self):
        own = places()[1]
        return pltpu.make_async_copy(self.source(own), self.target(own), self.local)

    def start(self, place):
        own = places()[1]

        @pl.when(place != own)
        def _():
            self.remote(place, own, own).start()

        @pl.when(place == own)
        def _():
            self.own().start()

    def start_all(self):
        total, own = places()

        def begin(step, _):
            self.remote(lax.rem(own + step, total), own, own).start()
            return 0

        lax.fori_loop(1, total, begin, 0)
        self.own().start()

    def finish(self):
        total, own = places()

        def end(step, _):
            place = lax.rem(own + step, total)
            copy = self.remote(place, place, place)
            copy.wait_send()
            copy.wait_recv()
            return 0

        lax.fori_loop(1, total, end, 0)
        self.own().wait()


def swap_semaphores(total):
    return [
        pltpu.SemaphoreType.DMA((total,)),
        pltpu.SemaphoreType.DMA((total,)),
        pltpu.SemaphoreType.DMA,
    ]


class Spread:
    def __init__(self, shard, full, stage, near, far_send, far_recv, dp_send, dp_recv, local):
        self.shard, self.full, self.stage = shard, full, stage
        self.near, self.far_send, self.far_recv = near, far_send, far_recv
        self.dp_send, self.dp_recv, self.local = dp_send, dp_recv, local
        self.sp, self.dp = lax.axis_index("sp"), lax.axis_index("dp")
        self.core = self.sp + 1 - 2 * lax.rem(self.sp, 2)
        self.other = 2 - 2 * (self.sp // 2)
        self.half = shard.shape[1] // 2
        self.rows = pl.ds(pl.multiple_of(self.dp * self.half, self.half), self.half)
        self.dp_rows = pl.ds(pl.multiple_of((1 - self.dp) * self.half, self.half), self.half)

    def to_core(self):
        return pltpu.make_async_remote_copy(
            src_ref=self.shard.at[self.core],
            dst_ref=self.full.at[self.sp],
            send_sem=self.near.at[0],
            recv_sem=self.near.at[1],
            device_id={"sp": self.core},
            device_id_type=pl.DeviceIdType.MESH,
        )

    def to_far(self, turn):
        return pltpu.make_async_remote_copy(
            src_ref=self.shard.at[self.other + turn, self.rows],
            dst_ref=self.full.at[self.sp, self.rows],
            send_sem=self.far_send.at[turn],
            recv_sem=self.far_recv.at[lax.rem(self.sp, 2)],
            device_id={"sp": self.other + turn},
            device_id_type=pl.DeviceIdType.MESH,
        )

    def from_far(self, turn):
        return pltpu.make_async_remote_copy(
            src_ref=self.shard.at[self.other + turn, self.rows],
            dst_ref=self.full.at[self.other + turn, self.rows],
            send_sem=self.far_send.at[turn],
            recv_sem=self.far_recv.at[turn],
            device_id={"sp": self.other + turn},
            device_id_type=pl.DeviceIdType.MESH,
        )

    def to_dp(self, turn):
        block = self.full.at[self.other + turn, self.rows]
        return pltpu.make_async_remote_copy(
            src_ref=block,
            dst_ref=block,
            send_sem=self.dp_send.at[turn],
            recv_sem=self.dp_recv.at[turn],
            device_id={"dp": 1 - self.dp},
            device_id_type=pl.DeviceIdType.MESH,
        )

    def from_dp(self, turn):
        block = self.full.at[self.other + turn, self.dp_rows]
        return pltpu.make_async_remote_copy(
            src_ref=block,
            dst_ref=block,
            send_sem=self.dp_send.at[turn],
            recv_sem=self.dp_recv.at[turn],
            device_id={"dp": 1 - self.dp},
            device_id_type=pl.DeviceIdType.MESH,
        )

    def own_in(self):
        return pltpu.make_async_copy(self.shard.at[self.sp], self.stage, self.local.at[0])

    def own_out(self):
        return pltpu.make_async_copy(self.stage, self.full.at[self.sp], self.local.at[1])

    def start_cross(self):
        self.own_in().start()
        self.to_far(0).start()
        self.to_far(1).start()
        self.to_core().start()

    def finish_cross(self):
        self.own_in().wait()
        self.own_out().start()
        for turn in range(2):
            self.from_far(turn).wait_recv()
            self.to_far(turn).wait_send()
        self.to_core().wait_send()
        self.to_core().wait_recv()
        self.own_out().wait()

    def start_share(self):
        self.to_dp(0).start()
        self.to_dp(1).start()

    def finish_share(self):
        for turn in range(2):
            self.from_dp(turn).wait_recv()
            self.to_dp(turn).wait_send()


def pair_semaphores():
    return pltpu.SemaphoreType.DMA((2,))


def cross_scratch(shard):
    return [pltpu.VMEM(shard.shape[1:], shard.dtype)] + [pair_semaphores()] * 4


def share_scratch():
    return [pair_semaphores()] * 2


def crossing(shard, full, stage, near, far_send, far_recv, local):
    return Spread(shard, full, stage, near, far_send, far_recv, None, None, local)


def sharing(full, dp_send, dp_recv):
    return Spread(full, full, None, None, None, None, dp_send, dp_recv, None)


def greet_dp():
    pl.semaphore_signal(
        pltpu.get_barrier_semaphore(),
        inc=1,
        device_id={"dp": 1 - lax.axis_index("dp")},
        device_id_type=pl.DeviceIdType.MESH,
    )


def route(ids_ref, fill_ref, slots_ref, taking_ref):
    count = fill_ref.shape[1]
    group = EXPERTS // lax.axis_size("fs")
    fill_row = fill_ref[...].astype(F32)
    fill_column = jnp.broadcast_to(fill_row, (8, count)).T[:, 0:1]
    earlier = (fill_column < fill_row).astype(BF16)
    experts = lax.broadcasted_iota(jnp.int32, (EXPERTS, count), 0)
    named = [(experts == ids_ref[j : j + 1, :]).astype(F32) for j in range(TOPK)]
    counts = dot32((named[0] + named[1]).astype(BF16), earlier)
    slots = []
    for j in range(TOPK):
        rank = jnp.sum(counts * named[j], axis=0, keepdims=True).astype(jnp.int32)
        choice = ids_ref[j : j + 1, :]
        holder = lax.rem(choice, group) * lax.axis_size("fs") + choice // group
        slots.append(jnp.where(rank < CAP, holder * CAP + rank, -1))
        slots_ref[j : j + 1, :] = slots[j]
    total = taking_ref.shape[0]
    half = total // 2
    for start in (0, half):
        slot_ids = start + lax.broadcasted_iota(jnp.int32, (half, count), 0)
        taken = (slot_ids == slots[0]) | (slot_ids == slots[1])
        taking_ref[start : start + half, :] = taken.astype(F32).astype(BF16)


def spread_rows(taking_ref, rows_ref, out_ref):
    total, cap, _ = out_ref.shape
    half = total // 2
    for first in (0, half):
        rows = dot32(taking_ref[first * cap : (first + half) * cap, :], rows_ref[...])
        for place in range(half):
            out_ref[first + place] = rows[place * cap : (place + 1) * cap].astype(BF16)


def front_kernel(
    scale,
    tokens_ref,
    query_ref,
    key_ref,
    value_ref,
    small_ref,
    ids_ref,
    fill_ref,
    cot_ref,
    cos_ref,
    sin_ref,
    gate_shard,
    up_shard,
    down_shard,
    slots_ref,
    taking_ref,
    normed_ref,
    weight_ref,
    qkv_ref,
    o_ref,
    lse_ref,
    got_ref,
    cots_ref,
    gate_full,
    up_full,
    down_full,
    seq,
    pack,
    pack_got,
    weight_feat,
    cot_out,
    k_rot,
    z_send,
    z_recv,
    core_send,
    core_recv,
    y_send,
    y_recv,
    late_send,
    late_recv,
    up_send,
    up_recv,
    down_send,
    down_recv,
    pack_send,
    pack_recv,
    local,
    cot_send,
    cot_recv,
    cot_local,
    send,
    recv,
    out_local,
    gate_dp_send,
    gate_dp_recv,
    up_dp_send,
    up_dp_recv,
    *cross,
):
    fs_count, sp_count = lax.axis_size("fs"), lax.axis_size("sp")
    fs_place, sp_place = lax.axis_index("fs"), lax.axis_index("sp")
    heads, length, _ = k_rot.shape
    wide = heads * HEAD_DIM
    seg = tokens_ref.shape[1]
    block = fs_count * seg
    core = sp_place + 1 - 2 * lax.rem(sp_place, 2)
    across = lax.rem(sp_place + 2, sp_count)
    beyond = lax.rem(core + 2, sp_count)

    def fs_peer(step):
        return lax.rem(fs_place + step, fs_count)

    def sp_peer(step):
        return lax.rem(sp_place + step, sp_count)

    def move(source, target, send_sem, recv_sem, where):
        return pltpu.make_async_remote_copy(
            src_ref=source,
            dst_ref=target,
            send_sem=send_sem,
            recv_sem=recv_sem,
            device_id=where,
            device_id_type=pl.DeviceIdType.MESH,
        )

    def each(count, body):
        def run(index, _):
            body(index)
            return 0

        lax.fori_loop(1, count, run, 0)

    greet_places()
    greet_dp()
    part = query_ref.shape[1] // sp_count
    for place in range(sp_count):
        for kind, source in enumerate((query_ref, key_ref, value_ref)):
            pack[place, :, kind * part : (kind + 1) * part] = source[
                :, place * part : (place + 1) * part
            ]
        pack[place, :, 3 * part :] = small_ref[:, : pack.shape[2] - 3 * part]
    await_places(1)

    def pack_move(place, owner, mark):
        return move(
            pack.at[place],
            pack_got.at[owner, fs_place],
            pack_send.at[place],
            pack_recv.at[mark],
            {"sp": place},
        )

    def z_move(place, owner):
        return move(
            tokens_ref.at[place],
            seq.at[sp_place, owner],
            z_send.at[place],
            z_recv.at[owner],
            {"fs": place},
        )

    def to_core(source, mark):
        return move(
            source, seq.at[sp_place, mark], core_send.at[mark], core_recv.at[mark], {"sp": core}
        )

    def to_across(source, mark):
        return move(
            source, seq.at[sp_place, mark], y_send.at[mark], y_recv.at[mark], {"sp": across}
        )

    def late(mark):
        rows = seq.at[across, mark]
        return move(rows, rows, late_send.at[mark], late_recv.at[mark], {"sp": core})

    def upward(mark):
        rows = pack_got.at[:, mark]
        return move(rows, rows, up_send.at[mark], up_recv.at[mark], {"fs": fs_peer(1)})

    def downward(mark):
        rows = pack_got.at[:, mark]
        return move(
            rows, rows, down_send.at[mark], down_recv.at[mark], {"fs": fs_peer(fs_count - 1)}
        )

    each(sp_count, lambda step: pack_move(sp_peer(step), sp_place, sp_place).start())
    each(fs_count, lambda step: z_move(fs_peer(step), fs_place).start())
    own_tokens = tokens_ref.at[fs_place]
    to_across(own_tokens, fs_place).start()
    to_core(own_tokens, fs_place).start()
    own_seq = pltpu.make_async_copy(own_tokens, seq.at[sp_place, fs_place], local.at[0])
    own_pack = pltpu.make_async_copy(
        pack.at[sp_place], pack_got.at[sp_place, fs_place], local.at[1]
    )
    own_seq.start()
    own_pack.start()
    own_pack.wait()

    def pack_here(step):
        mark = sp_peer(step)
        pack_move(mark, mark, mark).wait_recv()

    each(sp_count, pack_here)
    has_up = fs_place < fs_count - 1
    has_down = fs_place > 0

    @pl.when(has_up)
    def _():
        upward(fs_place).start()

    @pl.when(has_down)
    def _():
        downward(fs_place).start()

    route(ids_ref, fill_ref, slots_ref, taking_ref)
    spread_rows(taking_ref, cot_ref, cot_out)

    def relay(step):
        below, above = fs_place - step, fs_place + step

        @pl.when(below >= 0)
        def _():
            upward(below).wait_recv()

        @pl.when((below >= 0) & has_up)
        def _():
            upward(below).start()

        @pl.when(above < fs_count)
        def _():
            downward(above).wait_recv()

        @pl.when((above < fs_count) & has_down)
        def _():
            downward(above).start()

        mark = fs_peer(step)
        z_move(mark, mark).wait_recv()
        rows = seq.at[sp_place, mark]
        to_across(rows, mark).start()
        to_core(rows, mark).start()

    each(fs_count, relay)
    cots = Swap(
        lambda place: cot_out.at[place],
        lambda place: cots_ref.at[place],
        cot_send,
        cot_recv,
        cot_local,
    )
    cots.start_all()
    size = len(cross) // 3
    gate = crossing(gate_shard, gate_full, *cross[:size])
    up = crossing(up_shard, up_full, *cross[size : 2 * size])
    down = crossing(down_shard, down_full, *cross[2 * size :])
    gate.start_cross()
    up.start_cross()
    down.start_cross()

    def pass_on(mark, _):
        to_across(own_tokens, mark).wait_recv()
        late(mark).start()
        return 0

    lax.fori_loop(0, fs_count, pass_on, 0)
    own_seq.wait()
    packed = pack_got[...].reshape(weight_ref.shape)
    weight_ref[...] = packed
    weight_feat[...] = packed.T
    gain_row = weight_feat[3 * wide : 3 * wide + 1, :].astype(F32)

    def head_rows(kind, head):
        return columns(kind * heads + head, HEAD_DIM)

    def project(place):
        own_columns = columns(place, block)
        rows = seq[place].reshape(block, seq.shape[3]).astype(F32)
        scaled = lax.rsqrt(jnp.mean(rows * rows, axis=-1, keepdims=True) + EPSILON)
        normed = (rows * scaled * gain_row).astype(BF16)
        normed_ref[own_columns, :] = normed
        qkv_ref[:, own_columns] = dot_nt(weight_feat[: 3 * wide, :], normed).astype(BF16)

        def turn_keys(head, _):
            rotated = turn(
                qkv_ref[head_rows(1, head), own_columns].astype(F32),
                cos_ref[:, own_columns],
                sin_ref[:, own_columns],
            )
            k_rot[head, own_columns, :] = rotated.T.astype(BF16)
            return 0

        lax.fori_loop(0, heads, turn_keys, 0)

    def from_core(mark, _):
        to_core(own_tokens, mark).wait_recv()
        return 0

    def from_late(mark, _):
        late(mark).wait_recv()
        return 0

    lax.fori_loop(0, fs_count, from_core, 0)
    lax.fori_loop(0, fs_count, from_late, 0)

    def project_step(step, _):
        project(sp_peer(step))
        return 0

    lax.fori_loop(0, sp_count, project_step, 0)

    exchange = Swap(
        lambda place: o_ref.at[:, columns(place, seg)],
        lambda place: got_ref.at[
            columns(place // fs_count, wide), columns(lax.rem(place, fs_count), seg)
        ],
        send,
        recv,
        out_local,
    )

    def attend_block(place):
        own_columns = columns(place, block)

        def attend_head(head, _):
            query = turn(
                qkv_ref[head_rows(0, head), own_columns].astype(F32),
                cos_ref[:, own_columns],
                sin_ref[:, own_columns],
            ).astype(BF16)

            def scores_at(index):
                return dot32(k_rot[head, columns(index, block), :], query) * scale

            def weighted(index, weights):
                values = qkv_ref[head_rows(2, head), columns(index, block)]
                return dot32(values, weights.astype(BF16))

            scores = jnp.where(causal(block), scores_at(place), MASKED)
            first_max = jnp.max(scores, axis=0, keepdims=True)
            weights = jnp.exp(scores - first_max)
            first_sum = jnp.sum(weights, axis=0, keepdims=True)

            def step(index, carried):
                running_max, running_sum, running_acc = carried
                part = scores_at(index)
                new_max = jnp.maximum(running_max, jnp.max(part, axis=0, keepdims=True))
                part = jnp.exp(part - new_max)
                factor = jnp.exp(running_max - new_max)
                return (
                    new_max,
                    running_sum * factor + jnp.sum(part, axis=0, keepdims=True),
                    running_acc * factor + weighted(index, part),
                )

            final_max, final_sum, final_acc = lax.fori_loop(
                0, place, step, (first_max, first_sum, weighted(place, weights))
            )
            o_ref[columns(head, HEAD_DIM), own_columns] = (final_acc / final_sum).astype(BF16)
            lse_ref[head, :, own_columns] = final_max + jnp.log(final_sum)
            return 0

        lax.fori_loop(0, heads, attend_head, 0)

    gate_share = sharing(gate_full, gate_dp_send, gate_dp_recv)
    up_share = sharing(up_full, up_dp_send, up_dp_recv)

    def step(index, _):
        place = length // block - 1 - index
        attend_block(place)

        def begin(part, _):
            exchange.start(place * fs_count + part)
            return 0

        lax.fori_loop(0, fs_count, begin, 0)

        @pl.when(index == 0)
        def _():
            gate.finish_cross()
            gate_share.start_share()

        @pl.when(index == 1)
        def _():
            up.finish_cross()
            up_share.start_share()

        return 0

    lax.fori_loop(0, length // block, step, 0)
    exchange.finish()
    cots.finish()
    down.finish_cross()
    gate_share.finish_share()
    up_share.finish_share()

    def end(mark, _):
        to_core(own_tokens, mark).wait_send()
        to_across(own_tokens, mark).wait_send()
        late(mark).wait_send()

        @pl.when(has_up & (mark <= fs_place))
        def _():
            upward(mark).wait_send()

        @pl.when(has_down & (mark >= fs_place))
        def _():
            downward(mark).wait_send()

        return 0

    lax.fori_loop(0, fs_count, end, 0)
    each(sp_count, lambda step: pack_move(sp_peer(step), sp_place, sp_place).wait_send())
    each(fs_count, lambda step: z_move(fs_peer(step), fs_place).wait_send())


def front(
    tokens, query, key, value, small, ids, fill, cots, cosine, sine, gate, up, down, score_scale
):
    sp_count, fs_count = lax.axis_size("sp"), lax.axis_size("fs")
    total = sp_count * fs_count
    fs_sems = pltpu.SemaphoreType.DMA((fs_count,))
    sp_sems = pltpu.SemaphoreType.DMA((sp_count,))
    rows, width = query.shape
    wide = width // sp_count
    heads = wide // HEAD_DIM
    seg = tokens.shape[1]
    length = total * seg
    pack = (rows, -(-(3 * wide + 2 + EXPERTS) // LANES) * LANES)
    count = ids.shape[1]
    slot_rows = (total, CAP, width)
    return pl.pallas_call(
        functools.partial(front_kernel, score_scale),
        in_specs=[IN_PLACE] + [VMEM_WHOLE] * 9 + [IN_PLACE] * 3,
        out_specs=[VMEM_WHOLE] * 7 + [IN_PLACE] * 5,
        out_shape=[
            jax.ShapeDtypeStruct((TOPK, count), jnp.int32),
            jax.ShapeDtypeStruct((total * CAP, count), BF16),
            jax.ShapeDtypeStruct((length, width), BF16),
            jax.ShapeDtypeStruct((width, pack[1]), BF16),
            jax.ShapeDtypeStruct((3 * wide, length), BF16),
            jax.ShapeDtypeStruct((wide, length), BF16),
            jax.ShapeDtypeStruct((heads, 1, length), F32),
            jax.ShapeDtypeStruct((width, fs_count * seg), BF16),
            jax.ShapeDtypeStruct(slot_rows, BF16),
        ]
        + [jax.ShapeDtypeStruct(shard.shape, shard.dtype) for shard in (gate, up, down)],
        scratch_shapes=[
            pltpu.VMEM((sp_count, fs_count) + tokens.shape[1:], BF16),
            pltpu.VMEM((sp_count,) + pack, BF16),
            pltpu.VMEM((sp_count, fs_count) + pack, BF16),
            pltpu.VMEM((pack[1], width), BF16),
            pltpu.VMEM(slot_rows, BF16),
            pltpu.VMEM((heads, length, HEAD_DIM), BF16),
        ]
        + [fs_sems] * 12
        + [sp_sems] * 2
        + [pair_semaphores()]
        + swap_semaphores(total)
        + swap_semaphores(total)
        + share_scratch()
        + share_scratch()
        + cross_scratch(gate)
        + cross_scratch(up)
        + cross_scratch(down),
        compiler_params=remote_params(1),
        cost_estimate=pl.CostEstimate(
            flops=100_000_000_000, bytes_accessed=4_000_000, transcendentals=0
        ),
        name="front",
    )(tokens, query, key, value, small, ids, fill, cots, cosine, sine, gate, up, down)


def attend_grad_kernel(
    block,
    scale,
    qkv_ref,
    cos_ref,
    sin_ref,
    o_ref,
    lse_ref,
    ga_ref,
    normed_ref,
    weight_ref,
    sums_ref,
    back_out_ref,
    got_ref,
    spread_ref,
    back_ref,
    tail_ref,
    grad_ref,
    near_out,
    near_got,
    pair_out,
    pair_got,
    far_out,
    far_got,
    own_part,
    reduced,
    go_feat,
    q_feat,
    q_rows,
    k_feat,
    k_rows,
    v_rows,
    go_rows,
    delta,
    dq_acc,
    dk_acc,
    dv_acc,
    probs,
    weight_acc,
    tail_send,
    stage,
    send_in,
    recv_in,
    local_in,
    part_sems,
    send_z,
    recv_z,
    local_z,
    send_sums,
    recv_sums,
    local_sums,
    send_back,
    recv_back,
    local_back,
    send_tail,
    recv_tail,
    local_tail,
):
    heads, length, _ = q_rows.shape
    wide = heads * HEAD_DIM
    total, own = places()
    seg = length // total
    fs_count, sp_count = lax.axis_size("fs"), lax.axis_size("sp")
    fs_place, sp_place = lax.axis_index("fs"), lax.axis_index("sp")
    greet_places()

    def head_rows(kind, head):
        return columns(kind * heads + head, HEAD_DIM)

    def prepare(head, _):
        rotated = turn(qkv_ref[head_rows(0, head), :].astype(F32), cos_ref[...], sin_ref[...])
        q_feat[columns(head, HEAD_DIM), :] = rotated.astype(BF16)
        q_rows[head] = rotated.T.astype(BF16)
        rotated = turn(qkv_ref[head_rows(1, head), :].astype(F32), cos_ref[...], sin_ref[...])
        k_feat[columns(head, HEAD_DIM), :] = rotated.astype(BF16)
        k_rows[head] = rotated.T.astype(BF16)
        v_rows[head] = qkv_ref[head_rows(2, head), :].astype(F32).T.astype(BF16)
        return 0

    arrival = Swap(
        lambda place: ga_ref.at[
            columns(place // fs_count, wide), columns(lax.rem(place, fs_count), seg)
        ],
        lambda place: go_feat.at[:, columns(place, seg)],
        send_in,
        recv_in,
        local_in,
    )
    await_places()
    arrival.start_all()
    back = Swap(
        lambda place: back_out_ref.at[place],
        lambda place: back_ref.at[place],
        send_back,
        recv_back,
        local_back,
    )
    back.start_all()
    lax.fori_loop(0, heads, prepare, 0)
    dq_acc[...] = jnp.zeros_like(dq_acc)
    weight_acc[...] = jnp.zeros_like(weight_acc)
    dk_acc[...] = jnp.zeros_like(dk_acc)
    dv_acc[...] = jnp.zeros_like(dv_acc)
    count = length // block
    down = 1 - sp_place // (sp_count // 2)

    def pair_columns(turn_index, step):
        place = turn_index + down * (count - 1 - 2 * turn_index)
        other = place + step - 2 * step * down
        queries = columns(other + down * (place - other), block)
        return queries, columns(place + down * (other - place), block)

    def pair_slot(turn_index, step):
        return turn_index * (2 * count - turn_index + 1) // 2 + step

    def form(head, _):
        rows = columns(head, HEAD_DIM)

        def pair(turn_index, step, masked):
            queries, keys = pair_columns(turn_index, step)
            scores = dot32(k_rows[head, keys, :], q_feat[rows, queries]) * scale
            weights = jnp.exp(scores - lse_ref[head, :, queries])
            if masked:
                weights = jnp.where(causal(block), weights, 0.0)
            probs[head, pair_slot(turn_index, step)] = weights.astype(BF16)

        def turns(turn_index, _):
            pair(turn_index, 0, True)

            def steps(step, _):
                pair(turn_index, step, False)
                return 0

            lax.fori_loop(1, count - turn_index, steps, 0)
            return 0

        lax.fori_loop(0, count, turns, 0)
        return 0

    lax.fori_loop(0, heads, form, 0)
    arrival.finish()

    def prepare_grad(head, _):
        grad = go_feat[columns(head, HEAD_DIM), :].astype(F32)
        go_rows[head] = grad.T.astype(BF16)
        delta[head] = jnp.sum(
            grad * o_ref[columns(head, HEAD_DIM), :].astype(F32), axis=0, keepdims=True
        )
        return 0

    lax.fori_loop(0, heads, prepare_grad, 0)

    core = sp_place + 1 - 2 * lax.rem(sp_place, 2)
    across = lax.rem(sp_place + 2, sp_count)

    def part_move(index, source, target, place):
        return pltpu.make_async_remote_copy(
            src_ref=source,
            dst_ref=target,
            send_sem=part_sems.at[0, index],
            recv_sem=part_sems.at[1, index],
            device_id={"sp": place},
            device_id_type=pl.DeviceIdType.MESH,
        )

    to_near = part_move(0, near_out, near_got, core)
    to_pair = part_move(1, pair_out, pair_got, core)
    to_far = part_move(2, far_out, far_got, across)

    def to_fs(place, mark):
        return pltpu.make_async_remote_copy(
            src_ref=reduced.at[columns(place, seg), :],
            dst_ref=got_ref.at[columns(mark, seg), :],
            send_sem=send_z.at[place],
            recv_sem=recv_z.at[mark],
            device_id={"fs": place},
            device_id_type=pl.DeviceIdType.MESH,
        )


    def segment(turn_index, _):
        place = turn_index + down * (count - 1 - 2 * turn_index)
        own_columns = columns(place, block)
        own_cos, own_sin = cos_ref[:, own_columns], sin_ref[:, own_columns]

        def segment_head(head, _):
            rows = columns(head, HEAD_DIM)

            def pair(step):
                queries, keys = pair_columns(turn_index, step)
                low = probs[head, pair_slot(turn_index, step)]
                weights = low.astype(F32)
                reach = dot32(v_rows[head, keys, :], go_feat[rows, queries])
                slopes = (weights * (reach - delta[head, :, queries]) * scale).astype(BF16)
                dq_acc[rows, queries] += dot32(k_feat[rows, keys], slopes)
                dk_acc[head, keys, :] += dot32(slopes, q_rows[head, queries, :])
                dv_acc[head, keys, :] += dot32(low, go_rows[head, queries, :])

            pair(0)

            def step(index, _):
                pair(index)
                return 0

            lax.fori_loop(1, count - turn_index, step, 0)
            grad_ref[head_rows(0, head), own_columns] = turn_back(
                dq_acc[rows, own_columns], own_cos, own_sin
            ).astype(BF16)
            grad_ref[head_rows(1, head), own_columns] = turn_back(
                dk_acc[head, own_columns, :].T, own_cos, own_sin
            ).astype(BF16)
            grad_ref[head_rows(2, head), own_columns] = dv_acc[head, own_columns, :].T.astype(BF16)
            return 0

        lax.fori_loop(0, heads, segment_head, 0)
        part = dot32(weight_ref[...], grad_ref[:, own_columns])

        @pl.when(place == sp_place)
        def _():
            own_part[...] = part

        @pl.when(place == core)
        def _():
            near_out[...] = part.astype(BF16)
            to_near.start()

        @pl.when(place == lax.rem(core + 2, sp_count))
        def _():
            pair_out[...] = part.astype(BF16)
            to_pair.start()

        @pl.when(place == across)
        def _():
            to_pair.wait_recv()
            far_out[...] = (part + pair_got[...].astype(F32)).astype(BF16)
            to_far.start()

        weight_acc[...] += dot32(grad_ref[:, own_columns], normed_ref[own_columns, :])
        return 0

    lax.fori_loop(0, count, segment, 0)

    def to_owner(place, mark):
        return pltpu.make_async_remote_copy(
            src_ref=sums_ref.at[place],
            dst_ref=spread_ref.at[mark],
            send_sem=send_sums.at[place],
            recv_sem=recv_sums.at[mark],
            device_id={"sp": place},
            device_id_type=pl.DeviceIdType.MESH,
        )

    def begin_sums(step, _):
        to_owner(lax.rem(sp_place + step, sp_count), sp_place).start()
        return 0

    lax.fori_loop(1, sp_count, begin_sums, 0)
    own_in = pltpu.make_async_copy(sums_ref.at[sp_place], stage, local_sums.at[0])
    own_out = pltpu.make_async_copy(stage, spread_ref.at[sp_place], local_sums.at[1])
    own_in.start()
    shard, wide_all = tail_send.shape[1], 3 * wide
    flipped = weight_acc[...].T
    for place in range(tail_send.shape[0]):
        tail_send[place, :, :wide_all] = flipped[place * shard : (place + 1) * shard].astype(BF16)
    tail = Swap(
        lambda place: tail_send.at[place],
        lambda place: tail_ref.at[place],
        send_tail,
        recv_tail,
        local_tail,
    )

    to_near.wait_recv()
    own_part[...] += near_got[...].astype(F32)
    to_far.wait_recv()
    own_part[...] += far_got[...].astype(F32)
    reduced[...] = own_part[...].T.astype(BF16)

    def begin_z(step, _):
        to_fs(lax.rem(fs_place + step, fs_count), fs_place).start()
        return 0

    lax.fori_loop(1, fs_count, begin_z, 0)
    own_z = pltpu.make_async_copy(
        reduced.at[columns(fs_place, seg), :], got_ref.at[columns(fs_place, seg), :], local_z
    )
    own_z.start()
    tail.start_all()

    to_near.wait_send()
    to_pair.wait_send()
    to_far.wait_send()

    def end_z(step, _):
        place = lax.rem(fs_place + step, fs_count)
        to_fs(place, place).wait_recv()
        to_fs(place, place).wait_send()
        return 0

    lax.fori_loop(1, fs_count, end_z, 0)
    own_z.wait()
    own_in.wait()
    own_out.start()

    def end_sums(step, _):
        place = lax.rem(sp_place + step, sp_count)
        to_owner(place, place).wait_recv()
        to_owner(place, place).wait_send()
        return 0

    lax.fori_loop(1, sp_count, end_sums, 0)
    own_out.wait()
    back.finish()
    tail.finish()


def attention_block(length, seg):
    return lax.axis_size("fs") * seg


def attend_grad(
    qkv, cosine, sine, out, lse, grad_attended, normed, weight, sums, back, score_scale
):
    length = qkv.shape[1]
    heads = qkv.shape[0] // (3 * HEAD_DIM)
    sp_count, fs_count = lax.axis_size("sp"), lax.axis_size("fs")
    total = sp_count * fs_count
    seg = length // total
    block = attention_block(length, seg)
    wide = heads * HEAD_DIM
    width = normed.shape[1]
    tail = (total, width // total, -(-3 * wide // LANES) * LANES)
    sp_sems = pltpu.SemaphoreType.DMA((sp_count,))
    fs_sems = pltpu.SemaphoreType.DMA((fs_count,))
    return pl.pallas_call(
        functools.partial(attend_grad_kernel, block, score_scale),
        in_specs=[VMEM_WHOLE] * 8 + [IN_PLACE] * 2,
        out_specs=[IN_PLACE] * 4,
        out_shape=[
            jax.ShapeDtypeStruct((block, width), BF16),
            jax.ShapeDtypeStruct(sums.shape, BF16),
            jax.ShapeDtypeStruct(back.shape, BF16),
            jax.ShapeDtypeStruct(tail, BF16),
        ],
        scratch_shapes=[
            pltpu.VMEM((3 * wide, length), BF16),
            pltpu.VMEM((width, block), BF16),
            pltpu.VMEM((width, block), BF16),
            pltpu.VMEM((width, block), BF16),
            pltpu.VMEM((width, block), BF16),
            pltpu.VMEM((width, block), BF16),
            pltpu.VMEM((width, block), BF16),
            pltpu.VMEM((width, block), F32),
            pltpu.VMEM((block, width), BF16),
            pltpu.VMEM((wide, length), BF16),
            pltpu.VMEM((wide, length), BF16),
            pltpu.VMEM((heads, length, HEAD_DIM), BF16),
            pltpu.VMEM((wide, length), BF16),
            pltpu.VMEM((heads, length, HEAD_DIM), BF16),
            pltpu.VMEM((heads, length, HEAD_DIM), BF16),
            pltpu.VMEM((heads, length, HEAD_DIM), BF16),
            pltpu.VMEM((heads, 1, length), F32),
            pltpu.VMEM((wide, length), F32),
            pltpu.VMEM((heads, length, HEAD_DIM), F32),
            pltpu.VMEM((heads, length, HEAD_DIM), F32),
            pltpu.VMEM((heads, sp_count * (sp_count + 1) // 2, block, block), BF16),
            pltpu.VMEM((3 * wide, width), F32),
            pltpu.VMEM(tail, BF16),
            pltpu.VMEM(sums.shape[1:], BF16),
        ]
        + swap_semaphores(total)
        + [pltpu.SemaphoreType.DMA((2, 3)), fs_sems, fs_sems, pltpu.SemaphoreType.DMA]
        + [sp_sems, sp_sems, pair_semaphores()]
        + swap_semaphores(total)
        + swap_semaphores(total),
        compiler_params=remote_params(2),
        cost_estimate=pl.CostEstimate(
            flops=60_000_000_000, bytes_accessed=8_000_000, transcendentals=0
        ),
        name="attend_grad",
    )(qkv, cosine, sine, out, lse, grad_attended, normed, weight, sums, back)


def slope_of(gate_val, sigmoid):
    return sigmoid * (1.0 + gate_val * (1.0 - sigmoid))


def dispatch_kernel(
    x_ref,
    g_ref,
    gate_ref,
    up_ref,
    down_ref,
    rows_ref,
    note_ref,
    crossed_ref,
    y_ref,
    gx_ref,
    grads_ref,
    got_ref,
    got_note_ref,
    full_ref,
    x_feat,
    gate_stage,
    up_stage,
    down_stage,
    send,
    recv,
    local,
    send_note,
    recv_note,
    local_note,
    dp_send,
    dp_recv,
    stage_sem,
):
    step = pl.program_id(0)
    tiles = pl.num_programs(0)
    total = rows_ref.shape[0]
    width = x_ref.shape[1]
    own_tile = gate_ref.shape[1] // (width // total) * LANES
    rows = Swap(
        lambda place: rows_ref.at[place], lambda place: got_ref.at[place], send, recv, local
    )
    notes = Swap(
        lambda place: note_ref.at[place],
        lambda place: got_note_ref.at[place],
        send_note,
        recv_note,
        local_note,
    )
    share = sharing(full_ref, dp_send, dp_recv)

    def to_grads(index):
        turn = lax.rem(index, 2)
        high = gate_stage.shape[2]
        weight_rows = grads_ref.shape[1] // 3
        owners, lane_rows = down_stage.shape[1], down_stage.shape[2]
        return [
            pltpu.make_async_copy(
                gate_stage.at[turn], grads_ref.at[:, columns(index, high)], stage_sem.at[0, turn]
            ),
            pltpu.make_async_copy(
                up_stage.at[turn],
                grads_ref.at[
                    :, pl.ds(pl.multiple_of(weight_rows + index * high, high), high)
                ],
                stage_sem.at[1, turn],
            ),
            pltpu.make_async_copy(
                down_stage.at[turn],
                grads_ref.at[
                    pl.ds(index * owners, owners), pl.ds(2 * weight_rows, lane_rows)
                ],
                stage_sem.at[2, turn],
            ),
        ]

    @pl.when(step == 0)
    def _():
        greet_places()
        greet_dp()
        x_feat[...] = x_ref[...].T
        y_ref[...] = jnp.zeros_like(y_ref)
        gx_ref[...] = jnp.zeros_like(gx_ref)
        await_places(1)
        notes.start_all()
        rows.start_all()
        share.start_share()

    own_gate = from_lane_blocks(gate_ref, width // total)
    own_up = from_lane_blocks(up_ref, width // total)
    own_down = from_lane_blocks(down_ref, LANES * down_ref.shape[1] // width)
    gate_val = dot32(x_ref[...], own_gate)
    up_val = dot32(x_ref[...], own_up)
    sigmoid = jax.nn.sigmoid(gate_val)
    swished = gate_val * sigmoid
    hidden = swished * up_val
    hidden_low = hidden.astype(BF16)
    grad_hidden = dot_nt(g_ref[...], own_down)
    gate_part = (grad_hidden * up_val * slope_of(gate_val, sigmoid)).astype(BF16)
    up_part = (grad_hidden * swished).astype(BF16)
    y_ref[...] += dot32(hidden_low, own_down)
    gx_ref[...] += dot_nt(gate_part, own_gate) + dot_nt(up_part, own_up)
    ddown = dot32(hidden.T.astype(BF16), g_ref[...]).astype(BF16)
    dgate = dot32(x_feat[...], gate_part).astype(BF16)
    dup = dot32(x_feat[...], up_part).astype(BF16)
    turn = lax.rem(step, 2)

    @pl.when(step >= 2)
    def _():
        for copy in to_grads(step - 2):
            copy.wait()

    shard = width // total
    for part in range(own_tile // LANES):
        lanes_here = slice(part * LANES, (part + 1) * LANES)
        rows_here = slice(part * shard, (part + 1) * shard)
        gate_stage[turn, :, rows_here, :] = dgate[:, lanes_here].reshape(total, shard, LANES)
        up_stage[turn, :, rows_here, :] = dup[:, lanes_here].reshape(total, shard, LANES)
    owners, owned = down_stage.shape[1], own_tile // down_stage.shape[1]
    for part in range(width // LANES):
        down_stage[turn, :, part * owned : (part + 1) * owned, :] = ddown[
            :, part * LANES : (part + 1) * LANES
        ].reshape(owners, owned, LANES)
    for copy in to_grads(step):
        copy.start()

    @pl.when(step == tiles - 1)
    def _():
        for index in (tiles - 2, tiles - 1):
            for copy in to_grads(index):
                copy.wait()
        notes.finish()
        rows.finish()
        share.finish_share()


def dispatch(own_x, own_g, own_pack, sent, note, crossed):
    total, cap, width = sent.shape
    own_rows = own_pack.shape[1] // 3
    tiles = own_rows * total * LANES // width // 256
    own_count = own_x.shape[0]
    high = own_rows // tiles
    owners = total // tiles
    whole = pl.BlockSpec((own_count, width), lambda i: (0, 0), pipeline_mode=pl.Buffered(1))
    return pl.pallas_call(
        dispatch_kernel,
        grid=(tiles,),
        in_specs=[
            whole,
            whole,
            pl.BlockSpec((total, high, LANES), lambda i: (0, i, 0)),
            pl.BlockSpec((total, high, LANES), lambda i: (0, tiles + i, 0)),
            pl.BlockSpec((owners, own_rows, LANES), lambda i: (i, 2, 0)),
        ]
        + [IN_PLACE] * 3,
        out_specs=[whole, whole] + [IN_PLACE] * 4,
        out_shape=[jax.ShapeDtypeStruct((own_count, width), F32)] * 2
        + [
            jax.ShapeDtypeStruct(array.shape, array.dtype)
            for array in (own_pack, sent, note, crossed)
        ],
        input_output_aliases={7: 5},
        scratch_shapes=[
            pltpu.VMEM((width, own_count), BF16),
            pltpu.VMEM((2, total, high, LANES), BF16),
            pltpu.VMEM((2, total, high, LANES), BF16),
            pltpu.VMEM((2, owners, own_rows, LANES), BF16),
        ]
        + swap_semaphores(total)
        + swap_semaphores(total)
        + share_scratch()
        + [pltpu.SemaphoreType.DMA((3, 2))],
        compiler_params=remote_params(3),
        cost_estimate=pl.CostEstimate(
            flops=40_000_000_000, bytes_accessed=20_000_000, transcendentals=0
        ),
        name="dispatch",
    )(own_x, own_g, own_pack, own_pack, own_pack, sent, note, crossed)


def from_lane_blocks(ref, rows):
    owners, high, lanes = ref.shape
    return jnp.concatenate(
        [
            ref[:, part * rows : (part + 1) * rows, :].reshape(owners * rows, lanes)
            for part in range(high // rows)
        ],
        axis=1,
    )


def to_lane_blocks(matrix):
    rows, wide = matrix.shape
    blocks = jnp.transpose(matrix.reshape(rows, wide // LANES, LANES), (1, 0, 2))
    return blocks.reshape(rows * wide // LANES, LANES)


def expert_kernel(
    x_ref,
    c_ref,
    note_ref,
    gate_ref,
    up_ref,
    down_ref,
    y_ref,
    dgate_ref,
    dup_ref,
    sum_ref,
    other_up_ref,
    got_ref,
    got_note_ref,
    x_feat,
    g_feat,
    gate_of_row,
    acc,
    dots,
    hidden_all,
    gate_all,
    up_all,
    gx_send,
    dots_send,
    ddown_all,
    other_all,
    up_sent,
    send,
    recv,
    local,
    send_note,
    recv_note,
    local_note,
    ddown_send,
    ddown_recv,
    sum_sem,
    half_send,
    half_recv,
):
    step = pl.program_id(0)
    tiles = pl.num_programs(0) // 2
    total, cap, width = gx_send.shape
    tile = hidden_all.shape[2]
    lanes = dots.shape[1]
    rows = Swap(
        lambda place: gx_send.at[place], lambda place: got_ref.at[place], send, recv, local
    )
    notes = Swap(
        lambda place: dots_send.at[place],
        lambda place: got_note_ref.at[place],
        send_note,
        recv_note,
        local_note,
    )

    def to_dp(index):
        return pltpu.make_async_remote_copy(
            src_ref=ddown_all.at[index],
            dst_ref=other_all.at[index],
            send_sem=ddown_send.at[index],
            recv_sem=ddown_recv.at[index],
            device_id={"dp": 1 - lax.axis_index("dp")},
            device_id_type=pl.DeviceIdType.MESH,
        )

    def up_to_dp(index):
        return pltpu.make_async_remote_copy(
            src_ref=up_sent.at[index],
            dst_ref=other_up_ref.at[:, columns(index, tile)],
            send_sem=half_send.at[index],
            recv_sem=half_recv.at[index],
            device_id={"dp": 1 - lax.axis_index("dp")},
            device_id_type=pl.DeviceIdType.MESH,
        )

    def block(place):
        return slice(place * cap, (place + 1) * cap)

    @pl.when(step == 0)
    def _():
        greet_places()
        greet_dp()
        x_feat[...] = x_ref[...].T
        for place in range(total):
            gate_of_row[block(place), :] = jnp.broadcast_to(
                note_ref[place].T[:cap, 0:1], (cap, lanes)
            )
        grads = gate_of_row[:, 0:1] * c_ref[...].astype(F32)
        g_feat[...] = grads.astype(BF16).T
        acc[...] = jnp.zeros_like(acc)
        dots[...] = jnp.zeros_like(dots)
        await_places(1)

    @pl.when(step < tiles)
    def _():
        gate_val = dot32(x_ref[...], gate_ref[...])
        up_val = dot32(x_ref[...], up_ref[...])
        sigmoid = jax.nn.sigmoid(gate_val)
        swished = gate_val * sigmoid
        hidden = (swished * up_val).astype(BF16)
        reach = dot32(c_ref[...], down_ref[...])
        product = hidden.astype(F32) * reach
        for part in range(tile // lanes):
            dots[...] += product[:, part * lanes : (part + 1) * lanes]
        grad_hidden = gate_of_row[:, 0:1] * reach
        gate_part = (grad_hidden * up_val * slope_of(gate_val, sigmoid)).astype(BF16)
        up_part = (grad_hidden * swished).astype(BF16)
        acc[...] += dot_nt(gate_part, gate_ref[...]) + dot_nt(up_part, up_ref[...])
        hidden_all[step] = hidden
        gate_all[step] = gate_part
        up_all[step] = up_part
        ddown = dot32(g_feat[...], hidden).astype(BF16)
        ddown_all[step] = ddown
        to_dp(step).start()

    @pl.when(step == tiles - 1)
    def _():
        for place in range(total):
            gx_send[place] = acc[block(place), :].astype(BF16)
            dots_send[place, 0:1, :cap] = jnp.sum(dots[block(place), :].T, axis=0, keepdims=True)
        acc[...] = jnp.zeros_like(acc)
        rows.start_all()
        notes.start_all()

    @pl.when(step >= tiles)
    def _():
        here = step - tiles
        hidden = hidden_all[here]
        acc[...] += dot_nt(hidden, down_ref[...])
        dgate_ref[...] = dot32(x_feat[...], gate_all[here]).astype(BF16)
        dup = dot32(x_feat[...], up_all[here]).astype(BF16)
        dup_ref[...] = dup

        @pl.when(here < tiles // 2)
        def _():
            up_sent[here] = dup
            up_to_dp(here).start()

    @pl.when(step == 2 * tiles - 1)
    def _():
        for place in range(total):
            y_ref[place] = (gate_of_row[block(place), 0:1] * acc[block(place), :]).astype(BF16)

        def out(index):
            return pltpu.make_async_copy(
                other_all.at[index], sum_ref.at[:, columns(index, tile)], sum_sem.at[index]
            )

        def add(index, _):
            to_dp(index).wait()
            total = ddown_all[index].astype(F32) + other_all[index].astype(F32)
            other_all[index] = total.astype(BF16)
            out(index).start()
            return 0

        lax.fori_loop(0, tiles, add, 0)
        rows.finish()
        notes.finish()

        def end(index, _):
            out(index).wait()
            return 0

        lax.fori_loop(0, tiles, end, 0)

        def end_half(index, _):
            up_to_dp(index).wait()
            return 0

        lax.fori_loop(0, tiles // 2, end_half, 0)


def expert_pass(rows, cots, note, gate, up, down):
    total, cap, width = rows.shape
    count = total * cap
    hidden = gate.shape[1]
    tile = 256
    tiles = hidden // tile
    lanes = note.shape[2]
    once = pl.Buffered(1)
    whole = pl.BlockSpec((count, width), lambda i: (0, 0), pipeline_mode=once)
    whole_note = pl.BlockSpec(note.shape, lambda i: (0, 0, 0), pipeline_mode=once)
    early = pl.BlockSpec((width, tile), lambda i: (0, jnp.minimum(i, tiles - 1)))
    both = pl.BlockSpec((width, tile), lambda i: (0, lax.rem(i, tiles)))
    late = pl.BlockSpec((width, tile), lambda i: (0, jnp.clip(i - tiles, 0, tiles - 1)))
    return pl.pallas_call(
        expert_kernel,
        grid=(2 * tiles,),
        in_specs=[whole, whole, whole_note, early, early, both],
        out_specs=[pl.BlockSpec(rows.shape, lambda i: (0, 0, 0), pipeline_mode=once)]
        + [late, late]
        + [IN_PLACE] * 4,
        out_shape=[jax.ShapeDtypeStruct(rows.shape, BF16)]
        + [jax.ShapeDtypeStruct((width, hidden), BF16)] * 2
        + [
            jax.ShapeDtypeStruct((width, hidden), BF16),
            jax.ShapeDtypeStruct((width, hidden // 2), BF16),
            jax.ShapeDtypeStruct(rows.shape, BF16),
            jax.ShapeDtypeStruct(note.shape, F32),
        ],
        scratch_shapes=[
            pltpu.VMEM((width, count), BF16),
            pltpu.VMEM((width, count), BF16),
            pltpu.VMEM((count, lanes), F32),
            pltpu.VMEM((count, width), F32),
            pltpu.VMEM((count, lanes), F32),
            pltpu.VMEM((tiles, count, tile), BF16),
            pltpu.VMEM((tiles, count, tile), BF16),
            pltpu.VMEM((tiles, count, tile), BF16),
            pltpu.VMEM(rows.shape, BF16),
            pltpu.VMEM(note.shape, F32),
            pltpu.VMEM((tiles, width, tile), BF16),
            pltpu.VMEM((tiles, width, tile), BF16),
            pltpu.VMEM((tiles // 2, width, tile), BF16),
        ]
        + swap_semaphores(total)
        + swap_semaphores(total)
        + [
            pltpu.SemaphoreType.DMA((tiles,)),
            pltpu.SemaphoreType.DMA((tiles,)),
            pltpu.SemaphoreType.DMA((tiles,)),
            pltpu.SemaphoreType.DMA((tiles // 2,)),
            pltpu.SemaphoreType.DMA((tiles // 2,)),
        ],
        compiler_params=remote_params(4),
        cost_estimate=pl.CostEstimate(
            flops=80_000_000_000, bytes_accessed=30_000_000, transcendentals=0
        ),
        name="expert_pass",
    )(
        rows.reshape(count, width),
        cots.reshape(count, width),
        note,
        gate,
        up,
        down,
    )


def swap_sum(value, axis):
    if lax.axis_size(axis) == 2:
        other = lax.ppermute(value, axis, [(0, 1), (1, 0)])
        return value.astype(F32) + other.astype(F32)
    return lax.psum(value, axis).astype(F32)


def exchange(chunks):
    return lax.all_to_all(chunks, ("sp", "fs"), split_axis=0, concat_axis=0, tiled=True)


def per_device_split(
    tokens,
    expert_ids,
    fill_order,
    attention_gain,
    query_weight,
    key_weight,
    value_weight,
    output_weight,
    mixer_gain,
    router_weight,
    shared_gate,
    shared_up,
    shared_down,
    expert_gate,
    expert_up,
    expert_down,
    cotangent,
):
    seq_count, seg_rows, width = tokens.shape
    token_count = seq_count * seg_rows
    fs_count = lax.axis_size("fs")
    sp_count = lax.axis_size("sp")
    place_count = fs_count * sp_count
    local_heads = HEADS // sp_count
    flat_width = local_heads * HEAD_DIM
    score_scale = HEAD_DIM ** (-0.5)
    length = place_count * seg_rows
    shard_rows = query_weight.shape[0]
    qkv_width = 3 * flat_width

    cot_rows = cotangent.reshape(token_count, width)
    small = jnp.concatenate(
        [
            attention_gain[:, None],
            mixer_gain[:, None],
            router_weight,
            jnp.zeros((shard_rows, LANES - 2 - EXPERTS), BF16),
        ],
        axis=1,
    )
    def gather_all(shard):
        return lax.all_gather(shard, ("sp", "fs"), axis=0, tiled=True)

    half = HEAD_DIM // 2
    frequency = 10000.0 ** (-jnp.arange(half, dtype=F32) / half)
    angles = frequency[:, None] * jnp.arange(length, dtype=jnp.int32).astype(F32)[None, :]
    cosine, sine = jnp.cos(angles), jnp.sin(angles)
    output_full = gather_all(output_weight)
    shared_pack = gather_all(
        jnp.concatenate(
            [to_lane_blocks(shared_gate), to_lane_blocks(shared_up), to_lane_blocks(shared_down)]
        )[None]
    )
    slot_total = CAP * EXPERTS
    (
        slots,
        taking,
        normed_seq,
        own_pack,
        qkv,
        out_heads,
        lse,
        attended,
        arrived_cots,
        gate_own,
        up_own,
        down_crossed,
    ) = front(
        tokens,
        query_weight,
        key_weight,
        value_weight,
        small,
        expert_ids.reshape(token_count, TOPK).T,
        fill_order.reshape(1, token_count),
        cot_rows,
        cosine,
        sine,
        expert_gate,
        expert_up,
        expert_down,
        score_scale,
    )
    qkv_own = own_pack[:, :qkv_width]
    gain_one = own_pack[:, qkv_width].astype(F32)
    gain_two = own_pack[:, qkv_width + 1].astype(F32)
    router_full = own_pack[:, qkv_width + 2 : qkv_width + 2 + EXPERTS]
    residual = tokens.astype(F32).reshape(token_count, width)

    def outer(left, right):
        return lax.dot_general(left, right, (((0,), (0,)), ((), ())), preferred_element_type=F32)

    middle = residual + outer(attended, output_full)
    mixed_in = norm_apply(middle, gain_two).astype(BF16)

    logits = dot32(mixed_in, router_full)
    def gate_values(raw_logits):
        shifted = jnp.exp(raw_logits - jnp.max(raw_logits, axis=-1, keepdims=True))
        router_probs = shifted / jnp.sum(shifted, axis=-1, keepdims=True)
        picked = jnp.sum(router_probs[:, None, :] * onehot_float, axis=2)
        return picked / jnp.sum(picked, axis=1, keepdims=True)

    choices = expert_ids.reshape(token_count, TOPK)
    expert_onehot = choices[:, :, None] == jnp.arange(EXPERTS, dtype=jnp.int32)[None, None, :]
    onehot_float = expert_onehot.astype(F32)
    gate_weights, gate_pull = jax.vjp(gate_values, logits)
    slot_ids = jnp.arange(slot_total, dtype=jnp.int32)
    takes_a = slot_ids[:, None] == slots[0][None, :]
    takes_b = slot_ids[:, None] == slots[1][None, :]

    gate_of_slot = jnp.sum(
        jnp.where(takes_a, gate_weights[None, :, 0], 0.0)
        + jnp.where(takes_b, gate_weights[None, :, 1], 0.0),
        axis=1,
    )
    outgoing = dot32(taking, mixed_in).astype(BF16)
    note = jnp.pad(
        gate_of_slot.reshape(place_count, 1, CAP), ((0, 0), (0, NOTE_ROWS - 1), (0, LANES - CAP))
    )
    shared_out, grad_mixed_shared, grad_shared, rows, notes, down_own = dispatch(
        mixed_in,
        cot_rows,
        shared_pack,
        outgoing.reshape(place_count, CAP, width),
        note,
        down_crossed,
    )
    grad_shared = lax.psum_scatter(grad_shared, ("sp", "fs"), scatter_dimension=0)
    expert_out, dgate, dup, sum_down, other_up_half, grad_returned, dots = expert_pass(
        rows,
        arrived_cots,
        notes,
        gate_own.reshape(width, -1),
        up_own.reshape(width, -1),
        down_own.reshape(width, -1),
    )
    grad_returned = grad_returned.reshape(slot_total, width)
    dots = dots[:, 0, :CAP].reshape(slot_total)

    def to_dp(value):
        return lax.ppermute(value, "dp", [(0, 1), (1, 0)])

    def sum_of(grad, other):
        total = (grad.astype(F32) + other.astype(F32)).astype(BF16)
        return total.reshape(sp_count, width // sp_count, grad.shape[1])

    def spread(parts):
        return lax.all_to_all(parts, "sp", split_axis=0, concat_axis=0, tiled=True).astype(F32)

    other_gate, other_up = to_dp(dgate), to_dp(dup[:, other_up_half.shape[1] :])

    grad_result = cot_rows.astype(F32)
    grad_gates = jnp.stack(
        [
            jnp.sum(jnp.where(slots[j][:, None] == slot_ids[None, :], dots[None, :], 0.0), axis=1)
            for j in range(TOPK)
        ],
        axis=1,
    )
    (grad_logits,) = gate_pull(grad_gates)
    grad_logits = grad_logits.astype(BF16)
    grad_router = outer(mixed_in, grad_logits)
    grad_mixed = (
        outer(taking, grad_returned) + dot_nt(grad_logits, router_full) + grad_mixed_shared
    )
    _, norm_two_pull = jax.vjp(norm_apply, middle, gain_two)
    grad_middle_part, grad_gain_two = norm_two_pull(grad_mixed)
    grad_middle = grad_result + grad_middle_part
    grad_proj = grad_middle.astype(BF16)
    grad_output_matrix = dot32(attended, grad_proj)
    grad_attended = dot_nt(output_full, grad_proj).astype(BF16)
    dense = jnp.concatenate(
        [
            grad_output_matrix.astype(BF16),
            grad_router.astype(BF16),
            jnp.pad(grad_gain_two[:, None], ((0, 0), (0, LANES - EXPERTS - 1))).astype(BF16),
        ],
        axis=1,
    )
    grad_normed, sum_down, returned, tail = attend_grad(
        qkv,
        cosine,
        sine,
        out_heads,
        lse,
        grad_attended,
        normed_seq,
        qkv_own,
        sum_down.reshape(sp_count, width // sp_count, -1),
        expert_out,
        score_scale,
    )
    other_gate, other_up, grad_shared, grad_normed = lax.optimization_barrier(
        (other_gate, other_up, grad_shared, grad_normed)
    )
    dense = lax.psum_scatter(dense, ("sp", "fs"), scatter_dimension=0, tiled=True)
    parts_up, tail, sum_down, returned, grad_normed = lax.optimization_barrier(
        (
            sum_of(dup, jnp.concatenate([other_up_half, other_up], axis=1)),
            tail,
            sum_down,
            returned,
            grad_normed,
        )
    )
    sum_up = spread(parts_up)
    sum_gate = spread(sum_of(dgate, other_gate))
    dense, sum_gate = lax.optimization_barrier((dense, sum_gate))
    sum_down = sum_down.astype(F32)
    output = (middle + shared_out + outer(taking, returned.reshape(slot_total, width))).astype(BF16)
    grad_normed = grad_normed.astype(F32)
    _, norm_one_pull = jax.vjp(lambda values: norm_apply(values, gain_one), residual)
    (grad_residual_part,) = norm_one_pull(grad_normed)
    grad_tokens = grad_middle + grad_residual_part

    tail = tail.reshape(sp_count, fs_count, shard_rows, tail.shape[2])[:, :, :, :qkv_width]
    tail = jnp.sum(tail.astype(F32), axis=1).astype(BF16)
    sum_dense = swap_sum(dense, "dp")
    sum_shared = swap_sum(grad_shared, "dp")
    sum_tail = swap_sum(tail, "dp")
    sum_qkv = sum_tail.reshape(sp_count, shard_rows, 3, flat_width)
    sum_qkv = jnp.transpose(sum_qkv, (2, 1, 0, 3)).reshape(3, shard_rows, width)
    sum_gain_one = sum(
        jnp.sum(weight.astype(F32) * grad, axis=1)
        for weight, grad in zip((query_weight, key_weight, value_weight), sum_qkv)
    ) / attention_gain.astype(F32)
    weight_rows = grad_shared.shape[0] // 3

    def lane_blocks(flat, high):
        blocks = flat.reshape(-1, high, LANES)
        return jnp.transpose(blocks, (1, 0, 2)).reshape(high, -1)

    sum_shared_gate = lane_blocks(sum_shared[:weight_rows], shard_rows)
    sum_shared_up = lane_blocks(sum_shared[weight_rows : 2 * weight_rows], shard_rows)
    sum_shared_down = lane_blocks(sum_shared[2 * weight_rows :], shared_down.shape[0])
    return (
        output.reshape(tokens.shape),
        grad_tokens.reshape(tokens.shape),
        sum_gain_one,
        sum_qkv[0],
        sum_qkv[1],
        sum_qkv[2],
        sum_dense[:, :width],
        sum_dense[:, width + EXPERTS],
        sum_dense[:, width : width + EXPERTS],
        sum_shared_gate,
        sum_shared_up,
        sum_shared_down,
        sum_gate,
        sum_up,
        sum_down,
    )


def per_device_any(*shards):
    fs_count, sp_count = lax.axis_size("fs"), lax.axis_size("sp")
    same = shards[0].shape[0] == fs_count and EXPERTS == 4 * fs_count
    if same and sp_count == 4 and lax.axis_size("dp") == 2:
        return per_device_split(*shards)
    return per_device(*shards)


def solution(mesh):
    placed = (
        P("dp", ("sp", "fs"), None),
        P("dp", ("sp", "fs"), None),
        P("dp", ("sp", "fs")),
        P(("sp", "fs")),
        P(("sp", "fs"), None),
        P(("sp", "fs"), None),
        P(("sp", "fs"), None),
        P(("sp", "fs"), None),
        P(("sp", "fs")),
        P(("sp", "fs"), None),
        P(("sp", "fs"), None),
        P(("sp", "fs"), None),
        P(("sp", "fs"), None),
        P("fs", "sp", None),
        P("fs", "sp", None),
        P("fs", "sp", None),
        P("dp", ("sp", "fs"), None),
    )
    return jax.shard_map(
        per_device_any,
        mesh=mesh,
        in_specs=placed,
        out_specs=(
            P("dp", ("sp", "fs"), None),
            P("dp", ("sp", "fs"), None),
            P(("sp", "fs")),
            P(("sp", "fs"), None),
            P(("sp", "fs"), None),
            P(("sp", "fs"), None),
            P(("sp", "fs"), None),
            P(("sp", "fs")),
            P(("sp", "fs"), None),
            P(("sp", "fs"), None),
            P(("sp", "fs"), None),
            P(("sp", "fs"), None),
            P("fs", "sp", None),
            P("fs", "sp", None),
            P("fs", "sp", None),
        ),
        check_vma=False,
    )
```

```python
import functools
import math

import jax
import jax.numpy as jnp
from jax import lax
from jax.experimental import pallas as pl
from jax.experimental.pallas import tpu as pltpu
from jax.sharding import PartitionSpec as P

HEADS = 12
HEAD_DIM = 64
EXPERTS = 16
TOPK = 2
CAP = 72


EPSILON = 1e-06
MASKED = -1e30


def norm_apply(values, gain_row):
    inverse_root = lax.rsqrt(jnp.mean(values * values, axis=-1, keepdims=True) + EPSILON)
    return values * inverse_root * gain_row


def swish(values):
    return values * jax.nn.sigmoid(values)


def glu_product(gate_part, up_part):
    return swish(gate_part) * up_part


def rotate(values, positions):
    half_dim = values.shape[-1] // 2
    frequency = 10000.0 ** (-jnp.arange(half_dim, dtype=jnp.float32) / half_dim)
    angles = positions.astype(jnp.float32)[:, None] * frequency[None, :]
    cosine_table = jnp.cos(angles)[:, None, :]
    sine_table = jnp.sin(angles)[:, None, :]
    front_part = values[..., :half_dim]
    back_part = values[..., half_dim:]
    return jnp.concatenate(
        [
            front_part * cosine_table - back_part * sine_table,
            back_part * cosine_table + front_part * sine_table,
        ],
        axis=-1,
    )


def place_rows(indices, quarter_rows, segment_rows, fs_count):
    source_device = indices // quarter_rows
    row_inside = indices % quarter_rows
    return (
        row_inside // segment_rows * fs_count + source_device
    ) * segment_rows + row_inside % segment_rows


def to_heads(stacked):
    return lax.all_to_all(stacked, "sp", split_axis=3, concat_axis=2, tiled=True)


def to_tokens(stacked):
    return lax.all_to_all(stacked, "sp", split_axis=2, concat_axis=3, tiled=True)


def to_experts(buffer):
    return lax.all_to_all(buffer, "fs", split_axis=1, concat_axis=0, tiled=True)


def from_experts(buffer):
    return lax.all_to_all(buffer, "fs", split_axis=0, concat_axis=1, tiled=True)


def score_grads(
    query_part,
    query_rows,
    key_part,
    value_part,
    key_rows,
    grad_part,
    lse_part,
    delta_part,
    score_scale,
):
    allowed = key_rows[None, None, None, :] <= query_rows[None, None, :, None]
    scores = (
        jnp.einsum("bqhd,bkhd->bhqk", query_part, key_part, preferred_element_type=jnp.float32)
        * score_scale
    )
    weights = jnp.where(allowed, jnp.exp(scores - lse_part[..., None]), 0.0)
    grad_value = jnp.einsum(
        "bhqk,bqhd->bkhd",
        weights.astype(jnp.bfloat16),
        grad_part,
        preferred_element_type=jnp.float32,
    )
    grad_weights = jnp.einsum(
        "bqhd,bkhd->bhqk", grad_part, value_part, preferred_element_type=jnp.float32
    )
    grad_scores = (weights * (grad_weights - delta_part[..., None]) * score_scale).astype(
        jnp.bfloat16
    )
    grad_query = jnp.einsum(
        "bhqk,bkhd->bqhd", grad_scores, key_part, preferred_element_type=jnp.float32
    )
    grad_key = jnp.einsum(
        "bhqk,bqhd->bkhd", grad_scores, query_part, preferred_element_type=jnp.float32
    )
    return (grad_query, grad_key, grad_value)


def per_device(
    tokens,
    expert_ids,
    fill_order,
    attention_gain,
    query_weight,
    key_weight,
    value_weight,
    output_weight,
    mixer_gain,
    router_weight,
    shared_gate,
    shared_up,
    shared_down,
    expert_gate,
    expert_up,
    expert_down,
    cotangent,
):
    seq_count, seg_rows, model_width = tokens.shape
    token_count = seq_count * seg_rows
    fs_count = lax.axis_size("fs")
    sp_count = lax.axis_size("sp")
    fs_place = lax.axis_index("fs")
    local_heads = HEADS // sp_count
    score_scale = HEAD_DIM ** (-0.5)
    (
        gain_full,
        query_full,
        key_full,
        value_full,
        output_full,
        mixer_full,
        router_full,
        shared_gate_full,
        shared_up_full,
        shared_down_full,
    ) = (
        lax.all_gather(attention_gain, ("sp", "fs"), axis=0, tiled=True),
        lax.all_gather(query_weight, ("sp", "fs"), axis=0, tiled=True),
        lax.all_gather(key_weight, ("sp", "fs"), axis=0, tiled=True),
        lax.all_gather(value_weight, ("sp", "fs"), axis=0, tiled=True),
        lax.all_gather(output_weight, ("sp", "fs"), axis=0, tiled=True),
        lax.all_gather(mixer_gain, ("sp", "fs"), axis=0, tiled=True),
        lax.all_gather(router_weight, ("sp", "fs"), axis=0, tiled=True),
        lax.all_gather(shared_gate, ("sp", "fs"), axis=0, tiled=True),
        lax.all_gather(shared_up, ("sp", "fs"), axis=0, tiled=True),
        lax.all_gather(shared_down, ("sp", "fs"), axis=0, tiled=True),
    )
    expert_gate_full, expert_up_full, expert_down_full = (
        lax.all_gather(expert_gate, "sp", axis=1, tiled=True),
        lax.all_gather(expert_up, "sp", axis=1, tiled=True),
        lax.all_gather(expert_down, "sp", axis=1, tiled=True),
    )
    residual = tokens.astype(jnp.float32)
    gain_one = gain_full.astype(jnp.float32)
    gain_two = mixer_full.astype(jnp.float32)
    normed = norm_apply(residual, gain_one).astype(jnp.bfloat16)
    query_raw = jnp.dot(normed, query_full, preferred_element_type=jnp.float32).astype(jnp.bfloat16)
    key_raw = jnp.dot(normed, key_full, preferred_element_type=jnp.float32).astype(jnp.bfloat16)
    value_raw = jnp.dot(normed, value_full, preferred_element_type=jnp.float32).astype(jnp.bfloat16)
    heads_view = to_heads(jnp.stack([query_raw, key_raw, value_raw]))
    quarter_rows = heads_view.shape[2]
    head_shape = (seq_count, quarter_rows, local_heads, HEAD_DIM)
    flat_width = local_heads * HEAD_DIM
    own_rows = place_rows(
        fs_place * quarter_rows + jnp.arange(quarter_rows, dtype=jnp.int32),
        quarter_rows,
        seg_rows,
        fs_count,
    )

    def rotate_own(values):
        return rotate(values, own_rows)

    query_rot = rotate_own(heads_view[0].reshape(head_shape).astype(jnp.float32)).astype(
        jnp.bfloat16
    )
    key_rot = rotate_own(heads_view[1].reshape(head_shape).astype(jnp.float32)).astype(jnp.bfloat16)
    key_flat = key_rot.reshape(seq_count, quarter_rows, flat_width)
    value_flat = heads_view[2]
    keys_all, values_all = (
        lax.all_gather(key_flat, "fs", axis=1, tiled=True),
        lax.all_gather(value_flat, "fs", axis=1, tiled=True),
    )
    total_rows = keys_all.shape[1]
    block_rows = math.gcd(quarter_rows, 512)
    part_shape = (seq_count, block_rows, local_heads, HEAD_DIM)
    offsets = jnp.arange(total_rows // block_rows, dtype=jnp.int32) * block_rows

    def key_slices(offset):
        key_part = lax.dynamic_slice_in_dim(keys_all, offset, block_rows, 1).reshape(part_shape)
        value_part = lax.dynamic_slice_in_dim(values_all, offset, block_rows, 1).reshape(part_shape)
        key_rows = place_rows(
            offset + jnp.arange(block_rows, dtype=jnp.int32), quarter_rows, seg_rows, fs_count
        )
        return (key_part, value_part, key_rows)

    def forward_block(carried, offset):
        running_max, running_sum, running_acc = carried
        key_part, value_part, key_rows = key_slices(offset)
        allowed = key_rows[None, None, None, :] <= own_rows[None, None, :, None]
        scores = (
            jnp.einsum("bqhd,bkhd->bhqk", query_rot, key_part, preferred_element_type=jnp.float32)
            * score_scale
        )
        scores = jnp.where(allowed, scores, MASKED)
        new_max = jnp.maximum(running_max, jnp.max(scores, axis=-1))
        weights = jnp.where(allowed, jnp.exp(scores - new_max[..., None]), 0.0)
        factor = jnp.exp(running_max - new_max)
        running_sum = running_sum * factor + jnp.sum(weights, axis=-1)
        running_acc = running_acc * factor[..., None] + jnp.einsum(
            "bhqk,bkhd->bhqd",
            weights.astype(jnp.bfloat16),
            value_part,
            preferred_element_type=jnp.float32,
        )
        return ((new_max, running_sum, running_acc), None)

    start_state = (
        jnp.full((seq_count, local_heads, quarter_rows), MASKED, jnp.float32),
        jnp.zeros((seq_count, local_heads, quarter_rows), jnp.float32),
        jnp.zeros((seq_count, local_heads, quarter_rows, HEAD_DIM), jnp.float32),
    )
    (final_max, final_sum, final_acc), _ = lax.scan(forward_block, start_state, offsets)
    attended_heads = (final_acc / final_sum[..., None]).astype(jnp.bfloat16)
    log_total = final_max + jnp.log(final_sum)
    attended_view = jnp.transpose(attended_heads, (0, 2, 1, 3))
    attended_flat = attended_view.reshape(seq_count, quarter_rows, flat_width)
    attended_tokens = to_tokens(attended_flat[None])[0]
    middle = residual + jnp.dot(attended_tokens, output_full, preferred_element_type=jnp.float32)
    mixed_in = norm_apply(middle, gain_two).astype(jnp.bfloat16)
    token_rows = mixed_in.reshape(token_count, model_width)
    logits = jnp.dot(token_rows, router_full, preferred_element_type=jnp.float32)
    choices = expert_ids.reshape(token_count, TOPK)
    expert_onehot = choices[:, :, None] == jnp.arange(EXPERTS, dtype=jnp.int32)[None, None, :]
    onehot_float = expert_onehot.astype(jnp.float32)

    def gate_values(raw_logits):
        shifted = jnp.exp(raw_logits - jnp.max(raw_logits, axis=-1, keepdims=True))
        router_probs = shifted / jnp.sum(shifted, axis=-1, keepdims=True)
        picked = jnp.sum(router_probs[:, None, :] * onehot_float, axis=2)
        return picked / jnp.sum(picked, axis=1, keepdims=True)

    gate_weights, gate_pull = jax.vjp(gate_values, logits)
    shared_gate_val = jnp.dot(mixed_in, shared_gate_full, preferred_element_type=jnp.float32)
    shared_up_val = jnp.dot(mixed_in, shared_up_full, preferred_element_type=jnp.float32)
    shared_hidden_full, shared_pull = jax.vjp(glu_product, shared_gate_val, shared_up_val)
    shared_hidden = shared_hidden_full.astype(jnp.bfloat16)
    shared_out = jnp.dot(shared_hidden, shared_down_full, preferred_element_type=jnp.float32)
    onehot_int = expert_onehot.astype(jnp.int32)
    per_token = jnp.sum(onehot_int, axis=1)
    fill_rank = fill_order.reshape(token_count)
    earlier = (fill_rank[None, :] < fill_rank[:, None]).astype(jnp.int32)
    counts = jnp.dot(earlier, per_token, preferred_element_type=jnp.int32)
    slot_ranks = jnp.sum(counts[:, None, :] * onehot_int, axis=2)
    slot_total = CAP * EXPERTS
    slots = jnp.where(slot_ranks < CAP, slot_ranks * EXPERTS + choices, slot_total).reshape(-1)
    outgoing = (
        jnp.zeros((slot_total, model_width), jnp.bfloat16)
        .at[slots]
        .set(jnp.repeat(token_rows, TOPK, axis=0), mode="drop")
    )
    incoming = to_experts(outgoing.reshape(CAP, EXPERTS, model_width))
    expert_gate_val = jnp.einsum(
        "red,edf->ref", incoming, expert_gate_full, preferred_element_type=jnp.float32
    )
    expert_up_val = jnp.einsum(
        "red,edf->ref", incoming, expert_up_full, preferred_element_type=jnp.float32
    )
    expert_hidden_full, expert_pull = jax.vjp(glu_product, expert_gate_val, expert_up_val)
    expert_hidden = expert_hidden_full.astype(jnp.bfloat16)
    expert_out = jnp.einsum(
        "ref,edf->red", expert_hidden, expert_down_full, preferred_element_type=jnp.float32
    ).astype(jnp.bfloat16)
    returned = from_experts(expert_out).reshape(slot_total, model_width)
    padded = jnp.concatenate([returned, jnp.zeros((1, model_width), jnp.bfloat16)], axis=0)
    picked_rows = padded[slots].reshape(token_count, TOPK, model_width).astype(jnp.float32)
    combined = jnp.sum(gate_weights[:, :, None] * picked_rows, axis=1)
    result = (
        middle.reshape(token_count, model_width)
        + shared_out.reshape(token_count, model_width)
        + combined
    )
    output = result.astype(jnp.bfloat16).reshape(seq_count, seg_rows, model_width)
    grad_result = cotangent.astype(jnp.float32).reshape(token_count, model_width)
    grad_gates = jnp.sum(grad_result[:, None, :] * picked_rows, axis=2)
    grad_slots = (
        (gate_weights[:, :, None] * grad_result[:, None, :])
        .astype(jnp.bfloat16)
        .reshape(token_count * TOPK, model_width)
    )
    grad_outgoing = (
        jnp.zeros((slot_total, model_width), jnp.bfloat16).at[slots].set(grad_slots, mode="drop")
    )
    grad_incoming = to_experts(grad_outgoing.reshape(CAP, EXPERTS, model_width))
    grad_expert_down = jnp.einsum(
        "red,ref->edf", grad_incoming, expert_hidden, preferred_element_type=jnp.float32
    )
    grad_expert_hidden = jnp.einsum(
        "red,edf->ref", grad_incoming, expert_down_full, preferred_element_type=jnp.float32
    )
    grad_gate_part, grad_up_part = expert_pull(grad_expert_hidden)
    grad_gate_part = grad_gate_part.astype(jnp.bfloat16)
    grad_up_part = grad_up_part.astype(jnp.bfloat16)
    grad_expert_gate = jnp.einsum(
        "red,ref->edf", incoming, grad_gate_part, preferred_element_type=jnp.float32
    )
    grad_expert_up = jnp.einsum(
        "red,ref->edf", incoming, grad_up_part, preferred_element_type=jnp.float32
    )
    grad_pair_rows = (
        jnp.einsum(
            "ref,edf->red", grad_gate_part, expert_gate_full, preferred_element_type=jnp.float32
        )
        + jnp.einsum(
            "ref,edf->red", grad_up_part, expert_up_full, preferred_element_type=jnp.float32
        )
    ).astype(jnp.bfloat16)
    grad_returned = from_experts(grad_pair_rows).reshape(slot_total, model_width)
    grad_padded = jnp.concatenate(
        [grad_returned, jnp.zeros((1, model_width), jnp.bfloat16)], axis=0
    )
    grad_mixed = jnp.sum(
        grad_padded[slots].reshape(token_count, TOPK, model_width).astype(jnp.float32), axis=1
    )
    (grad_logits,) = gate_pull(grad_gates)
    grad_logits = grad_logits.astype(jnp.bfloat16)
    grad_router = jnp.einsum(
        "td,te->de", token_rows, grad_logits, preferred_element_type=jnp.float32
    )
    grad_mixed = grad_mixed + jnp.einsum(
        "te,de->td", grad_logits, router_full, preferred_element_type=jnp.float32
    )
    grad_shared_out = grad_result.astype(jnp.bfloat16).reshape(seq_count, seg_rows, model_width)
    grad_shared_down = jnp.einsum(
        "blf,bld->fd", shared_hidden, grad_shared_out, preferred_element_type=jnp.float32
    )
    grad_shared_hidden = jnp.einsum(
        "bld,fd->blf", grad_shared_out, shared_down_full, preferred_element_type=jnp.float32
    )
    grad_shared_gate_part, grad_shared_up_part = shared_pull(grad_shared_hidden)
    grad_shared_gate_part = grad_shared_gate_part.astype(jnp.bfloat16)
    grad_shared_up_part = grad_shared_up_part.astype(jnp.bfloat16)
    grad_shared_gate = jnp.einsum(
        "bld,blf->df", mixed_in, grad_shared_gate_part, preferred_element_type=jnp.float32
    )
    grad_shared_up = jnp.einsum(
        "bld,blf->df", mixed_in, grad_shared_up_part, preferred_element_type=jnp.float32
    )
    grad_mixed = (
        grad_mixed.reshape(seq_count, seg_rows, model_width)
        + jnp.einsum(
            "blf,df->bld",
            grad_shared_gate_part,
            shared_gate_full,
            preferred_element_type=jnp.float32,
        )
        + jnp.einsum(
            "blf,df->bld", grad_shared_up_part, shared_up_full, preferred_element_type=jnp.float32
        )
    )
    _, norm_two_pull = jax.vjp(norm_apply, middle, gain_two)
    grad_middle_part, grad_gain_two = norm_two_pull(grad_mixed)
    grad_middle = grad_result.reshape(seq_count, seg_rows, model_width) + grad_middle_part
    grad_proj = grad_middle.astype(jnp.bfloat16)
    grad_output_matrix = jnp.einsum(
        "bld,ble->de", attended_tokens, grad_proj, preferred_element_type=jnp.float32
    )
    grad_attended = jnp.einsum(
        "ble,de->bld", grad_proj, output_full, preferred_element_type=jnp.float32
    ).astype(jnp.bfloat16)
    grad_attended_heads = to_heads(grad_attended[None])[0].reshape(head_shape)
    delta_rows = jnp.einsum(
        "bqhd,bqhd->bhq",
        grad_attended_heads,
        attended_flat.reshape(head_shape),
        preferred_element_type=jnp.float32,
    )

    def key_step(grad_query, offset):
        key_part, value_part, key_rows = key_slices(offset)
        part_query, part_key, part_value = score_grads(
            query_rot,
            own_rows,
            key_part,
            value_part,
            key_rows,
            grad_attended_heads,
            log_total,
            delta_rows,
            score_scale,
        )
        flat_shape = (seq_count, block_rows, flat_width)
        return (
            grad_query + part_query,
            (part_key.reshape(flat_shape), part_value.reshape(flat_shape)),
        )

    grad_query_rot, (key_terms, value_terms) = lax.scan(
        key_step, jnp.zeros(head_shape, jnp.float32), offsets
    )
    own_keys, own_values = (
        lax.psum_scatter(
            key_terms.astype(jnp.bfloat16), "fs", scatter_dimension=0, tiled=True
        ).astype(jnp.float32),
        lax.psum_scatter(
            value_terms.astype(jnp.bfloat16), "fs", scatter_dimension=0, tiled=True
        ).astype(jnp.float32),
    )
    grad_key_rot = jnp.moveaxis(own_keys, 0, 1).reshape(head_shape)
    grad_value = jnp.moveaxis(own_values, 0, 1).reshape(head_shape)
    _, rope_pull = jax.vjp(rotate_own, jnp.zeros(head_shape, jnp.float32))
    (grad_query_raw,) = rope_pull(grad_query_rot)
    (grad_key_raw,) = rope_pull(grad_key_rot)
    stacked_grads = (
        jnp.stack([grad_query_raw, grad_key_raw, grad_value])
        .astype(jnp.bfloat16)
        .reshape(3, seq_count, quarter_rows, flat_width)
    )
    token_grads = to_tokens(stacked_grads)
    grad_query_matrix = jnp.einsum(
        "bld,ble->de", normed, token_grads[0], preferred_element_type=jnp.float32
    )
    grad_key_matrix = jnp.einsum(
        "bld,ble->de", normed, token_grads[1], preferred_element_type=jnp.float32
    )
    grad_value_matrix = jnp.einsum(
        "bld,ble->de", normed, token_grads[2], preferred_element_type=jnp.float32
    )
    grad_normed = (
        jnp.einsum("ble,de->bld", token_grads[0], query_full, preferred_element_type=jnp.float32)
        + jnp.einsum("ble,de->bld", token_grads[1], key_full, preferred_element_type=jnp.float32)
        + jnp.einsum("ble,de->bld", token_grads[2], value_full, preferred_element_type=jnp.float32)
    )
    _, norm_one_pull = jax.vjp(norm_apply, residual, gain_one)
    grad_residual_part, grad_gain_one = norm_one_pull(grad_normed)
    grad_tokens = grad_middle + grad_residual_part
    (
        part_gain_one,
        part_query,
        part_key,
        part_value,
        part_output,
        part_gain_two,
        part_router,
        part_shared_gate,
        part_shared_up,
        part_shared_down,
    ) = (
        lax.psum_scatter(
            grad_gain_one.astype(jnp.bfloat16), ("sp", "fs"), scatter_dimension=0, tiled=True
        ).astype(jnp.float32),
        lax.psum_scatter(
            grad_query_matrix.astype(jnp.bfloat16), ("sp", "fs"), scatter_dimension=0, tiled=True
        ).astype(jnp.float32),
        lax.psum_scatter(
            grad_key_matrix.astype(jnp.bfloat16), ("sp", "fs"), scatter_dimension=0, tiled=True
        ).astype(jnp.float32),
        lax.psum_scatter(
            grad_value_matrix.astype(jnp.bfloat16), ("sp", "fs"), scatter_dimension=0, tiled=True
        ).astype(jnp.float32),
        lax.psum_scatter(
            grad_output_matrix.astype(jnp.bfloat16), ("sp", "fs"), scatter_dimension=0, tiled=True
        ).astype(jnp.float32),
        lax.psum_scatter(
            grad_gain_two.astype(jnp.bfloat16), ("sp", "fs"), scatter_dimension=0, tiled=True
        ).astype(jnp.float32),
        lax.psum_scatter(
            grad_router.astype(jnp.bfloat16), ("sp", "fs"), scatter_dimension=0, tiled=True
        ).astype(jnp.float32),
        lax.psum_scatter(
            grad_shared_gate.astype(jnp.bfloat16), ("sp", "fs"), scatter_dimension=0, tiled=True
        ).astype(jnp.float32),
        lax.psum_scatter(
            grad_shared_up.astype(jnp.bfloat16), ("sp", "fs"), scatter_dimension=0, tiled=True
        ).astype(jnp.float32),
        lax.psum_scatter(
            grad_shared_down.astype(jnp.bfloat16), ("sp", "fs"), scatter_dimension=0, tiled=True
        ).astype(jnp.float32),
    )
    own_gate, own_up, own_down = (
        lax.psum_scatter(
            grad_expert_gate.astype(jnp.bfloat16), "sp", scatter_dimension=1, tiled=True
        ).astype(jnp.float32),
        lax.psum_scatter(
            grad_expert_up.astype(jnp.bfloat16), "sp", scatter_dimension=1, tiled=True
        ).astype(jnp.float32),
        lax.psum_scatter(
            grad_expert_down.astype(jnp.bfloat16), "sp", scatter_dimension=1, tiled=True
        ).astype(jnp.float32),
    )
    (
        sum_gain_one,
        sum_query,
        sum_key,
        sum_value,
        sum_output,
        sum_gain_two,
        sum_router,
        sum_shared_gate,
        sum_shared_up,
        sum_shared_down,
        sum_gate,
        sum_up,
        sum_down,
    ) = (
        lax.psum(part_gain_one.astype(jnp.bfloat16), "dp").astype(jnp.float32),
        lax.psum(part_query.astype(jnp.bfloat16), "dp").astype(jnp.float32),
        lax.psum(part_key.astype(jnp.bfloat16), "dp").astype(jnp.float32),
        lax.psum(part_value.astype(jnp.bfloat16), "dp").astype(jnp.float32),
        lax.psum(part_output.astype(jnp.bfloat16), "dp").astype(jnp.float32),
        lax.psum(part_gain_two.astype(jnp.bfloat16), "dp").astype(jnp.float32),
        lax.psum(part_router.astype(jnp.bfloat16), "dp").astype(jnp.float32),
        lax.psum(part_shared_gate.astype(jnp.bfloat16), "dp").astype(jnp.float32),
        lax.psum(part_shared_up.astype(jnp.bfloat16), "dp").astype(jnp.float32),
        lax.psum(part_shared_down.astype(jnp.bfloat16), "dp").astype(jnp.float32),
        lax.psum(own_gate.astype(jnp.bfloat16), "dp").astype(jnp.float32),
        lax.psum(own_up.astype(jnp.bfloat16), "dp").astype(jnp.float32),
        lax.psum(own_down.astype(jnp.bfloat16), "dp").astype(jnp.float32),
    )
    return (
        output,
        grad_tokens,
        sum_gain_one,
        sum_query,
        sum_key,
        sum_value,
        sum_output,
        sum_gain_two,
        sum_router,
        sum_shared_gate,
        sum_shared_up,
        sum_shared_down,
        sum_gate,
        sum_up,
        sum_down,
    )


BF16 = jnp.bfloat16
F32 = jnp.float32
LANES = 128
NOTE_ROWS = 8
VMEM_WHOLE = pl.BlockSpec(memory_space=pltpu.VMEM)
IN_PLACE = pl.BlockSpec(memory_space=pl.ANY)
ROOM = 60 * 1024 * 1024


def dot32(left, right):
    return jnp.dot(left, right, preferred_element_type=F32)


def dot_nt(left, right):
    return lax.dot_general(left, right, (((1,), (1,)), ((), ())), preferred_element_type=F32)


def turn(values, cosine, sine):
    half = values.shape[0] // 2
    front, back = values[:half], values[half:]
    return jnp.concatenate([front * cosine - back * sine, back * cosine + front * sine], axis=0)


def turn_back(values, cosine, sine):
    half = values.shape[0] // 2
    front, back = values[:half], values[half:]
    return jnp.concatenate([front * cosine + back * sine, back * cosine - front * sine], axis=0)


def causal(block):
    keys = lax.broadcasted_iota(jnp.int32, (block, block), 0)
    queries = lax.broadcasted_iota(jnp.int32, (block, block), 1)
    return keys <= queries


def remote_params(number):
    return pltpu.CompilerParams(
        collective_id=number, has_side_effects=True, vmem_limit_bytes=ROOM
    )


def places():
    sp_count, fs_count = lax.axis_size("sp"), lax.axis_size("fs")
    own = lax.axis_index("sp") * fs_count + lax.axis_index("fs")
    return sp_count * fs_count, own


def at_place(place):
    fs_count = lax.axis_size("fs")
    return {"sp": place // fs_count, "fs": lax.rem(place, fs_count)}


def greet_places():
    total, own = places()
    barrier = pltpu.get_barrier_semaphore()

    def greet(step, _):
        pl.semaphore_signal(
            barrier,
            inc=1,
            device_id=at_place(lax.rem(own + step, total)),
            device_id_type=pl.DeviceIdType.MESH,
        )
        return 0

    lax.fori_loop(1, total, greet, 0)


def await_places(others=0):
    pl.semaphore_wait(pltpu.get_barrier_semaphore(), places()[0] - 1 + others)


def columns(index, size):
    return pl.ds(pl.multiple_of(index * size, size), size)


class Swap:
    def __init__(self, source, target, send, recv, local):
        self.source, self.target = source, target
        self.send, self.recv, self.local = send, recv, local

    def remote(self, place, landing, mark):
        return pltpu.make_async_remote_copy(
            src_ref=self.source(place),
            dst_ref=self.target(landing),
            send_sem=self.send.at[place],
            recv_sem=self.recv.at[mark],
            device_id=at_place(place),
            device_id_type=pl.DeviceIdType.MESH,
        )

    def own(self):
        own = places()[1]
        return pltpu.make_async_copy(self.source(own), self.target(own), self.local)

    def start(self, place):
        own = places()[1]

        @pl.when(place != own)
        def _():
            self.remote(place, own, own).start()

        @pl.when(place == own)
        def _():
            self.own().start()

    def start_all(self):
        total, own = places()

        def begin(step, _):
            self.remote(lax.rem(own + step, total), own, own).start()
            return 0

        lax.fori_loop(1, total, begin, 0)
        self.own().start()

    def finish(self):
        total, own = places()

        def end(step, _):
            place = lax.rem(own + step, total)
            copy = self.remote(place, place, place)
            copy.wait_send()
            copy.wait_recv()
            return 0

        lax.fori_loop(1, total, end, 0)
        self.own().wait()


def swap_semaphores(total):
    return [
        pltpu.SemaphoreType.DMA((total,)),
        pltpu.SemaphoreType.DMA((total,)),
        pltpu.SemaphoreType.DMA,
    ]


class Spread:
    def __init__(self, shard, full, stage, near, far_send, far_recv, dp_send, dp_recv, local):
        self.shard, self.full, self.stage = shard, full, stage
        self.near, self.far_send, self.far_recv = near, far_send, far_recv
        self.dp_send, self.dp_recv, self.local = dp_send, dp_recv, local
        self.sp, self.dp = lax.axis_index("sp"), lax.axis_index("dp")
        self.core = self.sp + 1 - 2 * lax.rem(self.sp, 2)
        self.other = 2 - 2 * (self.sp // 2)
        self.half = shard.shape[1] // 2
        self.rows = pl.ds(pl.multiple_of(self.dp * self.half, self.half), self.half)
        self.dp_rows = pl.ds(pl.multiple_of((1 - self.dp) * self.half, self.half), self.half)

    def to_core(self):
        return pltpu.make_async_remote_copy(
            src_ref=self.shard.at[self.core],
            dst_ref=self.full.at[self.sp],
            send_sem=self.near.at[0],
            recv_sem=self.near.at[1],
            device_id={"sp": self.core},
            device_id_type=pl.DeviceIdType.MESH,
        )

    def to_far(self, turn):
        return pltpu.make_async_remote_copy(
            src_ref=self.shard.at[self.other + turn, self.rows],
            dst_ref=self.full.at[self.sp, self.rows],
            send_sem=self.far_send.at[turn],
            recv_sem=self.far_recv.at[lax.rem(self.sp, 2)],
            device_id={"sp": self.other + turn},
            device_id_type=pl.DeviceIdType.MESH,
        )

    def from_far(self, turn):
        return pltpu.make_async_remote_copy(
            src_ref=self.shard.at[self.other + turn, self.rows],
            dst_ref=self.full.at[self.other + turn, self.rows],
            send_sem=self.far_send.at[turn],
            recv_sem=self.far_recv.at[turn],
            device_id={"sp": self.other + turn},
            device_id_type=pl.DeviceIdType.MESH,
        )

    def to_dp(self, turn):
        block = self.full.at[self.other + turn, self.rows]
        return pltpu.make_async_remote_copy(
            src_ref=block,
            dst_ref=block,
            send_sem=self.dp_send.at[turn],
            recv_sem=self.dp_recv.at[turn],
            device_id={"dp": 1 - self.dp},
            device_id_type=pl.DeviceIdType.MESH,
        )

    def from_dp(self, turn):
        block = self.full.at[self.other + turn, self.dp_rows]
        return pltpu.make_async_remote_copy(
            src_ref=block,
            dst_ref=block,
            send_sem=self.dp_send.at[turn],
            recv_sem=self.dp_recv.at[turn],
            device_id={"dp": 1 - self.dp},
            device_id_type=pl.DeviceIdType.MESH,
        )

    def own_in(self):
        return pltpu.make_async_copy(self.shard.at[self.sp], self.stage, self.local.at[0])

    def own_out(self):
        return pltpu.make_async_copy(self.stage, self.full.at[self.sp], self.local.at[1])

    def start_cross(self):
        self.own_in().start()
        self.to_far(0).start()
        self.to_far(1).start()
        self.to_core().start()

    def finish_cross(self):
        self.own_in().wait()
        self.own_out().start()
        for turn in range(2):
            self.from_far(turn).wait_recv()
            self.to_far(turn).wait_send()
        self.to_core().wait_send()
        self.to_core().wait_recv()
        self.own_out().wait()

    def start_share(self):
        self.to_dp(0).start()
        self.to_dp(1).start()

    def finish_share(self):
        for turn in range(2):
            self.from_dp(turn).wait_recv()
            self.to_dp(turn).wait_send()


def pair_semaphores():
    return pltpu.SemaphoreType.DMA((2,))


def cross_scratch(shard):
    return [pltpu.VMEM(shard.shape[1:], shard.dtype)] + [pair_semaphores()] * 4


def share_scratch():
    return [pair_semaphores()] * 2


def crossing(shard, full, stage, near, far_send, far_recv, local):
    return Spread(shard, full, stage, near, far_send, far_recv, None, None, local)


def sharing(full, dp_send, dp_recv):
    return Spread(full, full, None, None, None, None, dp_send, dp_recv, None)


def greet_dp():
    pl.semaphore_signal(
        pltpu.get_barrier_semaphore(),
        inc=1,
        device_id={"dp": 1 - lax.axis_index("dp")},
        device_id_type=pl.DeviceIdType.MESH,
    )


def route(ids_ref, fill_ref, slots_ref, taking_ref):
    count = fill_ref.shape[1]
    group = EXPERTS // lax.axis_size("fs")
    fill_row = fill_ref[...].astype(F32)
    fill_column = jnp.broadcast_to(fill_row, (8, count)).T[:, 0:1]
    earlier = (fill_column < fill_row).astype(BF16)
    experts = lax.broadcasted_iota(jnp.int32, (EXPERTS, count), 0)
    named = [(experts == ids_ref[j : j + 1, :]).astype(F32) for j in range(TOPK)]
    counts = dot32((named[0] + named[1]).astype(BF16), earlier)
    slots = []
    for j in range(TOPK):
        rank = jnp.sum(counts * named[j], axis=0, keepdims=True).astype(jnp.int32)
        choice = ids_ref[j : j + 1, :]
        holder = lax.rem(choice, group) * lax.axis_size("fs") + choice // group
        slots.append(jnp.where(rank < CAP, holder * CAP + rank, -1))
        slots_ref[j : j + 1, :] = slots[j]
    total = taking_ref.shape[0]
    half = total // 2
    for start in (0, half):
        slot_ids = start + lax.broadcasted_iota(jnp.int32, (half, count), 0)
        taken = (slot_ids == slots[0]) | (slot_ids == slots[1])
        taking_ref[start : start + half, :] = taken.astype(F32).astype(BF16)


def spread_rows(taking_ref, rows_ref, out_ref):
    total, cap, _ = out_ref.shape
    half = total // 2
    for first in (0, half):
        rows = dot32(taking_ref[first * cap : (first + half) * cap, :], rows_ref[...])
        for place in range(half):
            out_ref[first + place] = rows[place * cap : (place + 1) * cap].astype(BF16)


def front_kernel(
    scale,
    tokens_ref,
    query_ref,
    key_ref,
    value_ref,
    small_ref,
    ids_ref,
    fill_ref,
    cot_ref,
    cos_ref,
    sin_ref,
    gate_shard,
    up_shard,
    down_shard,
    slots_ref,
    taking_ref,
    normed_ref,
    weight_ref,
    qkv_ref,
    o_ref,
    lse_ref,
    got_ref,
    cots_ref,
    gate_full,
    up_full,
    down_full,
    seq,
    pack,
    pack_got,
    weight_feat,
    cot_out,
    k_rot,
    z_send,
    z_recv,
    core_send,
    core_recv,
    y_send,
    y_recv,
    late_send,
    late_recv,
    up_send,
    up_recv,
    down_send,
    down_recv,
    pack_send,
    pack_recv,
    local,
    cot_send,
    cot_recv,
    cot_local,
    send,
    recv,
    out_local,
    gate_dp_send,
    gate_dp_recv,
    up_dp_send,
    up_dp_recv,
    *cross,
):
    fs_count, sp_count = lax.axis_size("fs"), lax.axis_size("sp")
    fs_place, sp_place = lax.axis_index("fs"), lax.axis_index("sp")
    heads, length, _ = k_rot.shape
    wide = heads * HEAD_DIM
    seg = tokens_ref.shape[1]
    block = fs_count * seg
    core = sp_place + 1 - 2 * lax.rem(sp_place, 2)
    across = lax.rem(sp_place + 2, sp_count)
    beyond = lax.rem(core + 2, sp_count)

    def fs_peer(step):
        return lax.rem(fs_place + step, fs_count)

    def sp_peer(step):
        return lax.rem(sp_place + step, sp_count)

    def move(source, target, send_sem, recv_sem, where):
        return pltpu.make_async_remote_copy(
            src_ref=source,
            dst_ref=target,
            send_sem=send_sem,
            recv_sem=recv_sem,
            device_id=where,
            device_id_type=pl.DeviceIdType.MESH,
        )

    def each(count, body):
        def run(index, _):
            body(index)
            return 0

        lax.fori_loop(1, count, run, 0)

    greet_places()
    greet_dp()
    part = query_ref.shape[1] // sp_count
    for place in range(sp_count):
        for kind, source in enumerate((query_ref, key_ref, value_ref)):
            pack[place, :, kind * part : (kind + 1) * part] = source[
                :, place * part : (place + 1) * part
            ]
        pack[place, :, 3 * part :] = small_ref[:, : pack.shape[2] - 3 * part]
    await_places(1)

    def pack_move(place, owner, mark):
        return move(
            pack.at[place],
            pack_got.at[owner, fs_place],
            pack_send.at[place],
            pack_recv.at[mark],
            {"sp": place},
        )

    def z_move(place, owner):
        return move(
            tokens_ref.at[place],
            seq.at[sp_place, owner],
            z_send.at[place],
            z_recv.at[owner],
            {"fs": place},
        )

    def to_core(source, mark):
        return move(
            source, seq.at[sp_place, mark], core_send.at[mark], core_recv.at[mark], {"sp": core}
        )

    def to_across(source, mark):
        return move(
            source, seq.at[sp_place, mark], y_send.at[mark], y_recv.at[mark], {"sp": across}
        )

    def late(mark):
        rows = seq.at[across, mark]
        return move(rows, rows, late_send.at[mark], late_recv.at[mark], {"sp": core})

    def upward(mark):
        rows = pack_got.at[:, mark]
        return move(rows, rows, up_send.at[mark], up_recv.at[mark], {"fs": fs_peer(1)})

    def downward(mark):
        rows = pack_got.at[:, mark]
        return move(
            rows, rows, down_send.at[mark], down_recv.at[mark], {"fs": fs_peer(fs_count - 1)}
        )

    each(sp_count, lambda step: pack_move(sp_peer(step), sp_place, sp_place).start())
    each(fs_count, lambda step: z_move(fs_peer(step), fs_place).start())
    own_tokens = tokens_ref.at[fs_place]
    to_across(own_tokens, fs_place).start()
    to_core(own_tokens, fs_place).start()
    own_seq = pltpu.make_async_copy(own_tokens, seq.at[sp_place, fs_place], local.at[0])
    own_pack = pltpu.make_async_copy(
        pack.at[sp_place], pack_got.at[sp_place, fs_place], local.at[1]
    )
    own_seq.start()
    own_pack.start()
    own_pack.wait()

    def pack_here(step):
        mark = sp_peer(step)
        pack_move(mark, mark, mark).wait_recv()

    each(sp_count, pack_here)
    has_up = fs_place < fs_count - 1
    has_down = fs_place > 0

    @pl.when(has_up)
    def _():
        upward(fs_place).start()

    @pl.when(has_down)
    def _():
        downward(fs_place).start()

    route(ids_ref, fill_ref, slots_ref, taking_ref)
    spread_rows(taking_ref, cot_ref, cot_out)

    def relay(step):
        below, above = fs_place - step, fs_place + step

        @pl.when(below >= 0)
        def _():
            upward(below).wait_recv()

        @pl.when((below >= 0) & has_up)
        def _():
            upward(below).start()

        @pl.when(above < fs_count)
        def _():
            downward(above).wait_recv()

        @pl.when((above < fs_count) & has_down)
        def _():
            downward(above).start()

        mark = fs_peer(step)
        z_move(mark, mark).wait_recv()
        rows = seq.at[sp_place, mark]
        to_across(rows, mark).start()
        to_core(rows, mark).start()

    each(fs_count, relay)
    cots = Swap(
        lambda place: cot_out.at[place],
        lambda place: cots_ref.at[place],
        cot_send,
        cot_recv,
        cot_local,
    )
    cots.start_all()
    size = len(cross) // 3
    gate = crossing(gate_shard, gate_full, *cross[:size])
    up = crossing(up_shard, up_full, *cross[size : 2 * size])
    down = crossing(down_shard, down_full, *cross[2 * size :])
    gate.start_cross()
    up.start_cross()
    down.start_cross()

    def pass_on(mark, _):
        to_across(own_tokens, mark).wait_recv()
        late(mark).start()
        return 0

    lax.fori_loop(0, fs_count, pass_on, 0)
    own_seq.wait()
    packed = pack_got[...].reshape(weight_ref.shape)
    weight_ref[...] = packed
    weight_feat[...] = packed.T
    gain_row = weight_feat[3 * wide : 3 * wide + 1, :].astype(F32)

    def head_rows(kind, head):
        return columns(kind * heads + head, HEAD_DIM)

    def project(place):
        own_columns = columns(place, block)
        rows = seq[place].reshape(block, seq.shape[3]).astype(F32)
        scaled = lax.rsqrt(jnp.mean(rows * rows, axis=-1, keepdims=True) + EPSILON)
        normed = (rows * scaled * gain_row).astype(BF16)
        normed_ref[own_columns, :] = normed
        qkv_ref[:, own_columns] = dot_nt(weight_feat[: 3 * wide, :], normed).astype(BF16)

        def turn_keys(head, _):
            rotated = turn(
                qkv_ref[head_rows(1, head), own_columns].astype(F32),
                cos_ref[:, own_columns],
                sin_ref[:, own_columns],
            )
            k_rot[head, own_columns, :] = rotated.T.astype(BF16)
            return 0

        lax.fori_loop(0, heads, turn_keys, 0)

    def from_core(mark, _):
        to_core(own_tokens, mark).wait_recv()
        return 0

    def from_late(mark, _):
        late(mark).wait_recv()
        return 0

    lax.fori_loop(0, fs_count, from_core, 0)
    lax.fori_loop(0, fs_count, from_late, 0)

    def project_step(step, _):
        project(sp_peer(step))
        return 0

    lax.fori_loop(0, sp_count, project_step, 0)

    exchange = Swap(
        lambda place: o_ref.at[:, columns(place, seg)],
        lambda place: got_ref.at[
            columns(place // fs_count, wide), columns(lax.rem(place, fs_count), seg)
        ],
        send,
        recv,
        out_local,
    )

    def attend_block(place):
        own_columns = columns(place, block)

        def attend_head(head, _):
            query = turn(
                qkv_ref[head_rows(0, head), own_columns].astype(F32),
                cos_ref[:, own_columns],
                sin_ref[:, own_columns],
            ).astype(BF16)

            def scores_at(index):
                return dot32(k_rot[head, columns(index, block), :], query) * scale

            def weighted(index, weights):
                values = qkv_ref[head_rows(2, head), columns(index, block)]
                return dot32(values, weights.astype(BF16))

            scores = jnp.where(causal(block), scores_at(place), MASKED)
            first_max = jnp.max(scores, axis=0, keepdims=True)
            weights = jnp.exp(scores - first_max)
            first_sum = jnp.sum(weights, axis=0, keepdims=True)

            def step(index, carried):
                running_max, running_sum, running_acc = carried
                part = scores_at(index)
                new_max = jnp.maximum(running_max, jnp.max(part, axis=0, keepdims=True))
                part = jnp.exp(part - new_max)
                factor = jnp.exp(running_max - new_max)
                return (
                    new_max,
                    running_sum * factor + jnp.sum(part, axis=0, keepdims=True),
                    running_acc * factor + weighted(index, part),
                )

            final_max, final_sum, final_acc = lax.fori_loop(
                0, place, step, (first_max, first_sum, weighted(place, weights))
            )
            o_ref[columns(head, HEAD_DIM), own_columns] = (final_acc / final_sum).astype(BF16)
            lse_ref[head, :, own_columns] = final_max + jnp.log(final_sum)
            return 0

        lax.fori_loop(0, heads, attend_head, 0)

    gate_share = sharing(gate_full, gate_dp_send, gate_dp_recv)
    up_share = sharing(up_full, up_dp_send, up_dp_recv)

    def step(index, _):
        place = length // block - 1 - index
        attend_block(place)

        def begin(part, _):
            exchange.start(place * fs_count + part)
            return 0

        lax.fori_loop(0, fs_count, begin, 0)

        @pl.when(index == 0)
        def _():
            gate.finish_cross()
            gate_share.start_share()

        @pl.when(index == 1)
        def _():
            up.finish_cross()
            up_share.start_share()

        return 0

    lax.fori_loop(0, length // block, step, 0)
    exchange.finish()
    cots.finish()
    down.finish_cross()
    gate_share.finish_share()
    up_share.finish_share()

    def end(mark, _):
        to_core(own_tokens, mark).wait_send()
        to_across(own_tokens, mark).wait_send()
        late(mark).wait_send()

        @pl.when(has_up & (mark <= fs_place))
        def _():
            upward(mark).wait_send()

        @pl.when(has_down & (mark >= fs_place))
        def _():
            downward(mark).wait_send()

        return 0

    lax.fori_loop(0, fs_count, end, 0)
    each(sp_count, lambda step: pack_move(sp_peer(step), sp_place, sp_place).wait_send())
    each(fs_count, lambda step: z_move(fs_peer(step), fs_place).wait_send())


def front(
    tokens, query, key, value, small, ids, fill, cots, cosine, sine, gate, up, down, score_scale
):
    sp_count, fs_count = lax.axis_size("sp"), lax.axis_size("fs")
    total = sp_count * fs_count
    fs_sems = pltpu.SemaphoreType.DMA((fs_count,))
    sp_sems = pltpu.SemaphoreType.DMA((sp_count,))
    rows, width = query.shape
    wide = width // sp_count
    heads = wide // HEAD_DIM
    seg = tokens.shape[1]
    length = total * seg
    pack = (rows, -(-(3 * wide + 2 + EXPERTS) // LANES) * LANES)
    count = ids.shape[1]
    slot_rows = (total, CAP, width)
    return pl.pallas_call(
        functools.partial(front_kernel, score_scale),
        in_specs=[IN_PLACE] + [VMEM_WHOLE] * 9 + [IN_PLACE] * 3,
        out_specs=[VMEM_WHOLE] * 7 + [IN_PLACE] * 5,
        out_shape=[
            jax.ShapeDtypeStruct((TOPK, count), jnp.int32),
            jax.ShapeDtypeStruct((total * CAP, count), BF16),
            jax.ShapeDtypeStruct((length, width), BF16),
            jax.ShapeDtypeStruct((width, pack[1]), BF16),
            jax.ShapeDtypeStruct((3 * wide, length), BF16),
            jax.ShapeDtypeStruct((wide, length), BF16),
            jax.ShapeDtypeStruct((heads, 1, length), F32),
            jax.ShapeDtypeStruct((width, fs_count * seg), BF16),
            jax.ShapeDtypeStruct(slot_rows, BF16),
        ]
        + [jax.ShapeDtypeStruct(shard.shape, shard.dtype) for shard in (gate, up, down)],
        scratch_shapes=[
            pltpu.VMEM((sp_count, fs_count) + tokens.shape[1:], BF16),
            pltpu.VMEM((sp_count,) + pack, BF16),
            pltpu.VMEM((sp_count, fs_count) + pack, BF16),
            pltpu.VMEM((pack[1], width), BF16),
            pltpu.VMEM(slot_rows, BF16),
            pltpu.VMEM((heads, length, HEAD_DIM), BF16),
        ]
        + [fs_sems] * 12
        + [sp_sems] * 2
        + [pair_semaphores()]
        + swap_semaphores(total)
        + swap_semaphores(total)
        + share_scratch()
        + share_scratch()
        + cross_scratch(gate)
        + cross_scratch(up)
        + cross_scratch(down),
        compiler_params=remote_params(1),
        cost_estimate=pl.CostEstimate(
            flops=100_000_000_000, bytes_accessed=4_000_000, transcendentals=0
        ),
        name="front",
    )(tokens, query, key, value, small, ids, fill, cots, cosine, sine, gate, up, down)


def attend_grad_kernel(
    block,
    scale,
    qkv_ref,
    cos_ref,
    sin_ref,
    o_ref,
    lse_ref,
    ga_ref,
    normed_ref,
    weight_ref,
    sums_ref,
    back_out_ref,
    got_ref,
    spread_ref,
    back_ref,
    tail_ref,
    grad_ref,
    near_out,
    near_got,
    pair_out,
    pair_got,
    far_out,
    far_got,
    own_part,
    reduced,
    go_feat,
    q_feat,
    q_rows,
    k_feat,
    k_rows,
    v_rows,
    go_rows,
    delta,
    dq_acc,
    dk_acc,
    dv_acc,
    probs,
    weight_acc,
    tail_send,
    stage,
    send_in,
    recv_in,
    local_in,
    part_sems,
    send_z,
    recv_z,
    local_z,
    send_sums,
    recv_sums,
    local_sums,
    send_back,
    recv_back,
    local_back,
    send_tail,
    recv_tail,
    local_tail,
):
    heads, length, _ = q_rows.shape
    wide = heads * HEAD_DIM
    total, own = places()
    seg = length // total
    fs_count, sp_count = lax.axis_size("fs"), lax.axis_size("sp")
    fs_place, sp_place = lax.axis_index("fs"), lax.axis_index("sp")
    greet_places()

    def head_rows(kind, head):
        return columns(kind * heads + head, HEAD_DIM)

    def prepare(head, _):
        rotated = turn(qkv_ref[head_rows(0, head), :].astype(F32), cos_ref[...], sin_ref[...])
        q_feat[columns(head, HEAD_DIM), :] = rotated.astype(BF16)
        q_rows[head] = rotated.T.astype(BF16)
        rotated = turn(qkv_ref[head_rows(1, head), :].astype(F32), cos_ref[...], sin_ref[...])
        k_feat[columns(head, HEAD_DIM), :] = rotated.astype(BF16)
        k_rows[head] = rotated.T.astype(BF16)
        v_rows[head] = qkv_ref[head_rows(2, head), :].astype(F32).T.astype(BF16)
        return 0

    arrival = Swap(
        lambda place: ga_ref.at[
            columns(place // fs_count, wide), columns(lax.rem(place, fs_count), seg)
        ],
        lambda place: go_feat.at[:, columns(place, seg)],
        send_in,
        recv_in,
        local_in,
    )
    await_places()
    arrival.start_all()
    back = Swap(
        lambda place: back_out_ref.at[place],
        lambda place: back_ref.at[place],
        send_back,
        recv_back,
        local_back,
    )
    back.start_all()
    lax.fori_loop(0, heads, prepare, 0)
    dq_acc[...] = jnp.zeros_like(dq_acc)
    weight_acc[...] = jnp.zeros_like(weight_acc)
    dk_acc[...] = jnp.zeros_like(dk_acc)
    dv_acc[...] = jnp.zeros_like(dv_acc)
    count = length // block
    down = 1 - sp_place // (sp_count // 2)

    def pair_columns(turn_index, step):
        place = turn_index + down * (count - 1 - 2 * turn_index)
        other = place + step - 2 * step * down
        queries = columns(other + down * (place - other), block)
        return queries, columns(place + down * (other - place), block)

    def pair_slot(turn_index, step):
        return turn_index * (2 * count - turn_index + 1) // 2 + step

    def form(head, _):
        rows = columns(head, HEAD_DIM)

        def pair(turn_index, step, masked):
            queries, keys = pair_columns(turn_index, step)
            scores = dot32(k_rows[head, keys, :], q_feat[rows, queries]) * scale
            weights = jnp.exp(scores - lse_ref[head, :, queries])
            if masked:
                weights = jnp.where(causal(block), weights, 0.0)
            probs[head, pair_slot(turn_index, step)] = weights.astype(BF16)

        def turns(turn_index, _):
            pair(turn_index, 0, True)

            def steps(step, _):
                pair(turn_index, step, False)
                return 0

            lax.fori_loop(1, count - turn_index, steps, 0)
            return 0

        lax.fori_loop(0, count, turns, 0)
        return 0

    lax.fori_loop(0, heads, form, 0)
    arrival.finish()

    def prepare_grad(head, _):
        grad = go_feat[columns(head, HEAD_DIM), :].astype(F32)
        go_rows[head] = grad.T.astype(BF16)
        delta[head] = jnp.sum(
            grad * o_ref[columns(head, HEAD_DIM), :].astype(F32), axis=0, keepdims=True
        )
        return 0

    lax.fori_loop(0, heads, prepare_grad, 0)

    core = sp_place + 1 - 2 * lax.rem(sp_place, 2)
    across = lax.rem(sp_place + 2, sp_count)

    def part_move(index, source, target, place):
        return pltpu.make_async_remote_copy(
            src_ref=source,
            dst_ref=target,
            send_sem=part_sems.at[0, index],
            recv_sem=part_sems.at[1, index],
            device_id={"sp": place},
            device_id_type=pl.DeviceIdType.MESH,
        )

    to_near = part_move(0, near_out, near_got, core)
    to_pair = part_move(1, pair_out, pair_got, core)
    to_far = part_move(2, far_out, far_got, across)

    def to_fs(place, mark):
        return pltpu.make_async_remote_copy(
            src_ref=reduced.at[columns(place, seg), :],
            dst_ref=got_ref.at[columns(mark, seg), :],
            send_sem=send_z.at[place],
            recv_sem=recv_z.at[mark],
            device_id={"fs": place},
            device_id_type=pl.DeviceIdType.MESH,
        )


    def segment(turn_index, _):
        place = turn_index + down * (count - 1 - 2 * turn_index)
        own_columns = columns(place, block)
        own_cos, own_sin = cos_ref[:, own_columns], sin_ref[:, own_columns]

        def segment_head(head, _):
            rows = columns(head, HEAD_DIM)

            def pair(step):
                queries, keys = pair_columns(turn_index, step)
                low = probs[head, pair_slot(turn_index, step)]
                weights = low.astype(F32)
                reach = dot32(v_rows[head, keys, :], go_feat[rows, queries])
                slopes = (weights * (reach - delta[head, :, queries]) * scale).astype(BF16)
                dq_acc[rows, queries] += dot32(k_feat[rows, keys], slopes)
                dk_acc[head, keys, :] += dot32(slopes, q_rows[head, queries, :])
                dv_acc[head, keys, :] += dot32(low, go_rows[head, queries, :])

            pair(0)

            def step(index, _):
                pair(index)
                return 0

            lax.fori_loop(1, count - turn_index, step, 0)
            grad_ref[head_rows(0, head), own_columns] = turn_back(
                dq_acc[rows, own_columns], own_cos, own_sin
            ).astype(BF16)
            grad_ref[head_rows(1, head), own_columns] = turn_back(
                dk_acc[head, own_columns, :].T, own_cos, own_sin
            ).astype(BF16)
            grad_ref[head_rows(2, head), own_columns] = dv_acc[head, own_columns, :].T.astype(BF16)
            return 0

        lax.fori_loop(0, heads, segment_head, 0)
        part = dot32(weight_ref[...], grad_ref[:, own_columns])

        @pl.when(place == sp_place)
        def _():
            own_part[...] = part

        @pl.when(place == core)
        def _():
            near_out[...] = part.astype(BF16)
            to_near.start()

        @pl.when(place == lax.rem(core + 2, sp_count))
        def _():
            pair_out[...] = part.astype(BF16)
            to_pair.start()

        @pl.when(place == across)
        def _():
            to_pair.wait_recv()
            far_out[...] = (part + pair_got[...].astype(F32)).astype(BF16)
            to_far.start()

        weight_acc[...] += dot32(grad_ref[:, own_columns], normed_ref[own_columns, :])
        return 0

    lax.fori_loop(0, count, segment, 0)

    def to_owner(place, mark):
        return pltpu.make_async_remote_copy(
            src_ref=sums_ref.at[place],
            dst_ref=spread_ref.at[mark],
            send_sem=send_sums.at[place],
            recv_sem=recv_sums.at[mark],
            device_id={"sp": place},
            device_id_type=pl.DeviceIdType.MESH,
        )

    def begin_sums(step, _):
        to_owner(lax.rem(sp_place + step, sp_count), sp_place).start()
        return 0

    lax.fori_loop(1, sp_count, begin_sums, 0)
    own_in = pltpu.make_async_copy(sums_ref.at[sp_place], stage, local_sums.at[0])
    own_out = pltpu.make_async_copy(stage, spread_ref.at[sp_place], local_sums.at[1])
    own_in.start()
    shard, wide_all = tail_send.shape[1], 3 * wide
    flipped = weight_acc[...].T
    for place in range(tail_send.shape[0]):
        tail_send[place, :, :wide_all] = flipped[place * shard : (place + 1) * shard].astype(BF16)
    tail = Swap(
        lambda place: tail_send.at[place],
        lambda place: tail_ref.at[place],
        send_tail,
        recv_tail,
        local_tail,
    )

    to_near.wait_recv()
    own_part[...] += near_got[...].astype(F32)
    to_far.wait_recv()
    own_part[...] += far_got[...].astype(F32)
    reduced[...] = own_part[...].T.astype(BF16)

    def begin_z(step, _):
        to_fs(lax.rem(fs_place + step, fs_count), fs_place).start()
        return 0

    lax.fori_loop(1, fs_count, begin_z, 0)
    own_z = pltpu.make_async_copy(
        reduced.at[columns(fs_place, seg), :], got_ref.at[columns(fs_place, seg), :], local_z
    )
    own_z.start()
    tail.start_all()

    to_near.wait_send()
    to_pair.wait_send()
    to_far.wait_send()

    def end_z(step, _):
        place = lax.rem(fs_place + step, fs_count)
        to_fs(place, place).wait_recv()
        to_fs(place, place).wait_send()
        return 0

    lax.fori_loop(1, fs_count, end_z, 0)
    own_z.wait()
    own_in.wait()
    own_out.start()

    def end_sums(step, _):
        place = lax.rem(sp_place + step, sp_count)
        to_owner(place, place).wait_recv()
        to_owner(place, place).wait_send()
        return 0

    lax.fori_loop(1, sp_count, end_sums, 0)
    own_out.wait()
    back.finish()
    tail.finish()


def attention_block(length, seg):
    return lax.axis_size("fs") * seg


def attend_grad(
    qkv, cosine, sine, out, lse, grad_attended, normed, weight, sums, back, score_scale
):
    length = qkv.shape[1]
    heads = qkv.shape[0] // (3 * HEAD_DIM)
    sp_count, fs_count = lax.axis_size("sp"), lax.axis_size("fs")
    total = sp_count * fs_count
    seg = length // total
    block = attention_block(length, seg)
    wide = heads * HEAD_DIM
    width = normed.shape[1]
    tail = (total, width // total, -(-3 * wide // LANES) * LANES)
    sp_sems = pltpu.SemaphoreType.DMA((sp_count,))
    fs_sems = pltpu.SemaphoreType.DMA((fs_count,))
    return pl.pallas_call(
        functools.partial(attend_grad_kernel, block, score_scale),
        in_specs=[VMEM_WHOLE] * 8 + [IN_PLACE] * 2,
        out_specs=[IN_PLACE] * 4,
        out_shape=[
            jax.ShapeDtypeStruct((block, width), BF16),
            jax.ShapeDtypeStruct(sums.shape, BF16),
            jax.ShapeDtypeStruct(back.shape, BF16),
            jax.ShapeDtypeStruct(tail, BF16),
        ],
        scratch_shapes=[
            pltpu.VMEM((3 * wide, length), BF16),
            pltpu.VMEM((width, block), BF16),
            pltpu.VMEM((width, block), BF16),
            pltpu.VMEM((width, block), BF16),
            pltpu.VMEM((width, block), BF16),
            pltpu.VMEM((width, block), BF16),
            pltpu.VMEM((width, block), BF16),
            pltpu.VMEM((width, block), F32),
            pltpu.VMEM((block, width), BF16),
            pltpu.VMEM((wide, length), BF16),
            pltpu.VMEM((wide, length), BF16),
            pltpu.VMEM((heads, length, HEAD_DIM), BF16),
            pltpu.VMEM((wide, length), BF16),
            pltpu.VMEM((heads, length, HEAD_DIM), BF16),
            pltpu.VMEM((heads, length, HEAD_DIM), BF16),
            pltpu.VMEM((heads, length, HEAD_DIM), BF16),
            pltpu.VMEM((heads, 1, length), F32),
            pltpu.VMEM((wide, length), F32),
            pltpu.VMEM((heads, length, HEAD_DIM), F32),
            pltpu.VMEM((heads, length, HEAD_DIM), F32),
            pltpu.VMEM((heads, sp_count * (sp_count + 1) // 2, block, block), BF16),
            pltpu.VMEM((3 * wide, width), F32),
            pltpu.VMEM(tail, BF16),
            pltpu.VMEM(sums.shape[1:], BF16),
        ]
        + swap_semaphores(total)
        + [pltpu.SemaphoreType.DMA((2, 3)), fs_sems, fs_sems, pltpu.SemaphoreType.DMA]
        + [sp_sems, sp_sems, pair_semaphores()]
        + swap_semaphores(total)
        + swap_semaphores(total),
        compiler_params=remote_params(2),
        cost_estimate=pl.CostEstimate(
            flops=60_000_000_000, bytes_accessed=8_000_000, transcendentals=0
        ),
        name="attend_grad",
    )(qkv, cosine, sine, out, lse, grad_attended, normed, weight, sums, back)


def slope_of(gate_val, sigmoid):
    return sigmoid * (1.0 + gate_val * (1.0 - sigmoid))


def dispatch_kernel(
    x_ref,
    g_ref,
    gate_ref,
    up_ref,
    down_ref,
    rows_ref,
    note_ref,
    crossed_ref,
    y_ref,
    gx_ref,
    grads_ref,
    got_ref,
    got_note_ref,
    full_ref,
    x_feat,
    gate_stage,
    up_stage,
    down_stage,
    send,
    recv,
    local,
    send_note,
    recv_note,
    local_note,
    dp_send,
    dp_recv,
    stage_sem,
):
    step = pl.program_id(0)
    tiles = pl.num_programs(0)
    total = rows_ref.shape[0]
    width = x_ref.shape[1]
    own_tile = gate_ref.shape[1] // (width // total) * LANES
    rows = Swap(
        lambda place: rows_ref.at[place], lambda place: got_ref.at[place], send, recv, local
    )
    notes = Swap(
        lambda place: note_ref.at[place],
        lambda place: got_note_ref.at[place],
        send_note,
        recv_note,
        local_note,
    )
    share = sharing(full_ref, dp_send, dp_recv)

    def to_grads(index):
        turn = lax.rem(index, 2)
        high = gate_stage.shape[2]
        weight_rows = grads_ref.shape[1] // 3
        owners, lane_rows = down_stage.shape[1], down_stage.shape[2]
        return [
            pltpu.make_async_copy(
                gate_stage.at[turn], grads_ref.at[:, columns(index, high)], stage_sem.at[0, turn]
            ),
            pltpu.make_async_copy(
                up_stage.at[turn],
                grads_ref.at[
                    :, pl.ds(pl.multiple_of(weight_rows + index * high, high), high)
                ],
                stage_sem.at[1, turn],
            ),
            pltpu.make_async_copy(
                down_stage.at[turn],
                grads_ref.at[
                    pl.ds(index * owners, owners), pl.ds(2 * weight_rows, lane_rows)
                ],
                stage_sem.at[2, turn],
            ),
        ]

    @pl.when(step == 0)
    def _():
        greet_places()
        greet_dp()
        x_feat[...] = x_ref[...].T
        y_ref[...] = jnp.zeros_like(y_ref)
        gx_ref[...] = jnp.zeros_like(gx_ref)
        await_places(1)
        notes.start_all()
        rows.start_all()
        share.start_share()

    own_gate = from_lane_blocks(gate_ref, width // total)
    own_up = from_lane_blocks(up_ref, width // total)
    own_down = from_lane_blocks(down_ref, LANES * down_ref.shape[1] // width)
    gate_val = dot32(x_ref[...], own_gate)
    up_val = dot32(x_ref[...], own_up)
    sigmoid = jax.nn.sigmoid(gate_val)
    swished = gate_val * sigmoid
    hidden = swished * up_val
    hidden_low = hidden.astype(BF16)
    grad_hidden = dot_nt(g_ref[...], own_down)
    gate_part = (grad_hidden * up_val * slope_of(gate_val, sigmoid)).astype(BF16)
    up_part = (grad_hidden * swished).astype(BF16)
    y_ref[...] += dot32(hidden_low, own_down)
    gx_ref[...] += dot_nt(gate_part, own_gate) + dot_nt(up_part, own_up)
    ddown = dot32(hidden.T.astype(BF16), g_ref[...]).astype(BF16)
    dgate = dot32(x_feat[...], gate_part).astype(BF16)
    dup = dot32(x_feat[...], up_part).astype(BF16)
    turn = lax.rem(step, 2)

    @pl.when(step >= 2)
    def _():
        for copy in to_grads(step - 2):
            copy.wait()

    shard = width // total
    for part in range(own_tile // LANES):
        lanes_here = slice(part * LANES, (part + 1) * LANES)
        rows_here = slice(part * shard, (part + 1) * shard)
        gate_stage[turn, :, rows_here, :] = dgate[:, lanes_here].reshape(total, shard, LANES)
        up_stage[turn, :, rows_here, :] = dup[:, lanes_here].reshape(total, shard, LANES)
    owners, owned = down_stage.shape[1], own_tile // down_stage.shape[1]
    for part in range(width // LANES):
        down_stage[turn, :, part * owned : (part + 1) * owned, :] = ddown[
            :, part * LANES : (part + 1) * LANES
        ].reshape(owners, owned, LANES)
    for copy in to_grads(step):
        copy.start()

    @pl.when(step == tiles - 1)
    def _():
        for index in (tiles - 2, tiles - 1):
            for copy in to_grads(index):
                copy.wait()
        notes.finish()
        rows.finish()
        share.finish_share()


def dispatch(own_x, own_g, own_pack, sent, note, crossed):
    total, cap, width = sent.shape
    own_rows = own_pack.shape[1] // 3
    tiles = own_rows * total * LANES // width // 256
    own_count = own_x.shape[0]
    high = own_rows // tiles
    owners = total // tiles
    whole = pl.BlockSpec((own_count, width), lambda i: (0, 0), pipeline_mode=pl.Buffered(1))
    return pl.pallas_call(
        dispatch_kernel,
        grid=(tiles,),
        in_specs=[
            whole,
            whole,
            pl.BlockSpec((total, high, LANES), lambda i: (0, i, 0)),
            pl.BlockSpec((total, high, LANES), lambda i: (0, tiles + i, 0)),
            pl.BlockSpec((owners, own_rows, LANES), lambda i: (i, 2, 0)),
        ]
        + [IN_PLACE] * 3,
        out_specs=[whole, whole] + [IN_PLACE] * 4,
        out_shape=[jax.ShapeDtypeStruct((own_count, width), F32)] * 2
        + [
            jax.ShapeDtypeStruct(array.shape, array.dtype)
            for array in (own_pack, sent, note, crossed)
        ],
        input_output_aliases={7: 5},
        scratch_shapes=[
            pltpu.VMEM((width, own_count), BF16),
            pltpu.VMEM((2, total, high, LANES), BF16),
            pltpu.VMEM((2, total, high, LANES), BF16),
            pltpu.VMEM((2, owners, own_rows, LANES), BF16),
        ]
        + swap_semaphores(total)
        + swap_semaphores(total)
        + share_scratch()
        + [pltpu.SemaphoreType.DMA((3, 2))],
        compiler_params=remote_params(3),
        cost_estimate=pl.CostEstimate(
            flops=40_000_000_000, bytes_accessed=20_000_000, transcendentals=0
        ),
        name="dispatch",
    )(own_x, own_g, own_pack, own_pack, own_pack, sent, note, crossed)


def from_lane_blocks(ref, rows):
    owners, high, lanes = ref.shape
    return jnp.concatenate(
        [
            ref[:, part * rows : (part + 1) * rows, :].reshape(owners * rows, lanes)
            for part in range(high // rows)
        ],
        axis=1,
    )


def to_lane_blocks(matrix):
    rows, wide = matrix.shape
    blocks = jnp.transpose(matrix.reshape(rows, wide // LANES, LANES), (1, 0, 2))
    return blocks.reshape(rows * wide // LANES, LANES)


def expert_kernel(
    x_ref,
    c_ref,
    note_ref,
    gate_ref,
    up_ref,
    down_ref,
    y_ref,
    dgate_ref,
    dup_ref,
    dup_late_ref,
    sum_ref,
    other_up_ref,
    got_ref,
    got_note_ref,
    x_feat,
    g_feat,
    gate_of_row,
    acc,
    dots,
    hidden_all,
    gate_all,
    up_all,
    gx_send,
    dots_send,
    ddown_all,
    other_all,
    up_sent,
    send,
    recv,
    local,
    send_note,
    recv_note,
    local_note,
    ddown_send,
    ddown_recv,
    sum_sem,
    half_send,
    half_recv,
):
    step = pl.program_id(0)
    tiles = pl.num_programs(0) // 2
    total, cap, width = gx_send.shape
    tile = hidden_all.shape[2]
    lanes = dots.shape[1]
    rows = Swap(
        lambda place: gx_send.at[place], lambda place: got_ref.at[place], send, recv, local
    )
    notes = Swap(
        lambda place: dots_send.at[place],
        lambda place: got_note_ref.at[place],
        send_note,
        recv_note,
        local_note,
    )

    def to_dp(index):
        return pltpu.make_async_remote_copy(
            src_ref=ddown_all.at[index],
            dst_ref=other_all.at[index],
            send_sem=ddown_send.at[index],
            recv_sem=ddown_recv.at[index],
            device_id={"dp": 1 - lax.axis_index("dp")},
            device_id_type=pl.DeviceIdType.MESH,
        )

    def up_to_dp(index):
        return pltpu.make_async_remote_copy(
            src_ref=up_sent.at[index],
            dst_ref=other_up_ref.at[:, columns(index, tile)],
            send_sem=half_send.at[index],
            recv_sem=half_recv.at[index],
            device_id={"dp": 1 - lax.axis_index("dp")},
            device_id_type=pl.DeviceIdType.MESH,
        )

    def block(place):
        return slice(place * cap, (place + 1) * cap)

    @pl.when(step == 0)
    def _():
        greet_places()
        greet_dp()
        x_feat[...] = x_ref[...].T
        for place in range(total):
            gate_of_row[block(place), :] = jnp.broadcast_to(
                note_ref[place].T[:cap, 0:1], (cap, lanes)
            )
        grads = gate_of_row[:, 0:1] * c_ref[...].astype(F32)
        g_feat[...] = grads.astype(BF16).T
        acc[...] = jnp.zeros_like(acc)
        dots[...] = jnp.zeros_like(dots)
        await_places(1)

    @pl.when(step < tiles)
    def _():
        gate_val = dot32(x_ref[...], gate_ref[...])
        up_val = dot32(x_ref[...], up_ref[...])
        sigmoid = jax.nn.sigmoid(gate_val)
        swished = gate_val * sigmoid
        hidden = (swished * up_val).astype(BF16)
        reach = dot32(c_ref[...], down_ref[...])
        product = hidden.astype(F32) * reach
        for part in range(tile // lanes):
            dots[...] += product[:, part * lanes : (part + 1) * lanes]
        grad_hidden = gate_of_row[:, 0:1] * reach
        gate_part = (grad_hidden * up_val * slope_of(gate_val, sigmoid)).astype(BF16)
        up_part = (grad_hidden * swished).astype(BF16)
        acc[...] += dot_nt(gate_part, gate_ref[...]) + dot_nt(up_part, up_ref[...])
        hidden_all[step] = hidden
        gate_all[step] = gate_part
        up_all[step] = up_part
        ddown = dot32(g_feat[...], hidden).astype(BF16)
        ddown_all[step] = ddown
        to_dp(step).start()

    @pl.when(step == tiles - 1)
    def _():
        for place in range(total):
            gx_send[place] = acc[block(place), :].astype(BF16)
            dots_send[place, 0:1, :cap] = jnp.sum(dots[block(place), :].T, axis=0, keepdims=True)
        acc[...] = jnp.zeros_like(acc)
        rows.start_all()
        notes.start_all()

    @pl.when(step >= tiles)
    def _():
        here = step - tiles
        hidden = hidden_all[here]
        acc[...] += dot_nt(hidden, down_ref[...])
        dgate_ref[...] = dot32(x_feat[...], gate_all[here]).astype(BF16)
        dup = dot32(x_feat[...], up_all[here]).astype(BF16)

        @pl.when(here >= tiles // 2)
        def _():
            dup_late_ref[...] = dup

        @pl.when(here < tiles // 2)
        def _():
            dup_ref[...] = dup
            up_sent[here] = dup
            up_to_dp(here).start()

    @pl.when(step == 2 * tiles - 1)
    def _():
        for place in range(total):
            y_ref[place] = (gate_of_row[block(place), 0:1] * acc[block(place), :]).astype(BF16)

        def out(index):
            return pltpu.make_async_copy(
                other_all.at[index], sum_ref.at[:, columns(index, tile)], sum_sem.at[index]
            )

        def add(index, _):
            to_dp(index).wait()
            total = ddown_all[index].astype(F32) + other_all[index].astype(F32)
            other_all[index] = total.astype(BF16)
            out(index).start()
            return 0

        lax.fori_loop(0, tiles, add, 0)
        rows.finish()
        notes.finish()

        def end(index, _):
            out(index).wait()
            return 0

        lax.fori_loop(0, tiles, end, 0)

        def end_half(index, _):
            up_to_dp(index).wait()
            return 0

        lax.fori_loop(0, tiles // 2, end_half, 0)


def expert_pass(rows, cots, note, gate, up, down):
    total, cap, width = rows.shape
    count = total * cap
    hidden = gate.shape[1]
    tile = 256
    tiles = hidden // tile
    lanes = note.shape[2]
    once = pl.Buffered(1)
    whole = pl.BlockSpec((count, width), lambda i: (0, 0), pipeline_mode=once)
    whole_note = pl.BlockSpec(note.shape, lambda i: (0, 0, 0), pipeline_mode=once)
    early = pl.BlockSpec((width, tile), lambda i: (0, jnp.minimum(i, tiles - 1)))
    both = pl.BlockSpec((width, tile), lambda i: (0, lax.rem(i, tiles)))
    late = pl.BlockSpec((width, tile), lambda i: (0, jnp.clip(i - tiles, 0, tiles - 1)))
    half = tiles // 2
    late_first = pl.BlockSpec((width, tile), lambda i: (0, jnp.clip(i - tiles, 0, half - 1)))
    late_last = pl.BlockSpec((width, tile), lambda i: (0, jnp.clip(i - tiles - half, 0, half - 1)))
    return pl.pallas_call(
        expert_kernel,
        grid=(2 * tiles,),
        in_specs=[whole, whole, whole_note, early, early, both],
        out_specs=[pl.BlockSpec(rows.shape, lambda i: (0, 0, 0), pipeline_mode=once)]
        + [late, late_first, late_last]
        + [IN_PLACE] * 4,
        out_shape=[jax.ShapeDtypeStruct(rows.shape, BF16)]
        + [jax.ShapeDtypeStruct((width, hidden), BF16)]
        + [jax.ShapeDtypeStruct((width, hidden // 2), BF16)] * 2
        + [
            jax.ShapeDtypeStruct((width, hidden), BF16),
            jax.ShapeDtypeStruct((width, hidden // 2), BF16),
            jax.ShapeDtypeStruct(rows.shape, BF16),
            jax.ShapeDtypeStruct(note.shape, F32),
        ],
        scratch_shapes=[
            pltpu.VMEM((width, count), BF16),
            pltpu.VMEM((width, count), BF16),
            pltpu.VMEM((count, lanes), F32),
            pltpu.VMEM((count, width), F32),
            pltpu.VMEM((count, lanes), F32),
            pltpu.VMEM((tiles, count, tile), BF16),
            pltpu.VMEM((tiles, count, tile), BF16),
            pltpu.VMEM((tiles, count, tile), BF16),
            pltpu.VMEM(rows.shape, BF16),
            pltpu.VMEM(note.shape, F32),
            pltpu.VMEM((tiles, width, tile), BF16),
            pltpu.VMEM((tiles, width, tile), BF16),
            pltpu.VMEM((tiles // 2, width, tile), BF16),
        ]
        + swap_semaphores(total)
        + swap_semaphores(total)
        + [
            pltpu.SemaphoreType.DMA((tiles,)),
            pltpu.SemaphoreType.DMA((tiles,)),
            pltpu.SemaphoreType.DMA((tiles,)),
            pltpu.SemaphoreType.DMA((tiles // 2,)),
            pltpu.SemaphoreType.DMA((tiles // 2,)),
        ],
        compiler_params=remote_params(4),
        cost_estimate=pl.CostEstimate(
            flops=80_000_000_000, bytes_accessed=30_000_000, transcendentals=0
        ),
        name="expert_pass",
    )(
        rows.reshape(count, width),
        cots.reshape(count, width),
        note,
        gate,
        up,
        down,
    )


def swap_sum(value, axis):
    if lax.axis_size(axis) == 2:
        other = lax.ppermute(value, axis, [(0, 1), (1, 0)])
        return value.astype(F32) + other.astype(F32)
    return lax.psum(value, axis).astype(F32)


def exchange(chunks):
    return lax.all_to_all(chunks, ("sp", "fs"), split_axis=0, concat_axis=0, tiled=True)


def per_device_split(
    tokens,
    expert_ids,
    fill_order,
    attention_gain,
    query_weight,
    key_weight,
    value_weight,
    output_weight,
    mixer_gain,
    router_weight,
    shared_gate,
    shared_up,
    shared_down,
    expert_gate,
    expert_up,
    expert_down,
    cotangent,
):
    seq_count, seg_rows, width = tokens.shape
    token_count = seq_count * seg_rows
    fs_count = lax.axis_size("fs")
    sp_count = lax.axis_size("sp")
    place_count = fs_count * sp_count
    local_heads = HEADS // sp_count
    flat_width = local_heads * HEAD_DIM
    score_scale = HEAD_DIM ** (-0.5)
    length = place_count * seg_rows
    shard_rows = query_weight.shape[0]
    qkv_width = 3 * flat_width

    cot_rows = cotangent.reshape(token_count, width)
    small = jnp.concatenate(
        [
            attention_gain[:, None],
            mixer_gain[:, None],
            router_weight,
            jnp.zeros((shard_rows, LANES - 2 - EXPERTS), BF16),
        ],
        axis=1,
    )
    def gather_all(shard):
        return lax.all_gather(shard, ("sp", "fs"), axis=0, tiled=True)

    half = HEAD_DIM // 2
    frequency = 10000.0 ** (-jnp.arange(half, dtype=F32) / half)
    angles = frequency[:, None] * jnp.arange(length, dtype=jnp.int32).astype(F32)[None, :]
    cosine, sine = jnp.cos(angles), jnp.sin(angles)
    output_full = gather_all(output_weight)
    shared_pack = gather_all(
        jnp.concatenate(
            [to_lane_blocks(shared_gate), to_lane_blocks(shared_up), to_lane_blocks(shared_down)]
        )[None]
    )
    slot_total = CAP * EXPERTS
    (
        slots,
        taking,
        normed_seq,
        own_pack,
        qkv,
        out_heads,
        lse,
        attended,
        arrived_cots,
        gate_own,
        up_own,
        down_crossed,
    ) = front(
        tokens,
        query_weight,
        key_weight,
        value_weight,
        small,
        expert_ids.reshape(token_count, TOPK).T,
        fill_order.reshape(1, token_count),
        cot_rows,
        cosine,
        sine,
        expert_gate,
        expert_up,
        expert_down,
        score_scale,
    )
    qkv_own = own_pack[:, :qkv_width]
    gain_one = own_pack[:, qkv_width].astype(F32)
    gain_two = own_pack[:, qkv_width + 1].astype(F32)
    router_full = own_pack[:, qkv_width + 2 : qkv_width + 2 + EXPERTS]
    residual = tokens.astype(F32).reshape(token_count, width)

    def outer(left, right):
        return lax.dot_general(left, right, (((0,), (0,)), ((), ())), preferred_element_type=F32)

    middle = residual + outer(attended, output_full)
    mixed_in = norm_apply(middle, gain_two).astype(BF16)

    logits = dot32(mixed_in, router_full)
    def gate_values(raw_logits):
        shifted = jnp.exp(raw_logits - jnp.max(raw_logits, axis=-1, keepdims=True))
        router_probs = shifted / jnp.sum(shifted, axis=-1, keepdims=True)
        picked = jnp.sum(router_probs[:, None, :] * onehot_float, axis=2)
        return picked / jnp.sum(picked, axis=1, keepdims=True)

    choices = expert_ids.reshape(token_count, TOPK)
    expert_onehot = choices[:, :, None] == jnp.arange(EXPERTS, dtype=jnp.int32)[None, None, :]
    onehot_float = expert_onehot.astype(F32)
    gate_weights, gate_pull = jax.vjp(gate_values, logits)
    slot_ids = jnp.arange(slot_total, dtype=jnp.int32)
    takes_a = slot_ids[:, None] == slots[0][None, :]
    takes_b = slot_ids[:, None] == slots[1][None, :]

    gate_of_slot = jnp.sum(
        jnp.where(takes_a, gate_weights[None, :, 0], 0.0)
        + jnp.where(takes_b, gate_weights[None, :, 1], 0.0),
        axis=1,
    )
    outgoing = dot32(taking, mixed_in).astype(BF16)
    note = jnp.pad(
        gate_of_slot.reshape(place_count, 1, CAP), ((0, 0), (0, NOTE_ROWS - 1), (0, LANES - CAP))
    )
    shared_out, grad_mixed_shared, grad_shared, rows, notes, down_own = dispatch(
        mixed_in,
        cot_rows,
        shared_pack,
        outgoing.reshape(place_count, CAP, width),
        note,
        down_crossed,
    )
    grad_shared = lax.psum_scatter(grad_shared, ("sp", "fs"), scatter_dimension=0)
    expert_out, dgate, dup, dup_late, sum_down, other_up_half, grad_returned, dots = expert_pass(
        rows,
        arrived_cots,
        notes,
        gate_own.reshape(width, -1),
        up_own.reshape(width, -1),
        down_own.reshape(width, -1),
    )
    grad_returned = grad_returned.reshape(slot_total, width)
    dots = dots[:, 0, :CAP].reshape(slot_total)

    def to_dp(value):
        return lax.ppermute(value, "dp", [(0, 1), (1, 0)])

    def sum_of(grad, other):
        total = (grad.astype(F32) + other.astype(F32)).astype(BF16)
        return total.reshape(sp_count, width // sp_count, grad.shape[1])

    def spread(parts):
        return lax.all_to_all(parts, "sp", split_axis=0, concat_axis=0, tiled=True).astype(F32)

    other_gate, other_up = to_dp(dgate), to_dp(dup_late)

    grad_result = cot_rows.astype(F32)
    grad_gates = jnp.stack(
        [
            jnp.sum(jnp.where(slots[j][:, None] == slot_ids[None, :], dots[None, :], 0.0), axis=1)
            for j in range(TOPK)
        ],
        axis=1,
    )
    (grad_logits,) = gate_pull(grad_gates)
    grad_logits = grad_logits.astype(BF16)
    grad_router = outer(mixed_in, grad_logits)
    grad_mixed = (
        outer(taking, grad_returned) + dot_nt(grad_logits, router_full) + grad_mixed_shared
    )
    _, norm_two_pull = jax.vjp(norm_apply, middle, gain_two)
    grad_middle_part, grad_gain_two = norm_two_pull(grad_mixed)
    grad_middle = grad_result + grad_middle_part
    grad_proj = grad_middle.astype(BF16)
    grad_output_matrix = dot32(attended, grad_proj)
    grad_attended = dot_nt(output_full, grad_proj).astype(BF16)
    dense = jnp.concatenate(
        [
            grad_output_matrix.astype(BF16),
            grad_router.astype(BF16),
            jnp.pad(grad_gain_two[:, None], ((0, 0), (0, LANES - EXPERTS - 1))).astype(BF16),
        ],
        axis=1,
    )
    grad_normed, sum_down, returned, tail = attend_grad(
        qkv,
        cosine,
        sine,
        out_heads,
        lse,
        grad_attended,
        normed_seq,
        qkv_own,
        sum_down.reshape(sp_count, width // sp_count, -1),
        expert_out,
        score_scale,
    )
    other_gate, other_up, grad_shared, grad_normed = lax.optimization_barrier(
        (other_gate, other_up, grad_shared, grad_normed)
    )
    dense = lax.psum_scatter(dense, ("sp", "fs"), scatter_dimension=0, tiled=True)
    parts_up, tail, sum_down, returned, grad_normed = lax.optimization_barrier(
        (
            sum_of(
                jnp.concatenate([dup, dup_late], axis=1),
                jnp.concatenate([other_up_half, other_up], axis=1),
            ),
            tail,
            sum_down,
            returned,
            grad_normed,
        )
    )
    sum_up = spread(parts_up)
    sum_gate = spread(sum_of(dgate, other_gate))
    dense, sum_gate = lax.optimization_barrier((dense, sum_gate))
    sum_down = sum_down.astype(F32)
    output = (middle + shared_out + outer(taking, returned.reshape(slot_total, width))).astype(BF16)
    grad_normed = grad_normed.astype(F32)
    _, norm_one_pull = jax.vjp(lambda values: norm_apply(values, gain_one), residual)
    (grad_residual_part,) = norm_one_pull(grad_normed)
    grad_tokens = grad_middle + grad_residual_part

    tail = tail.reshape(sp_count, fs_count, shard_rows, tail.shape[2])[:, :, :, :qkv_width]
    tail = jnp.sum(tail.astype(F32), axis=1).astype(BF16)
    sum_dense = swap_sum(dense, "dp")
    sum_shared = swap_sum(grad_shared, "dp")
    sum_tail = swap_sum(tail, "dp")
    sum_qkv = sum_tail.reshape(sp_count, shard_rows, 3, flat_width)
    sum_qkv = jnp.transpose(sum_qkv, (2, 1, 0, 3)).reshape(3, shard_rows, width)
    sum_gain_one = sum(
        jnp.sum(weight.astype(F32) * grad, axis=1)
        for weight, grad in zip((query_weight, key_weight, value_weight), sum_qkv)
    ) / attention_gain.astype(F32)
    weight_rows = grad_shared.shape[0] // 3

    def lane_blocks(flat, high):
        blocks = flat.reshape(-1, high, LANES)
        return jnp.transpose(blocks, (1, 0, 2)).reshape(high, -1)

    sum_shared_gate = lane_blocks(sum_shared[:weight_rows], shard_rows)
    sum_shared_up = lane_blocks(sum_shared[weight_rows : 2 * weight_rows], shard_rows)
    sum_shared_down = lane_blocks(sum_shared[2 * weight_rows :], shared_down.shape[0])
    return (
        output.reshape(tokens.shape),
        grad_tokens.reshape(tokens.shape),
        sum_gain_one,
        sum_qkv[0],
        sum_qkv[1],
        sum_qkv[2],
        sum_dense[:, :width],
        sum_dense[:, width + EXPERTS],
        sum_dense[:, width : width + EXPERTS],
        sum_shared_gate,
        sum_shared_up,
        sum_shared_down,
        sum_gate,
        sum_up,
        sum_down,
    )


def per_device_any(*shards):
    fs_count, sp_count = lax.axis_size("fs"), lax.axis_size("sp")
    same = shards[0].shape[0] == fs_count and EXPERTS == 4 * fs_count
    if same and sp_count == 4 and lax.axis_size("dp") == 2:
        return per_device_split(*shards)
    return per_device(*shards)


def solution(mesh):
    placed = (
        P("dp", ("sp", "fs"), None),
        P("dp", ("sp", "fs"), None),
        P("dp", ("sp", "fs")),
        P(("sp", "fs")),
        P(("sp", "fs"), None),
        P(("sp", "fs"), None),
        P(("sp", "fs"), None),
        P(("sp", "fs"), None),
        P(("sp", "fs")),
        P(("sp", "fs"), None),
        P(("sp", "fs"), None),
        P(("sp", "fs"), None),
        P(("sp", "fs"), None),
        P("fs", "sp", None),
        P("fs", "sp", None),
        P("fs", "sp", None),
        P("dp", ("sp", "fs"), None),
    )
    return jax.shard_map(
        per_device_any,
        mesh=mesh,
        in_specs=placed,
        out_specs=(
            P("dp", ("sp", "fs"), None),
            P("dp", ("sp", "fs"), None),
            P(("sp", "fs")),
            P(("sp", "fs"), None),
            P(("sp", "fs"), None),
            P(("sp", "fs"), None),
            P(("sp", "fs"), None),
            P(("sp", "fs")),
            P(("sp", "fs"), None),
            P(("sp", "fs"), None),
            P(("sp", "fs"), None),
            P(("sp", "fs"), None),
            P("fs", "sp", None),
            P("fs", "sp", None),
            P("fs", "sp", None),
        ),
        check_vma=False,
    )
```
